32 devices in a mesh: batch: 8 (over y, x, core), head: 4 (over z).
Axes of the slice: x: 2, y: 2, z: 4, core: 2. Of those that a mesh axis runs over, the one named last changes fastest.
Arguments:
- layer_input: bfloat16 [16, 512, 768], P('batch', 'head'), may hold values from -6 to 6
- memory: bfloat16 [16, 512, 768], P('batch', 'head'), may hold values from -6 to 6
- dec_lengths: int32 [16], P('batch'), may hold values from 1 to 512, as said below
- enc_lengths: int32 [16], P('batch'), may hold values from 1 to 512, as said below
- self_gain: bfloat16 [768], replicated, may hold values from 0.099609375 to 1.8984375
- self_query: bfloat16 [768, 768], P(None, 'head'), may hold values from -0.0546875 to 0.0546875
- self_key_value: bfloat16 [2, 768, 768], P(None, None, 'head'), may hold values from -0.21875 to 0.21875
- self_out: bfloat16 [768, 768], P('head'), may hold values from -0.875 to 0.875
- rel_bias: bfloat16 [32, 12], P(None, 'head'), may hold values from -4 to 4
- cross_gain: bfloat16 [768], replicated, may hold values from 0.099609375 to 1.8984375
- cross_query: bfloat16 [768, 768], P(None, 'head'), may hold values from -0.0546875 to 0.0546875
- cross_key_value: bfloat16 [2, 768, 768], P(None, None, 'head'), may hold values from -0.21875 to 0.21875
- cross_out: bfloat16 [768, 768], P('head'), may hold values from -0.875 to 0.875
- feed_gain: bfloat16 [768], replicated, may hold values from 0.099609375 to 1.8984375
- feed_in: bfloat16 [2, 768, 2048], replicated, may hold values from -0.21875 to 0.21875
- feed_out: bfloat16 [2048, 768], replicated, may hold values from -0.125 to 0.125
- out_cotangent: bfloat16 [16, 512, 768], P('batch', 'head'), may hold values from -6 to 6
Outputs:
- layer_output: bfloat16 [16, 512, 768], P('batch', 'head')
- input_grad: float32 [16, 512, 768], P('batch', 'head')
- memory_grad: float32 [16, 512, 768], P('batch', 'head')
- self_gain_grad: float32 [768], replicated
- self_query_grad: float32 [768, 768], P('batch', 'head')
- self_key_value_grad: float32 [2, 768, 768], P(None, 'batch', 'head')
- self_out_grad: float32 [768, 768], P('head', 'batch')
- rel_bias_grad: float32 [32, 12], P(None, 'head')
- cross_gain_grad: float32 [768], replicated
- cross_query_grad: float32 [768, 768], P('batch', 'head')
- cross_key_value_grad: float32 [2, 768, 768], P(None, 'batch', 'head')
- cross_out_grad: float32 [768, 768], P('head', 'batch')
- feed_gain_grad: float32 [768], replicated
- feed_in_grad: float32 [2, 768, 2048], P(None, 'batch', 'head')
- feed_out_grad: float32 [2048, 768], P('head', 'batch')
The draws below stay inside these ranges and needn't reach their ends.
Inputs may be any that keep to these rules, and one draw needn't show every extreme that they name: `dec_lengths`: some sequence has exactly 512 decoder positions. `enc_lengths`: some sequence has exactly 512 encoder positions.
All inputs are finite; a program needn't handle non-finite values.
Results may differ from the reference program's by a relative error of at most 0.023.
The reference program's roundings to bfloat16 on the way count: a program that leaves them out, or rounds other values in their place, can miss the bound.
Values may be sent and summed in bfloat16 or wider, within the bound.
A program may use at most 256 MiB of HBM per device.

```python
import math
import jax
import jax.numpy as jnp
from jax import lax

D = 768
FF = 2048
H = 12
NB = 32
MAX_DIST = 128
LEN = 512
ELEN = 512
SEQS = 16
HD = 768


def ragged(key, seq_total, longest):
    octave_key, offset_key, place_key = jax.random.split(key, 3)
    shift_amount = jax.random.randint(octave_key, (seq_total,), 1, 8)
    base_length = jnp.right_shift(jnp.full((seq_total,), longest, jnp.int32), shift_amount)
    raw_offset = jax.random.randint(offset_key, (seq_total,), 0, longest)
    offset = raw_offset % jnp.maximum(base_length, 1)
    lengths = jnp.maximum(base_length + offset, 1)
    chosen = jax.random.randint(place_key, (), 0, seq_total)
    return jnp.where(jnp.arange(seq_total) == chosen, longest, lengths).astype(jnp.int32)


def draw_dec_lengths(key, part):
    return ragged(jax.random.fold_in(key, 11), SEQS, LEN)


def draw_enc_lengths(key, part):
    return ragged(jax.random.fold_in(key, 23), SEQS, ELEN)


def strengthened(result, own_key, source, target, parts, factor):
    owner, partner = [(jnp.arange(result.shape[dim]) // (result.shape[dim] // parts)).reshape([-1 if axis == dim else 1 for axis in range(result.ndim)]) for dim in (source, target)]
    chosen = jax.random.permutation(own_key, parts)[partner]
    strong = (owner == chosen) | (owner == (partner + parts // 2) % parts)
    return jnp.where(strong, factor * result, result)


def levels(key, extent, shards, smallest, top_value):
    factor_of, own = 1.0, jax.random.fold_in(key, 6)
    for position, parts in shards:
        draws = jnp.exp(jax.random.uniform(jax.random.fold_in(own, position), (parts,), jnp.float32, smallest / len(shards), top_value / len(shards)))
        factor_of = factor_of * jnp.repeat(draws, extent[position] // parts).reshape([-1 if axis == position else 1 for axis in range(len(extent))])
    return factor_of


def scatter_about(stream_key, dims, deviation, most, cuts=(), dtype=jnp.bfloat16):
    level = levels(stream_key, dims, cuts, -0.22, 0.18) if cuts else 1.0
    array = jax.random.normal(stream_key, dims, jnp.float32) * deviation * level
    return jnp.minimum(jnp.maximum(array, -most), most).astype(dtype)


def gaussian_with(key, extent, spread, bound, cuts, heavy, kind=jnp.bfloat16):
    values = spread * jax.random.normal(key, extent, jnp.float32)
    if cuts:
        values = values * levels(key, extent, cuts, -0.22, 0.18)
    return jnp.clip(strengthened(values, jax.random.fold_in(key, 3), *heavy), -bound, bound).astype(kind)


def setup_inputs(seed: int = 0) -> dict:
    key_of = jax.random.split(jax.random.key(seed), 18)
    layer_input = gaussian_with(key_of[0], (SEQS, LEN, D), 1.0, 6.0, ((0, 8), (1, 4)), (0, 2, 8, 2.0))
    memory = gaussian_with(key_of[1], (SEQS, ELEN, D), 1.0, 6.0, ((0, 8), (1, 4)), (0, 2, 8, 2.0))
    dec_lengths = draw_dec_lengths(jax.random.fold_in(key_of[17], 71), 0)
    enc_lengths = draw_enc_lengths(jax.random.fold_in(key_of[17], 71), 0)
    self_gain = jnp.clip(1.0 + 0.18 * jax.random.normal(key_of[4], (D,), jnp.float32), 0.099609375, 1.8984375).astype(jnp.bfloat16)
    self_query = scatter_about(key_of[5], (D, HD), (16 * D) ** -0.5, 0.0546875, ((1, 4),))
    self_key_value = scatter_about(key_of[6], (2, D, HD), D ** -0.5, 0.21875, ((2, 4),))
    self_out = scatter_about(key_of[7], (HD, D), (HD // 16) ** -0.5, 0.875, ((0, 4),))
    rel_bias = scatter_about(key_of[8], (NB, H), 1.0, 4.0, ((1, 4),))
    cross_gain = jnp.clip(1.0 + 0.18 * jax.random.normal(key_of[9], (D,), jnp.float32), 0.099609375, 1.8984375).astype(jnp.bfloat16)
    cross_query = scatter_about(key_of[10], (D, HD), (16 * D) ** -0.5, 0.0546875, ((1, 4),))
    cross_key_value = scatter_about(key_of[11], (2, D, HD), D ** -0.5, 0.21875, ((2, 4),))
    cross_out = scatter_about(key_of[12], (HD, D), (HD // 16) ** -0.5, 0.875, ((0, 4),))
    feed_gain = jnp.clip(1.0 + 0.18 * jax.random.normal(key_of[13], (D,), jnp.float32), 0.099609375, 1.8984375).astype(jnp.bfloat16)
    feed_in = scatter_about(key_of[14], (2, D, FF), D ** -0.5, 0.21875)
    feed_out = scatter_about(key_of[15], (FF, D), FF ** -0.5, 0.125)
    out_cotangent = scatter_about(key_of[16], (SEQS, LEN, D), 1.0, 6.0, ((0, 8), (1, 4)))
    return dict(layer_input=layer_input, memory=memory, dec_lengths=dec_lengths, enc_lengths=enc_lengths, self_gain=self_gain, self_query=self_query, self_key_value=self_key_value, self_out=self_out, rel_bias=rel_bias, cross_gain=cross_gain, cross_query=cross_query, cross_key_value=cross_key_value, cross_out=cross_out, feed_gain=feed_gain, feed_in=feed_in, feed_out=feed_out, out_cotangent=out_cotangent)


highest = lax.Precision.HIGHEST

@jax.custom_vjp
def low(v):
    return lax.optimization_barrier(v.astype(jnp.bfloat16)).astype(jnp.float32)

@jax.custom_vjp
def low_back(v):
    return v

def low_keep(v):
    return (low(v), None)

def low_pass(kept, grad):
    return (grad,)

def back_keep(v):
    return (v, None)

def back_low(kept, grad):
    return (low(grad),)
low.defvjp(low_keep, low_pass)
low_back.defvjp(back_keep, back_low)

def bucket_edges(num_buckets, max_distance):
    exact_part = num_buckets // 2
    edge_list = []
    for target in range(1, num_buckets - exact_part):
        distance = exact_part
        while math.floor(math.log(distance / exact_part) / math.log(max_distance / exact_part) * (num_buckets - exact_part)) < target:
            distance += 1
        edge_list.append(distance)
    return edge_list

def bucket_of(distance, num_buckets, max_distance):
    exact_part = num_buckets // 2
    counted = jnp.zeros(distance.shape, jnp.int32)
    for edge_value in bucket_edges(num_buckets, max_distance):
        counted = counted + (distance >= edge_value).astype(jnp.int32)
    return jnp.where(distance < exact_part, distance, exact_part + counted).astype(jnp.int32)

def normalize(activations, gain_vector):
    return activations * lax.rsqrt(lax.optimization_barrier(jnp.mean(activations * activations, axis=-1, keepdims=True)) + 1e-06) * gain_vector

def decoder_layer(weights, inputs, encoded, dec_len, enc_len):
    self_gain, self_query, self_key_value, self_out, rel_bias, cross_gain, cross_query, cross_key_value, cross_out, feed_gain, feed_in, feed_out = weights
    length = inputs.shape[1]
    enc_length = encoded.shape[1]
    num_heads = rel_bias.shape[1]
    head_size = self_query.shape[1] // num_heads

    def project(row_block, weight):
        product = jnp.einsum('std,de->ste', row_block, weight, precision=highest)
        return low_back(low(product)).reshape(row_block.shape[0], row_block.shape[1], num_heads, head_size)

    def attention(queries, key_block, value_block, score_bias, keep_mask, weight_out):
        scores = low_back(jnp.einsum('sqhd,skhd->shqk', queries, key_block, precision=highest) + score_bias)
        attn_probs = low(jax.nn.softmax(jnp.where(keep_mask, scores, -1e+30), axis=-1))
        context = jnp.einsum('shqk,skhd->sqhd', attn_probs, value_block, precision=highest)
        context = low_back(low(context.reshape(queries.shape[0], queries.shape[1], num_heads * head_size)))
        return low_back(jnp.einsum('ste,ed->std', context, weight_out, precision=highest))
    positions = jnp.arange(length)
    distance = positions[:, None] - positions[None, :]
    buckets = bucket_of(jnp.maximum(distance, 0), NB, MAX_DIST)
    self_bias = jnp.transpose(rel_bias[buckets], (2, 0, 1))[None]
    self_mask = (distance >= 0)[None, None] & (positions[None, None, None, :] < dec_len[:, None, None, None])
    cross_mask = jnp.arange(enc_length)[None, None, None, :] < enc_len[:, None, None, None]
    normed_one = low(normalize(inputs, self_gain))
    after_self = inputs + attention(project(normed_one, self_query), project(normed_one, self_key_value[0]), project(normed_one, self_key_value[1]), self_bias, self_mask, self_out)
    normed_two = low(normalize(after_self, cross_gain))
    after_cross = after_self + attention(project(normed_two, cross_query), project(encoded, cross_key_value[0]), project(encoded, cross_key_value[1]), 0.0, cross_mask, cross_out)
    normed_three = low(normalize(after_cross, feed_gain))
    gate_part = low_back(jnp.einsum('std,df->stf', normed_three, feed_in[0], precision=highest))
    up_part = low_back(jnp.einsum('std,df->stf', normed_three, feed_in[1], precision=highest))
    hidden = low(jax.nn.gelu(gate_part, approximate=True) * up_part)
    return after_cross + low_back(jnp.einsum('stf,fd->std', hidden, feed_out, precision=highest))

def reference(layer_input, memory, dec_lengths, enc_lengths, self_gain, self_query, self_key_value, self_out, rel_bias, cross_gain, cross_query, cross_key_value, cross_out, feed_gain, feed_in, feed_out, out_cotangent):
    weights = tuple((weight_item.astype(jnp.float32) for weight_item in (self_gain, self_query, self_key_value, self_out, rel_bias, cross_gain, cross_query, cross_key_value, cross_out, feed_gain, feed_in, feed_out)))
    blocks = SEQS // 8
    dec_blocks = dec_lengths.reshape(blocks, 8)
    enc_blocks = enc_lengths.reshape(blocks, 8)

    def forward(weight_set, inputs, encoded):

        def one_block(pieces):
            return jax.checkpoint(decoder_layer)(weight_set, pieces[0], pieces[1], pieces[2], pieces[3])
        outcome = lax.map(one_block, (inputs.reshape(blocks, 8, LEN, D), encoded.reshape(blocks, 8, ELEN, D), dec_blocks, enc_blocks))
        return outcome.reshape(SEQS, LEN, D)
    outcome, pullback = jax.vjp(forward, weights, layer_input.astype(jnp.float32), memory.astype(jnp.float32))
    grad_weights, grad_inputs, grad_memory = pullback(out_cotangent.astype(jnp.float32))
    return (outcome.astype(jnp.bfloat16), grad_inputs, grad_memory, grad_weights[0], grad_weights[1], grad_weights[2], grad_weights[3], grad_weights[4], grad_weights[5], grad_weights[6], grad_weights[7], grad_weights[8], grad_weights[9], grad_weights[10], grad_weights[11])
```

```python
import functools
import math

import jax
import jax.numpy as jnp
from jax import lax
from jax.experimental import pallas as pl
from jax.experimental.pallas import tpu as pltpu
from jax.sharding import PartitionSpec as P

NB = 32
MAX_DIST = 128
NEG = -1e30
VMEM_LIMIT = 56 * 1024 * 1024
F32 = jnp.float32
BF16 = jnp.bfloat16

highest = lax.Precision.HIGHEST


def bucket_edges(num_buckets, max_distance):
    exact_part = num_buckets // 2
    edge_list = []
    for target in range(1, num_buckets - exact_part):
        distance = exact_part
        while (
            math.floor(
                math.log(distance / exact_part)
                / math.log(max_distance / exact_part)
                * (num_buckets - exact_part)
            )
            < target
        ):
            distance += 1
        edge_list.append(distance)
    return edge_list


def bucket_of(distance, num_buckets, max_distance):
    exact_part = num_buckets // 2
    counted = jnp.zeros(distance.shape, jnp.int32)
    for edge_value in bucket_edges(num_buckets, max_distance):
        counted = counted + (distance >= edge_value).astype(jnp.int32)
    return jnp.where(distance < exact_part, distance, exact_part + counted).astype(jnp.int32)


def near_onehot(block):
    distance = block - jnp.arange(2 * block)
    distance = jnp.where(distance < 0, 2 * MAX_DIST, distance)
    return (
        bucket_of(distance, NB, MAX_DIST)[:, None] == jnp.arange(NB)[None, :]
    ).astype(F32)


def nn(a, b):
    return lax.dot_general(a, b, (((1,), (0,)), ((), ())), preferred_element_type=F32)


def nt(a, b):
    return lax.dot_general(a, b, (((1,), (1,)), ((), ())), preferred_element_type=F32)


def tn(a, b):
    return lax.dot_general(a, b, (((0,), (0,)), ((), ())), preferred_element_type=F32)


def rms(v):
    return lax.rsqrt(jnp.mean(v * v, axis=-1, keepdims=True) + 1e-06)


def norm_grads(y, gain, e):
    r = rms(y)
    xhat = y * r
    eg = e * gain
    dy = r * (eg - xhat * jnp.mean(eg * xhat, axis=-1, keepdims=True))
    return dy, jnp.sum(e * xhat, axis=0, keepdims=True)


def padded(v, width):
    extra = width - v.shape[1]
    if extra == 0:
        return v
    return jnp.concatenate([v, jnp.zeros((v.shape[0], extra), v.dtype)], axis=1)


def vmem():
    return pl.BlockSpec(memory_space=pltpu.VMEM)


def smem():
    return pl.BlockSpec(memory_space=pltpu.SMEM)


def params():
    return pltpu.CompilerParams(vmem_limit_bytes=VMEM_LIMIT)


def sds(shape, dtype):
    return jax.ShapeDtypeStruct(shape, dtype)


def bias_kernel(me_ref, w_ref, b_ref, ext_ref):
    heads, block, full = b_ref.shape
    me = me_ref[0]
    start = pl.multiple_of(me * block, block)
    width = 2 * block
    row_i = lax.broadcasted_iota(jnp.int32, (block, width), 0)
    col_i = lax.broadcasted_iota(jnp.int32, (block, width), 1)
    masked = (col_i - row_i) > block
    far = lax.broadcasted_iota(jnp.int32, ext_ref.shape, 1) < start

    def body(head, carry):
        row = w_ref[pl.ds(head, 1), :]
        tile = pltpu.roll(
            jnp.broadcast_to(row, (block, width)), 0, 1, stride=1, stride_axis=0
        )
        ext_ref[...] = jnp.where(far, row[:, width - 1 : width], NEG)
        ext_ref[:, pl.ds(start, width)] = jnp.where(masked, NEG, tile)
        b_ref[head] = ext_ref[:, block:]
        return carry

    lax.fori_loop(0, heads, body, 0)


def bias_tiles(me, table, block, full):
    heads = table.shape[0]
    return pl.pallas_call(
        bias_kernel,
        out_shape=sds((heads, block, full), F32),
        in_specs=[smem(), vmem()],
        out_specs=vmem(),
        scratch_shapes=[pltpu.VMEM((block, full + block), F32)],
        compiler_params=params(),
        name="bias_tiles",
    )(me, table)


def lane_groups(width, group, size):
    lane = lax.broadcasted_iota(jnp.int32, (1, width), 1)
    return [(lane // size) == a for a in range(group)]


def stack_heads(win, lanes):
    return jnp.concatenate([jnp.where(m, win, jnp.zeros_like(win)) for m in lanes], axis=0)


def join_heads(tall, lanes, rows):
    total = jnp.where(lanes[0], tall[:rows], 0.0)
    for a in range(1, len(lanes)):
        total = total + jnp.where(lanes[a], tall[a * rows : (a + 1) * rows], 0.0)
    return total


def forward_kernel(
    biased, group, size, len_ref, nq_ref, nk_ref, res_ref, wq_ref, wkv_ref, wo_ref, gain_ref, *rest
):
    if biased:
        b_ref, *rest = rest
    q_ref, k_ref, v_ref, c_ref, lse_ref, y_ref, n_ref = rest
    shards, rows, pw = q_ref.shape
    seqs = len_ref.shape[0]
    block = rows // seqs
    full = k_ref.shape[1] // seqs
    win = group * size
    lanes = lane_groups(pw, group, size)
    lane128 = lax.broadcasted_iota(jnp.int32, (block, 128), 1)
    key = lax.broadcasted_iota(jnp.int32, (1, full), 1)

    def body(h, carry):
        q_ref[h] = padded(nn(nq_ref[...], wq_ref[h]).astype(BF16), pw)
        kv = nn(nk_ref[...], wkv_ref[h]).astype(BF16)
        k_ref[h] = padded(kv[:, :win], pw)
        v_ref[h] = padded(kv[:, win:], pw)
        for s in range(seqs):
            kw = k_ref[h, s * full : (s + 1) * full, :]
            vw = v_ref[h, s * full : (s + 1) * full, :]
            qcat = stack_heads(q_ref[h, s * block : (s + 1) * block, :], lanes)
            sc = nt(qcat, kw)
            if biased:
                sc = sc + b_ref[pl.ds(h * group, group)].reshape(group * block, full)
            sc = jnp.where(key < len_ref[s], sc, NEG)
            top = jnp.max(sc, axis=-1, keepdims=True)
            e = jnp.exp(sc - top)
            total = jnp.sum(e, axis=-1, keepdims=True)
            p = (e * (1.0 / total)).astype(BF16)
            c = join_heads(nn(p, vw), lanes, block)
            c_ref[h, s * block : (s + 1) * block, :] = c.astype(BF16)
            lse = top + jnp.log(total)
            tile = jnp.zeros((block, 128), F32)
            for a in range(group):
                tile = jnp.where(lane128 == a, lse[a * block : (a + 1) * block], tile)
            lse_ref[h, s] = tile
        return carry

    lax.fori_loop(0, shards, body, 0)
    joined = jnp.concatenate([c_ref[h][:, :win] for h in range(shards)], axis=1)
    y = res_ref[...].astype(F32) + nn(joined, wo_ref[...])
    y_ref[...] = y
    n_ref[...] = (y * rms(y) * gain_ref[...]).astype(BF16)


def attend_forward(lens, nq, nk, res, wq, wkv, wo, gain, bias, group, size):
    rows, width = nq.shape
    shards = wq.shape[0]
    pw = -(-group * size // 128) * 128
    seqs = lens.shape[0]
    args = [lens, nq, nk, res, wq, wkv, wo, gain] + ([bias] if bias is not None else [])
    keys = nk.shape[0]
    flops = 2 * (rows + 2 * keys + rows) * width * width + 4 * rows * keys * width
    return pl.pallas_call(
        functools.partial(forward_kernel, bias is not None, group, size),
        out_shape=[
            sds((shards, rows, pw), BF16),
            sds((shards, keys, pw), BF16),
            sds((shards, keys, pw), BF16),
            sds((shards, rows, pw), BF16),
            sds((shards, seqs, rows // seqs, 128), F32),
            sds((rows, width), F32),
            sds((rows, width), BF16),
        ],
        in_specs=[smem()] + [vmem()] * (len(args) - 1),
        out_specs=[vmem()] * 7,
        compiler_params=params(),
        cost_estimate=pl.CostEstimate(
            flops=flops, bytes_accessed=16 << 20, transcendentals=rows * keys * 6
        ),
        name="attend_forward",
    )(*args)


def backward_kernel(
    biased,
    group,
    size,
    len_ref,
    me_ref,
    nq_ref,
    nk_ref,
    q_ref,
    k_ref,
    v_ref,
    c_ref,
    lse_ref,
    wq_ref,
    wkv_ref,
    wo_ref,
    dy_ref,
    gain_ref,
    *rest,
):
    if biased:
        b_ref, part_ref, gg_ref, w_ref, diag_ref, dc_ref, dq_ref, dkv_ref, acc_ref, nqt_ref, nkt_ref, dat_ref, sum_ref, ext_ref = rest
    else:
        y_ref, part_ref, gg_ref, w_ref, dprev_ref, dc_ref, dq_ref, dkv_ref, acc_ref, nqt_ref, nkt_ref, dat_ref = rest
    shards, rows, pw = q_ref.shape
    seqs = len_ref.shape[0]
    block = rows // seqs
    full = k_ref.shape[1] // seqs
    win = group * size
    lanes = lane_groups(pw, group, size)
    key = lax.broadcasted_iota(jnp.int32, (1, full), 1)
    me = me_ref[0]

    da = dy_ref[...].astype(BF16)
    nqt_ref[...] = nq_ref[...].T
    nkt_ref[...] = nk_ref[...].T
    dat_ref[...] = da.T
    if biased:
        ext_ref[:, :block] = jnp.zeros((block, block), F32)
        start = pl.multiple_of(me * block, block)
        far = lax.broadcasted_iota(jnp.int32, ext_ref.shape, 1) < start
        row8 = lax.broadcasted_iota(jnp.int32, (8, 2 * block), 0)
        lane_near = lax.broadcasted_iota(jnp.int32, (1, 2 * block), 1)

    def body(h, carry):
        wo_h = wo_ref[pl.ds(pl.multiple_of(h * win, size), win), :]
        dc_ref[...] = padded(nt(da, wo_h).astype(BF16), pw)
        for s in range(seqs):
            kw = k_ref[h, s * full : (s + 1) * full, :]
            vw = v_ref[h, s * full : (s + 1) * full, :]
            qcat = stack_heads(q_ref[h, s * block : (s + 1) * block, :], lanes)
            dcat = stack_heads(dc_ref[s * block : (s + 1) * block, :], lanes)
            sc = nt(qcat, kw)
            if biased:
                sc = sc + b_ref[pl.ds(h * group, group)].reshape(group * block, full)
            sc = jnp.where(key < len_ref[s], sc, NEG)
            lse_tile = lse_ref[h, s]
            lse = jnp.concatenate([lse_tile[:, a : a + 1] for a in range(group)], axis=0)
            p = jnp.exp(sc - lse)
            dp = nt(dcat, vw)
            ds = p * (dp - jnp.sum(p * dp, axis=-1, keepdims=True))
            ds = ds.astype(BF16)
            pb = p.astype(BF16)
            if biased:
                if s == 0:
                    sum_ref[...] = ds.astype(F32)
                else:
                    sum_ref[...] += ds.astype(F32)
            dq = join_heads(nn(ds, kw), lanes, block)
            dq_ref[s * block : (s + 1) * block, :] = dq.astype(BF16)
            dk = tn(ds, qcat).astype(BF16)
            dv = tn(pb, dcat).astype(BF16)
            dkv_ref[s * full : (s + 1) * full, :] = jnp.concatenate(
                [dk[:, :win], dv[:, :win]], axis=1
            )
        if biased:
            for a in range(group):
                ext_ref[:, block:] = sum_ref[a * block : (a + 1) * block, :]
                far_sum = jnp.sum(jnp.where(far, ext_ref[...], 0.0))
                fold = ext_ref[:, pl.ds(start, 2 * block)]
                half = block // 2
                while half >= 8:
                    fold = fold[:half] + pltpu.roll(fold[half:], 2 * block - half, 1)
                    half //= 2
                for bit in (4, 2, 1):
                    fold = jnp.where(
                        (row8 & bit) != 0, pltpu.roll(fold, 2 * block - bit, 1), fold
                    )
                line = jnp.sum(fold, axis=0, keepdims=True)
                line = line + jnp.where(lane_near == 2 * block - 1, far_sum, 0.0)
                diag_ref[pl.ds(h * group + a, 1), :] = line
        dkv = dkv_ref[...]
        dq_h = dq_ref[...][:, :win]
        kv_term = nt(dkv, wkv_ref[h])
        q_term = nt(dq_h, wq_ref[h])
        w_ref[h] = jnp.concatenate(
            [
                nn(nkt_ref[...], dkv).astype(BF16),
                nn(nqt_ref[...], dq_h).astype(BF16),
                nn(dat_ref[...], c_ref[h][:, :win]).astype(BF16),
            ],
            axis=1,
        )

        @pl.when(h == 0)
        def _():
            acc_ref[: seqs * full, :] = kv_term
            acc_ref[seqs * full :, :] = q_term

        @pl.when(h != 0)
        def _():
            acc_ref[: seqs * full, :] += kv_term
            acc_ref[seqs * full :, :] += q_term

        return carry

    lax.fori_loop(0, shards, body, 0)
    if biased:
        for s in range(seqs):
            own = pl.ds(pl.multiple_of(s * full + me * block, block), block)
            acc_ref[own, :] += acc_ref[seqs * full + s * block : seqs * full + (s + 1) * block, :]
        total = acc_ref[: seqs * full, :]
        part_ref[...] = total.astype(BF16)
        gg_ref[...] = (
            jnp.sum(total * nk_ref[...].astype(F32), axis=0, keepdims=True) / gain_ref[...]
        )
    else:
        part_ref[...] = acc_ref[: seqs * full, :].astype(BF16)
        dy, gg = norm_grads(y_ref[...], gain_ref[...], acc_ref[seqs * full :, :])
        dprev_ref[...] = dy_ref[...] + dy
        gg_ref[...] = gg


def attend_backward(lens, me, nq, nk, saved, wq, wkv, wo, dy, gain, extra, biased, group, size):
    q, k, v, c, lse = saved
    rows, width = nq.shape
    shards, keys, pw = k.shape
    block = rows // lens.shape[0]
    full = keys // lens.shape[0]
    win = group * size
    args = [lens, me, nq, nk, q, k, v, c, lse, wq, wkv, wo, dy, gain, extra]
    out_shape = [
        sds((keys, width), BF16),
        sds((1, width), F32),
        sds((shards, width, 4 * win), BF16),
        sds((shards * group, 2 * block), F32) if biased else sds((rows, width), F32),
    ]
    scratch = [
        pltpu.VMEM((rows, pw), BF16),
        pltpu.VMEM((rows, pw), BF16),
        pltpu.VMEM((keys, 2 * win), BF16),
        pltpu.VMEM((keys + rows, width), F32),
        pltpu.VMEM((width, rows), BF16),
        pltpu.VMEM((width, keys), BF16),
        pltpu.VMEM((width, rows), BF16),
    ]
    if biased:
        scratch += [
            pltpu.VMEM((group * block, full), F32),
            pltpu.VMEM((block, full + block), F32),
        ]
    flops = 4 * (rows + 2 * keys + rows) * width * width + 10 * rows * full * width
    return pl.pallas_call(
        functools.partial(backward_kernel, biased, group, size),
        out_shape=out_shape,
        in_specs=[smem(), smem()] + [vmem()] * (len(args) - 2),
        out_specs=[vmem()] * 4,
        scratch_shapes=scratch,
        compiler_params=params(),
        cost_estimate=pl.CostEstimate(
            flops=flops, bytes_accessed=24 << 20, transcendentals=rows * full * 12
        ),
        name="attend_backward",
    )(*args)


def feed_kernel(
    y_ref, n_ref, cot_ref, win_ref, wout_ref, gain_ref, out_ref, dy_ref, gg_ref, w_ref,
    acc_ref, dn_ref, nt_ref, ct_ref,
):
    step = pl.program_id(0)
    part = wout_ref.shape[0]

    @pl.when(step == 0)
    def _():
        nt_ref[...] = n_ref[...].T
        ct_ref[...] = cot_ref[...].T
        acc_ref[...] = y_ref[...]
        dn_ref[...] = jnp.zeros_like(dn_ref)

    n = n_ref[...]
    cot = cot_ref[...]
    g = nn(n, win_ref[0])
    u = nn(n, win_ref[1])
    dh = nt(cot, wout_ref[...])
    scale = math.sqrt(2.0 / math.pi)
    square = g * g
    t = jnp.tanh(scale * (g + 0.044715 * square * g))
    half = 0.5 * (1.0 + t)
    gelu = g * half
    hid = (gelu * u).astype(BF16)
    slope = half + 0.5 * g * (1.0 - t * t) * (scale * (1.0 + 3 * 0.044715 * square))
    dg = (dh * u * slope).astype(BF16)
    du = (dh * gelu).astype(BF16)
    acc_ref[...] += nn(hid, wout_ref[...])
    dn_ref[...] += nt(dg, win_ref[0]) + nt(du, win_ref[1])
    w_ref[0, :, :part] = nn(nt_ref[...], dg).astype(BF16)
    w_ref[0, :, part : 2 * part] = nn(nt_ref[...], du).astype(BF16)
    w_ref[0, :, 2 * part :] = nn(ct_ref[...], hid).astype(BF16)

    @pl.when(step == pl.num_programs(0) - 1)
    def _():
        out_ref[...] = acc_ref[...].astype(BF16)
        dy, gg = norm_grads(y_ref[...], gain_ref[...], dn_ref[...])
        dy_ref[...] = cot_ref[...].astype(F32) + dy
        gg_ref[...] = gg


def feed(y, n, cot, w_in, w_out, gain, shards):
    rows, width = y.shape
    hidden = w_out.shape[0]
    part = hidden // shards
    fixed = lambda shape: pl.BlockSpec(shape, lambda j: (0,) * len(shape))
    return pl.pallas_call(
        feed_kernel,
        grid=(shards,),
        out_shape=[
            sds((rows, width), BF16),
            sds((rows, width), F32),
            sds((1, width), F32),
            sds((shards, width, 3 * part), BF16),
        ],
        in_specs=[
            fixed((rows, width)),
            fixed((rows, width)),
            fixed((rows, width)),
            pl.BlockSpec((2, width, part), lambda j: (0, 0, j)),
            pl.BlockSpec((part, width), lambda j: (j, 0)),
            fixed((1, width)),
        ],
        out_specs=[
            fixed((rows, width)),
            fixed((rows, width)),
            fixed((1, width)),
            pl.BlockSpec((1, width, 3 * part), lambda j: (j, 0, 0)),
        ],
        scratch_shapes=[
            pltpu.VMEM((rows, width), F32),
            pltpu.VMEM((rows, width), F32),
            pltpu.VMEM((width, rows), BF16),
            pltpu.VMEM((width, rows), BF16),
        ],
        compiler_params=params(),
        cost_estimate=pl.CostEstimate(
            flops=18 * rows * width * hidden, bytes_accessed=24 << 20, transcendentals=rows * hidden
        ),
        name="feed",
    )(y, n, cot, w_in, w_out, gain)


def per_device(
    layer_input,
    memory,
    dec_lengths,
    enc_lengths,
    self_gain,
    self_query,
    self_key_value,
    self_out,
    rel_bias,
    cross_gain,
    cross_query,
    cross_key_value,
    cross_out,
    feed_gain,
    feed_in,
    feed_out,
    out_cotangent,
):
    shards = lax.axis_size("head")
    me = lax.axis_index("head").astype(jnp.int32).reshape(1)
    batch_count = lax.axis_size("batch")
    batch_index = lax.axis_index("batch")
    seqs, block, width = layer_input.shape
    group = rel_bias.shape[1]
    size = self_query.shape[1] // group
    win = group * size
    full = block * shards
    enc_full = memory.shape[1] * shards
    rows = seqs * block
    slice_width = width // batch_count
    part = feed_in.shape[2] // shards
    sg, cg, fg = (g.astype(F32).reshape(1, width) for g in (self_gain, cross_gain, feed_gain))

    x = layer_input.reshape(rows, width)
    x32 = x.astype(F32)
    n1 = (x32 * rms(x32) * sg).astype(BF16)
    n1_all = lax.all_gather(n1.reshape(seqs, block, width), "head", axis=1, tiled=True)
    n1_all = n1_all.reshape(seqs * full, width)

    def take(weight, axis):
        length = weight.shape[axis] // batch_count
        return lax.dynamic_slice_in_dim(weight, batch_index * length, length, axis)

    projections = jnp.concatenate(
        [take(self_query, 0), take(self_key_value[0], 0), take(self_key_value[1], 0),
         take(cross_query, 0), take(cross_key_value[0], 0), take(cross_key_value[1], 0)], axis=1
    )
    projections = lax.all_gather(projections, ("head", "batch"), axis=0, tiled=True)
    projections = projections.reshape(shards, width, 6 * win)
    wq1, wkv1 = projections[:, :, :win], projections[:, :, win : 3 * win]
    wq2, wkv2 = projections[:, :, 3 * win : 4 * win], projections[:, :, 4 * win :]
    outs = jnp.concatenate([take(self_out, 1), take(cross_out, 1)], axis=1)
    outs = lax.all_gather(outs, "head", axis=0, tiled=True)
    outs = lax.all_gather(outs.reshape(width, 2, slice_width), "batch", axis=2, tiled=True)
    wo1, wo2 = outs[:, 0], outs[:, 1]
    table = lax.all_gather(rel_bias.T, "head", axis=0, tiled=True).astype(F32)
    onehot = near_onehot(block)
    near = jnp.einsum("hb,tb->ht", table, onehot, precision=highest)
    bias = bias_tiles(me, near, block, full)
    memory_all = lax.all_gather(memory, "head", axis=1, tiled=True).reshape(seqs * enc_full, width)

    *saved1, y1, n2 = attend_forward(
        dec_lengths, n1, n1_all, x, wq1, wkv1, wo1, cg, bias, group, size
    )
    *saved2, y2, n3 = attend_forward(
        enc_lengths, n2, memory_all, y1, wq2, wkv2, wo2, fg, None, group, size
    )
    result, dy2, gain3, feed_w = feed(
        y2, n3, out_cotangent.reshape(rows, width), feed_in, feed_out, fg, shards
    )
    memory_part, gain2, cross_w, dy1 = attend_backward(
        enc_lengths, me, n2, memory_all, saved2, wq2, wkv2, wo2, dy2, cg, y1, False, group, size
    )
    input_part, gain1, self_w, diag = attend_backward(
        dec_lengths, me, n1, n1_all, saved1, wq1, wkv1, wo1, dy1, sg, bias, True, group, size
    )

    feed_w = lax.psum_scatter(
        feed_w.reshape(shards * width, 3 * part), ("head", "batch"), scatter_dimension=0, tiled=True
    ).astype(F32)
    memory_grad = lax.psum_scatter(
        memory_part.reshape(seqs, enc_full, width), "head", scatter_dimension=1, tiled=True
    ).astype(F32)
    dn1 = lax.psum_scatter(
        input_part.reshape(seqs, full, width), "head", scatter_dimension=1, tiled=True
    ).astype(F32)
    pair_w = jnp.concatenate(
        [self_w.reshape(shards * width, 4 * win), cross_w.reshape(shards * width, 4 * win)], axis=1
    )
    pair_w = lax.psum_scatter(
        pair_w, ("head", "batch"), scatter_dimension=0, tiled=True
    ).astype(F32)
    dx, _ = norm_grads(x32, sg, dn1.reshape(rows, width))
    input_grad = (dy1 + dx).reshape(seqs, block, width)
    table_grad = jnp.einsum("tb,ht->bh", onehot, diag, precision=highest)
    gains, table_grad = lax.psum(
        (jnp.concatenate([gain1, gain2, gain3], axis=0), table_grad), ("batch", "head")
    )
    table_grad = lax.dynamic_slice_in_dim(table_grad, me[0] * group, group, 1)

    def split(w):
        kv = jnp.stack([w[:, :win], w[:, win : 2 * win]])
        return w[:, 2 * win : 3 * win], kv, w[:, 3 * win :].T

    self_q, self_kv, self_o = split(pair_w[:, : 4 * win])
    cross_q, cross_kv, cross_o = split(pair_w[:, 4 * win :])
    return (
        result.reshape(seqs, block, width),
        input_grad,
        memory_grad,
        gains[0],
        self_q,
        self_kv,
        self_o,
        table_grad,
        gains[1],
        cross_q,
        cross_kv,
        cross_o,
        gains[2],
        jnp.stack([feed_w[:, :part], feed_w[:, part : 2 * part]]),
        feed_w[:, 2 * part :].T,
    )


def solution(mesh):
    return jax.shard_map(
        per_device,
        mesh=mesh,
        in_specs=(
            P("batch", "head", None),
            P("batch", "head", None),
            P("batch"),
            P("batch"),
            P(),
            P(None, "head"),
            P(None, None, "head"),
            P("head", None),
            P(None, "head"),
            P(),
            P(None, "head"),
            P(None, None, "head"),
            P("head", None),
            P(),
            P(),
            P(),
            P("batch", "head", None),
        ),
        out_specs=(
            P("batch", "head", None),
            P("batch", "head", None),
            P("batch", "head", None),
            P(),
            P("batch", "head"),
            P(None, "batch", "head"),
            P("head", "batch"),
            P(None, "head"),
            P(),
            P("batch", "head"),
            P(None, "batch", "head"),
            P("head", "batch"),
            P(),
            P(None, "batch", "head"),
            P("head", "batch"),
        ),
        check_vma=False,
    )
```

```python
import functools
import math

import jax
import jax.numpy as jnp
from jax import lax
from jax.experimental import pallas as pl
from jax.experimental.pallas import tpu as pltpu
from jax.sharding import PartitionSpec as P

NB = 32
MAX_DIST = 128
NEG = -1e30
VMEM_LIMIT = 56 * 1024 * 1024
F32 = jnp.float32
BF16 = jnp.bfloat16

highest = lax.Precision.HIGHEST


def bucket_edges(num_buckets, max_distance):
    exact_part = num_buckets // 2
    edge_list = []
    for target in range(1, num_buckets - exact_part):
        distance = exact_part
        while (
            math.floor(
                math.log(distance / exact_part)
                / math.log(max_distance / exact_part)
                * (num_buckets - exact_part)
            )
            < target
        ):
            distance += 1
        edge_list.append(distance)
    return edge_list


def bucket_of(distance, num_buckets, max_distance):
    exact_part = num_buckets // 2
    counted = jnp.zeros(distance.shape, jnp.int32)
    for edge_value in bucket_edges(num_buckets, max_distance):
        counted = counted + (distance >= edge_value).astype(jnp.int32)
    return jnp.where(distance < exact_part, distance, exact_part + counted).astype(jnp.int32)


def near_onehot(block):
    distance = block - jnp.arange(2 * block)
    distance = jnp.where(distance < 0, 2 * MAX_DIST, distance)
    return (
        bucket_of(distance, NB, MAX_DIST)[:, None] == jnp.arange(NB)[None, :]
    ).astype(F32)


def nn(a, b):
    return lax.dot_general(a, b, (((1,), (0,)), ((), ())), preferred_element_type=F32)


def nt(a, b):
    return lax.dot_general(a, b, (((1,), (1,)), ((), ())), preferred_element_type=F32)


def tn(a, b):
    return lax.dot_general(a, b, (((0,), (0,)), ((), ())), preferred_element_type=F32)


def rms(v):
    return lax.rsqrt(jnp.mean(v * v, axis=-1, keepdims=True) + 1e-06)


def norm_grads(y, gain, e):
    r = rms(y)
    xhat = y * r
    eg = e * gain
    dy = r * (eg - xhat * jnp.mean(eg * xhat, axis=-1, keepdims=True))
    return dy, jnp.sum(e * xhat, axis=0, keepdims=True)


def padded(v, width):
    extra = width - v.shape[1]
    if extra == 0:
        return v
    return jnp.concatenate([v, jnp.zeros((v.shape[0], extra), v.dtype)], axis=1)


def put_rows(ref, value, order):
    step = value.shape[0] // len(order)
    for source, slot in enumerate(order):
        ref[slot * step : (slot + 1) * step, :] = value[source * step : (source + 1) * step, :]


def vmem():
    return pl.BlockSpec(memory_space=pltpu.VMEM)


def smem():
    return pl.BlockSpec(memory_space=pltpu.SMEM)


def params():
    return pltpu.CompilerParams(vmem_limit_bytes=VMEM_LIMIT)


def sds(shape, dtype):
    return jax.ShapeDtypeStruct(shape, dtype)


def bias_kernel(me_ref, table_ref, onehot_ref, b_ref, ext_ref, line_ref):
    heads, block, full = b_ref.shape
    shards = table_ref.shape[0]
    group = heads // shards
    me = me_ref[0]
    start = pl.multiple_of(me * block, block)
    width = 2 * block
    row_i = lax.broadcasted_iota(jnp.int32, (block, width), 0)
    col_i = lax.broadcasted_iota(jnp.int32, (block, width), 1)
    masked = (col_i - row_i) > block
    far = lax.broadcasted_iota(jnp.int32, ext_ref.shape, 1) < start

    def body(h, carry):
        line_ref[...] = tn(table_ref[h], onehot_ref[...])
        for a in range(group):
            row = line_ref[a : a + 1, :]
            tile = pltpu.roll(
                jnp.broadcast_to(row, (block, width)), 0, 1, stride=1, stride_axis=0
            )
            ext_ref[...] = jnp.where(far, row[:, width - 1 : width], NEG)
            ext_ref[:, pl.ds(start, width)] = jnp.where(masked, NEG, tile)
            b_ref[h * group + a] = ext_ref[:, block:]
        return carry

    lax.fori_loop(0, shards, body, 0)


def bias_tiles(me, tables, onehot, group, block, full):
    shards, buckets, lanes = tables.shape
    return pl.pallas_call(
        bias_kernel,
        out_shape=sds((shards * group, block, full), F32),
        in_specs=[smem(), vmem(), vmem()],
        out_specs=vmem(),
        scratch_shapes=[
            pltpu.VMEM((block, full + block), F32),
            pltpu.VMEM((lanes, 2 * block), F32),
        ],
        compiler_params=params(),
        name="bias_tiles",
    )(me, tables, onehot)


def lane_groups(width, group, size):
    lane = lax.broadcasted_iota(jnp.int32, (1, width), 1)
    return [(lane // size) == a for a in range(group)]


def stack_heads(win, lanes):
    return jnp.concatenate([jnp.where(m, win, jnp.zeros_like(win)) for m in lanes], axis=0)


def join_heads(tall, lanes, rows):
    total = jnp.where(lanes[0], tall[:rows], 0.0)
    for a in range(1, len(lanes)):
        total = total + jnp.where(lanes[a], tall[a * rows : (a + 1) * rows], 0.0)
    return total


def forward_kernel(
    biased, group, size, len_ref, nq_ref, nk_ref, res_ref, wq_ref, wkv_ref, wo_ref, gain_ref, *rest
):
    if biased:
        b_ref, *rest = rest
    q_ref, k_ref, v_ref, c_ref, lse_ref, y_ref, n_ref = rest
    shards, rows, pw = q_ref.shape
    seqs = len_ref.shape[0]
    block = rows // seqs
    full = k_ref.shape[1] // seqs
    win = group * size
    lanes = lane_groups(pw, group, size)
    lane128 = lax.broadcasted_iota(jnp.int32, (block, 128), 1)
    key = lax.broadcasted_iota(jnp.int32, (1, full), 1)

    def body(h, carry):
        q_ref[h] = padded(nt(nq_ref[...], wq_ref[h]).astype(BF16), pw)
        k_ref[h] = padded(nt(nk_ref[...], wkv_ref[h, 0]).astype(BF16), pw)
        v_ref[h] = padded(nt(nk_ref[...], wkv_ref[h, 1]).astype(BF16), pw)
        for s in range(seqs):
            kw = k_ref[h, s * full : (s + 1) * full, :]
            vw = v_ref[h, s * full : (s + 1) * full, :]
            qcat = stack_heads(q_ref[h, s * block : (s + 1) * block, :], lanes)
            sc = nt(qcat, kw)
            if biased:
                sc = sc + b_ref[pl.ds(h * group, group)].reshape(group * block, full)
            sc = jnp.where(key < len_ref[s], sc, NEG)
            top = jnp.max(sc, axis=-1, keepdims=True)
            e = jnp.exp(sc - top)
            total = jnp.sum(e, axis=-1, keepdims=True)
            p = (e * (1.0 / total)).astype(BF16)
            c = join_heads(nn(p, vw), lanes, block)
            c_ref[h, s * block : (s + 1) * block, :] = c.astype(BF16)
            lse = top + jnp.log(total)
            tile = jnp.zeros((block, 128), F32)
            for a in range(group):
                tile = jnp.where(lane128 == a, lse[a * block : (a + 1) * block], tile)
            lse_ref[h, s] = tile
        return carry

    lax.fori_loop(0, shards, body, 0)
    joined = jnp.concatenate([c_ref[h][:, :win] for h in range(shards)], axis=1)
    y = res_ref[...].astype(F32) + nn(joined, wo_ref[...])
    y_ref[...] = y
    n_ref[...] = (y * rms(y) * gain_ref[...]).astype(BF16)


def attend_forward(lens, nq, nk, res, wq, wkv, wo, gain, bias, group, size):
    rows, width = nq.shape
    shards = wq.shape[0]
    pw = -(-group * size // 128) * 128
    seqs = lens.shape[0]
    args = [lens, nq, nk, res, wq, wkv, wo, gain] + ([bias] if bias is not None else [])
    keys = nk.shape[0]
    flops = 2 * (rows + 2 * keys + rows) * width * width + 4 * rows * keys * width
    return pl.pallas_call(
        functools.partial(forward_kernel, bias is not None, group, size),
        out_shape=[
            sds((shards, rows, pw), BF16),
            sds((shards, keys, pw), BF16),
            sds((shards, keys, pw), BF16),
            sds((shards, rows, pw), BF16),
            sds((shards, seqs, rows // seqs, 128), F32),
            sds((rows, width), F32),
            sds((rows, width), BF16),
        ],
        in_specs=[smem()] + [vmem()] * (len(args) - 1),
        out_specs=[vmem()] * 7,
        compiler_params=params(),
        cost_estimate=pl.CostEstimate(
            flops=flops, bytes_accessed=16 << 20, transcendentals=rows * keys * 6
        ),
        name="attend_forward",
    )(*args)


def backward_kernel(
    biased,
    group,
    size,
    order,
    len_ref,
    me_ref,
    nq_ref,
    nk_ref,
    q_ref,
    k_ref,
    v_ref,
    c_ref,
    lse_ref,
    wq_ref,
    wkv_ref,
    wo_ref,
    dy_ref,
    gain_ref,
    *rest,
):
    if biased:
        b_ref, part_ref, gg_ref, w_ref, diag_ref, dc_ref, dq_ref, dkv_ref, acc_ref, nqt_ref, nkt_ref, dat_ref, sum_ref, ext_ref = rest
    else:
        y_ref, part_ref, gg_ref, w_ref, dprev_ref, dc_ref, dq_ref, dkv_ref, acc_ref, nqt_ref, nkt_ref, dat_ref = rest
    shards, rows, pw = q_ref.shape
    seqs = len_ref.shape[0]
    block = rows // seqs
    full = k_ref.shape[1] // seqs
    win = group * size
    lanes = lane_groups(pw, group, size)
    key = lax.broadcasted_iota(jnp.int32, (1, full), 1)
    me = me_ref[0]

    da = dy_ref[...].astype(BF16)
    put_rows(nqt_ref, nq_ref[...].T, order)
    put_rows(nkt_ref, nk_ref[...].T, order)
    put_rows(dat_ref, da.T, order)
    if biased:
        ext_ref[:, :block] = jnp.zeros((block, block), F32)
        start = pl.multiple_of(me * block, block)
        far = lax.broadcasted_iota(jnp.int32, ext_ref.shape, 1) < start
        row8 = lax.broadcasted_iota(jnp.int32, (8, 2 * block), 0)
        lane_near = lax.broadcasted_iota(jnp.int32, (1, 2 * block), 1)

    def body(h, carry):
        wo_h = wo_ref[pl.ds(pl.multiple_of(h * win, size), win), :]
        dc_ref[...] = padded(nt(da, wo_h).astype(BF16), pw)
        for s in range(seqs):
            kw = k_ref[h, s * full : (s + 1) * full, :]
            vw = v_ref[h, s * full : (s + 1) * full, :]
            qcat = stack_heads(q_ref[h, s * block : (s + 1) * block, :], lanes)
            dcat = stack_heads(dc_ref[s * block : (s + 1) * block, :], lanes)
            sc = nt(qcat, kw)
            if biased:
                sc = sc + b_ref[pl.ds(h * group, group)].reshape(group * block, full)
            sc = jnp.where(key < len_ref[s], sc, NEG)
            lse_tile = lse_ref[h, s]
            lse = jnp.concatenate([lse_tile[:, a : a + 1] for a in range(group)], axis=0)
            p = jnp.exp(sc - lse)
            dp = nt(dcat, vw)
            ds = p * (dp - jnp.sum(p * dp, axis=-1, keepdims=True))
            ds = ds.astype(BF16)
            pb = p.astype(BF16)
            if biased:
                if s == 0:
                    sum_ref[...] = ds.astype(F32)
                else:
                    sum_ref[...] += ds.astype(F32)
            dq = join_heads(nn(ds, kw), lanes, block)
            dq_ref[s * block : (s + 1) * block, :] = dq.astype(BF16)
            dk = tn(ds, qcat).astype(BF16)
            dv = tn(pb, dcat).astype(BF16)
            dkv_ref[s * full : (s + 1) * full, :] = jnp.concatenate(
                [dk[:, :win], dv[:, :win]], axis=1
            )
        if biased:
            for a in range(group):
                ext_ref[:, block:] = sum_ref[a * block : (a + 1) * block, :]
                far_sum = jnp.sum(jnp.where(far, ext_ref[...], 0.0))
                fold = ext_ref[:, pl.ds(start, 2 * block)]
                half = block // 2
                while half >= 8:
                    fold = fold[:half] + pltpu.roll(fold[half:], 2 * block - half, 1)
                    half //= 2
                for bit in (4, 2, 1):
                    fold = jnp.where(
                        (row8 & bit) != 0, pltpu.roll(fold, 2 * block - bit, 1), fold
                    )
                line = jnp.sum(fold, axis=0, keepdims=True)
                line = line + jnp.where(lane_near == 2 * block - 1, far_sum, 0.0)
                diag_ref[pl.ds(h * group + a, 1), :] = line
        dkv = dkv_ref[...]
        dq_h = dq_ref[...][:, :win]
        kv_term = nn(dkv[:, :win], wkv_ref[h, 0]) + nn(dkv[:, win:], wkv_ref[h, 1])
        q_term = nn(dq_h, wq_ref[h])
        w_ref[h] = jnp.concatenate(
            [
                nn(nkt_ref[...], dkv).astype(BF16),
                nn(nqt_ref[...], dq_h).astype(BF16),
                nn(dat_ref[...], c_ref[h][:, :win]).astype(BF16),
            ],
            axis=1,
        )

        @pl.when(h == 0)
        def _():
            acc_ref[: seqs * full, :] = kv_term
            acc_ref[seqs * full :, :] = q_term

        @pl.when(h != 0)
        def _():
            acc_ref[: seqs * full, :] += kv_term
            acc_ref[seqs * full :, :] += q_term

        return carry

    lax.fori_loop(0, shards, body, 0)
    if biased:
        for s in range(seqs):
            own = pl.ds(pl.multiple_of(s * full + me * block, block), block)
            acc_ref[own, :] += acc_ref[seqs * full + s * block : seqs * full + (s + 1) * block, :]
        total = acc_ref[: seqs * full, :]
        part_ref[...] = total.astype(BF16)
        gg_ref[...] = (
            jnp.sum(total * nk_ref[...].astype(F32), axis=0, keepdims=True) / gain_ref[...]
        )
    else:
        part_ref[...] = acc_ref[: seqs * full, :].astype(BF16)
        dy, gg = norm_grads(y_ref[...], gain_ref[...], acc_ref[seqs * full :, :])
        dprev_ref[...] = dy_ref[...] + dy
        gg_ref[...] = gg


def attend_backward(
    lens, me, nq, nk, saved, wq, wkv, wo, dy, gain, extra, biased, group, size, order
):
    q, k, v, c, lse = saved
    rows, width = nq.shape
    shards, keys, pw = k.shape
    block = rows // lens.shape[0]
    full = keys // lens.shape[0]
    win = group * size
    args = [lens, me, nq, nk, q, k, v, c, lse, wq, wkv, wo, dy, gain, extra]
    out_shape = [
        sds((keys, width), BF16),
        sds((1, width), F32),
        sds((shards, width, 4 * win), BF16),
        sds((shards * group, 2 * block), F32) if biased else sds((rows, width), F32),
    ]
    scratch = [
        pltpu.VMEM((rows, pw), BF16),
        pltpu.VMEM((rows, pw), BF16),
        pltpu.VMEM((keys, 2 * win), BF16),
        pltpu.VMEM((keys + rows, width), F32),
        pltpu.VMEM((width, rows), BF16),
        pltpu.VMEM((width, keys), BF16),
        pltpu.VMEM((width, rows), BF16),
    ]
    if biased:
        scratch += [
            pltpu.VMEM((group * block, full), F32),
            pltpu.VMEM((block, full + block), F32),
        ]
    flops = 4 * (rows + 2 * keys + rows) * width * width + 10 * rows * full * width
    return pl.pallas_call(
        functools.partial(backward_kernel, biased, group, size, order),
        out_shape=out_shape,
        in_specs=[smem(), smem()] + [vmem()] * (len(args) - 2),
        out_specs=[vmem()] * 4,
        scratch_shapes=scratch,
        compiler_params=params(),
        cost_estimate=pl.CostEstimate(
            flops=flops, bytes_accessed=24 << 20, transcendentals=rows * full * 12
        ),
        name="attend_backward",
    )(*args)


def feed_kernel(
    order, y_ref, n_ref, cot_ref, win_ref, wout_ref, gain_ref, out_ref, dy_ref, gg_ref, w_ref,
    acc_ref, dn_ref, nt_ref, ct_ref,
):
    step = pl.program_id(0)
    part = wout_ref.shape[0]

    @pl.when(step == 0)
    def _():
        put_rows(nt_ref, n_ref[...].T, order)
        put_rows(ct_ref, cot_ref[...].T, order)
        acc_ref[...] = y_ref[...]
        dn_ref[...] = jnp.zeros_like(dn_ref)

    n = n_ref[...]
    cot = cot_ref[...]
    g = nn(n, win_ref[0])
    u = nn(n, win_ref[1])
    dh = nt(cot, wout_ref[...])
    scale = math.sqrt(2.0 / math.pi)
    square = g * g
    t = jnp.tanh(scale * (g + 0.044715 * square * g))
    half = 0.5 * (1.0 + t)
    gelu = g * half
    hid = (gelu * u).astype(BF16)
    slope = half + 0.5 * g * (1.0 - t * t) * (scale * (1.0 + 3 * 0.044715 * square))
    dg = (dh * u * slope).astype(BF16)
    du = (dh * gelu).astype(BF16)
    acc_ref[...] += nn(hid, wout_ref[...])
    dn_ref[...] += nt(dg, win_ref[0]) + nt(du, win_ref[1])
    w_ref[0, :, :part] = nn(nt_ref[...], dg).astype(BF16)
    w_ref[0, :, part : 2 * part] = nn(nt_ref[...], du).astype(BF16)
    w_ref[0, :, 2 * part :] = nn(ct_ref[...], hid).astype(BF16)

    @pl.when(step == pl.num_programs(0) - 1)
    def _():
        out_ref[...] = acc_ref[...].astype(BF16)
        dy, gg = norm_grads(y_ref[...], gain_ref[...], dn_ref[...])
        dy_ref[...] = cot_ref[...].astype(F32) + dy
        gg_ref[...] = gg


def feed(y, n, cot, w_in, w_out, gain, shards, order):
    rows, width = y.shape
    hidden = w_out.shape[0]
    part = hidden // shards
    fixed = lambda shape: pl.BlockSpec(shape, lambda j: (0,) * len(shape))
    return pl.pallas_call(
        functools.partial(feed_kernel, order),
        grid=(shards,),
        out_shape=[
            sds((rows, width), BF16),
            sds((rows, width), F32),
            sds((1, width), F32),
            sds((shards, width, 3 * part), BF16),
        ],
        in_specs=[
            fixed((rows, width)),
            fixed((rows, width)),
            fixed((rows, width)),
            pl.BlockSpec((2, width, part), lambda j: (0, 0, j)),
            pl.BlockSpec((part, width), lambda j: (j, 0)),
            fixed((1, width)),
        ],
        out_specs=[
            fixed((rows, width)),
            fixed((rows, width)),
            fixed((1, width)),
            pl.BlockSpec((1, width, 3 * part), lambda j: (j, 0, 0)),
        ],
        scratch_shapes=[
            pltpu.VMEM((rows, width), F32),
            pltpu.VMEM((rows, width), F32),
            pltpu.VMEM((width, rows), BF16),
            pltpu.VMEM((width, rows), BF16),
        ],
        compiler_params=params(),
        cost_estimate=pl.CostEstimate(
            flops=18 * rows * width * hidden, bytes_accessed=24 << 20, transcendentals=rows * hidden
        ),
        name="feed",
    )(y, n, cot, w_in, w_out, gain)


MESH = pl.DeviceIdType.MESH


def place():
    b = lax.axis_index("batch")
    me = lax.axis_index("head")
    core = lax.rem(b, 2)
    x = lax.rem(lax.div(b, 2), 2)
    y = lax.div(b, 4)
    return b, me, core, x, y


def near_devices(b, me, core, x, y, shards):
    over_core = (b + 1 - 2 * core, me)
    over_x = (b + 2 - 4 * x, me)
    over_y = (b + 4 - 8 * y, me)
    across = (b + 2 - 4 * x + 4 - 8 * y, me)
    ahead = [(b, lax.rem(me + k, shards)) for k in range(1, shards)]
    return over_core, over_x, over_y, across, ahead


def greet(devices):
    barrier = pltpu.get_barrier_semaphore()
    for device in devices:
        pl.semaphore_signal(barrier, inc=1, device_id=device, device_id_type=MESH)
    pl.semaphore_wait(barrier, len(devices))


def remote(src, dst, send, recv, device):
    return pltpu.make_async_remote_copy(
        src_ref=src,
        dst_ref=dst,
        send_sem=send,
        recv_sem=recv,
        device_id=device,
        device_id_type=MESH,
    )


def gather_kernel(n, *refs):
    shard_refs, table_ref = refs[:n], refs[n]
    full_refs, tables_ref = refs[n + 1 : 2 * n + 1], refs[2 * n + 1]
    (zs, zr, ps, pr, cs, cr, ts, tr, local) = refs[2 * n + 2 :]
    shards = tables_ref.shape[0]
    b, me, core, x, y = place()
    over_core, over_x, over_y, across, ahead = near_devices(b, me, core, x, y, shards)
    greet([over_core, over_x, over_y, across] + ahead)
    slot = core * 4 + lax.div(b, 2)

    def window(ref, first, count):
        step = ref.shape[-2] // 8
        rows = pl.ds(pl.multiple_of(first * step, step), count * step)
        return ref.at[:, rows, :]

    started = []

    def start(copy):
        copy.start()
        started.append(copy)
        return copy

    from_z, from_plane, from_core = {}, {}, {}
    for k in range(1, shards):
        start(remote(table_ref, tables_ref.at[me], ts.at[k - 1], tr.at[k - 1], ahead[k - 1]))
    for i in range(n):
        for k in range(1, shards):
            from_z[i, k] = start(
                remote(
                    window(shard_refs[i], slot, 1),
                    window(full_refs[i].at[me], slot, 1),
                    zs.at[i, k - 1],
                    zr.at[i, k - 1],
                    ahead[k - 1],
                )
            )
    copies = [pltpu.make_async_copy(table_ref, tables_ref.at[me], local.at[n])]
    copies += [
        pltpu.make_async_copy(shard_refs[i], full_refs[i].at[me], local.at[i]) for i in range(n)
    ]
    for copy in copies:
        copy.start()
    for i in range(n):
        for k in range(1, shards):
            from_z[i, k].wait_recv()
            piece = window(full_refs[i].at[lax.rem(me + shards - k, shards)], slot, 1)
            for d, device in enumerate((over_x, over_y, across)):
                from_plane[i, k, d] = start(
                    remote(piece, piece, ps.at[i, k - 1, d], pr.at[i, k - 1, d], device)
                )
    for i in range(n):
        for k in range(1, shards):
            for d in range(3):
                from_plane[i, k, d].wait_recv()
            half = window(full_refs[i].at[lax.rem(me + shards - k, shards)], core * 4, 4)
            from_core[i, k] = start(
                remote(half, half, cs.at[i, k - 1], cr.at[i, k - 1], over_core)
            )
    for copy in from_core.values():
        copy.wait_recv()
    for k in range(1, shards):
        started[k - 1].wait_recv()
    for copy in started:
        copy.wait_send()
    for copy in copies:
        copy.wait()


def gather_weights(weights, table, shards):
    n = len(weights)
    anywhere = pl.BlockSpec(memory_space=pl.ANY)
    dma = pltpu.SemaphoreType.DMA
    return pl.pallas_call(
        functools.partial(gather_kernel, n),
        out_shape=[sds((shards, *w.shape), w.dtype) for w in weights]
        + [sds((shards, *table.shape), table.dtype)],
        in_specs=[anywhere] * (n + 1),
        out_specs=[anywhere] * (n + 1),
        scratch_shapes=[
            dma((n, shards - 1)),
            dma((n, shards - 1)),
            dma((n, shards - 1, 3)),
            dma((n, shards - 1, 3)),
            dma((n, shards - 1)),
            dma((n, shards - 1)),
            dma((shards - 1,)),
            dma((shards - 1,)),
            dma((n + 1,)),
        ],
        compiler_params=pltpu.CompilerParams(
            collective_id=0, has_side_effects=True, vmem_limit_bytes=VMEM_LIMIT
        ),
        name="gather_weights",
    )(*weights, table)


def reduce_kernel(items, w_count, *refs):
    w_refs, small_ref = refs[:w_count], refs[w_count]
    out_refs, small_out = refs[w_count + 1 : 2 * w_count + 1], refs[2 * w_count + 1]
    (own, rc, r1a, r1b, r2a, r2b, tot, rz, sr, lsem, cs, cr, s1, q1, s2, q2, zs, zr, ms, mr) = refs[
        2 * w_count + 2 :
    ]
    shards = w_refs[0].shape[0]
    cols = own.shape[-1]
    half = cols // 2
    b, me, core, x, y = place()
    over_core, over_x, over_y, across, ahead = near_devices(b, me, core, x, y, shards)
    greet([over_core, over_x, over_y] + ahead)
    chunks = [(i, k) for i in range(len(items)) for k in range(shards)]
    owner = [lax.rem(me + 1 + k, shards) for k in range(shards)]
    started = []

    def start(copy):
        copy.start()
        started.append(copy)
        return copy

    small = [start(remote(small_ref, sr.at[0], ms.at[0], mr.at[0], over_core))]
    load, first, second, third, last = {}, {}, {}, {}, {}

    def stage_load(c):
        i, k = chunks[c]
        w, col = items[i]
        piece = lambda side: w_refs[w].at[owner[k], side, :, :, :, pl.ds(col, cols)]
        load[c] = pltpu.make_async_copy(piece(core), own.at[c], lsem.at[c])
        load[c].start()
        first[c] = start(remote(piece(1 - core), rc.at[c], cs.at[c], cr.at[c], over_core))

    def stage_core(c):
        load[c].wait()
        first[c].wait_recv()
        own[c] = own[c] + rc[c]
        second[c] = [
            start(
                remote(
                    own.at[c, :, 1 - x, :, pl.ds(0, half)],
                    r1a.at[c],
                    s1.at[c, 0],
                    q1.at[c, 0],
                    over_x,
                )
            ),
            start(
                remote(
                    own.at[c, 1 - y, :, :, pl.ds(half, half)],
                    r1b.at[c],
                    s1.at[c, 1],
                    q1.at[c, 1],
                    over_y,
                )
            ),
        ]

    def stage_first(c):
        for copy in second[c]:
            copy.wait_recv()
        for other in range(2):
            r1a[c, other] = r1a[c, other] + own[c, other, x, :, :half]
            r1b[c, other] = r1b[c, other] + own[c, y, other, :, half:]
        third[c] = [
            start(remote(r1a.at[c, 1 - y], r2a.at[c], s2.at[c, 0], q2.at[c, 0], over_y)),
            start(remote(r1b.at[c, 1 - x], r2b.at[c], s2.at[c, 1], q2.at[c, 1], over_x)),
        ]

    def stage_second(c):
        i, k = chunks[c]
        for copy in third[c]:
            copy.wait_recv()
        tot[c, :, :half] = r1a[c, y] + r2a[c]
        tot[c, :, half:] = r1b[c, x] + r2b[c]
        if k < shards - 1:
            last[i, k] = start(
                remote(tot.at[c], rz.at[i, k], zs.at[i, k], zr.at[i, k], (b, owner[k]))
            )

    for c in range(len(chunks)):
        stage_load(c)
    for t in range(len(chunks) + 3):
        if t < len(chunks):
            stage_core(t)
        if t == 0:
            small[0].wait_recv()
            sr[6] = small_ref[...] + sr[0]
            small.append(start(remote(sr.at[6], sr.at[1], ms.at[1], mr.at[1], over_x)))
        if t == 2:
            small[1].wait_recv()
            sr[7] = sr[6] + sr[1]
            small.append(start(remote(sr.at[7], sr.at[2], ms.at[2], mr.at[2], over_y)))
        if t == 4:
            small[2].wait_recv()
            sr[8] = sr[7] + sr[2]
            for k in range(shards - 1):
                small.append(
                    start(remote(sr.at[8], sr.at[3 + k], ms.at[3 + k], mr.at[3 + k], ahead[k]))
                )
        if 0 <= t - 1 < len(chunks):
            stage_first(t - 1)
        if 0 <= t - 3 < len(chunks):
            stage_second(t - 3)
    total = sr[8]
    for k in range(shards - 1):
        small[3 + k].wait_recv()
        total = total + sr[3 + k]
    small_out[...] = total
    for i, (w, col) in enumerate(items):
        total = tot[i * shards + shards - 1].astype(F32)
        for k in range(shards - 1):
            last[i, k].wait_recv()
            total = total + rz[i, k].astype(F32)
        out_refs[w][:, col : col + cols] = total
    for copy in started:
        copy.wait_send()


def reduce_blocks(arrays, small, cols):
    shards, tall = arrays[0].shape[:2]
    rows = tall // 8
    items = [(w, col) for w, a in enumerate(arrays) for col in range(0, a.shape[2], cols)]
    n = len(items) * shards
    half = cols // 2
    anywhere = pl.BlockSpec(memory_space=pl.ANY)
    dma = pltpu.SemaphoreType.DMA
    return pl.pallas_call(
        functools.partial(reduce_kernel, items, len(arrays)),
        out_shape=[sds((rows, a.shape[2]), F32) for a in arrays] + [sds(small.shape, F32)],
        in_specs=[anywhere] * len(arrays) + [vmem()],
        out_specs=[vmem()] * (len(arrays) + 1),
        scratch_shapes=[
            pltpu.VMEM((n, 2, 2, rows, cols), BF16),
            pltpu.VMEM((n, 2, 2, rows, cols), BF16),
            pltpu.VMEM((n, 2, rows, half), BF16),
            pltpu.VMEM((n, 2, rows, half), BF16),
            pltpu.VMEM((n, rows, half), BF16),
            pltpu.VMEM((n, rows, half), BF16),
            pltpu.VMEM((n, rows, cols), BF16),
            pltpu.VMEM((len(items), shards - 1, rows, cols), BF16),
            pltpu.VMEM((9, *small.shape), F32),
            dma((n,)),
            dma((n,)),
            dma((n,)),
            dma((n, 2)),
            dma((n, 2)),
            dma((n, 2)),
            dma((n, 2)),
            dma((len(items), shards - 1)),
            dma((len(items), shards - 1)),
            dma((6,)),
            dma((6,)),
        ],
        compiler_params=pltpu.CompilerParams(
            collective_id=1, has_side_effects=True, vmem_limit_bytes=VMEM_LIMIT
        ),
        name="reduce_blocks",
    )(*[a.reshape(shards, 2, 2, 2, rows, a.shape[2]) for a in arrays], small)


def per_device(
    layer_input,
    memory,
    dec_lengths,
    enc_lengths,
    self_gain,
    self_query,
    self_key_value,
    self_out,
    rel_bias,
    cross_gain,
    cross_query,
    cross_key_value,
    cross_out,
    feed_gain,
    feed_in,
    feed_out,
    out_cotangent,
):
    shards = lax.axis_size("head")
    me = lax.axis_index("head").astype(jnp.int32).reshape(1)
    batch_count = lax.axis_size("batch")
    seqs, block, width = layer_input.shape
    group = rel_bias.shape[1]
    size = self_query.shape[1] // group
    win = group * size
    full = block * shards
    enc_full = memory.shape[1] * shards
    rows = seqs * block
    part = feed_in.shape[2] // shards
    sg, cg, fg = (g.astype(F32).reshape(1, width) for g in (self_gain, cross_gain, feed_gain))

    x = layer_input.reshape(rows, width)
    x32 = x.astype(F32)
    n1 = (x32 * rms(x32) * sg).astype(BF16)
    n1_all = lax.all_gather(n1.reshape(seqs, block, width), "head", axis=1, tiled=True)
    n1_all = n1_all.reshape(seqs * full, width)

    tight = batch_count == 8 and shards == 4
    order = tuple((i % 2) * 4 + i // 2 for i in range(8)) if tight else (0,)
    table = jnp.pad(rel_bias, ((0, 0), (0, 128 - group)))
    flip = lambda w: jnp.swapaxes(w, -1, -2)
    weights = [flip(self_query)[None], flip(self_key_value), self_out[None]]
    weights += [flip(cross_query)[None], flip(cross_key_value), cross_out[None]]
    if tight:
        *weights, tables = gather_weights(weights, table, shards)
    else:
        weights = [lax.all_gather(w, "head", axis=0) for w in weights]
        tables = lax.all_gather(table, "head", axis=0)
    wq1, wkv1, wo1, wq2, wkv2, wo2 = weights
    wq1, wq2 = wq1[:, 0], wq2[:, 0]
    wo1, wo2 = wo1.reshape(width, width), wo2.reshape(width, width)
    onehot = near_onehot(block)
    bias = bias_tiles(me, tables, onehot.T.astype(BF16), group, block, full)
    memory_all = lax.all_gather(memory, "head", axis=1, tiled=True).reshape(seqs * enc_full, width)

    *saved1, y1, n2 = attend_forward(
        dec_lengths, n1, n1_all, x, wq1, wkv1, wo1, cg, bias, group, size
    )
    *saved2, y2, n3 = attend_forward(
        enc_lengths, n2, memory_all, y1, wq2, wkv2, wo2, fg, None, group, size
    )
    result, dy2, gain3, feed_w = feed(
        y2, n3, out_cotangent.reshape(rows, width), feed_in, feed_out, fg, shards, order
    )
    memory_part, gain2, cross_w, dy1 = attend_backward(
        enc_lengths, me, n2, memory_all, saved2, wq2, wkv2, wo2, dy2, cg, y1, False, group, size, order
    )
    input_part, gain1, self_w, diag = attend_backward(
        dec_lengths, me, n1, n1_all, saved1, wq1, wkv1, wo1, dy1, sg, bias, True, group, size, order
    )

    memory_grad = lax.psum_scatter(
        memory_part.reshape(seqs, enc_full, width), "head", scatter_dimension=1, tiled=True
    ).astype(F32)
    dn1 = lax.psum_scatter(
        input_part.reshape(seqs, full, width), "head", scatter_dimension=1, tiled=True
    ).astype(F32)
    lines = jnp.concatenate([gain1, gain2, gain3], axis=0).reshape(-1, 2 * block)
    spare = -(lines.shape[0] + diag.shape[0]) % 8
    small = jnp.concatenate([lines, diag, jnp.zeros((spare, 2 * block), F32)], axis=0)
    if tight:
        feed_w, cross_w, self_w, small = reduce_blocks([feed_w, cross_w, self_w], small, 4 * win)
    else:
        feed_w, cross_w, self_w = (
            lax.psum_scatter(
                w.reshape(shards * width, w.shape[2]).astype(F32),
                ("head", "batch"),
                scatter_dimension=0,
                tiled=True,
            )
            for w in (feed_w, cross_w, self_w)
        )
        small = lax.psum(small, ("batch", "head"))
    gains = small[: lines.shape[0]].reshape(3, width)
    diag = lax.dynamic_slice_in_dim(small, lines.shape[0] + me[0] * group, group, 0)
    table_grad = jnp.einsum("tb,ht->bh", onehot, diag, precision=highest)
    dx, _ = norm_grads(x32, sg, dn1.reshape(rows, width))
    input_grad = (dy1 + dx).reshape(seqs, block, width)

    def split(w):
        kv = jnp.stack([w[:, :win], w[:, win : 2 * win]])
        return w[:, 2 * win : 3 * win], kv, w[:, 3 * win :].T

    self_q, self_kv, self_o = split(self_w)
    cross_q, cross_kv, cross_o = split(cross_w)
    return (
        result.reshape(seqs, block, width),
        input_grad,
        memory_grad,
        gains[0],
        self_q,
        self_kv,
        self_o,
        table_grad,
        gains[1],
        cross_q,
        cross_kv,
        cross_o,
        gains[2],
        jnp.stack([feed_w[:, :part], feed_w[:, part : 2 * part]]),
        feed_w[:, 2 * part :].T,
    )


def solution(mesh):
    return jax.shard_map(
        per_device,
        mesh=mesh,
        in_specs=(
            P("batch", "head", None),
            P("batch", "head", None),
            P("batch"),
            P("batch"),
            P(),
            P(None, "head"),
            P(None, None, "head"),
            P("head", None),
            P(None, "head"),
            P(),
            P(None, "head"),
            P(None, None, "head"),
            P("head", None),
            P(),
            P(),
            P(),
            P("batch", "head", None),
        ),
        out_specs=(
            P("batch", "head", None),
            P("batch", "head", None),
            P("batch", "head", None),
            P(),
            P("batch", "head"),
            P(None, "batch", "head"),
            P("head", "batch"),
            P(None, "head"),
            P(),
            P("batch", "head"),
            P(None, "batch", "head"),
            P("head", "batch"),
            P(),
            P(None, "batch", "head"),
            P("head", "batch"),
        ),
        check_vma=False,
    )
```

```python
import functools
import math

import jax
import jax.numpy as jnp
from jax import lax
from jax.experimental import pallas as pl
from jax.experimental.pallas import tpu as pltpu
from jax.sharding import PartitionSpec as P

NB = 32
MAX_DIST = 128
NEG = -1e30
VMEM_LIMIT = 56 * 1024 * 1024
F32 = jnp.float32
BF16 = jnp.bfloat16

highest = lax.Precision.HIGHEST


def bucket_edges(num_buckets, max_distance):
    exact_part = num_buckets // 2
    edge_list = []
    for target in range(1, num_buckets - exact_part):
        distance = exact_part
        while (
            math.floor(
                math.log(distance / exact_part)
                / math.log(max_distance / exact_part)
                * (num_buckets - exact_part)
            )
            < target
        ):
            distance += 1
        edge_list.append(distance)
    return edge_list


def bucket_of(distance, num_buckets, max_distance):
    exact_part = num_buckets // 2
    counted = jnp.zeros(distance.shape, jnp.int32)
    for edge_value in bucket_edges(num_buckets, max_distance):
        counted = counted + (distance >= edge_value).astype(jnp.int32)
    return jnp.where(distance < exact_part, distance, exact_part + counted).astype(jnp.int32)


def near_onehot(block):
    distance = block - jnp.arange(2 * block)
    distance = jnp.where(distance < 0, 2 * MAX_DIST, distance)
    return (
        bucket_of(distance, NB, MAX_DIST)[:, None] == jnp.arange(NB)[None, :]
    ).astype(F32)


def nn(a, b):
    return lax.dot_general(a, b, (((1,), (0,)), ((), ())), preferred_element_type=F32)


def nt(a, b):
    return lax.dot_general(a, b, (((1,), (1,)), ((), ())), preferred_element_type=F32)


def tn(a, b):
    return lax.dot_general(a, b, (((0,), (0,)), ((), ())), preferred_element_type=F32)


def rms(v):
    return lax.rsqrt(jnp.mean(v * v, axis=-1, keepdims=True) + 1e-06)


def norm_grads(y, gain, e):
    r = rms(y)
    xhat = y * r
    eg = e * gain
    dy = r * (eg - xhat * jnp.mean(eg * xhat, axis=-1, keepdims=True))
    return dy, jnp.sum(e * xhat, axis=0, keepdims=True)


def padded(v, width):
    extra = width - v.shape[1]
    if extra == 0:
        return v
    return jnp.concatenate([v, jnp.zeros((v.shape[0], extra), v.dtype)], axis=1)


def put_rows(ref, value, order):
    step = value.shape[0] // len(order)
    for source, slot in enumerate(order):
        ref[slot * step : (slot + 1) * step, :] = value[source * step : (source + 1) * step, :]


def vmem():
    return pl.BlockSpec(memory_space=pltpu.VMEM)


def smem():
    return pl.BlockSpec(memory_space=pltpu.SMEM)


def params():
    return pltpu.CompilerParams(vmem_limit_bytes=VMEM_LIMIT)


def sds(shape, dtype):
    return jax.ShapeDtypeStruct(shape, dtype)


def bias_kernel(me_ref, table_ref, onehot_ref, b_ref, ext_ref, line_ref):
    heads, block, full = b_ref.shape
    shards = table_ref.shape[0]
    group = heads // shards
    me = me_ref[0]
    start = pl.multiple_of(me * block, block)
    width = 2 * block
    row_i = lax.broadcasted_iota(jnp.int32, (block, width), 0)
    col_i = lax.broadcasted_iota(jnp.int32, (block, width), 1)
    masked = (col_i - row_i) > block
    far = lax.broadcasted_iota(jnp.int32, ext_ref.shape, 1) < start

    def body(h, carry):
        line_ref[...] = tn(table_ref[h], onehot_ref[...])
        for a in range(group):
            row = line_ref[a : a + 1, :]
            tile = pltpu.roll(
                jnp.broadcast_to(row, (block, width)), 0, 1, stride=1, stride_axis=0
            )
            ext_ref[...] = jnp.where(far, row[:, width - 1 : width], NEG)
            ext_ref[:, pl.ds(start, width)] = jnp.where(masked, NEG, tile)
            b_ref[h * group + a] = ext_ref[:, block:]
        return carry

    lax.fori_loop(0, shards, body, 0)


def bias_tiles(me, tables, onehot, group, block, full):
    shards, buckets, lanes = tables.shape
    return pl.pallas_call(
        bias_kernel,
        out_shape=sds((shards * group, block, full), F32),
        in_specs=[smem(), vmem(), vmem()],
        out_specs=vmem(),
        scratch_shapes=[
            pltpu.VMEM((block, full + block), F32),
            pltpu.VMEM((lanes, 2 * block), F32),
        ],
        compiler_params=params(),
        name="bias_tiles",
    )(me, tables, onehot)


def lane_groups(width, group, size):
    lane = lax.broadcasted_iota(jnp.int32, (1, width), 1)
    return [(lane // size) == a for a in range(group)]


def stack_heads(win, lanes):
    return jnp.concatenate([jnp.where(m, win, jnp.zeros_like(win)) for m in lanes], axis=0)


def join_heads(tall, lanes, rows):
    total = jnp.where(lanes[0], tall[:rows], 0.0)
    for a in range(1, len(lanes)):
        total = total + jnp.where(lanes[a], tall[a * rows : (a + 1) * rows], 0.0)
    return total


def forward_kernel(
    biased, group, size, len_ref, nq_ref, nk_ref, res_ref, wq_ref, wkv_ref, wo_ref, gain_ref, *rest
):
    if biased:
        b_ref, *rest = rest
    q_ref, k_ref, v_ref, c_ref, lse_ref, y_ref, n_ref = rest
    shards, rows, pw = q_ref.shape
    seqs = len_ref.shape[0]
    block = rows // seqs
    full = k_ref.shape[1] // seqs
    win = group * size
    lanes = lane_groups(pw, group, size)
    lane128 = lax.broadcasted_iota(jnp.int32, (block, 128), 1)
    key = lax.broadcasted_iota(jnp.int32, (1, full), 1)

    def body(h, carry):
        q_ref[h] = padded(nt(nq_ref[...], wq_ref[h]).astype(BF16), pw)
        k_ref[h] = padded(nt(nk_ref[...], wkv_ref[h, 0]).astype(BF16), pw)
        v_ref[h] = padded(nt(nk_ref[...], wkv_ref[h, 1]).astype(BF16), pw)
        for s in range(seqs):
            kw = k_ref[h, s * full : (s + 1) * full, :]
            vw = v_ref[h, s * full : (s + 1) * full, :]
            qcat = stack_heads(q_ref[h, s * block : (s + 1) * block, :], lanes)
            sc = nt(qcat, kw)
            if biased:
                sc = sc + b_ref[pl.ds(h * group, group)].reshape(group * block, full)
            sc = jnp.where(key < len_ref[s], sc, NEG)
            top = jnp.max(sc, axis=-1, keepdims=True)
            e = jnp.exp(sc - top)
            total = jnp.sum(e, axis=-1, keepdims=True)
            p = (e * (1.0 / total)).astype(BF16)
            c = join_heads(nn(p, vw), lanes, block)
            c_ref[h, s * block : (s + 1) * block, :] = c.astype(BF16)
            lse = top + jnp.log(total)
            tile = jnp.zeros((block, 128), F32)
            for a in range(group):
                tile = jnp.where(lane128 == a, lse[a * block : (a + 1) * block], tile)
            lse_ref[h, s] = tile
        return carry

    lax.fori_loop(0, shards, body, 0)
    joined = jnp.concatenate([c_ref[h][:, :win] for h in range(shards)], axis=1)
    y = res_ref[...].astype(F32) + nn(joined, wo_ref[...])
    y_ref[...] = y
    n_ref[...] = (y * rms(y) * gain_ref[...]).astype(BF16)


def attend_forward(lens, nq, nk, res, wq, wkv, wo, gain, bias, group, size):
    rows, width = nq.shape
    shards = wq.shape[0]
    pw = -(-group * size // 128) * 128
    seqs = lens.shape[0]
    args = [lens, nq, nk, res, wq, wkv, wo, gain] + ([bias] if bias is not None else [])
    keys = nk.shape[0]
    flops = 2 * (rows + 2 * keys + rows) * width * width + 4 * rows * keys * width
    return pl.pallas_call(
        functools.partial(forward_kernel, bias is not None, group, size),
        out_shape=[
            sds((shards, rows, pw), BF16),
            sds((shards, keys, pw), BF16),
            sds((shards, keys, pw), BF16),
            sds((shards, rows, pw), BF16),
            sds((shards, seqs, rows // seqs, 128), F32),
            sds((rows, width), F32),
            sds((rows, width), BF16),
        ],
        in_specs=[smem()] + [vmem()] * (len(args) - 1),
        out_specs=[vmem()] * 7,
        compiler_params=params(),
        cost_estimate=pl.CostEstimate(
            flops=flops, bytes_accessed=16 << 20, transcendentals=rows * keys * 6
        ),
        name="attend_forward",
    )(*args)


def backward_kernel(
    biased,
    group,
    size,
    order,
    len_ref,
    me_ref,
    nq_ref,
    nk_ref,
    q_ref,
    k_ref,
    v_ref,
    c_ref,
    lse_ref,
    wq_ref,
    wkv_ref,
    wo_ref,
    dy_ref,
    gain_ref,
    *rest,
):
    if biased:
        b_ref, part_ref, gg_ref, w_ref, diag_ref, dc_ref, dq_ref, dkv_ref, acc_ref, nqt_ref, nkt_ref, dat_ref, sum_ref, ext_ref = rest
    else:
        y_ref, part_ref, gg_ref, w_ref, dprev_ref, dc_ref, dq_ref, dkv_ref, acc_ref, nqt_ref, nkt_ref, dat_ref = rest
    shards, rows, pw = q_ref.shape
    seqs = len_ref.shape[0]
    block = rows // seqs
    full = k_ref.shape[1] // seqs
    win = group * size
    lanes = lane_groups(pw, group, size)
    key = lax.broadcasted_iota(jnp.int32, (1, full), 1)
    me = me_ref[0]

    da = dy_ref[...].astype(BF16)
    put_rows(nqt_ref, nq_ref[...].T, order)
    put_rows(nkt_ref, nk_ref[...].T, order)
    put_rows(dat_ref, da.T, order)
    if biased:
        ext_ref[:, :block] = jnp.zeros((block, block), F32)
        start = pl.multiple_of(me * block, block)
        far = lax.broadcasted_iota(jnp.int32, ext_ref.shape, 1) < start
        row8 = lax.broadcasted_iota(jnp.int32, (8, 2 * block), 0)
        lane_near = lax.broadcasted_iota(jnp.int32, (1, 2 * block), 1)

    def body(h, carry):
        wo_h = wo_ref[pl.ds(pl.multiple_of(h * win, size), win), :]
        dc_ref[...] = padded(nt(da, wo_h).astype(BF16), pw)
        for s in range(seqs):
            kw = k_ref[h, s * full : (s + 1) * full, :]
            vw = v_ref[h, s * full : (s + 1) * full, :]
            qcat = stack_heads(q_ref[h, s * block : (s + 1) * block, :], lanes)
            dcat = stack_heads(dc_ref[s * block : (s + 1) * block, :], lanes)
            sc = nt(qcat, kw)
            if biased:
                sc = sc + b_ref[pl.ds(h * group, group)].reshape(group * block, full)
            sc = jnp.where(key < len_ref[s], sc, NEG)
            lse_tile = lse_ref[h, s]
            lse = jnp.concatenate([lse_tile[:, a : a + 1] for a in range(group)], axis=0)
            p = jnp.exp(sc - lse)
            dp = nt(dcat, vw)
            ds = p * (dp - jnp.sum(p * dp, axis=-1, keepdims=True))
            ds = ds.astype(BF16)
            pb = p.astype(BF16)
            if biased:
                if s == 0:
                    sum_ref[...] = ds.astype(F32)
                else:
                    sum_ref[...] += ds.astype(F32)
            dq = join_heads(nn(ds, kw), lanes, block)
            dq_ref[s * block : (s + 1) * block, :] = dq.astype(BF16)
            dk = tn(ds, qcat).astype(BF16)
            dv = tn(pb, dcat).astype(BF16)
            dkv_ref[s * full : (s + 1) * full, :] = jnp.concatenate(
                [dk[:, :win], dv[:, :win]], axis=1
            )
        if biased:
            for a in range(group):
                ext_ref[:, block:] = sum_ref[a * block : (a + 1) * block, :]
                far_sum = jnp.sum(jnp.where(far, ext_ref[...], 0.0))
                fold = ext_ref[:, pl.ds(start, 2 * block)]
                half = block // 2
                while half >= 8:
                    fold = fold[:half] + pltpu.roll(fold[half:], 2 * block - half, 1)
                    half //= 2
                for bit in (4, 2, 1):
                    fold = jnp.where(
                        (row8 & bit) != 0, pltpu.roll(fold, 2 * block - bit, 1), fold
                    )
                line = jnp.sum(fold, axis=0, keepdims=True)
                line = line + jnp.where(lane_near == 2 * block - 1, far_sum, 0.0)
                diag_ref[pl.ds(h * group + a, 1), :] = line
        dkv = dkv_ref[...]
        dq_h = dq_ref[...][:, :win]
        kv_term = nn(dkv[:, :win], wkv_ref[h, 0]) + nn(dkv[:, win:], wkv_ref[h, 1])
        q_term = nn(dq_h, wq_ref[h])
        w_ref[h] = jnp.concatenate(
            [
                nn(nkt_ref[...], dkv).astype(BF16),
                nn(nqt_ref[...], dq_h).astype(BF16),
                nn(dat_ref[...], c_ref[h][:, :win]).astype(BF16),
            ],
            axis=1,
        )

        @pl.when(h == 0)
        def _():
            acc_ref[: seqs * full, :] = kv_term
            acc_ref[seqs * full :, :] = q_term

        @pl.when(h != 0)
        def _():
            acc_ref[: seqs * full, :] += kv_term
            acc_ref[seqs * full :, :] += q_term

        return carry

    lax.fori_loop(0, shards, body, 0)
    if biased:
        for s in range(seqs):
            own = pl.ds(pl.multiple_of(s * full + me * block, block), block)
            acc_ref[own, :] += acc_ref[seqs * full + s * block : seqs * full + (s + 1) * block, :]
        total = acc_ref[: seqs * full, :]
        part_ref[...] = total.astype(BF16)
        gg_ref[...] = (
            jnp.sum(total * nk_ref[...].astype(F32), axis=0, keepdims=True) / gain_ref[...]
        )
    else:
        part_ref[...] = acc_ref[: seqs * full, :].astype(BF16)
        dy, gg = norm_grads(y_ref[...], gain_ref[...], acc_ref[seqs * full :, :])
        dprev_ref[...] = dy_ref[...] + dy
        gg_ref[...] = gg


def attend_backward(
    lens, me, nq, nk, saved, wq, wkv, wo, dy, gain, extra, biased, group, size, order
):
    q, k, v, c, lse = saved
    rows, width = nq.shape
    shards, keys, pw = k.shape
    block = rows // lens.shape[0]
    full = keys // lens.shape[0]
    win = group * size
    args = [lens, me, nq, nk, q, k, v, c, lse, wq, wkv, wo, dy, gain, extra]
    out_shape = [
        sds((keys, width), BF16),
        sds((1, width), F32),
        sds((shards, width, 4 * win), BF16),
        sds((shards * group, 2 * block), F32) if biased else sds((rows, width), F32),
    ]
    scratch = [
        pltpu.VMEM((rows, pw), BF16),
        pltpu.VMEM((rows, pw), BF16),
        pltpu.VMEM((keys, 2 * win), BF16),
        pltpu.VMEM((keys + rows, width), F32),
        pltpu.VMEM((width, rows), BF16),
        pltpu.VMEM((width, keys), BF16),
        pltpu.VMEM((width, rows), BF16),
    ]
    if biased:
        scratch += [
            pltpu.VMEM((group * block, full), F32),
            pltpu.VMEM((block, full + block), F32),
        ]
    flops = 4 * (rows + 2 * keys + rows) * width * width + 10 * rows * full * width
    return pl.pallas_call(
        functools.partial(backward_kernel, biased, group, size, order),
        out_shape=out_shape,
        in_specs=[smem(), smem()] + [vmem()] * (len(args) - 2),
        out_specs=[vmem()] * 4,
        scratch_shapes=scratch,
        compiler_params=params(),
        cost_estimate=pl.CostEstimate(
            flops=flops, bytes_accessed=24 << 20, transcendentals=rows * full * 12
        ),
        name="attend_backward",
    )(*args)


def feed_kernel(
    order, y_ref, n_ref, cot_ref, win_ref, wout_ref, gain_ref, out_ref, dy_ref, gg_ref, w_ref,
    acc_ref, dn_ref, nt_ref, ct_ref,
):
    step = pl.program_id(0)
    part = wout_ref.shape[0]

    @pl.when(step == 0)
    def _():
        put_rows(nt_ref, n_ref[...].T, order)
        put_rows(ct_ref, cot_ref[...].T, order)
        acc_ref[...] = y_ref[...]
        dn_ref[...] = jnp.zeros_like(dn_ref)

    n = n_ref[...]
    cot = cot_ref[...]
    g = nn(n, win_ref[0])
    u = nn(n, win_ref[1])
    dh = nt(cot, wout_ref[...])
    scale = math.sqrt(2.0 / math.pi)
    square = g * g
    t = jnp.tanh(scale * (g + 0.044715 * square * g))
    half = 0.5 * (1.0 + t)
    gelu = g * half
    hid = (gelu * u).astype(BF16)
    slope = half + 0.5 * g * (1.0 - t * t) * (scale * (1.0 + 3 * 0.044715 * square))
    dg = (dh * u * slope).astype(BF16)
    du = (dh * gelu).astype(BF16)
    acc_ref[...] += nn(hid, wout_ref[...])
    dn_ref[...] += nt(dg, win_ref[0]) + nt(du, win_ref[1])
    w_ref[0, :, :part] = nn(nt_ref[...], dg).astype(BF16)
    w_ref[0, :, part : 2 * part] = nn(nt_ref[...], du).astype(BF16)
    w_ref[0, :, 2 * part :] = nn(ct_ref[...], hid).astype(BF16)

    @pl.when(step == pl.num_programs(0) - 1)
    def _():
        out_ref[...] = acc_ref[...].astype(BF16)
        dy, gg = norm_grads(y_ref[...], gain_ref[...], dn_ref[...])
        dy_ref[...] = cot_ref[...].astype(F32) + dy
        gg_ref[...] = gg


def feed(y, n, cot, w_in, w_out, gain, shards, order):
    rows, width = y.shape
    hidden = w_out.shape[0]
    part = hidden // shards
    fixed = lambda shape: pl.BlockSpec(shape, lambda j: (0,) * len(shape))
    return pl.pallas_call(
        functools.partial(feed_kernel, order),
        grid=(shards,),
        out_shape=[
            sds((rows, width), BF16),
            sds((rows, width), F32),
            sds((1, width), F32),
            sds((shards, width, 3 * part), BF16),
        ],
        in_specs=[
            fixed((rows, width)),
            fixed((rows, width)),
            fixed((rows, width)),
            pl.BlockSpec((2, width, part), lambda j: (0, 0, j)),
            pl.BlockSpec((part, width), lambda j: (j, 0)),
            fixed((1, width)),
        ],
        out_specs=[
            fixed((rows, width)),
            fixed((rows, width)),
            fixed((1, width)),
            pl.BlockSpec((1, width, 3 * part), lambda j: (j, 0, 0)),
        ],
        scratch_shapes=[
            pltpu.VMEM((rows, width), F32),
            pltpu.VMEM((rows, width), F32),
            pltpu.VMEM((width, rows), BF16),
            pltpu.VMEM((width, rows), BF16),
        ],
        compiler_params=params(),
        cost_estimate=pl.CostEstimate(
            flops=18 * rows * width * hidden, bytes_accessed=24 << 20, transcendentals=rows * hidden
        ),
        name="feed",
    )(y, n, cot, w_in, w_out, gain)


MESH = pl.DeviceIdType.MESH


def place():
    b = lax.axis_index("batch")
    me = lax.axis_index("head")
    core = lax.rem(b, 2)
    x = lax.rem(lax.div(b, 2), 2)
    y = lax.div(b, 4)
    return b, me, core, x, y


def near_devices(b, me, core, x, y, shards):
    over_core = (b + 1 - 2 * core, me)
    over_x = (b + 2 - 4 * x, me)
    over_y = (b + 4 - 8 * y, me)
    across = (b + 2 - 4 * x + 4 - 8 * y, me)
    ahead = [(b, lax.rem(me + k, shards)) for k in range(1, shards)]
    return over_core, over_x, over_y, across, ahead


def greet(devices):
    barrier = pltpu.get_barrier_semaphore()
    for device in devices:
        pl.semaphore_signal(barrier, inc=1, device_id=device, device_id_type=MESH)
    pl.semaphore_wait(barrier, len(devices))


def remote(src, dst, send, recv, device):
    return pltpu.make_async_remote_copy(
        src_ref=src,
        dst_ref=dst,
        send_sem=send,
        recv_sem=recv,
        device_id=device,
        device_id_type=MESH,
    )


def gather_kernel(n, *refs):
    shard_refs, table_ref = refs[:n], refs[n]
    full_refs, tables_ref = refs[n + 1 : 2 * n + 1], refs[2 * n + 1]
    (zs, zr, ps, pr, cs, cr, ts, tr, local) = refs[2 * n + 2 :]
    shards = tables_ref.shape[0]
    b, me, core, x, y = place()
    over_core, over_x, over_y, across, ahead = near_devices(b, me, core, x, y, shards)
    greet([over_core, over_x, over_y, across] + ahead)
    slot = core * 4 + lax.div(b, 2)

    def window(ref, first, count):
        step = ref.shape[-2] // 8
        rows = pl.ds(pl.multiple_of(first * step, step), count * step)
        return ref.at[:, rows, :]

    started = []

    def start(copy):
        copy.start()
        started.append(copy)
        return copy

    from_z, from_plane, from_core = {}, {}, {}
    for k in range(1, shards):
        start(remote(table_ref, tables_ref.at[me], ts.at[k - 1], tr.at[k - 1], ahead[k - 1]))
    for i in range(n):
        for k in range(1, shards):
            from_z[i, k] = start(
                remote(
                    window(shard_refs[i], slot, 1),
                    window(full_refs[i].at[me], slot, 1),
                    zs.at[i, k - 1],
                    zr.at[i, k - 1],
                    ahead[k - 1],
                )
            )
    copies = [pltpu.make_async_copy(table_ref, tables_ref.at[me], local.at[n])]
    copies += [
        pltpu.make_async_copy(shard_refs[i], full_refs[i].at[me], local.at[i]) for i in range(n)
    ]
    for copy in copies:
        copy.start()
    for i in range(n):
        for k in range(1, shards):
            from_z[i, k].wait_recv()
            piece = window(full_refs[i].at[lax.rem(me + shards - k, shards)], slot, 1)
            for d, device in enumerate((over_x, over_y, across)):
                from_plane[i, k, d] = start(
                    remote(piece, piece, ps.at[i, k - 1, d], pr.at[i, k - 1, d], device)
                )
    for i in range(n):
        for k in range(1, shards):
            for d in range(3):
                from_plane[i, k, d].wait_recv()
            half = window(full_refs[i].at[lax.rem(me + shards - k, shards)], core * 4, 4)
            from_core[i, k] = start(
                remote(half, half, cs.at[i, k - 1], cr.at[i, k - 1], over_core)
            )
    for copy in from_core.values():
        copy.wait_recv()
    for k in range(1, shards):
        started[k - 1].wait_recv()
    for copy in started:
        copy.wait_send()
    for copy in copies:
        copy.wait()


def gather_weights(weights, table, shards):
    n = len(weights)
    anywhere = pl.BlockSpec(memory_space=pl.ANY)
    dma = pltpu.SemaphoreType.DMA
    return pl.pallas_call(
        functools.partial(gather_kernel, n),
        out_shape=[sds((shards, *w.shape), w.dtype) for w in weights]
        + [sds((shards, *table.shape), table.dtype)],
        in_specs=[anywhere] * (n + 1),
        out_specs=[anywhere] * (n + 1),
        scratch_shapes=[
            dma((n, shards - 1)),
            dma((n, shards - 1)),
            dma((n, shards - 1, 3)),
            dma((n, shards - 1, 3)),
            dma((n, shards - 1)),
            dma((n, shards - 1)),
            dma((shards - 1,)),
            dma((shards - 1,)),
            dma((n + 1,)),
        ],
        compiler_params=pltpu.CompilerParams(
            collective_id=0, has_side_effects=True, vmem_limit_bytes=VMEM_LIMIT
        ),
        name="gather_weights",
    )(*weights, table)


def flipped(bit, by):
    return bit + by - 2 * bit * by


class Links:
    def __init__(self):
        b, me, core, x, y = place()
        self.me, self.core, self.x, self.y = me, core, x, y
        self.high, self.low = lax.div(me, 2), lax.rem(me, 2)
        self.pair, self.far, self.cross = self.owner(1), self.owner(2), self.owner(0)
        self.over_core = (b + 1 - 2 * core, me)
        self.over_x = (b + 2 - 4 * x, me)
        self.over_y = (b + 4 - 8 * y, me)
        self.to_pair, self.to_far, self.to_cross = (b, self.pair), (b, self.far), (b, self.cross)

    def owner(self, k):
        by_low, by_high = 1 - k // 2, 1 - k % 2
        return 2 * flipped(self.high, by_high) + flipped(self.low, by_low)

    def greet(self):
        greet(
            [self.over_core, self.over_x, self.over_y, self.to_pair, self.to_far, self.to_cross]
        )


class Sums:
    @staticmethod
    def scratch(chunks, rows, cols):
        items, half = chunks // 4, cols // 2
        dma = pltpu.SemaphoreType.DMA
        return [
            pltpu.VMEM((chunks, 2, 2, rows, cols), BF16),
            pltpu.VMEM((chunks, 2, 2, rows, cols), BF16),
            pltpu.VMEM((chunks, 2, rows, half), BF16),
            pltpu.VMEM((chunks, 2, rows, half), BF16),
            pltpu.VMEM((chunks, rows, half), BF16),
            pltpu.VMEM((chunks, rows, half), BF16),
            pltpu.VMEM((chunks, rows, cols), BF16),
            pltpu.VMEM((items, 3, rows, cols), BF16),
            dma((chunks,)),
            dma((chunks,)),
            dma((chunks,)),
            dma((chunks, 2)),
            dma((chunks, 2)),
            dma((chunks, 2)),
            dma((chunks, 2)),
            dma((items, 3)),
            dma((items, 3)),
        ]

    count = 17

    def __init__(self, links, refs):
        (self.own, self.rc, self.r1a, self.r1b, self.r2a, self.r2b, self.tot, self.rz) = refs[:8]
        (self.ls, self.cs, self.cr, self.s1, self.q1, self.s2, self.q2, self.zs, self.zr) = refs[8:]
        self.links = links
        self.chunks, self.cols = self.own.shape[0], self.own.shape[-1]
        self.half = self.cols // 2

    def piece(self, w_ref, c, side, base):
        start = pl.multiple_of(((c - base) // 4) * self.cols, self.cols)
        return w_ref.at[self.links.owner((c - base) % 4), side, :, :, :, pl.ds(start, self.cols)]

    def local(self, w_ref, c, base):
        return pltpu.make_async_copy(
            self.piece(w_ref, c, self.links.core, base), self.own.at[c], self.ls.at[c]
        )

    def over_core(self, c, source):
        return remote(
            source, self.rc.at[c], self.cs.at[c], self.cr.at[c], self.links.over_core
        )

    def load(self, w_ref, c, base=0):
        self.local(w_ref, c, base).start()
        self.over_core(c, self.piece(w_ref, c, 1 - self.links.core, base)).start()

    def firsts(self, c):
        links, half = self.links, self.half
        return (
            remote(
                self.own.at[c, :, 1 - links.x, :, pl.ds(0, half)],
                self.r1a.at[c],
                self.s1.at[c, 0],
                self.q1.at[c, 0],
                links.over_x,
            ),
            remote(
                self.own.at[c, 1 - links.y, :, :, pl.ds(half, half)],
                self.r1b.at[c],
                self.s1.at[c, 1],
                self.q1.at[c, 1],
                links.over_y,
            ),
        )

    def seconds(self, c):
        links = self.links
        return (
            remote(
                self.r1a.at[c, 1 - links.y],
                self.r2a.at[c],
                self.s2.at[c, 0],
                self.q2.at[c, 0],
                links.over_y,
            ),
            remote(
                self.r1b.at[c, 1 - links.x],
                self.r2b.at[c],
                self.s2.at[c, 1],
                self.q2.at[c, 1],
                links.over_x,
            ),
        )

    def along(self, item, slot, c):
        device = self.links.to_far if slot == 2 else self.links.to_pair
        return remote(
            self.tot.at[c],
            self.rz.at[item, slot],
            self.zs.at[item, slot],
            self.zr.at[item, slot],
            device,
        )

    def core(self, c, base=0, w_ref=None, mine=None):
        if mine is None:
            self.local(w_ref, c, base).wait()
            mine = self.own[c]
        self.over_core(c, self.rc.at[c]).wait_recv()
        self.own[c] = mine + self.rc[c]
        for copy in self.firsts(c):
            copy.start()

    def first(self, c):
        for copy in self.firsts(c):
            copy.wait_recv()
        links, half = self.links, self.half
        for other in range(2):
            self.r1a[c, other] = self.r1a[c, other] + self.own[c, other, links.x, :, :half]
            self.r1b[c, other] = self.r1b[c, other] + self.own[c, links.y, other, :, half:]
        for copy in self.seconds(c):
            copy.start()

    def second(self, c):
        for copy in self.seconds(c):
            copy.wait_recv()
        links, half = self.links, self.half
        self.tot[c, :, :half] = self.r1a[c, links.y] + self.r2a[c]
        self.tot[c, :, half:] = self.r1b[c, links.x] + self.r2b[c]
        item, k = c // 4, c % 4
        for slot in range(2):

            @pl.when(k == slot)
            def _(slot=slot):
                self.along(item, slot, c).start()

        @pl.when(k == 2)
        def _():
            self.along(item, 0, c).wait_recv()
            self.tot[c] = self.tot[c] + self.rz[item, 0]
            self.along(item, 2, c).start()

    def finish(self, item):
        c = 4 * item
        for slot in (1, 2):
            self.along(item, slot, c).wait_recv()
        total = self.tot[c + 3].astype(F32)
        return total + self.rz[item, 1].astype(F32) + self.rz[item, 2].astype(F32)

    def drain(self):
        def body(c, carry):
            self.over_core(c, self.rc.at[c]).wait_send()
            for copy in self.firsts(c) + self.seconds(c):
                copy.wait_send()
            return carry

        lax.fori_loop(0, self.chunks, body, 0)
        for item in range(self.chunks // 4):
            for slot in range(3):
                self.along(item, slot, 4 * item).wait_send()


class Rows:
    @staticmethod
    def scratch(rows, width):
        dma = pltpu.SemaphoreType.DMA
        return [
            pltpu.VMEM((4, rows, width), BF16),
            pltpu.VMEM((3, rows, width), BF16),
            dma((3,)),
            dma((3,)),
        ]

    count = 4

    def __init__(self, links, refs):
        self.links = links
        self.buf, self.rx, self.ss, self.rs = refs

    def copy(self, slot):
        links = self.links
        block = (links.cross, links.pair, links.far)[slot]
        device = links.to_far if slot == 2 else links.to_pair
        return remote(
            self.buf.at[block], self.rx.at[slot], self.ss.at[slot], self.rs.at[slot], device
        )

    def start(self):
        self.copy(0).start()
        self.copy(1).start()

    def middle(self):
        self.copy(0).wait_recv()
        far = self.links.far
        self.buf[far] = self.buf[far] + self.rx[0]
        self.copy(2).start()

    def finish(self):
        for slot in (1, 2):
            self.copy(slot).wait_recv()
        return self.rx[1].astype(F32) + self.rx[2].astype(F32)

    def drain(self):
        for slot in range(3):
            self.copy(slot).wait_send()


def head_grads(qw, kw, vw, dcw, lse_tile, bias, keep, lanes):
    block, group = qw.shape[0], len(lanes)
    qcat, dcat = stack_heads(qw, lanes), stack_heads(dcw, lanes)
    sc = nt(qcat, kw)
    if bias is not None:
        sc = sc + bias
    sc = jnp.where(keep, sc, NEG)
    lse = jnp.concatenate([lse_tile[:, a : a + 1] for a in range(group)], axis=0)
    p = jnp.exp(sc - lse)
    dp = nt(dcat, vw)
    ds = (p * (dp - jnp.sum(p * dp, axis=-1, keepdims=True))).astype(BF16)
    dq = join_heads(nn(ds, kw), lanes, block).astype(BF16)
    dk = tn(ds, qcat).astype(BF16)
    dv = tn(p.astype(BF16), dcat).astype(BF16)
    return ds, dq, dk, dv


def diagonal_line(near, far_sum):
    block, width = near.shape
    half = block // 2
    while half >= 8:
        near = near[:half] + pltpu.roll(near[half:], width - half, 1)
        half //= 2
    row8 = lax.broadcasted_iota(jnp.int32, (8, width), 0)
    for bit in (4, 2, 1):
        near = jnp.where((row8 & bit) != 0, pltpu.roll(near, width - bit, 1), near)
    line = jnp.sum(near, axis=0, keepdims=True)
    lane = lax.broadcasted_iota(jnp.int32, (1, width), 1)
    return line + jnp.where(lane == width - 1, far_sum, 0.0)


def linked_kernel(biased, group, size, order, *refs):
    (len_ref, nq_ref, nk_ref, q_ref, k_ref, v_ref, c_ref, lse_ref, wq_ref, wkv_ref, wo_ref) = refs[:11]
    dy_ref, gain_ref, given_ref, refs = refs[11], refs[12], refs[13], refs[14:]
    if biased:
        bias_ref, x_ref, rows_ref, lines_ref, grad_ref, mem_ref, given_out, own_out, small_out, *refs = refs
    else:
        y_ref, dprev_ref, gg_ref, w_ref, later_ref, mem_ref, given_out, *refs = refs
    dq_ref, dkv_ref, acck_ref, accq_ref, nqt_ref, nkt_ref, dat_ref, *refs = refs
    links = Links()
    sums = Sums(links, refs[: Sums.count])
    refs = refs[Sums.count :]
    exchanges = []
    for _ in range(3 if biased else 1):
        exchanges.append(Rows(links, refs[: Rows.count]))
        refs = refs[Rows.count :]
    if biased:
        ds_ref, ext_ref, wtmp_ref, diag_ref, sr, ms, mr = refs
    shards, rows, pw = q_ref.shape
    seqs = len_ref.shape[0]
    block = rows // seqs
    full = k_ref.shape[1] // seqs
    win = group * size
    lanes = lane_groups(pw, group, size)
    key = lax.broadcasted_iota(jnp.int32, (1, full), 1)
    me = links.me
    start = pl.multiple_of(me * block, block)
    ready = 4 if biased else 8
    lag = 1 if biased else 0

    links.greet()
    for c in range(ready):
        sums.load(given_ref, c)
    if biased:
        exchanges[0].buf[...] = rows_ref[...]
        exchanges[0].start()

    def core(c):
        if biased:

            @pl.when(c < ready)
            def _():
                sums.core(c, w_ref=given_ref)

            @pl.when(c >= ready)
            def _():
                sums.core(c, mine=wtmp_ref[c - ready, links.core])

        else:
            sums.core(c, w_ref=given_ref)

    def tick(t):
        for stage, late in ((core, 0), (sums.first, 1), (sums.second, 3)):
            c = t - lag - late

            @pl.when((c >= 0) & (c < sums.chunks))
            def _(stage=stage, c=c):
                stage(c)

    da = dy_ref[...].astype(BF16)
    put_rows(nqt_ref, nq_ref[...].T, order)
    put_rows(nkt_ref, nk_ref[...].T, order)
    put_rows(dat_ref, da.T, order)
    if biased:
        ext_ref[:, :block] = jnp.zeros((block, block), F32)
        far = lax.broadcasted_iota(jnp.int32, ext_ref.shape, 1) < start

    for s in range(seqs):
        mine = slice(s * block, (s + 1) * block)
        theirs = slice(s * full, (s + 1) * full)

        def body(k, carry):
            h = links.owner(k)
            wo_h = wo_ref[pl.ds(pl.multiple_of(h * win, size), win), :]
            dcw = padded(nt(da[mine], wo_h).astype(BF16), pw)
            bias = None
            if biased:
                bias = bias_ref[pl.ds(h * group, group)].reshape(group * block, full)
            ds, dq, dk, dv = head_grads(
                q_ref[h, mine, :],
                k_ref[h, theirs, :],
                v_ref[h, theirs, :],
                dcw,
                lse_ref[h, s],
                bias,
                key < len_ref[s],
                lanes,
            )
            dkv = jnp.concatenate([dk[:, :win], dv[:, :win]], axis=1)
            dkv_ref[h, theirs, :] = dkv
            dq_ref[h, mine, :] = dq
            kv_term = nn(dkv[:, :win], wkv_ref[h, 0]) + nn(dkv[:, win:], wkv_ref[h, 1])
            q_term = nn(dq[:, :win], wq_ref[h])

            @pl.when(k == 0)
            def _():
                acck_ref[...] = kv_term
                accq_ref[mine, :] = q_term

            @pl.when(k != 0)
            def _():
                acck_ref[...] += kv_term
                accq_ref[mine, :] += q_term

            if biased and s < seqs - 1:
                ds_ref[h] = ds if s == 0 else ds_ref[h] + ds
            if biased and s == seqs - 1:
                whole = ds_ref[h].astype(F32) + ds.astype(F32)
                for a in range(group):
                    ext_ref[:, block:] = whole[a * block : (a + 1) * block, :]
                    far_sum = jnp.sum(jnp.where(far, ext_ref[...], 0.0))
                    near = ext_ref[:, pl.ds(start, 2 * block)]
                    diag_ref[pl.ds(h * group + a, 1), :] = diagonal_line(near, far_sum)
            if s == seqs - 1:
                dkv = dkv_ref[h]
                w = jnp.concatenate(
                    [
                        nn(nkt_ref[...], dkv).astype(BF16),
                        nn(nqt_ref[...], dq_ref[h][:, :win]).astype(BF16),
                        nn(dat_ref[...], c_ref[h][:, :win]).astype(BF16),
                    ],
                    axis=1,
                ).reshape(2, 2, 2, w_rows, 4 * win)
                if biased:
                    wtmp_ref[k] = w
                    sums.over_core(ready + k, wtmp_ref.at[k, 1 - links.core]).start()
                else:
                    w_ref[h] = w
            tick(4 * s + k)
            return carry

        w_rows = nqt_ref.shape[0] // 8
        lax.fori_loop(0, shards, body, 0)
        if biased:
            acck_ref[pl.ds(start, block), :] += accq_ref[mine, :]
            total = acck_ref[...]
            part = jnp.sum(total * nk_ref[theirs, :].astype(F32), axis=0, keepdims=True)
            gain1 = part if s == 0 else gain1 + part
            mover = exchanges[1 + s]
            mover.buf[...] = total.astype(BF16).reshape(shards, block, -1)
            mover.start()
            grad_ref[mine, :] = acck_ref[pl.ds(start, block), :]
            if s == 0:
                exchanges[0].middle()
        elif s == 0:
            exchanges[0].buf[...] = acck_ref[...].astype(BF16).reshape(shards, block, -1)
            exchanges[0].start()
            mem_ref[...] = acck_ref[pl.ds(start, block), :]
        else:
            later_ref[...] = acck_ref[...].astype(BF16).reshape(shards, block, -1)

    steps = range(4 * seqs, lag + sums.chunks + 3)
    if not biased:
        exchanges[0].middle()
        dy, gg = norm_grads(y_ref[...], gain_ref[...], accq_ref[...])
        dprev_ref[...] = dy_ref[...] + dy
        gg_ref[...] = gg
        for t in steps:
            tick(t)
        mem_ref[...] += exchanges[0].finish()
        for item in range(sums.chunks // 4):
            cols = slice(item * sums.cols, (item + 1) * sums.cols)
            given_out[:, cols] = sums.finish(item)
    else:
        gain1 = gain1 / gain_ref[...]
        width = gain1.shape[1]
        exchanges[1].middle()
        diag_ref[shards * group :, :] = jnp.zeros_like(diag_ref[shards * group :, :])
        lines = lines_ref.shape[0]
        sr[0, : diag_ref.shape[0], :] = diag_ref[...]
        sr[0, diag_ref.shape[0] :, :] = lines_ref[...]
        for j in range(width // (2 * block)):
            row = diag_ref.shape[0] + j
            sr[0, row : row + 1, :] = gain1[:, j * 2 * block : (j + 1) * 2 * block]
        hops = [links.over_core, links.over_x, links.over_y, links.to_pair, links.to_far]

        def hop(i):
            return remote(sr.at[i], sr.at[len(hops) + 1 + i], ms.at[i], mr.at[i], hops[i])

        hop(0).start()
        for i in range(max(len(steps), len(hops))):
            if i < len(steps):
                tick(steps[i])
            if i < len(hops):
                hop(i).wait_recv()
                sr[i + 1] = sr[i] + sr[len(hops) + 1 + i]
                if i + 1 < len(hops):
                    hop(i + 1).start()
            if i == 1:
                exchanges[2].middle()
        small_out[...] = sr[len(hops)]
        mem_ref[...] = exchanges[0].buf[me].astype(F32) + exchanges[0].finish()
        given_out[...] = sums.finish(0)
        for s in range(seqs):
            mine = slice(s * block, (s + 1) * block)
            dn = grad_ref[mine, :] + exchanges[1 + s].finish()
            dx, _ = norm_grads(x_ref[mine, :].astype(F32), gain_ref[...], dn)
            grad_ref[mine, :] = dy_ref[mine, :] + dx
        own_out[...] = sums.finish(1)
        for i in range(len(hops)):
            hop(i).wait_send()
    for mover in exchanges:
        mover.drain()
    sums.drain()


def linked_backward(lens, nq, nk, saved, wq, wkv, wo, dy, gain, given, extras, biased, group, size, order):
    q, k, v, c, lse = saved
    rows, width = nq.shape
    shards, keys, pw = k.shape
    seqs = lens.shape[0]
    block, full, win = rows // seqs, keys // seqs, group * size
    cols = 4 * win
    share = width // 8
    given = given.reshape(shards, 2, 2, 2, share, -1)
    args = [lens, nq, nk, q, k, v, c, lse, wq, wkv, wo, dy, gain, given, *extras]
    chunks = 8
    if biased:
        lines = extras[3].shape[0]
        diag_rows = -(-shards * group // 8) * 8
        out_shape = [
            sds((rows, width), F32),
            sds((block, width), F32),
            sds((share, cols), F32),
            sds((share, cols), F32),
            sds((diag_rows + lines, 2 * block), F32),
        ]
    else:
        out_shape = [
            sds((rows, width), F32),
            sds((1, width), F32),
            sds((shards, 2, 2, 2, share, cols), BF16),
            sds((shards, block, width), BF16),
            sds((block, width), F32),
            sds((share, given.shape[-1]), F32),
        ]
    scratch = [
        pltpu.VMEM((shards, rows, pw), BF16),
        pltpu.VMEM((shards, keys, 2 * win), BF16),
        pltpu.VMEM((full, width), F32),
        pltpu.VMEM((rows, width), F32),
        pltpu.VMEM((width, rows), BF16),
        pltpu.VMEM((width, keys), BF16),
        pltpu.VMEM((width, rows), BF16),
    ]
    scratch += Sums.scratch(chunks, share, cols)
    for _ in range(3 if biased else 1):
        scratch += Rows.scratch(block, width)
    if biased:
        dma = pltpu.SemaphoreType.DMA
        scratch += [
            pltpu.VMEM((shards, group * block, full), BF16),
            pltpu.VMEM((block, full + block), F32),
            pltpu.VMEM((shards, 2, 2, 2, share, cols), BF16),
            pltpu.VMEM((diag_rows, 2 * block), F32),
            pltpu.VMEM((11, diag_rows + lines, 2 * block), F32),
            dma((5,)),
            dma((5,)),
        ]
    in_specs = [smem()] + [vmem()] * (len(args) - 1)
    in_specs[13] = pl.BlockSpec(memory_space=pl.ANY)
    return pl.pallas_call(
        functools.partial(linked_kernel, biased, group, size, order),
        out_shape=out_shape,
        in_specs=in_specs,
        out_specs=[vmem()] * len(out_shape),
        scratch_shapes=scratch,
        compiler_params=pltpu.CompilerParams(
            collective_id=2 if biased else 1, has_side_effects=True, vmem_limit_bytes=VMEM_LIMIT
        ),
        name="self_backward" if biased else "cross_backward",
    )(*args)


def per_device(
    layer_input,
    memory,
    dec_lengths,
    enc_lengths,
    self_gain,
    self_query,
    self_key_value,
    self_out,
    rel_bias,
    cross_gain,
    cross_query,
    cross_key_value,
    cross_out,
    feed_gain,
    feed_in,
    feed_out,
    out_cotangent,
):
    shards = lax.axis_size("head")
    me = lax.axis_index("head").astype(jnp.int32).reshape(1)
    batch_count = lax.axis_size("batch")
    seqs, block, width = layer_input.shape
    group = rel_bias.shape[1]
    size = self_query.shape[1] // group
    win = group * size
    full = block * shards
    enc_full = memory.shape[1] * shards
    rows = seqs * block
    part = feed_in.shape[2] // shards
    sg, cg, fg = (g.astype(F32).reshape(1, width) for g in (self_gain, cross_gain, feed_gain))

    x = layer_input.reshape(rows, width)
    x32 = x.astype(F32)
    n1 = (x32 * rms(x32) * sg).astype(BF16)
    n1_all = lax.all_gather(n1.reshape(seqs, block, width), "head", axis=1, tiled=True)
    n1_all = n1_all.reshape(seqs * full, width)

    tight = batch_count == 8 and shards == 4 and seqs == 2
    order = tuple((i % 2) * 4 + i // 2 for i in range(8)) if tight else (0,)
    table = jnp.pad(rel_bias, ((0, 0), (0, 128 - group)))
    flip = lambda w: jnp.swapaxes(w, -1, -2)
    weights = [flip(self_query)[None], flip(self_key_value), self_out[None]]
    weights += [flip(cross_query)[None], flip(cross_key_value), cross_out[None]]
    if tight:
        *weights, tables = gather_weights(weights, table, shards)
    else:
        weights = [lax.all_gather(w, "head", axis=0) for w in weights]
        tables = lax.all_gather(table, "head", axis=0)
    wq1, wkv1, wo1, wq2, wkv2, wo2 = weights
    wq1, wq2 = wq1[:, 0], wq2[:, 0]
    wo1, wo2 = wo1.reshape(width, width), wo2.reshape(width, width)
    onehot = near_onehot(block)
    bias = bias_tiles(me, tables, onehot.T.astype(BF16), group, block, full)
    memory_all = lax.all_gather(memory, "head", axis=1, tiled=True).reshape(seqs * enc_full, width)

    *saved1, y1, n2 = attend_forward(
        dec_lengths, n1, n1_all, x, wq1, wkv1, wo1, cg, bias, group, size
    )
    *saved2, y2, n3 = attend_forward(
        enc_lengths, n2, memory_all, y1, wq2, wkv2, wo2, fg, None, group, size
    )
    result, dy2, gain3, feed_w = feed(
        y2, n3, out_cotangent.reshape(rows, width), feed_in, feed_out, fg, shards, order
    )
    gain_rows = width // (2 * block)
    if tight:
        dy1, gain2, cross_w, memory_later, memory_first, feed_w = linked_backward(
            enc_lengths, n2, memory_all, saved2, wq2, wkv2, wo2, dy2, cg, feed_w, [y1],
            False, group, size, order,
        )
        lines = jnp.concatenate([jnp.zeros((1, width), F32), gain2, gain3], axis=0)
        lines = lines.reshape(-1, 2 * block)
        lines = jnp.pad(lines, ((0, -lines.shape[0] % 8), (0, 0)))
        input_grad, memory_last, cross_w, self_w, small = linked_backward(
            dec_lengths, n1, n1_all, saved1, wq1, wkv1, wo1, dy1, sg, cross_w,
            [bias, x, memory_later, lines], True, group, size, order,
        )
        memory_grad = jnp.stack([memory_first, memory_last])
        diag, lines = small[: -lines.shape[0]], small[-lines.shape[0] :]
    else:
        memory_part, gain2, cross_w, dy1 = attend_backward(
            enc_lengths, me, n2, memory_all, saved2, wq2, wkv2, wo2, dy2, cg, y1,
            False, group, size, order,
        )
        input_part, gain1, self_w, diag = attend_backward(
            dec_lengths, me, n1, n1_all, saved1, wq1, wkv1, wo1, dy1, sg, bias,
            True, group, size, order,
        )
        memory_grad = lax.psum_scatter(
            memory_part.reshape(seqs, enc_full, width), "head", scatter_dimension=1, tiled=True
        ).astype(F32)
        dn1 = lax.psum_scatter(
            input_part.reshape(seqs, full, width), "head", scatter_dimension=1, tiled=True
        ).astype(F32)
        feed_w, cross_w, self_w = (
            lax.psum_scatter(
                w.reshape(shards * width, w.shape[2]).astype(F32),
                ("head", "batch"),
                scatter_dimension=0,
                tiled=True,
            )
            for w in (feed_w, cross_w, self_w)
        )
        lines = jnp.concatenate([gain1, gain2, gain3], axis=0).reshape(-1, 2 * block)
        diag, lines = lax.psum((diag, lines), ("batch", "head"))
        dx, _ = norm_grads(x32, sg, dn1.reshape(rows, width))
        input_grad = dy1 + dx
    gains = lines[: 3 * gain_rows].reshape(3, width)
    diag = lax.dynamic_slice_in_dim(diag, me[0] * group, group, 0)
    table_grad = jnp.einsum("tb,ht->bh", onehot, diag, precision=highest)

    def split(w):
        kv = jnp.stack([w[:, :win], w[:, win : 2 * win]])
        return w[:, 2 * win : 3 * win], kv, w[:, 3 * win :].T

    self_q, self_kv, self_o = split(self_w)
    cross_q, cross_kv, cross_o = split(cross_w)
    return (
        result.reshape(seqs, block, width),
        input_grad.reshape(seqs, block, width),
        memory_grad,
        gains[0],
        self_q,
        self_kv,
        self_o,
        table_grad,
        gains[1],
        cross_q,
        cross_kv,
        cross_o,
        gains[2],
        jnp.stack([feed_w[:, :part], feed_w[:, part : 2 * part]]),
        feed_w[:, 2 * part :].T,
    )


def solution(mesh):
    return jax.shard_map(
        per_device,
        mesh=mesh,
        in_specs=(
            P("batch", "head", None),
            P("batch", "head", None),
            P("batch"),
            P("batch"),
            P(),
            P(None, "head"),
            P(None, None, "head"),
            P("head", None),
            P(None, "head"),
            P(),
            P(None, "head"),
            P(None, None, "head"),
            P("head", None),
            P(),
            P(),
            P(),
            P("batch", "head", None),
        ),
        out_specs=(
            P("batch", "head", None),
            P("batch", "head", None),
            P("batch", "head", None),
            P(),
            P("batch", "head"),
            P(None, "batch", "head"),
            P("head", "batch"),
            P(None, "head"),
            P(),
            P("batch", "head"),
            P(None, "batch", "head"),
            P("head", "batch"),
            P(),
            P(None, "batch", "head"),
            P("head", "batch"),
        ),
        check_vma=False,
    )
```

```python
import functools
import math

import jax
import jax.numpy as jnp
from jax import lax
from jax.experimental import pallas as pl
from jax.experimental.pallas import tpu as pltpu
from jax.sharding import PartitionSpec as P

NB = 32
MAX_DIST = 128
NEG = -1e30
VMEM_LIMIT = 60 * 1024 * 1024
F32 = jnp.float32
BF16 = jnp.bfloat16

highest = lax.Precision.HIGHEST


def bucket_edges(num_buckets, max_distance):
    exact_part = num_buckets // 2
    edge_list = []
    for target in range(1, num_buckets - exact_part):
        distance = exact_part
        while (
            math.floor(
                math.log(distance / exact_part)
                / math.log(max_distance / exact_part)
                * (num_buckets - exact_part)
            )
            < target
        ):
            distance += 1
        edge_list.append(distance)
    return edge_list


def bucket_of(distance, num_buckets, max_distance):
    exact_part = num_buckets // 2
    counted = jnp.zeros(distance.shape, jnp.int32)
    for edge_value in bucket_edges(num_buckets, max_distance):
        counted = counted + (distance >= edge_value).astype(jnp.int32)
    return jnp.where(distance < exact_part, distance, exact_part + counted).astype(jnp.int32)


def near_onehot(block):
    distance = block - jnp.arange(2 * block)
    distance = jnp.where(distance < 0, 2 * MAX_DIST, distance)
    return (
        bucket_of(distance, NB, MAX_DIST)[:, None] == jnp.arange(NB)[None, :]
    ).astype(F32)


def nn(a, b):
    return lax.dot_general(a, b, (((1,), (0,)), ((), ())), preferred_element_type=F32)


def nt(a, b):
    return lax.dot_general(a, b, (((1,), (1,)), ((), ())), preferred_element_type=F32)


def tn(a, b):
    return lax.dot_general(a, b, (((0,), (0,)), ((), ())), preferred_element_type=F32)


def rms(v):
    mean = jnp.mean(v * v, axis=-1, keepdims=True) + 1e-06
    r = lax.rsqrt(mean)
    return r * (1.5 - 0.5 * mean * r * r)


def norm_grads(y, gain, e):
    r = rms(y)
    xhat = y * r
    eg = e * gain
    dy = r * (eg - xhat * jnp.mean(eg * xhat, axis=-1, keepdims=True))
    return dy, jnp.sum(e * xhat, axis=0, keepdims=True)


def padded(v, width):
    extra = width - v.shape[1]
    if extra == 0:
        return v
    return jnp.concatenate([v, jnp.zeros((v.shape[0], extra), v.dtype)], axis=1)


def put_rows(ref, value, order):
    step = value.shape[0] // len(order)
    for source, slot in enumerate(order):
        ref[slot * step : (slot + 1) * step, :] = value[source * step : (source + 1) * step, :]


def vmem():
    return pl.BlockSpec(memory_space=pltpu.VMEM)


def smem():
    return pl.BlockSpec(memory_space=pltpu.SMEM)


def params():
    return pltpu.CompilerParams(vmem_limit_bytes=VMEM_LIMIT)


def sds(shape, dtype):
    return jax.ShapeDtypeStruct(shape, dtype)


def build_bias(me, table_ref, onehot_ref, b_ref, ext_ref, line_ref):
    heads, block, full = b_ref.shape
    shards = table_ref.shape[0]
    group = heads // shards
    start = pl.multiple_of(me * block, block)
    width = 2 * block
    row_i = lax.broadcasted_iota(jnp.int32, (block, width), 0)
    col_i = lax.broadcasted_iota(jnp.int32, (block, width), 1)
    masked = (col_i - row_i) > block
    far = lax.broadcasted_iota(jnp.int32, ext_ref.shape, 1) < start

    def body(h, carry):
        line_ref[...] = tn(table_ref[h], onehot_ref[...])
        for a in range(group):
            row = line_ref[a : a + 1, :]
            tile = pltpu.roll(
                jnp.broadcast_to(row, (block, width)), 0, 1, stride=1, stride_axis=0
            )
            ext_ref[...] = jnp.where(far, row[:, width - 1 : width], NEG)
            ext_ref[:, pl.ds(start, width)] = jnp.where(masked, NEG, tile)
            b_ref[h * group + a] = ext_ref[:, block:].astype(BF16)
        return carry

    lax.fori_loop(0, shards, body, 0)


def bias_kernel(me_ref, *refs):
    build_bias(me_ref[0], *refs)


def bias_tiles(me, tables, onehot, group, block, full):
    shards, buckets, lanes = tables.shape
    return pl.pallas_call(
        bias_kernel,
        out_shape=sds((shards * group, block, full), BF16),
        in_specs=[smem(), vmem(), vmem()],
        out_specs=vmem(),
        scratch_shapes=[
            pltpu.VMEM((block, full + block), F32),
            pltpu.VMEM((lanes, 2 * block), F32),
        ],
        compiler_params=params(),
        name="bias_tiles",
    )(me, tables, onehot)


def lane_groups(width, group, size):
    lane = lax.broadcasted_iota(jnp.int32, (1, width), 1)
    return [(lane // size) == a for a in range(group)]


def stack_heads(win, lanes):
    return jnp.concatenate([jnp.where(m, win, jnp.zeros_like(win)) for m in lanes], axis=0)


def join_heads(tall, lanes, rows):
    total = jnp.where(lanes[0], tall[:rows], 0.0)
    for a in range(1, len(lanes)):
        total = total + jnp.where(lanes[a], tall[a * rows : (a + 1) * rows], 0.0)
    return total


def head_context(qw, kw, vw, bias, keep, lanes):
    block, group = qw.shape[0], len(lanes)
    sc = nt(stack_heads(qw, lanes), kw)
    if bias is not None:
        sc = sc + bias
    sc = jnp.where(keep, sc, NEG)
    top = jnp.max(sc, axis=-1, keepdims=True)
    e = jnp.exp(sc - top)
    total = jnp.sum(e, axis=-1, keepdims=True)
    p = (e * (1.0 / total)).astype(BF16)
    c = join_heads(nn(p, vw), lanes, block).astype(BF16)
    lse = top + jnp.log(total)
    lane = lax.broadcasted_iota(jnp.int32, (block, 128), 1)
    tile = jnp.zeros((block, 128), F32)
    for a in range(group):
        tile = jnp.where(lane == a, lse[a * block : (a + 1) * block], tile)
    return c, tile


def forward_kernel(
    biased, group, size, len_ref, nq_ref, nk_ref, res_ref, wq_ref, wkv_ref, wo_ref, gain_ref, *rest
):
    if biased:
        b_ref, *rest = rest
    q_ref, k_ref, v_ref, c_ref, lse_ref, y_ref, n_ref = rest
    shards, rows, pw = q_ref.shape
    seqs = len_ref.shape[0]
    block = rows // seqs
    full = k_ref.shape[1] // seqs
    win = group * size
    lanes = lane_groups(pw, group, size)
    key = lax.broadcasted_iota(jnp.int32, (1, full), 1)

    def body(h, carry):
        q_ref[h] = padded(nt(nq_ref[...], wq_ref[h]).astype(BF16), pw)
        k_ref[h] = padded(nt(nk_ref[...], wkv_ref[h, 0]).astype(BF16), pw)
        v_ref[h] = padded(nt(nk_ref[...], wkv_ref[h, 1]).astype(BF16), pw)
        for s in range(seqs):
            bias = None
            if biased:
                bias = b_ref[pl.ds(h * group, group)].reshape(group * block, full).astype(F32)
            c, lse_ref[h, s] = head_context(
                q_ref[h, s * block : (s + 1) * block, :],
                k_ref[h, s * full : (s + 1) * full, :],
                v_ref[h, s * full : (s + 1) * full, :],
                bias,
                key < len_ref[s],
                lanes,
            )
            c_ref[h, s * block : (s + 1) * block, :] = c
        return carry

    lax.fori_loop(0, shards, body, 0)
    joined = jnp.concatenate([c_ref[h][:, :win] for h in range(shards)], axis=1)
    y = res_ref[...].astype(F32) + nn(joined, wo_ref[...])
    y_ref[...] = y
    n_ref[...] = (y * rms(y) * gain_ref[...]).astype(BF16)


def attend_forward(lens, nq, nk, res, wq, wkv, wo, gain, bias, group, size):
    rows, width = nq.shape
    shards = wq.shape[0]
    pw = -(-group * size // 128) * 128
    seqs = lens.shape[0]
    args = [lens, nq, nk, res, wq, wkv, wo, gain] + ([bias] if bias is not None else [])
    keys = nk.shape[0]
    flops = 2 * (rows + 2 * keys + rows) * width * width + 4 * rows * keys * width
    return pl.pallas_call(
        functools.partial(forward_kernel, bias is not None, group, size),
        out_shape=[
            sds((shards, rows, pw), BF16),
            sds((shards, keys, pw), BF16),
            sds((shards, keys, pw), BF16),
            sds((shards, rows, pw), BF16),
            sds((shards, seqs, rows // seqs, 128), F32),
            sds((rows, width), F32),
            sds((rows, width), BF16),
        ],
        in_specs=[smem()] + [vmem()] * (len(args) - 1),
        out_specs=[vmem()] * 7,
        compiler_params=params(),
        cost_estimate=pl.CostEstimate(
            flops=flops, bytes_accessed=16 << 20, transcendentals=rows * keys * 6
        ),
        name="attend_forward",
    )(*args)


def backward_kernel(
    biased,
    group,
    size,
    order,
    len_ref,
    me_ref,
    nq_ref,
    nk_ref,
    q_ref,
    k_ref,
    v_ref,
    c_ref,
    lse_ref,
    wq_ref,
    wkv_ref,
    wo_ref,
    dy_ref,
    gain_ref,
    *rest,
):
    if biased:
        b_ref, part_ref, gg_ref, w_ref, diag_ref, dc_ref, dq_ref, dkv_ref, acc_ref, nqt_ref, nkt_ref, dat_ref, sum_ref, ext_ref = rest
    else:
        y_ref, part_ref, gg_ref, w_ref, dprev_ref, dc_ref, dq_ref, dkv_ref, acc_ref, nqt_ref, nkt_ref, dat_ref = rest
    shards, rows, pw = q_ref.shape
    seqs = len_ref.shape[0]
    block = rows // seqs
    full = k_ref.shape[1] // seqs
    win = group * size
    lanes = lane_groups(pw, group, size)
    key = lax.broadcasted_iota(jnp.int32, (1, full), 1)
    me = me_ref[0]

    da = dy_ref[...].astype(BF16)
    put_rows(nqt_ref, nq_ref[...].T, order)
    put_rows(nkt_ref, nk_ref[...].T, order)
    put_rows(dat_ref, da.T, order)
    if biased:
        ext_ref[:, :block] = jnp.zeros((block, block), F32)
        start = pl.multiple_of(me * block, block)
        far = lax.broadcasted_iota(jnp.int32, ext_ref.shape, 1) < start
        row8 = lax.broadcasted_iota(jnp.int32, (8, 2 * block), 0)
        lane_near = lax.broadcasted_iota(jnp.int32, (1, 2 * block), 1)

    def body(h, carry):
        wo_h = wo_ref[pl.ds(pl.multiple_of(h * win, size), win), :]
        dc_ref[...] = padded(nt(da, wo_h).astype(BF16), pw)
        for s in range(seqs):
            kw = k_ref[h, s * full : (s + 1) * full, :]
            vw = v_ref[h, s * full : (s + 1) * full, :]
            qcat = stack_heads(q_ref[h, s * block : (s + 1) * block, :], lanes)
            dcat = stack_heads(dc_ref[s * block : (s + 1) * block, :], lanes)
            sc = nt(qcat, kw)
            if biased:
                sc = sc + b_ref[pl.ds(h * group, group)].reshape(group * block, full).astype(F32)
            sc = jnp.where(key < len_ref[s], sc, NEG)
            lse_tile = lse_ref[h, s]
            lse = jnp.concatenate([lse_tile[:, a : a + 1] for a in range(group)], axis=0)
            p = jnp.exp(sc - lse)
            dp = nt(dcat, vw)
            ds = p * (dp - jnp.sum(p * dp, axis=-1, keepdims=True))
            ds = ds.astype(BF16)
            pb = p.astype(BF16)
            if biased:
                if s == 0:
                    sum_ref[...] = ds.astype(F32)
                else:
                    sum_ref[...] += ds.astype(F32)
            dq = join_heads(nn(ds, kw), lanes, block)
            dq_ref[s * block : (s + 1) * block, :] = dq.astype(BF16)
            dk = tn(ds, qcat).astype(BF16)
            dv = tn(pb, dcat).astype(BF16)
            dkv_ref[s * full : (s + 1) * full, :] = jnp.concatenate(
                [dk[:, :win], dv[:, :win]], axis=1
            )
        if biased:
            for a in range(group):
                ext_ref[:, block:] = sum_ref[a * block : (a + 1) * block, :]
                far_sum = jnp.sum(jnp.where(far, ext_ref[...], 0.0))
                fold = ext_ref[:, pl.ds(start, 2 * block)]
                half = block // 2
                while half >= 8:
                    fold = fold[:half] + pltpu.roll(fold[half:], 2 * block - half, 1)
                    half //= 2
                for bit in (4, 2, 1):
                    fold = jnp.where(
                        (row8 & bit) != 0, pltpu.roll(fold, 2 * block - bit, 1), fold
                    )
                line = jnp.sum(fold, axis=0, keepdims=True)
                line = line + jnp.where(lane_near == 2 * block - 1, far_sum, 0.0)
                diag_ref[pl.ds(h * group + a, 1), :] = line
        dkv = dkv_ref[...]
        dq_h = dq_ref[...][:, :win]
        kv_term = nn(dkv[:, :win], wkv_ref[h, 0]) + nn(dkv[:, win:], wkv_ref[h, 1])
        q_term = nn(dq_h, wq_ref[h])
        w_ref[h] = jnp.concatenate(
            [
                nn(nkt_ref[...], dkv).astype(BF16),
                nn(nqt_ref[...], dq_h).astype(BF16),
                nn(dat_ref[...], c_ref[h][:, :win]).astype(BF16),
            ],
            axis=1,
        )

        @pl.when(h == 0)
        def _():
            acc_ref[: seqs * full, :] = kv_term
            acc_ref[seqs * full :, :] = q_term

        @pl.when(h != 0)
        def _():
            acc_ref[: seqs * full, :] += kv_term
            acc_ref[seqs * full :, :] += q_term

        return carry

    lax.fori_loop(0, shards, body, 0)
    if biased:
        for s in range(seqs):
            own = pl.ds(pl.multiple_of(s * full + me * block, block), block)
            acc_ref[own, :] += acc_ref[seqs * full + s * block : seqs * full + (s + 1) * block, :]
        total = acc_ref[: seqs * full, :]
        part_ref[...] = total.astype(BF16)
        gg_ref[...] = (
            jnp.sum(total * nk_ref[...].astype(F32), axis=0, keepdims=True) / gain_ref[...]
        )
    else:
        part_ref[...] = acc_ref[: seqs * full, :].astype(BF16)
        dy, gg = norm_grads(y_ref[...], gain_ref[...], acc_ref[seqs * full :, :])
        dprev_ref[...] = dy_ref[...] + dy
        gg_ref[...] = gg


def attend_backward(
    lens, me, nq, nk, saved, wq, wkv, wo, dy, gain, extra, biased, group, size, order
):
    q, k, v, c, lse = saved
    rows, width = nq.shape
    shards, keys, pw = k.shape
    block = rows // lens.shape[0]
    full = keys // lens.shape[0]
    win = group * size
    args = [lens, me, nq, nk, q, k, v, c, lse, wq, wkv, wo, dy, gain, extra]
    out_shape = [
        sds((keys, width), BF16),
        sds((1, width), F32),
        sds((shards, width, 4 * win), BF16),
        sds((shards * group, 2 * block), F32) if biased else sds((rows, width), F32),
    ]
    scratch = [
        pltpu.VMEM((rows, pw), BF16),
        pltpu.VMEM((rows, pw), BF16),
        pltpu.VMEM((keys, 2 * win), BF16),
        pltpu.VMEM((keys + rows, width), F32),
        pltpu.VMEM((width, rows), BF16),
        pltpu.VMEM((width, keys), BF16),
        pltpu.VMEM((width, rows), BF16),
    ]
    if biased:
        scratch += [
            pltpu.VMEM((group * block, full), F32),
            pltpu.VMEM((block, full + block), F32),
        ]
    flops = 4 * (rows + 2 * keys + rows) * width * width + 10 * rows * full * width
    return pl.pallas_call(
        functools.partial(backward_kernel, biased, group, size, order),
        out_shape=out_shape,
        in_specs=[smem(), smem()] + [vmem()] * (len(args) - 2),
        out_specs=[vmem()] * 4,
        scratch_shapes=scratch,
        compiler_params=params(),
        cost_estimate=pl.CostEstimate(
            flops=flops, bytes_accessed=24 << 20, transcendentals=rows * full * 12
        ),
        name="attend_backward",
    )(*args)


def feed_kernel(
    order, y_ref, n_ref, cot_ref, win_ref, wout_ref, gain_ref, out_ref, dy_ref, gg_ref, w_ref,
    acc_ref, dn_ref, nt_ref, ct_ref,
):
    step = pl.program_id(0)
    part = wout_ref.shape[0]

    @pl.when(step == 0)
    def _():
        put_rows(nt_ref, n_ref[...].T, order)
        put_rows(ct_ref, cot_ref[...].T, order)
        acc_ref[...] = y_ref[...]
        dn_ref[...] = jnp.zeros_like(dn_ref)

    n = n_ref[...]
    cot = cot_ref[...]
    g = nn(n, win_ref[0])
    u = nn(n, win_ref[1])
    dh = nt(cot, wout_ref[...])
    scale = math.sqrt(2.0 / math.pi)
    square = g * g
    t = jnp.tanh(scale * (g + 0.044715 * square * g))
    half = 0.5 * (1.0 + t)
    gelu = g * half
    hid = (gelu * u).astype(BF16)
    slope = half + 0.5 * g * (1.0 - t * t) * (scale * (1.0 + 3 * 0.044715 * square))
    dg = (dh * u * slope).astype(BF16)
    du = (dh * gelu).astype(BF16)
    acc_ref[...] += nn(hid, wout_ref[...])
    dn_ref[...] += nt(dg, win_ref[0]) + nt(du, win_ref[1])
    w_ref[0, :, :part] = nn(nt_ref[...], dg).astype(BF16)
    w_ref[0, :, part : 2 * part] = nn(nt_ref[...], du).astype(BF16)
    w_ref[0, :, 2 * part :] = nn(ct_ref[...], hid).astype(BF16)

    @pl.when(step == pl.num_programs(0) - 1)
    def _():
        out_ref[...] = acc_ref[...].astype(BF16)
        dy, gg = norm_grads(y_ref[...], gain_ref[...], dn_ref[...])
        dy_ref[...] = cot_ref[...].astype(F32) + dy
        gg_ref[...] = gg


def feed(y, n, cot, w_in, w_out, gain, shards, order):
    rows, width = y.shape
    hidden = w_out.shape[0]
    part = hidden // shards
    fixed = lambda shape: pl.BlockSpec(shape, lambda j: (0,) * len(shape))
    return pl.pallas_call(
        functools.partial(feed_kernel, order),
        grid=(shards,),
        out_shape=[
            sds((rows, width), BF16),
            sds((rows, width), F32),
            sds((1, width), F32),
            sds((shards, width, 3 * part), BF16),
        ],
        in_specs=[
            fixed((rows, width)),
            fixed((rows, width)),
            fixed((rows, width)),
            pl.BlockSpec((2, width, part), lambda j: (0, 0, j)),
            pl.BlockSpec((part, width), lambda j: (j, 0)),
            fixed((1, width)),
        ],
        out_specs=[
            fixed((rows, width)),
            fixed((rows, width)),
            fixed((1, width)),
            pl.BlockSpec((1, width, 3 * part), lambda j: (j, 0, 0)),
        ],
        scratch_shapes=[
            pltpu.VMEM((rows, width), F32),
            pltpu.VMEM((rows, width), F32),
            pltpu.VMEM((width, rows), BF16),
            pltpu.VMEM((width, rows), BF16),
        ],
        compiler_params=params(),
        cost_estimate=pl.CostEstimate(
            flops=18 * rows * width * hidden, bytes_accessed=24 << 20, transcendentals=rows * hidden
        ),
        name="feed",
    )(y, n, cot, w_in, w_out, gain)


MESH = pl.DeviceIdType.MESH


def place():
    b = lax.axis_index("batch")
    me = lax.axis_index("head")
    core = lax.rem(b, 2)
    x = lax.rem(lax.div(b, 2), 2)
    y = lax.div(b, 4)
    return b, me, core, x, y


def greet(devices):
    barrier = pltpu.get_barrier_semaphore()
    for device in devices:
        pl.semaphore_signal(barrier, inc=1, device_id=device, device_id_type=MESH)
    pl.semaphore_wait(barrier, len(devices))


def remote(src, dst, send, recv, device):
    return pltpu.make_async_remote_copy(
        src_ref=src,
        dst_ref=dst,
        send_sem=send,
        recv_sem=recv,
        device_id=device,
        device_id_type=MESH,
    )


def flipped(bit, by):
    return bit + by - 2 * bit * by


AHEAD = 2


class Links:
    def __init__(self):
        b, me, core, x, y = place()
        self.me, self.core, self.x, self.y = me, core, x, y
        self.high, self.low = lax.div(me, 2), lax.rem(me, 2)
        self.pair, self.far, self.cross = self.owner(1), self.owner(2), self.owner(0)
        self.over_core = (b + 1 - 2 * core, me)
        self.over_x = (b + 2 - 4 * x, me)
        self.over_y = (b + 4 - 8 * y, me)
        self.over_plane = (b + 2 - 4 * x + 4 - 8 * y, me)
        self.to_pair, self.to_far, self.to_cross = (b, self.pair), (b, self.far), (b, self.cross)

    def owner(self, k):
        by_low, by_high = 1 - k // 2, 1 - k % 2
        return 2 * flipped(self.high, by_high) + flipped(self.low, by_low)

    def greet(self):
        greet(
            [self.over_core, self.over_x, self.over_y, self.over_plane]
            + [self.to_pair, self.to_far, self.to_cross]
        )


class Sums:
    @staticmethod
    def scratch(chunks, rows, cols):
        items, half = chunks // 4, cols // 2
        dma = pltpu.SemaphoreType.DMA
        return [
            pltpu.VMEM((chunks, 2, 2, rows, cols), BF16),
            pltpu.VMEM((chunks, 2, 2, rows, cols), BF16),
            pltpu.VMEM((chunks, 2, rows, half), BF16),
            pltpu.VMEM((chunks, 2, rows, half), BF16),
            pltpu.VMEM((chunks, rows, half), BF16),
            pltpu.VMEM((chunks, rows, half), BF16),
            pltpu.VMEM((chunks, rows, cols), BF16),
            pltpu.VMEM((items, 3, rows, cols), BF16),
            dma((chunks,)),
            dma((chunks,)),
            dma((chunks,)),
            dma((chunks, 2)),
            dma((chunks, 2)),
            dma((chunks, 2)),
            dma((chunks, 2)),
            dma((items, 3)),
            dma((items, 3)),
        ]

    count = 17

    def __init__(self, links, refs):
        (self.own, self.rc, self.r1a, self.r1b, self.r2a, self.r2b, self.tot, self.rz) = refs[:8]
        (self.ls, self.cs, self.cr, self.s1, self.q1, self.s2, self.q2, self.zs, self.zr) = refs[8:]
        self.links = links
        self.chunks, self.cols = self.own.shape[0], self.own.shape[-1]
        self.half = self.cols // 2

    def piece(self, w_ref, c, side, left):
        start = pl.multiple_of((c // 4) * self.cols + left, 128)
        return w_ref.at[self.links.owner(c % 4), side, :, :, :, pl.ds(start, self.cols)]

    def local(self, w_ref, c, left):
        return pltpu.make_async_copy(
            self.piece(w_ref, c, self.links.core, left), self.own.at[c], self.ls.at[c]
        )

    def over_core(self, c, source):
        return remote(
            source, self.rc.at[c], self.cs.at[c], self.cr.at[c], self.links.over_core
        )

    def load(self, w_ref, c, left=0):
        self.local(w_ref, c, left).start()
        self.over_core(c, self.piece(w_ref, c, 1 - self.links.core, left)).start()

    def firsts(self, c):
        links, half = self.links, self.half
        return (
            remote(
                self.own.at[c, :, 1 - links.x, :, pl.ds(0, half)],
                self.r1a.at[c],
                self.s1.at[c, 0],
                self.q1.at[c, 0],
                links.over_x,
            ),
            remote(
                self.own.at[c, 1 - links.y, :, :, pl.ds(half, half)],
                self.r1b.at[c],
                self.s1.at[c, 1],
                self.q1.at[c, 1],
                links.over_y,
            ),
        )

    def seconds(self, c):
        links = self.links
        return (
            remote(
                self.r1a.at[c, 1 - links.y],
                self.r2a.at[c],
                self.s2.at[c, 0],
                self.q2.at[c, 0],
                links.over_y,
            ),
            remote(
                self.r1b.at[c, 1 - links.x],
                self.r2b.at[c],
                self.s2.at[c, 1],
                self.q2.at[c, 1],
                links.over_x,
            ),
        )

    def along(self, item, slot, c):
        device = self.links.to_far if slot == 2 else self.links.to_pair
        return remote(
            self.tot.at[c],
            self.rz.at[item, slot],
            self.zs.at[item, slot],
            self.zr.at[item, slot],
            device,
        )

    def core(self, c, w_ref=None, left=0):
        if w_ref is not None:
            self.local(w_ref, c, left).wait()
        self.over_core(c, self.rc.at[c]).wait_recv()
        x, y, half = 1 - self.links.x, 1 - self.links.y, self.half
        self.own[c, :, x, :, :half] = self.own[c, :, x, :, :half] + self.rc[c, :, x, :, :half]
        self.own[c, y, :, :, half:] = self.own[c, y, :, :, half:] + self.rc[c, y, :, :, half:]
        for copy in self.firsts(c):
            copy.start()

    def left(self, c, y):
        x, half = self.links.x, self.half
        total = self.own[c, y, x, :, :half].astype(F32) + self.rc[c, y, x, :, :half].astype(F32)
        return total + self.r1a[c, y].astype(F32)

    def right(self, c, x):
        y, half = self.links.y, self.half
        total = self.own[c, y, x, :, half:].astype(F32) + self.rc[c, y, x, :, half:].astype(F32)
        return total + self.r1b[c, x].astype(F32)

    def first(self, c):
        for copy in self.firsts(c):
            copy.wait_recv()
        x, y = 1 - self.links.x, 1 - self.links.y
        self.r1a[c, y] = self.left(c, y).astype(BF16)
        self.r1b[c, x] = self.right(c, x).astype(BF16)
        for copy in self.seconds(c):
            copy.start()

    def whole(self, c):
        left = self.left(c, self.links.y) + self.r2a[c].astype(F32)
        right = self.right(c, self.links.x) + self.r2b[c].astype(F32)
        return jnp.concatenate([left, right], axis=1)

    def second(self, c):
        for copy in self.seconds(c):
            copy.wait_recv()
        item, k = c // 4, c % 4
        for slot in range(2):

            @pl.when(k == slot)
            def _(slot=slot):
                self.tot[c] = self.whole(c).astype(BF16)
                self.along(item, slot, c).start()

        @pl.when(k == 2)
        def _():
            self.along(item, 0, c).wait_recv()
            self.tot[c] = (self.whole(c) + self.rz[item, 0].astype(F32)).astype(BF16)
            self.along(item, 2, c).start()

    def finish(self, item):
        c = 4 * item
        for slot in (1, 2):
            self.along(item, slot, c).wait_recv()
        return self.whole(c + 3) + self.rz[item, 1].astype(F32) + self.rz[item, 2].astype(F32)

    def drain(self):
        def body(c, carry):
            self.over_core(c, self.rc.at[c]).wait_send()
            for copy in self.firsts(c) + self.seconds(c):
                copy.wait_send()
            return carry

        lax.fori_loop(0, self.chunks, body, 0)
        for item in range(self.chunks // 4):
            for slot in range(3):
                self.along(item, slot, 4 * item).wait_send()


class Weights:
    @staticmethod
    def scratch(n):
        dma = pltpu.SemaphoreType.DMA
        return [dma((n, 3)), dma((n, 3)), dma((n, 3, 3)), dma((n, 3, 3)), dma((n, 3)), dma((n, 3))]

    def __init__(self, links, shards, fulls, sems):
        self.links, self.shards, self.fulls = links, shards, fulls
        self.zs, self.zr, self.ps, self.pr, self.cs, self.cr = sems
        self.n = len(shards)
        self.planes = (links.pair, links.far, links.cross)
        self.slot = links.core * 4 + links.y * 2 + links.x

    def window(self, ref, first, count):
        step = ref.shape[-2] // 8
        return ref.at[:, pl.ds(pl.multiple_of(first * step, step), count * step), :]

    def along(self, i, slot):
        links = self.links
        source = self.planes[1] if slot == 2 else links.me
        into = self.window(self.fulls[i].at[source], self.slot, 1)
        mine = into if slot == 2 else self.window(self.shards[i], self.slot, 1)
        device = links.to_far if slot == 1 else links.to_pair
        return remote(mine, into, self.zs.at[i, slot], self.zr.at[i, slot], device)

    def across(self, i, j, d):
        links = self.links
        piece = self.window(self.fulls[i].at[self.planes[j]], self.slot, 1)
        device = (links.over_x, links.over_y, links.over_plane)[d]
        return remote(piece, piece, self.ps.at[i, j, d], self.pr.at[i, j, d], device)

    def core(self, i, j):
        half = self.window(self.fulls[i].at[self.planes[j]], self.links.core * 4, 4)
        return remote(half, half, self.cs.at[i, j], self.cr.at[i, j], self.links.over_core)

    def start(self):
        for i in range(self.n):
            for slot in (0, 1):
                self.along(i, slot).start()

    def arrive(self, j):
        for i in range(self.n):
            self.along(i, j).wait_recv()
            if j == 1:
                self.along(i, 2).start()
            for d in range(3):
                self.across(i, j, d).start()

    def share(self, j):
        for i in range(self.n):
            for d in range(3):
                self.across(i, j, d).wait_recv()
            self.core(i, j).start()

    def finish(self, j):
        for i in range(self.n):
            self.core(i, j).wait_recv()

    def drain(self):
        for i in range(self.n):
            for j in range(3):
                self.along(i, j).wait_send()
                self.core(i, j).wait_send()
                for d in range(3):
                    self.across(i, j, d).wait_send()


class Gathered:
    def __init__(self, links, source, into, sems):
        self.links, self.source, self.into = links, source, into
        self.ss, self.rs = sems
        self.seqs, self.block = into.shape[0], into.shape[1] // 4

    def window(self, s, plane):
        rows = pl.ds(pl.multiple_of(plane * self.block, self.block), self.block)
        return self.into.at[s, rows, :]

    def copy(self, s, slot):
        links = self.links
        into = self.window(s, links.far if slot == 2 else links.me)
        mine = into if slot == 2 else self.source(s)
        device = links.to_far if slot == 1 else links.to_pair
        return remote(mine, into, self.ss.at[s, slot], self.rs.at[s, slot], device)

    def start(self):
        for s in range(self.seqs):
            for slot in (1, 0):
                self.copy(s, slot).start()

    def forward(self):
        for s in range(self.seqs):
            self.copy(s, 1).wait_recv()
            self.copy(s, 2).start()

    def finish(self):
        for s in range(self.seqs):
            for slot in (0, 2):
                self.copy(s, slot).wait_recv()

    def drain(self):
        for s in range(self.seqs):
            for slot in range(3):
                self.copy(s, slot).wait_send()


def front_kernel(group, size, *refs):
    len_ref, x_ref, self_gain_ref, cross_gain_ref, table_ref, onehot_ref, *refs = refs
    memory_ref, own_weights, refs = refs[0], refs[1:7], refs[7:]
    n_ref, y_ref, n2_ref, memory_out, *refs = refs
    self_out, cross_out, refs = refs[:3], refs[3:6], refs[6:]
    outs, kept, refs = refs[:7], refs[7:14], refs[14:]
    nall_ref, bias_ref, q_ref, k_ref, v_ref, c_ref, lse_ref = kept
    self_full, refs = refs[:3], refs[3:]
    tables_ref, ext_ref, line_ref, held_memory, *refs = refs
    held_cross, refs = refs[:3], refs[3:]
    (table_s, table_r, rows_s, rows_r, memory_s, memory_r, local, placed, held, done, *refs) = refs
    links = Links()
    me = links.me
    w1 = Weights(links, own_weights[:3], self_out, refs[:6])
    w2 = Weights(links, own_weights[3:], cross_out, refs[6:])
    shards, rows, pw = q_ref.shape
    seqs = len_ref.shape[0]
    block = rows // seqs
    full = block * shards
    win = group * size
    lanes = lane_groups(pw, group, size)
    key = lax.broadcasted_iota(jnp.int32, (1, full), 1)
    start = pl.multiple_of(me * block, block)
    rows_one = Gathered(
        links, lambda s: nall_ref.at[s, pl.ds(start, block), :], nall_ref, (rows_s, rows_r)
    )
    rows_memory = Gathered(links, lambda s: held_memory.at[s], memory_out, (memory_s, memory_r))

    links.greet()
    w1.start()
    heard = [
        remote(table_ref, tables_ref.at[me], table_s.at[i], table_r.at[i], to)
        for i, to in enumerate((links.to_pair, links.to_far, links.to_cross))
    ]
    for copy in heard:
        copy.start()
    taken = [
        pltpu.make_async_copy(own_weights[i], self_full[i].at[me], local.at[i]) for i in range(3)
    ]
    taken += [
        pltpu.make_async_copy(own_weights[3 + i], held_cross[i], local.at[3 + i]) for i in range(3)
    ]
    taken.append(pltpu.make_async_copy(memory_ref, held_memory, local.at[6]))
    for copy in taken:
        copy.start()
    x = x_ref[...].astype(F32)
    n_ref[...] = (x * rms(x) * self_gain_ref[...]).astype(BF16)
    for s in range(seqs):
        nall_ref[s, pl.ds(start, block), :] = n_ref[s * block : (s + 1) * block, :]
    tables_ref[me] = table_ref[...]
    w1.arrive(0)
    w1.arrive(1)
    rows_one.start()
    w1.arrive(2)
    for copy in heard:
        copy.wait_recv()
    build_bias(me, tables_ref, onehot_ref, bias_ref, ext_ref, line_ref)
    for copy in taken:
        copy.wait()
    put = [pltpu.make_async_copy(held_cross[i], cross_out[i].at[me], placed.at[i]) for i in range(3)]
    put += [
        pltpu.make_async_copy(self_full[i].at[me], self_out[i].at[me], placed.at[3 + i])
        for i in range(3)
    ]
    put += [
        pltpu.make_async_copy(held_memory.at[s], rows_memory.window(s, me), placed.at[6 + s])
        for s in range(seqs)
    ]
    for copy in put:
        copy.start()
    rows_one.forward()
    for j in range(3):
        w1.share(j)
    def hold(i, j):
        plane = w1.planes[j]
        return pltpu.make_async_copy(self_out[i].at[plane], self_full[i].at[plane], held.at[i, j])

    for j in range(3):
        w1.finish(j)
        for i in range(3):
            hold(i, j).start()
    rows_one.finish()
    w2.start()

    def keep(i, h=None):
        if h is None:
            return pltpu.make_async_copy(kept[i], outs[i], done.at[i, 0])
        return pltpu.make_async_copy(kept[i].at[h], outs[i].at[h], done.at[i, h])

    for i in range(2):
        keep(i).start()
    for j in range(3):
        for i in range(3):
            hold(i, j).wait()

    def body(k, carry):
        h = links.owner(lax.rem(k + 3, shards))
        nk = nall_ref[...].reshape(seqs * full, -1)
        q_ref[h] = padded(nt(n_ref[...], self_full[0][h, 0]).astype(BF16), pw)
        k_ref[h] = padded(nt(nk, self_full[1][h, 0]).astype(BF16), pw)
        v_ref[h] = padded(nt(nk, self_full[1][h, 1]).astype(BF16), pw)
        for s in range(seqs):
            c, lse_ref[h, s] = head_context(
                q_ref[h, s * block : (s + 1) * block, :],
                k_ref[h, s * full : (s + 1) * full, :],
                v_ref[h, s * full : (s + 1) * full, :],
                bias_ref[pl.ds(h * group, group)].reshape(group * block, full).astype(F32),
                key < len_ref[s],
                lanes,
            )
            c_ref[h, s * block : (s + 1) * block, :] = c
        for i in range(2, 7):
            keep(i, h).start()

        @pl.when(k == 0)
        def _():
            w2.arrive(0)
            w2.arrive(1)
            rows_memory.start()

        @pl.when(k == 1)
        def _():
            w2.arrive(2)

        return carry

    lax.fori_loop(0, shards, body, 0)
    joined = jnp.concatenate([c_ref[h][:, :win] for h in range(shards)], axis=1)
    out_weight = self_full[2][...].reshape(shards * win, -1)
    y = x_ref[...].astype(F32) + nn(joined, out_weight)
    y_ref[...] = y
    n2_ref[...] = (y * rms(y) * cross_gain_ref[...]).astype(BF16)
    for j in range(3):
        w2.share(j)
    rows_memory.forward()
    for j in range(3):
        w2.finish(j)
    rows_memory.finish()
    w1.drain()
    w2.drain()
    rows_one.drain()
    rows_memory.drain()
    for copy in heard:
        copy.wait_send()
    for copy in put:
        copy.wait()
    for i in range(2):
        keep(i).wait()
    for h in range(shards):
        for i in range(2, 7):
            keep(i, h).wait()


def front(lens, x, self_gain, cross_gain, table, onehot, memory, weights, shards, group, size):
    rows, width = x.shape
    seqs = lens.shape[0]
    block = rows // seqs
    full, keys = block * shards, rows * shards
    win = group * size
    pw = -(-win // 128) * 128
    fulls = [((shards, *w.shape), BF16) for w in weights]
    kept = [((seqs, full, width), BF16), ((shards * group, block, full), BF16)]
    kept += [((shards, n, pw), BF16) for n in (rows, keys, keys, rows)]
    kept.append(((shards, seqs, block, 128), F32))
    dma = pltpu.SemaphoreType.DMA
    anywhere = pl.BlockSpec(memory_space=pl.ANY)
    return pl.pallas_call(
        functools.partial(front_kernel, group, size),
        out_shape=[
            sds((rows, width), BF16),
            sds((rows, width), F32),
            sds((rows, width), BF16),
            sds((seqs, full, width), BF16),
        ]
        + [sds(*a) for a in fulls + kept],
        in_specs=[smem()] + [vmem()] * 5 + [anywhere] * 7,
        out_specs=[vmem()] * 3 + [anywhere] * 14,
        scratch_shapes=[pltpu.VMEM(*a) for a in kept + fulls[:3]]
        + [
            pltpu.VMEM((shards, *table.shape), BF16),
            pltpu.VMEM((block, full + block), F32),
            pltpu.VMEM((table.shape[1], 2 * block), F32),
            pltpu.VMEM(memory.shape, BF16),
        ]
        + [pltpu.VMEM(w.shape, BF16) for w in weights[3:]]
        + [
            dma((3,)),
            dma((3,)),
            dma((seqs, 3)),
            dma((seqs, 3)),
            dma((seqs, 3)),
            dma((seqs, 3)),
            dma((7,)),
            dma((6 + seqs,)),
            dma((3, 3)),
            dma((len(kept), shards)),
        ]
        + Weights.scratch(3)
        + Weights.scratch(3),
        compiler_params=pltpu.CompilerParams(
            collective_id=0, has_side_effects=True, vmem_limit_bytes=VMEM_LIMIT
        ),
        name="front",
    )(lens, x, self_gain, cross_gain, table, onehot, memory, *weights)


class Rows:
    @staticmethod
    def scratch(rows, width):
        dma = pltpu.SemaphoreType.DMA
        return [
            pltpu.VMEM((4, rows, width), BF16),
            pltpu.VMEM((3, rows, width), BF16),
            dma((3,)),
            dma((3,)),
        ]

    count = 4

    def __init__(self, links, refs):
        self.links = links
        self.buf, self.rx, self.ss, self.rs = refs

    def copy(self, slot):
        links = self.links
        block = (links.cross, links.far, links.pair)[slot]
        device = (links.to_cross, links.to_far, links.to_pair)[slot]
        return remote(
            self.buf.at[block], self.rx.at[slot], self.ss.at[slot], self.rs.at[slot], device
        )

    def start(self):
        for slot in range(3):
            self.copy(slot).start()

    def finish(self):
        for slot in range(3):
            self.copy(slot).wait_recv()
        return sum(self.rx[slot].astype(F32) for slot in range(3))

    def drain(self):
        for slot in range(3):
            self.copy(slot).wait_send()


def head_grads(qw, kw, vw, dcw, lse_tile, bias, keep, lanes):
    block, group = qw.shape[0], len(lanes)
    qcat, dcat = stack_heads(qw, lanes), stack_heads(dcw, lanes)
    sc = nt(qcat, kw)
    if bias is not None:
        sc = sc + bias
    sc = jnp.where(keep, sc, NEG)
    lse = jnp.concatenate([lse_tile[:, a : a + 1] for a in range(group)], axis=0)
    p = jnp.exp(sc - lse)
    dp = nt(dcat, vw)
    ds = (p * (dp - jnp.sum(p * dp, axis=-1, keepdims=True))).astype(BF16)
    dq = join_heads(nn(ds, kw), lanes, block).astype(BF16)
    dk = tn(ds, qcat).astype(BF16)
    dv = tn(p.astype(BF16), dcat).astype(BF16)
    return ds, dq, dk, dv


def diagonal_line(near, far_sum):
    block, width = near.shape
    half = block // 2
    while half >= 8:
        near = near[:half] + pltpu.roll(near[half:], width - half, 1)
        half //= 2
    row8 = lax.broadcasted_iota(jnp.int32, (8, width), 0)
    for bit in (4, 2, 1):
        near = jnp.where((row8 & bit) != 0, pltpu.roll(near, width - bit, 1), near)
    line = jnp.sum(near, axis=0, keepdims=True)
    lane = lax.broadcasted_iota(jnp.int32, (1, width), 1)
    return line + jnp.where(lane == width - 1, far_sum, 0.0)


def linked_kernel(biased, group, size, order, *refs):
    len_ref, dy_ref, gain_ref, given_ref, *refs = refs
    held_count = 11 if biased else 10
    held, refs = refs[:held_count], refs[held_count:]
    if biased:
        feed_ref, x_ref, rows_ref, lines_ref, *refs = refs
        grad_ref, mem_ref, feed_out, given_out, own_out, small_out, *refs = refs
    else:
        y_ref, dprev_ref, gg_ref, w_ref, later_ref, mem_ref, given_out, *refs = refs
    buffers, held_sem, refs = refs[:held_count], refs[held_count], refs[held_count + 1 :]
    nq_ref, nk_ref, c_ref, wo_ref, q_ref, k_ref, v_ref, lse_ref, wq_ref, wkv_ref = buffers[:10]
    bias_ref = buffers[-1]
    dq_ref, dkv_ref, acck_ref, accq_ref, nqt_ref, nkt_ref, dat_ref, wtmp_ref, *refs = refs
    links = Links()
    sums = Sums(links, refs[: Sums.count])
    refs = refs[Sums.count :]
    if biased:
        feed_sums = Sums(links, refs[: Sums.count])
        refs = refs[Sums.count :]
    exchanges = []
    for _ in range(3 if biased else 1):
        exchanges.append(Rows(links, refs[: Rows.count]))
        refs = refs[Rows.count :]
    if biased:
        ds_ref, ext_ref, diag_ref, sr, ms, mr = refs
    else:
        (w_sem,) = refs
    shards, rows, pw = q_ref.shape
    seqs = len_ref.shape[0]
    block = rows // seqs
    full = k_ref.shape[1] // seqs
    win = group * size
    lanes = lane_groups(pw, group, size)
    key = lax.broadcasted_iota(jnp.int32, (1, full), 1)
    me = links.me
    start = pl.multiple_of(me * block, block)
    def fetch(j, h=None):
        if h is None:
            return pltpu.make_async_copy(held[j], buffers[j], held_sem.at[j, 0])
        part = pl.ds(h * group, group) if j == 10 else h
        return pltpu.make_async_copy(held[j].at[part], buffers[j].at[part], held_sem.at[j, h])

    links.greet()
    if biased:
        exchanges[0].buf[...] = rows_ref[...]
        exchanges[0].start()
    for place in range(AHEAD):
        sums.load(given_ref, place)
    fetch(3).start()
    for k in range(shards):
        for j in range(4, held_count):
            fetch(j, links.owner(k)).start()
    for j in range(3):
        fetch(j).start()

    def stage(name, place):
        if name == "load":
            if not biased:
                sums.load(given_ref, place)
                return

            @pl.when(place < 4)
            def _():
                sums.load(given_ref, place)

            @pl.when(place >= 4)
            def _():
                feed_sums.load(feed_ref, place - 4, 2 * feed_sums.cols)

            return
        if not biased:
            run = getattr(sums, name)
            run(place, given_ref) if name == "core" else run(place)
            return

        @pl.when(place < 4)
        def _():
            sums.core(place, given_ref) if name == "core" else getattr(sums, name)(place)

        @pl.when((place >= 4) & (place < 8))
        def _():
            c = place - 4
            if name == "core":
                feed_sums.core(c, feed_ref, 2 * feed_sums.cols)
            else:
                getattr(feed_sums, name)(c)

        @pl.when(place >= 8)
        def _():
            getattr(sums, name)(place - 4)

    places = 12 if biased else sums.chunks
    late = (("load", -AHEAD), ("core", 0), ("first", 1), ("second", 3))

    def tick(t):
        for name, behind in late:
            place = t - behind

            @pl.when((place >= 0) & (place < (8 if name == "load" else places)))
            def _(name=name, place=place):
                stage(name, place)

    da = dy_ref[...].astype(BF16)
    if biased:
        ext_ref[:, :block] = jnp.zeros((block, block), F32)
        far = lax.broadcasted_iota(jnp.int32, ext_ref.shape, 1) < start
    fetch(3).wait()

    for s in range(seqs):
        mine = slice(s * block, (s + 1) * block)
        theirs = slice(s * full, (s + 1) * full)
        if s == seqs - 1:
            for j in (0, 2) if biased else range(3):
                fetch(j).wait()
            put_rows(nqt_ref, nq_ref[...].T, order)
            put_rows(nkt_ref, nk_ref[...].T, order)
            put_rows(dat_ref, da.T, order)

        def body(k, carry):
            h = links.owner(k)
            if s == 0:
                for j in range(4, held_count):
                    fetch(j, h).wait()
            wo_h = wo_ref[pl.ds(pl.multiple_of(h * win, size), win), :]
            dcw = padded(nt(da[mine], wo_h).astype(BF16), pw)
            bias = None
            if biased:
                bias = bias_ref[pl.ds(h * group, group)].reshape(group * block, full).astype(F32)
            ds, dq, dk, dv = head_grads(
                q_ref[h, mine, :],
                k_ref[h, theirs, :],
                v_ref[h, theirs, :],
                dcw,
                lse_ref[h, s],
                bias,
                key < len_ref[s],
                lanes,
            )
            dkv = jnp.concatenate([dk[:, :win], dv[:, :win]], axis=1)
            dkv_ref[h, theirs, :] = dkv
            dq_ref[h, mine, :] = dq
            kv_term = nn(dkv[:, :win], wkv_ref[h, 0]) + nn(dkv[:, win:], wkv_ref[h, 1])
            q_term = nn(dq[:, :win], wq_ref[h])

            @pl.when(k == 0)
            def _():
                acck_ref[...] = kv_term
                accq_ref[mine, :] = q_term

            @pl.when(k != 0)
            def _():
                acck_ref[...] += kv_term
                accq_ref[mine, :] += q_term

            if biased and s < seqs - 1:
                ds_ref[h] = ds if s == 0 else ds_ref[h] + ds
            if biased and s == seqs - 1:
                whole = ds_ref[h].astype(F32) + ds.astype(F32)
                for a in range(group):
                    ext_ref[:, block:] = whole[a * block : (a + 1) * block, :]
                    far_sum = jnp.sum(jnp.where(far, ext_ref[...], 0.0))
                    near = ext_ref[:, pl.ds(start, 2 * block)]
                    diag_ref[pl.ds(h * group + a, 1), :] = diagonal_line(near, far_sum)
            if s == seqs - 1:
                dkv = dkv_ref[h]

                def weight_rows(side):
                    rows = pl.ds(pl.multiple_of(side * 4 * w_rows, 4 * w_rows), 4 * w_rows)
                    return jnp.concatenate(
                        [
                            nn(nkt_ref[rows, :], dkv).astype(BF16),
                            nn(nqt_ref[rows, :], dq_ref[h][:, :win]).astype(BF16),
                            nn(dat_ref[rows, :], c_ref[h][:, :win]).astype(BF16),
                        ],
                        axis=1,
                    ).reshape(2, 2, w_rows, 4 * win)

                if biased:
                    wtmp_ref[k] = weight_rows(1 - links.core)
                    sums.over_core(4 + k, wtmp_ref.at[k]).start()
                    sums.own[4 + k] = weight_rows(links.core)
                else:
                    for side in range(2):
                        wtmp_ref[h, side] = weight_rows(side)
                    pltpu.make_async_copy(wtmp_ref.at[h], w_ref.at[h], w_sem.at[h]).start()
            tick(4 * s + k)
            return carry

        w_rows = nqt_ref.shape[0] // 8
        lax.fori_loop(0, shards, body, 0)
        if biased:
            acck_ref[pl.ds(start, block), :] += accq_ref[mine, :]
            total = acck_ref[...]
            if s == 0:
                fetch(1).wait()
            part = jnp.sum(total * nk_ref[theirs, :].astype(F32), axis=0, keepdims=True)
            gain1 = part if s == 0 else gain1 + part
            mover = exchanges[1 + s]
            mover.buf[...] = total.astype(BF16).reshape(shards, block, -1)
            mover.start()
            grad_ref[mine, :] = acck_ref[pl.ds(start, block), :]
        elif s == 0:
            exchanges[0].buf[...] = acck_ref[...].astype(BF16).reshape(shards, block, -1)
            exchanges[0].start()
            mem_ref[...] = acck_ref[pl.ds(start, block), :]
        else:
            later_ref[...] = acck_ref[...].astype(BF16).reshape(shards, block, -1)

    steps = range(4 * seqs, places + late[-1][1])
    if not biased:
        dy, gg = norm_grads(y_ref[...], gain_ref[...], accq_ref[...])
        dprev_ref[...] = dy_ref[...] + dy
        gg_ref[...] = gg
        for t in steps:
            tick(t)
        mem_ref[...] += exchanges[0].finish()
        for item in range(2):
            given_out[item] = sums.finish(item)
        for h in range(shards):
            pltpu.make_async_copy(wtmp_ref.at[h], w_ref.at[h], w_sem.at[h]).wait()
    else:
        gain1 = gain1 / gain_ref[...]
        width = gain1.shape[1]
        diag_ref[shards * group :, :] = jnp.zeros_like(diag_ref[shards * group :, :])
        lines = lines_ref.shape[0]
        sr[0, : diag_ref.shape[0], :] = diag_ref[...]
        sr[0, diag_ref.shape[0] :, :] = lines_ref[...]
        for j in range(width // (2 * block)):
            row = diag_ref.shape[0] + j
            sr[0, row : row + 1, :] = gain1[:, j * 2 * block : (j + 1) * 2 * block]
        plane = 2 + 2 * links.y + links.x
        hops = [(1, 0, links.over_core)]
        hops += [(plane, plane, to) for to in (links.over_x, links.over_y, links.over_plane)]
        hops += [(6 + me, 6 + me, to) for to in (links.to_pair, links.to_far, links.to_cross)]

        def hop(i):
            into, source, to = hops[i]
            return remote(sr.at[source], sr.at[into], ms.at[i], mr.at[i], to)

        hop(0).start()
        for i, t in enumerate(steps):
            tick(t)
            if i == 1:
                hop(0).wait_recv()
                sr[plane] = sr[0] + sr[1]
                for j in (1, 2, 3):
                    hop(j).start()
            if i == 3:
                for j in (1, 2, 3):
                    hop(j).wait_recv()
                sr[6 + me] = (sr[2] + sr[3]) + (sr[4] + sr[5])
                for j in (4, 5, 6):
                    hop(j).start()
        for j in (4, 5, 6):
            hop(j).wait_recv()
        small_out[...] = (sr[6] + sr[7]) + (sr[8] + sr[9])
        mem_ref[...] = exchanges[0].buf[me].astype(F32) + exchanges[0].finish()
        feed_out[...] = feed_sums.finish(0)
        given_out[...] = sums.finish(0)
        for s in range(seqs):
            mine = slice(s * block, (s + 1) * block)
            dn = grad_ref[mine, :] + exchanges[1 + s].finish()
            dx, _ = norm_grads(x_ref[mine, :].astype(F32), gain_ref[...], dn)
            grad_ref[mine, :] = dy_ref[mine, :] + dx
        own_out[...] = sums.finish(1)
        for i in range(len(hops)):
            hop(i).wait_send()
    for mover in exchanges:
        mover.drain()
    sums.drain()
    if biased:
        feed_sums.drain()


def linked_backward(lens, nq, nk, saved, wq, wkv, wo, dy, gain, given, extras, biased, group, size, order):
    q, k, v, c, lse = saved
    rows, width = nq.shape
    shards, keys, pw = k.shape
    seqs = lens.shape[0]
    block, full, win = rows // seqs, keys // seqs, group * size
    cols = 4 * win
    share = width // 8
    split = lambda w: w.reshape(shards, 2, 2, 2, share, -1)
    held = [nq, nk, c, wo, q, k, v, lse, wq, wkv]
    if biased:
        held.append(extras[1])
        extras = [split(extras[0]), *extras[2:]]
    args = [lens, dy, gain, split(given), *held, *extras]
    part = split(extras[0] if biased else given).shape[-1] // 3
    if biased:
        lines = extras[3].shape[0]
        diag_rows = -(-shards * group // 8) * 8
        out_shape = [
            sds((rows, width), F32),
            sds((block, width), F32),
            sds((share, part), F32),
            sds((share, cols), F32),
            sds((share, cols), F32),
            sds((diag_rows + lines, 2 * block), F32),
        ]
    else:
        out_shape = [
            sds((rows, width), F32),
            sds((1, width), F32),
            sds((shards, 2, 2, 2, share, cols), BF16),
            sds((shards, block, width), BF16),
            sds((block, width), F32),
            sds((2, share, part), F32),
        ]
    scratch = [pltpu.VMEM(a.shape, a.dtype) for a in held]
    scratch += [
        pltpu.SemaphoreType.DMA((len(held), shards)),
        pltpu.VMEM((shards, rows, pw), BF16),
        pltpu.VMEM((shards, keys, 2 * win), BF16),
        pltpu.VMEM((full, width), F32),
        pltpu.VMEM((rows, width), F32),
        pltpu.VMEM((width, rows), BF16),
        pltpu.VMEM((width, keys), BF16),
        pltpu.VMEM((width, rows), BF16),
    ]
    scratch.append(pltpu.VMEM((shards, *(() if biased else (2,)), 2, 2, share, cols), BF16))
    scratch += Sums.scratch(8, share, cols if biased else part)
    if biased:
        scratch += Sums.scratch(4, share, part)
    for _ in range(3 if biased else 1):
        scratch += Rows.scratch(block, width)
    if biased:
        dma = pltpu.SemaphoreType.DMA
        scratch += [
            pltpu.VMEM((shards, group * block, full), BF16),
            pltpu.VMEM((block, full + block), F32),
            pltpu.VMEM((diag_rows, 2 * block), F32),
            pltpu.VMEM((10, diag_rows + lines, 2 * block), F32),
            dma((7,)),
            dma((7,)),
        ]
    else:
        scratch.append(pltpu.SemaphoreType.DMA((shards,)))
    anywhere = pl.BlockSpec(memory_space=pl.ANY)
    in_specs = [smem(), vmem(), vmem(), anywhere] + [anywhere] * len(held)
    in_specs += [anywhere if biased else vmem()] + [vmem()] * (len(extras) - 1)
    out_specs = [vmem()] * len(out_shape)
    if not biased:
        out_specs[2] = anywhere
    return pl.pallas_call(
        functools.partial(linked_kernel, biased, group, size, order),
        out_shape=out_shape,
        in_specs=in_specs,
        out_specs=out_specs,
        scratch_shapes=scratch,
        compiler_params=pltpu.CompilerParams(
            collective_id=2 if biased else 1, has_side_effects=True, vmem_limit_bytes=VMEM_LIMIT
        ),
        name="self_backward" if biased else "cross_backward",
    )(*args)


def per_device(
    layer_input,
    memory,
    dec_lengths,
    enc_lengths,
    self_gain,
    self_query,
    self_key_value,
    self_out,
    rel_bias,
    cross_gain,
    cross_query,
    cross_key_value,
    cross_out,
    feed_gain,
    feed_in,
    feed_out,
    out_cotangent,
):
    shards = lax.axis_size("head")
    me = lax.axis_index("head").astype(jnp.int32).reshape(1)
    batch_count = lax.axis_size("batch")
    seqs, block, width = layer_input.shape
    group = rel_bias.shape[1]
    size = self_query.shape[1] // group
    win = group * size
    full = block * shards
    enc_full = memory.shape[1] * shards
    rows = seqs * block
    part = feed_in.shape[2] // shards
    sg, cg, fg = (g.astype(F32).reshape(1, width) for g in (self_gain, cross_gain, feed_gain))

    x = layer_input.reshape(rows, width)
    x32 = x.astype(F32)
    tight = batch_count == 8 and shards == 4 and seqs == 2
    order = tuple((i % 2) * 4 + i // 2 for i in range(8)) if tight else (0,)
    table = jnp.pad(rel_bias, ((0, 0), (0, 128 - group)))
    flip = lambda w: jnp.swapaxes(w, -1, -2)
    weights = [flip(self_query)[None], flip(self_key_value), self_out[None]]
    weights += [flip(cross_query)[None], flip(cross_key_value), cross_out[None]]
    onehot = near_onehot(block)
    lines_of = onehot.T.astype(BF16)
    if tight:
        n1, y1, n2, memory_all, wq1, wkv1, wo1, wq2, wkv2, wo2, n1_all, bias, *saved1 = front(
            dec_lengths, x, sg, cg, table, lines_of, memory, weights, shards, group, size
        )
        n1_all = n1_all.reshape(seqs * full, width)
    else:
        n1 = (x32 * rms(x32) * sg).astype(BF16)
        n1_all = lax.all_gather(n1.reshape(seqs, block, width), "head", axis=1, tiled=True)
        n1_all = n1_all.reshape(seqs * full, width)
        wq1, wkv1, wo1, wq2, wkv2, wo2 = [lax.all_gather(w, "head", axis=0) for w in weights]
        tables = lax.all_gather(table, "head", axis=0)
        bias = bias_tiles(me, tables, lines_of, group, block, full)
        memory_all = lax.all_gather(memory, "head", axis=1, tiled=True)
    memory_all = memory_all.reshape(seqs * enc_full, width)
    wq1, wq2 = wq1[:, 0], wq2[:, 0]
    wo1, wo2 = wo1.reshape(width, width), wo2.reshape(width, width)
    if not tight:
        *saved1, y1, n2 = attend_forward(
            dec_lengths, n1, n1_all, x, wq1, wkv1, wo1, cg, bias, group, size
        )
    *saved2, y2, n3 = attend_forward(
        enc_lengths, n2, memory_all, y1, wq2, wkv2, wo2, fg, None, group, size
    )
    result, dy2, gain3, feed_w = feed(
        y2, n3, out_cotangent.reshape(rows, width), feed_in, feed_out, fg, shards, order
    )
    gain_rows = width // (2 * block)
    if tight:
        dy1, gain2, cross_w, memory_later, memory_first, feed_in_grad = linked_backward(
            enc_lengths, n2, memory_all, saved2, wq2, wkv2, wo2, dy2, cg, feed_w, [y1],
            False, group, size, order,
        )
        lines = jnp.concatenate([jnp.zeros((1, width), F32), gain2, gain3], axis=0)
        lines = lines.reshape(-1, 2 * block)
        lines = jnp.pad(lines, ((0, -lines.shape[0] % 8), (0, 0)))
        input_grad, memory_last, feed_out_grad, cross_w, self_w, small = linked_backward(
            dec_lengths, n1, n1_all, saved1, wq1, wkv1, wo1, dy1, sg, cross_w,
            [feed_w, bias, x, memory_later, lines], True, group, size, order,
        )
        memory_grad = jnp.stack([memory_first, memory_last])
        diag, lines = small[: -lines.shape[0]], small[-lines.shape[0] :]
    else:
        memory_part, gain2, cross_w, dy1 = attend_backward(
            enc_lengths, me, n2, memory_all, saved2, wq2, wkv2, wo2, dy2, cg, y1,
            False, group, size, order,
        )
        input_part, gain1, self_w, diag = attend_backward(
            dec_lengths, me, n1, n1_all, saved1, wq1, wkv1, wo1, dy1, sg, bias,
            True, group, size, order,
        )
        memory_grad = lax.psum_scatter(
            memory_part.reshape(seqs, enc_full, width), "head", scatter_dimension=1, tiled=True
        ).astype(F32)
        dn1 = lax.psum_scatter(
            input_part.reshape(seqs, full, width), "head", scatter_dimension=1, tiled=True
        ).astype(F32)
        feed_w, cross_w, self_w = (
            lax.psum_scatter(
                w.reshape(shards * width, w.shape[2]).astype(F32),
                ("head", "batch"),
                scatter_dimension=0,
                tiled=True,
            )
            for w in (feed_w, cross_w, self_w)
        )
        lines = jnp.concatenate([gain1, gain2, gain3], axis=0).reshape(-1, 2 * block)
        diag, lines = lax.psum((diag, lines), ("batch", "head"))
        dx, _ = norm_grads(x32, sg, dn1.reshape(rows, width))
        input_grad = dy1 + dx
        feed_in_grad = jnp.stack([feed_w[:, :part], feed_w[:, part : 2 * part]])
        feed_out_grad = feed_w[:, 2 * part :]
    gains = lines[: 3 * gain_rows].reshape(3, width)
    diag = lax.dynamic_slice_in_dim(diag, me[0] * group, group, 0)
    table_grad = jnp.einsum("tb,ht->bh", onehot, diag, precision=highest)

    def split(w):
        kv = jnp.stack([w[:, :win], w[:, win : 2 * win]])
        return w[:, 2 * win : 3 * win], kv, w[:, 3 * win :].T

    self_q, self_kv, self_o = split(self_w)
    cross_q, cross_kv, cross_o = split(cross_w)
    return (
        result.reshape(seqs, block, width),
        input_grad.reshape(seqs, block, width),
        memory_grad,
        gains[0],
        self_q,
        self_kv,
        self_o,
        table_grad,
        gains[1],
        cross_q,
        cross_kv,
        cross_o,
        gains[2],
        feed_in_grad,
        feed_out_grad.T,
    )


def solution(mesh):
    return jax.shard_map(
        per_device,
        mesh=mesh,
        in_specs=(
            P("batch", "head", None),
            P("batch", "head", None),
            P("batch"),
            P("batch"),
            P(),
            P(None, "head"),
            P(None, None, "head"),
            P("head", None),
            P(None, "head"),
            P(),
            P(None, "head"),
            P(None, None, "head"),
            P("head", None),
            P(),
            P(),
            P(),
            P("batch", "head", None),
        ),
        out_specs=(
            P("batch", "head", None),
            P("batch", "head", None),
            P("batch", "head", None),
            P(),
            P("batch", "head"),
            P(None, "batch", "head"),
            P("head", "batch"),
            P(None, "head"),
            P(),
            P("batch", "head"),
            P(None, "batch", "head"),
            P("head", "batch"),
            P(),
            P(None, "batch", "head"),
            P("head", "batch"),
        ),
        check_vma=False,
    )
```

```python
import functools
import math

import jax
import jax.numpy as jnp
from jax import lax
from jax.experimental import pallas as pl
from jax.experimental.pallas import tpu as pltpu
from jax.sharding import PartitionSpec as P

NB = 32
MAX_DIST = 128
NEG = -1e30
VMEM_LIMIT = 60 * 1024 * 1024
F32 = jnp.float32
BF16 = jnp.bfloat16

highest = lax.Precision.HIGHEST


def bucket_edges(num_buckets, max_distance):
    exact_part = num_buckets // 2
    edge_list = []
    for target in range(1, num_buckets - exact_part):
        distance = exact_part
        while (
            math.floor(
                math.log(distance / exact_part)
                / math.log(max_distance / exact_part)
                * (num_buckets - exact_part)
            )
            < target
        ):
            distance += 1
        edge_list.append(distance)
    return edge_list


def bucket_of(distance, num_buckets, max_distance):
    exact_part = num_buckets // 2
    counted = jnp.zeros(distance.shape, jnp.int32)
    for edge_value in bucket_edges(num_buckets, max_distance):
        counted = counted + (distance >= edge_value).astype(jnp.int32)
    return jnp.where(distance < exact_part, distance, exact_part + counted).astype(jnp.int32)


def near_onehot(block):
    distance = block - jnp.arange(2 * block)
    distance = jnp.where(distance < 0, 2 * MAX_DIST, distance)
    return (
        bucket_of(distance, NB, MAX_DIST)[:, None] == jnp.arange(NB)[None, :]
    ).astype(F32)


def nn(a, b):
    return lax.dot_general(a, b, (((1,), (0,)), ((), ())), preferred_element_type=F32)


def nt(a, b):
    return lax.dot_general(a, b, (((1,), (1,)), ((), ())), preferred_element_type=F32)


def tn(a, b):
    return lax.dot_general(a, b, (((0,), (0,)), ((), ())), preferred_element_type=F32)


def rms(v):
    mean = jnp.mean(v * v, axis=-1, keepdims=True) + 1e-06
    r = lax.rsqrt(mean)
    return r * (1.5 - 0.5 * mean * r * r)


def norm_grads(y, gain, e):
    r = rms(y)
    xhat = y * r
    eg = e * gain
    dy = r * (eg - xhat * jnp.mean(eg * xhat, axis=-1, keepdims=True))
    return dy, jnp.sum(e * xhat, axis=0, keepdims=True)


def row(ref):
    return ref[...].astype(F32).reshape(1, -1)


def padded(v, width):
    extra = width - v.shape[1]
    if extra == 0:
        return v
    return jnp.concatenate([v, jnp.zeros((v.shape[0], extra), v.dtype)], axis=1)


def put_rows(ref, value, order):
    step = value.shape[0] // len(order)
    for source, slot in enumerate(order):
        ref[slot * step : (slot + 1) * step, :] = value[source * step : (source + 1) * step, :]


def vmem():
    return pl.BlockSpec(memory_space=pltpu.VMEM)


def smem():
    return pl.BlockSpec(memory_space=pltpu.SMEM)


def params():
    return pltpu.CompilerParams(vmem_limit_bytes=VMEM_LIMIT)


def sds(shape, dtype):
    return jax.ShapeDtypeStruct(shape, dtype)


def bucket_rows(block, count):
    distance = block - lax.broadcasted_iota(jnp.int32, (1, 2 * block), 1)
    distance = jnp.where(distance < 0, 2 * MAX_DIST, distance)
    bucket = bucket_of(distance, NB, MAX_DIST)
    return bucket == lax.broadcasted_iota(jnp.int32, (count, 2 * block), 0)


def build_bias(me, table_ref, b_ref, ext_ref, line_ref):
    heads, block, full = b_ref.shape
    shards = table_ref.shape[0]
    group = heads // shards
    start = pl.multiple_of(me * block, block)
    width = 2 * block
    row_i = lax.broadcasted_iota(jnp.int32, (block, width), 0)
    col_i = lax.broadcasted_iota(jnp.int32, (block, width), 1)
    masked = (col_i - row_i) > block
    far = lax.broadcasted_iota(jnp.int32, ext_ref.shape, 1) < start
    onehot = bucket_rows(block, table_ref.shape[2]).astype(BF16)

    def body(h, carry):
        line_ref[...] = nn(table_ref[h], onehot)
        for a in range(group):
            row = line_ref[a : a + 1, :]
            tile = pltpu.roll(
                jnp.broadcast_to(row, (block, width)), 0, 1, stride=1, stride_axis=0
            )
            ext_ref[...] = jnp.where(far, row[:, width - 1 : width], NEG)
            ext_ref[:, pl.ds(start, width)] = jnp.where(masked, NEG, tile)
            b_ref[h * group + a] = ext_ref[:, block:].astype(BF16)
        return carry

    lax.fori_loop(0, shards, body, 0)


def bias_kernel(me_ref, *refs):
    build_bias(me_ref[0], *refs)


def bias_tiles(me, tables, group, block, full):
    shards, lanes = tables.shape[:2]
    return pl.pallas_call(
        bias_kernel,
        out_shape=sds((shards * group, block, full), BF16),
        in_specs=[smem(), vmem()],
        out_specs=vmem(),
        scratch_shapes=[
            pltpu.VMEM((block, full + block), F32),
            pltpu.VMEM((lanes, 2 * block), F32),
        ],
        compiler_params=params(),
        name="bias_tiles",
    )(me, tables)


def lane_groups(width, group, size):
    lane = lax.broadcasted_iota(jnp.int32, (1, width), 1)
    return [(lane // size) == a for a in range(group)]


def stack_heads(win, lanes):
    return jnp.concatenate([jnp.where(m, win, jnp.zeros_like(win)) for m in lanes], axis=0)


def join_heads(tall, lanes, rows):
    total = jnp.where(lanes[0], tall[:rows], 0.0)
    for a in range(1, len(lanes)):
        total = total + jnp.where(lanes[a], tall[a * rows : (a + 1) * rows], 0.0)
    return total


def head_context(qw, kw, vw, bias, keep, lanes):
    block, group = qw.shape[0], len(lanes)
    sc = nt(stack_heads(qw, lanes), kw)
    if bias is not None:
        sc = sc + bias
    sc = jnp.where(keep, sc, NEG)
    top = jnp.max(sc, axis=-1, keepdims=True)
    e = jnp.exp(sc - top)
    total = jnp.sum(e, axis=-1, keepdims=True)
    p = (e * (1.0 / total)).astype(BF16)
    c = join_heads(nn(p, vw), lanes, block).astype(BF16)
    lse = top + jnp.log(total)
    lane = lax.broadcasted_iota(jnp.int32, (block, 128), 1)
    tile = jnp.zeros((block, 128), F32)
    for a in range(group):
        tile = jnp.where(lane == a, lse[a * block : (a + 1) * block], tile)
    return c, tile


def forward_kernel(
    biased, group, size, len_ref, nq_ref, nk_ref, res_ref, wq_ref, wkv_ref, wo_ref, gain_ref, *rest
):
    if biased:
        b_ref, *rest = rest
    q_ref, k_ref, v_ref, c_ref, lse_ref, y_ref, n_ref = rest
    shards, rows, pw = q_ref.shape
    seqs = len_ref.shape[0]
    block = rows // seqs
    full = k_ref.shape[1] // seqs
    win = group * size
    lanes = lane_groups(pw, group, size)
    key = lax.broadcasted_iota(jnp.int32, (1, full), 1)

    def body(h, carry):
        q_ref[h] = padded(nt(nq_ref[...], wq_ref[h]).astype(BF16), pw)
        k_ref[h] = padded(nt(nk_ref[...], wkv_ref[h, 0]).astype(BF16), pw)
        v_ref[h] = padded(nt(nk_ref[...], wkv_ref[h, 1]).astype(BF16), pw)
        for s in range(seqs):
            bias = None
            if biased:
                bias = b_ref[pl.ds(h * group, group)].reshape(group * block, full).astype(F32)
            c, lse_ref[h, s] = head_context(
                q_ref[h, s * block : (s + 1) * block, :],
                k_ref[h, s * full : (s + 1) * full, :],
                v_ref[h, s * full : (s + 1) * full, :],
                bias,
                key < len_ref[s],
                lanes,
            )
            c_ref[h, s * block : (s + 1) * block, :] = c
        return carry

    lax.fori_loop(0, shards, body, 0)
    joined = jnp.concatenate([c_ref[h][:, :win] for h in range(shards)], axis=1)
    y = res_ref[...].astype(F32) + nn(joined, wo_ref[...])
    y_ref[...] = y
    n_ref[...] = (y * rms(y) * row(gain_ref)).astype(BF16)


def attend_forward(lens, nq, nk, res, wq, wkv, wo, gain, bias, group, size):
    rows, width = nq.shape
    shards = wq.shape[0]
    pw = -(-group * size // 128) * 128
    seqs = lens.shape[0]
    args = [lens, nq, nk, res, wq, wkv, wo, gain] + ([bias] if bias is not None else [])
    keys = nk.shape[0]
    flops = 2 * (rows + 2 * keys + rows) * width * width + 4 * rows * keys * width
    return pl.pallas_call(
        functools.partial(forward_kernel, bias is not None, group, size),
        out_shape=[
            sds((shards, rows, pw), BF16),
            sds((shards, keys, pw), BF16),
            sds((shards, keys, pw), BF16),
            sds((shards, rows, pw), BF16),
            sds((shards, seqs, rows // seqs, 128), F32),
            sds((rows, width), F32),
            sds((rows, width), BF16),
        ],
        in_specs=[smem()] + [vmem()] * (len(args) - 1),
        out_specs=[vmem()] * 7,
        compiler_params=params(),
        cost_estimate=pl.CostEstimate(
            flops=flops, bytes_accessed=16 << 20, transcendentals=rows * keys * 6
        ),
        name="attend_forward",
    )(*args)


def backward_kernel(
    biased,
    group,
    size,
    order,
    len_ref,
    me_ref,
    nq_ref,
    nk_ref,
    q_ref,
    k_ref,
    v_ref,
    c_ref,
    lse_ref,
    wq_ref,
    wkv_ref,
    wo_ref,
    dy_ref,
    gain_ref,
    *rest,
):
    if biased:
        b_ref, part_ref, gg_ref, w_ref, diag_ref, dc_ref, dq_ref, dkv_ref, acc_ref, nqt_ref, nkt_ref, dat_ref, sum_ref, ext_ref = rest
    else:
        y_ref, part_ref, gg_ref, w_ref, dprev_ref, dc_ref, dq_ref, dkv_ref, acc_ref, nqt_ref, nkt_ref, dat_ref = rest
    shards, rows, pw = q_ref.shape
    seqs = len_ref.shape[0]
    block = rows // seqs
    full = k_ref.shape[1] // seqs
    win = group * size
    lanes = lane_groups(pw, group, size)
    key = lax.broadcasted_iota(jnp.int32, (1, full), 1)
    me = me_ref[0]

    da = dy_ref[...].astype(BF16)
    put_rows(nqt_ref, nq_ref[...].T, order)
    put_rows(nkt_ref, nk_ref[...].T, order)
    put_rows(dat_ref, da.T, order)
    if biased:
        ext_ref[:, :block] = jnp.zeros((block, block), F32)
        start = pl.multiple_of(me * block, block)
        far = lax.broadcasted_iota(jnp.int32, ext_ref.shape, 1) < start
        row8 = lax.broadcasted_iota(jnp.int32, (8, 2 * block), 0)
        lane_near = lax.broadcasted_iota(jnp.int32, (1, 2 * block), 1)

    def body(h, carry):
        wo_h = wo_ref[pl.ds(pl.multiple_of(h * win, size), win), :]
        dc_ref[...] = padded(nt(da, wo_h).astype(BF16), pw)
        for s in range(seqs):
            kw = k_ref[h, s * full : (s + 1) * full, :]
            vw = v_ref[h, s * full : (s + 1) * full, :]
            qcat = stack_heads(q_ref[h, s * block : (s + 1) * block, :], lanes)
            dcat = stack_heads(dc_ref[s * block : (s + 1) * block, :], lanes)
            sc = nt(qcat, kw)
            if biased:
                sc = sc + b_ref[pl.ds(h * group, group)].reshape(group * block, full).astype(F32)
            sc = jnp.where(key < len_ref[s], sc, NEG)
            lse_tile = lse_ref[h, s]
            lse = jnp.concatenate([lse_tile[:, a : a + 1] for a in range(group)], axis=0)
            p = jnp.exp(sc - lse)
            dp = nt(dcat, vw)
            ds = p * (dp - jnp.sum(p * dp, axis=-1, keepdims=True))
            ds = ds.astype(BF16)
            pb = p.astype(BF16)
            if biased:
                if s == 0:
                    sum_ref[...] = ds.astype(F32)
                else:
                    sum_ref[...] += ds.astype(F32)
            dq = join_heads(nn(ds, kw), lanes, block)
            dq_ref[s * block : (s + 1) * block, :] = dq.astype(BF16)
            dk = tn(ds, qcat).astype(BF16)
            dv = tn(pb, dcat).astype(BF16)
            dkv_ref[s * full : (s + 1) * full, :] = jnp.concatenate(
                [dk[:, :win], dv[:, :win]], axis=1
            )
        if biased:
            for a in range(group):
                ext_ref[:, block:] = sum_ref[a * block : (a + 1) * block, :]
                far_sum = jnp.sum(jnp.where(far, ext_ref[...], 0.0))
                fold = ext_ref[:, pl.ds(start, 2 * block)]
                half = block // 2
                while half >= 8:
                    fold = fold[:half] + pltpu.roll(fold[half:], 2 * block - half, 1)
                    half //= 2
                for bit in (4, 2, 1):
                    fold = jnp.where(
                        (row8 & bit) != 0, pltpu.roll(fold, 2 * block - bit, 1), fold
                    )
                line = jnp.sum(fold, axis=0, keepdims=True)
                line = line + jnp.where(lane_near == 2 * block - 1, far_sum, 0.0)
                diag_ref[pl.ds(h * group + a, 1), :] = line
        dkv = dkv_ref[...]
        dq_h = dq_ref[...][:, :win]
        kv_term = nn(dkv[:, :win], wkv_ref[h, 0]) + nn(dkv[:, win:], wkv_ref[h, 1])
        q_term = nn(dq_h, wq_ref[h])
        w_ref[h] = jnp.concatenate(
            [
                nn(nkt_ref[...], dkv).astype(BF16),
                nn(nqt_ref[...], dq_h).astype(BF16),
                nn(dat_ref[...], c_ref[h][:, :win]).astype(BF16),
            ],
            axis=1,
        )

        @pl.when(h == 0)
        def _():
            acc_ref[: seqs * full, :] = kv_term
            acc_ref[seqs * full :, :] = q_term

        @pl.when(h != 0)
        def _():
            acc_ref[: seqs * full, :] += kv_term
            acc_ref[seqs * full :, :] += q_term

        return carry

    lax.fori_loop(0, shards, body, 0)
    if biased:
        for s in range(seqs):
            own = pl.ds(pl.multiple_of(s * full + me * block, block), block)
            acc_ref[own, :] += acc_ref[seqs * full + s * block : seqs * full + (s + 1) * block, :]
        total = acc_ref[: seqs * full, :]
        part_ref[...] = total.astype(BF16)
        gg_ref[...] = (
            jnp.sum(total * nk_ref[...].astype(F32), axis=0, keepdims=True) / row(gain_ref)
        )
    else:
        part_ref[...] = acc_ref[: seqs * full, :].astype(BF16)
        dy, gg = norm_grads(y_ref[...], row(gain_ref), acc_ref[seqs * full :, :])
        dprev_ref[...] = dy_ref[...] + dy
        gg_ref[...] = gg


def attend_backward(
    lens, me, nq, nk, saved, wq, wkv, wo, dy, gain, extra, biased, group, size, order
):
    q, k, v, c, lse = saved
    rows, width = nq.shape
    shards, keys, pw = k.shape
    block = rows // lens.shape[0]
    full = keys // lens.shape[0]
    win = group * size
    args = [lens, me, nq, nk, q, k, v, c, lse, wq, wkv, wo, dy, gain, extra]
    out_shape = [
        sds((keys, width), BF16),
        sds((1, width), F32),
        sds((shards, width, 4 * win), BF16),
        sds((shards * group, 2 * block), F32) if biased else sds((rows, width), F32),
    ]
    scratch = [
        pltpu.VMEM((rows, pw), BF16),
        pltpu.VMEM((rows, pw), BF16),
        pltpu.VMEM((keys, 2 * win), BF16),
        pltpu.VMEM((keys + rows, width), F32),
        pltpu.VMEM((width, rows), BF16),
        pltpu.VMEM((width, keys), BF16),
        pltpu.VMEM((width, rows), BF16),
    ]
    if biased:
        scratch += [
            pltpu.VMEM((group * block, full), F32),
            pltpu.VMEM((block, full + block), F32),
        ]
    flops = 4 * (rows + 2 * keys + rows) * width * width + 10 * rows * full * width
    return pl.pallas_call(
        functools.partial(backward_kernel, biased, group, size, order),
        out_shape=out_shape,
        in_specs=[smem(), smem()] + [vmem()] * (len(args) - 2),
        out_specs=[vmem()] * 4,
        scratch_shapes=scratch,
        compiler_params=params(),
        cost_estimate=pl.CostEstimate(
            flops=flops, bytes_accessed=24 << 20, transcendentals=rows * full * 12
        ),
        name="attend_backward",
    )(*args)


def feed_kernel(
    order, y_ref, n_ref, cot_ref, win_ref, wout_ref, gain_ref, out_ref, dy_ref, gg_ref, w_ref,
    acc_ref, dn_ref, nt_ref, ct_ref,
):
    step = pl.program_id(0)
    part = wout_ref.shape[0]

    @pl.when(step == 0)
    def _():
        put_rows(nt_ref, n_ref[...].T, order)
        put_rows(ct_ref, cot_ref[...].T, order)
        acc_ref[...] = y_ref[...]
        dn_ref[...] = jnp.zeros_like(dn_ref)

    n = n_ref[...]
    cot = cot_ref[...]
    g = nn(n, win_ref[0])
    u = nn(n, win_ref[1])
    dh = nt(cot, wout_ref[...])
    scale = math.sqrt(2.0 / math.pi)
    square = g * g
    t = jnp.tanh(scale * (g + 0.044715 * square * g))
    half = 0.5 * (1.0 + t)
    gelu = g * half
    hid = (gelu * u).astype(BF16)
    slope = half + 0.5 * g * (1.0 - t * t) * (scale * (1.0 + 3 * 0.044715 * square))
    dg = (dh * u * slope).astype(BF16)
    du = (dh * gelu).astype(BF16)
    acc_ref[...] += nn(hid, wout_ref[...])
    dn_ref[...] += nt(dg, win_ref[0]) + nt(du, win_ref[1])
    w_ref[0, :, :part] = nn(nt_ref[...], dg).astype(BF16)
    w_ref[0, :, part : 2 * part] = nn(nt_ref[...], du).astype(BF16)
    w_ref[0, :, 2 * part :] = nn(ct_ref[...], hid).astype(BF16)

    @pl.when(step == pl.num_programs(0) - 1)
    def _():
        out_ref[...] = acc_ref[...].astype(BF16)
        dy, gg = norm_grads(y_ref[...], row(gain_ref), dn_ref[...])
        dy_ref[...] = cot_ref[...].astype(F32) + dy
        gg_ref[...] = gg


def feed(y, n, cot, w_in, w_out, gain, shards, order):
    rows, width = y.shape
    hidden = w_out.shape[0]
    part = hidden // shards
    fixed = lambda shape: pl.BlockSpec(shape, lambda j: (0,) * len(shape))
    return pl.pallas_call(
        functools.partial(feed_kernel, order),
        grid=(shards,),
        out_shape=[
            sds((rows, width), BF16),
            sds((rows, width), F32),
            sds((1, width), F32),
            sds((shards, width, 3 * part), BF16),
        ],
        in_specs=[
            fixed((rows, width)),
            fixed((rows, width)),
            fixed((rows, width)),
            pl.BlockSpec((2, width, part), lambda j: (0, 0, j)),
            pl.BlockSpec((part, width), lambda j: (j, 0)),
            fixed((width,)),
        ],
        out_specs=[
            fixed((rows, width)),
            fixed((rows, width)),
            fixed((1, width)),
            pl.BlockSpec((1, width, 3 * part), lambda j: (j, 0, 0)),
        ],
        scratch_shapes=[
            pltpu.VMEM((rows, width), F32),
            pltpu.VMEM((rows, width), F32),
            pltpu.VMEM((width, rows), BF16),
            pltpu.VMEM((width, rows), BF16),
        ],
        compiler_params=params(),
        cost_estimate=pl.CostEstimate(
            flops=18 * rows * width * hidden, bytes_accessed=24 << 20, transcendentals=rows * hidden
        ),
        name="feed",
    )(y, n, cot, w_in, w_out, gain)


MESH = pl.DeviceIdType.MESH


def place():
    b = lax.axis_index("batch")
    me = lax.axis_index("head")
    core = lax.rem(b, 2)
    x = lax.rem(lax.div(b, 2), 2)
    y = lax.div(b, 4)
    return b, me, core, x, y


def greet(devices):
    barrier = pltpu.get_barrier_semaphore()
    for device in devices:
        pl.semaphore_signal(barrier, inc=1, device_id=device, device_id_type=MESH)
    pl.semaphore_wait(barrier, len(devices))


def remote(src, dst, send, recv, device):
    return pltpu.make_async_remote_copy(
        src_ref=src,
        dst_ref=dst,
        send_sem=send,
        recv_sem=recv,
        device_id=device,
        device_id_type=MESH,
    )


def flipped(bit, by):
    return bit + by - 2 * bit * by


AHEAD = 2


class Links:
    def __init__(self):
        b, me, core, x, y = place()
        self.me, self.core, self.x, self.y = me, core, x, y
        self.high, self.low = lax.div(me, 2), lax.rem(me, 2)
        self.pair, self.far, self.cross = self.owner(1), self.owner(2), self.owner(0)
        self.over_core = (b + 1 - 2 * core, me)
        self.over_x = (b + 2 - 4 * x, me)
        self.over_y = (b + 4 - 8 * y, me)
        self.over_plane = (b + 2 - 4 * x + 4 - 8 * y, me)
        self.to_pair, self.to_far, self.to_cross = (b, self.pair), (b, self.far), (b, self.cross)

    def owner(self, k):
        by_low, by_high = 1 - k // 2, 1 - k % 2
        return 2 * flipped(self.high, by_high) + flipped(self.low, by_low)

    def greet(self):
        greet(
            [self.over_core, self.over_x, self.over_y, self.over_plane]
            + [self.to_pair, self.to_far, self.to_cross]
        )


class Sums:
    @staticmethod
    def scratch(chunks, rows, cols):
        items, half = chunks // 4, cols // 2
        dma = pltpu.SemaphoreType.DMA
        return [
            pltpu.VMEM((chunks, 2, 2, rows, cols), BF16),
            pltpu.VMEM((chunks, 2, 2, rows, cols), BF16),
            pltpu.VMEM((chunks, 2, rows, half), BF16),
            pltpu.VMEM((chunks, 2, rows, half), BF16),
            pltpu.VMEM((chunks, rows, half), BF16),
            pltpu.VMEM((chunks, rows, half), BF16),
            pltpu.VMEM((chunks, rows, cols), BF16),
            pltpu.VMEM((items, 3, rows, cols), BF16),
            dma((chunks,)),
            dma((chunks,)),
            dma((chunks,)),
            dma((chunks, 2)),
            dma((chunks, 2)),
            dma((chunks, 2)),
            dma((chunks, 2)),
            dma((items, 3)),
            dma((items, 3)),
        ]

    count = 17

    def __init__(self, links, refs):
        (self.own, self.rc, self.r1a, self.r1b, self.r2a, self.r2b, self.tot, self.rz) = refs[:8]
        (self.ls, self.cs, self.cr, self.s1, self.q1, self.s2, self.q2, self.zs, self.zr) = refs[8:]
        self.links = links
        self.chunks, self.cols = self.own.shape[0], self.own.shape[-1]
        self.half = self.cols // 2

    def piece(self, w_ref, c, side, left):
        start = pl.multiple_of((c // 4) * self.cols + left, 128)
        return w_ref.at[self.links.owner(c % 4), side, :, :, :, pl.ds(start, self.cols)]

    def local(self, w_ref, c, left):
        return pltpu.make_async_copy(
            self.piece(w_ref, c, self.links.core, left), self.own.at[c], self.ls.at[c]
        )

    def over_core(self, c, source):
        return remote(
            source, self.rc.at[c], self.cs.at[c], self.cr.at[c], self.links.over_core
        )

    def load(self, w_ref, c, left=0):
        self.local(w_ref, c, left).start()
        self.over_core(c, self.piece(w_ref, c, 1 - self.links.core, left)).start()

    def firsts(self, c):
        links, half = self.links, self.half
        return (
            remote(
                self.own.at[c, :, 1 - links.x, :, pl.ds(0, half)],
                self.r1a.at[c],
                self.s1.at[c, 0],
                self.q1.at[c, 0],
                links.over_x,
            ),
            remote(
                self.own.at[c, 1 - links.y, :, :, pl.ds(half, half)],
                self.r1b.at[c],
                self.s1.at[c, 1],
                self.q1.at[c, 1],
                links.over_y,
            ),
        )

    def seconds(self, c):
        links = self.links
        return (
            remote(
                self.r1a.at[c, 1 - links.y],
                self.r2a.at[c],
                self.s2.at[c, 0],
                self.q2.at[c, 0],
                links.over_y,
            ),
            remote(
                self.r1b.at[c, 1 - links.x],
                self.r2b.at[c],
                self.s2.at[c, 1],
                self.q2.at[c, 1],
                links.over_x,
            ),
        )

    def along(self, item, slot, c):
        device = self.links.to_far if slot == 2 else self.links.to_pair
        return remote(
            self.tot.at[c],
            self.rz.at[item, slot],
            self.zs.at[item, slot],
            self.zr.at[item, slot],
            device,
        )

    def core(self, c, w_ref=None, left=0):
        if w_ref is not None:
            self.local(w_ref, c, left).wait()
        self.over_core(c, self.rc.at[c]).wait_recv()
        x, y, half = 1 - self.links.x, 1 - self.links.y, self.half
        self.own[c, :, x, :, :half] = self.own[c, :, x, :, :half] + self.rc[c, :, x, :, :half]
        self.own[c, y, :, :, half:] = self.own[c, y, :, :, half:] + self.rc[c, y, :, :, half:]
        for copy in self.firsts(c):
            copy.start()

    def left(self, c, y):
        x, half = self.links.x, self.half
        total = self.own[c, y, x, :, :half].astype(F32) + self.rc[c, y, x, :, :half].astype(F32)
        return total + self.r1a[c, y].astype(F32)

    def right(self, c, x):
        y, half = self.links.y, self.half
        total = self.own[c, y, x, :, half:].astype(F32) + self.rc[c, y, x, :, half:].astype(F32)
        return total + self.r1b[c, x].astype(F32)

    def first(self, c):
        for copy in self.firsts(c):
            copy.wait_recv()
        x, y = 1 - self.links.x, 1 - self.links.y
        self.r1a[c, y] = self.left(c, y).astype(BF16)
        self.r1b[c, x] = self.right(c, x).astype(BF16)
        for copy in self.seconds(c):
            copy.start()

    def whole(self, c):
        left = self.left(c, self.links.y) + self.r2a[c].astype(F32)
        right = self.right(c, self.links.x) + self.r2b[c].astype(F32)
        return jnp.concatenate([left, right], axis=1)

    def second(self, c):
        for copy in self.seconds(c):
            copy.wait_recv()
        item, k = c // 4, c % 4
        for slot in range(2):

            @pl.when(k == slot)
            def _(slot=slot):
                self.tot[c] = self.whole(c).astype(BF16)
                self.along(item, slot, c).start()

        @pl.when(k == 2)
        def _():
            self.along(item, 0, c).wait_recv()
            self.tot[c] = (self.whole(c) + self.rz[item, 0].astype(F32)).astype(BF16)
            self.along(item, 2, c).start()

    def finish(self, item):
        c = 4 * item
        for slot in (1, 2):
            self.along(item, slot, c).wait_recv()
        return self.whole(c + 3) + self.rz[item, 1].astype(F32) + self.rz[item, 2].astype(F32)

    def drain(self):
        def body(c, carry):
            self.over_core(c, self.rc.at[c]).wait_send()
            for copy in self.firsts(c) + self.seconds(c):
                copy.wait_send()
            return carry

        lax.fori_loop(0, self.chunks, body, 0)
        for item in range(self.chunks // 4):
            for slot in range(3):
                self.along(item, slot, 4 * item).wait_send()


class Weights:
    @staticmethod
    def scratch(n):
        dma = pltpu.SemaphoreType.DMA
        return [dma((n, 3)), dma((n, 3)), dma((n, 3, 3)), dma((n, 3, 3)), dma((n, 3)), dma((n, 3))]

    def __init__(self, links, shards, fulls, sems):
        self.links, self.shards, self.fulls = links, shards, fulls
        self.zs, self.zr, self.ps, self.pr, self.cs, self.cr = sems
        self.n = len(shards)
        self.planes = (links.pair, links.far, links.cross)
        self.slot = links.core * 4 + links.y * 2 + links.x

    def window(self, ref, first, count):
        step = ref.shape[-2] // 8
        return ref.at[:, pl.ds(pl.multiple_of(first * step, step), count * step), :]

    def along(self, i, slot):
        links = self.links
        source = self.planes[1] if slot == 2 else links.me
        into = self.window(self.fulls[i].at[source], self.slot, 1)
        mine = into if slot == 2 else self.window(self.shards[i], self.slot, 1)
        device = links.to_far if slot == 1 else links.to_pair
        return remote(mine, into, self.zs.at[i, slot], self.zr.at[i, slot], device)

    def across(self, i, j, d):
        links = self.links
        piece = self.window(self.fulls[i].at[self.planes[j]], self.slot, 1)
        device = (links.over_x, links.over_y, links.over_plane)[d]
        return remote(piece, piece, self.ps.at[i, j, d], self.pr.at[i, j, d], device)

    def core(self, i, j):
        half = self.window(self.fulls[i].at[self.planes[j]], self.links.core * 4, 4)
        return remote(half, half, self.cs.at[i, j], self.cr.at[i, j], self.links.over_core)

    def start(self):
        for i in range(self.n):
            for slot in (0, 1):
                self.along(i, slot).start()

    def arrive(self, j):
        for i in range(self.n):
            self.along(i, j).wait_recv()
            if j == 1:
                self.along(i, 2).start()
            for d in range(3):
                self.across(i, j, d).start()

    def share(self, j):
        for i in range(self.n):
            for d in range(3):
                self.across(i, j, d).wait_recv()
            self.core(i, j).start()

    def finish(self, j):
        for i in range(self.n):
            self.core(i, j).wait_recv()

    def drain(self):
        for i in range(self.n):
            for j in range(3):
                self.along(i, j).wait_send()
                self.core(i, j).wait_send()
                for d in range(3):
                    self.across(i, j, d).wait_send()


class Gathered:
    def __init__(self, links, source, into, sems):
        self.links, self.source, self.into = links, source, into
        self.ss, self.rs = sems
        self.seqs, self.block = into.shape[0], into.shape[1] // 4

    def window(self, s, plane):
        rows = pl.ds(pl.multiple_of(plane * self.block, self.block), self.block)
        return self.into.at[s, rows, :]

    def copy(self, s, slot):
        links = self.links
        into = self.window(s, links.far if slot == 2 else links.me)
        mine = into if slot == 2 else self.source(s)
        device = links.to_far if slot == 1 else links.to_pair
        return remote(mine, into, self.ss.at[s, slot], self.rs.at[s, slot], device)

    def start(self):
        for s in range(self.seqs):
            for slot in (1, 0):
                self.copy(s, slot).start()

    def forward(self):
        for s in range(self.seqs):
            self.copy(s, 1).wait_recv()
            self.copy(s, 2).start()

    def take(self, slot):
        for s in range(self.seqs):
            self.copy(s, slot).wait_recv()

    def finish(self):
        for slot in (0, 2):
            self.take(slot)

    def drain(self):
        for s in range(self.seqs):
            for slot in range(3):
                self.copy(s, slot).wait_send()


def front_kernel(group, size, *refs):
    len_ref, enc_ref, x_ref, self_gain_ref, cross_gain_ref, feed_gain_ref, table_ref, *refs = refs
    memory_ref, own_weights, refs = refs[0], refs[1:7], refs[7:]
    n_ref, y_ref, n2_ref, y2_ref, n3_ref, memory_out, *refs = refs
    self_out, cross_out, refs = refs[:3], refs[3:6], refs[6:]
    outs, kept, refs = refs[:12], refs[12:24], refs[24:]
    nall_ref, bias_ref, q_ref, k_ref, v_ref, c_ref, lse_ref = kept[:7]
    q2_ref, k2_ref, v2_ref, c2_ref, lse2_ref = kept[7:]
    self_full, cross_full, refs = refs[:3], refs[3:6], refs[6:]
    tables_ref, ext_ref, line_ref, mem_ref, *refs = refs
    (table_s, table_r, rows_s, rows_r, memory_s, memory_r, local, placed, held, done, *refs) = refs
    links = Links()
    me = links.me
    w1 = Weights(links, own_weights[:3], self_out, refs[:6])
    w2 = Weights(links, own_weights[3:], cross_out, refs[6:])
    shards, rows, pw = q_ref.shape
    seqs = len_ref.shape[0]
    block = rows // seqs
    full = block * shards
    win = group * size
    lanes = lane_groups(pw, group, size)
    key = lax.broadcasted_iota(jnp.int32, (1, full), 1)
    start = pl.multiple_of(me * block, block)
    rows_one = Gathered(
        links, lambda s: nall_ref.at[s, pl.ds(start, block), :], nall_ref, (rows_s, rows_r)
    )
    rows_memory = Gathered(
        links, lambda s: mem_ref.at[s, pl.ds(start, block), :], memory_out, (memory_s, memory_r)
    )

    line_ref[...] = jnp.zeros_like(line_ref)
    line_ref[:group, :NB] = table_ref[...].astype(F32)
    tables_ref[me] = line_ref[:, : tables_ref.shape[2]].astype(BF16)
    links.greet()
    w1.start()
    heard = [
        remote(tables_ref.at[me], tables_ref.at[me], table_s.at[i], table_r.at[i], to)
        for i, to in enumerate((links.to_pair, links.to_far, links.to_cross))
    ]
    for copy in heard:
        copy.start()
    taken = [
        pltpu.make_async_copy(own_weights[i], self_full[i].at[me], local.at[i]) for i in range(3)
    ]
    taken += [
        pltpu.make_async_copy(own_weights[3 + i], cross_full[i].at[me], local.at[3 + i])
        for i in range(3)
    ]
    taken.append(
        pltpu.make_async_copy(memory_ref, mem_ref.at[:, pl.ds(start, block), :], local.at[6])
    )
    for copy in taken:
        copy.start()
    x = x_ref[...].astype(F32)
    n_ref[...] = (x * rms(x) * row(self_gain_ref)).astype(BF16)
    for s in range(seqs):
        nall_ref[s, pl.ds(start, block), :] = n_ref[s * block : (s + 1) * block, :]
    w1.arrive(0)
    w1.arrive(1)
    rows_one.start()
    w1.arrive(2)
    for copy in heard:
        copy.wait_recv()
    build_bias(me, tables_ref, bias_ref, ext_ref, line_ref)
    for copy in taken:
        copy.wait()
    put = [
        pltpu.make_async_copy(cross_full[i].at[me], cross_out[i].at[me], placed.at[i])
        for i in range(3)
    ]
    put += [
        pltpu.make_async_copy(self_full[i].at[me], self_out[i].at[me], placed.at[3 + i])
        for i in range(3)
    ]
    put += [
        pltpu.make_async_copy(
            rows_memory.source(s), rows_memory.window(s, me), placed.at[6 + s]
        )
        for s in range(seqs)
    ]
    for copy in put:
        copy.start()
    rows_one.forward()
    for j in range(3):
        w1.share(j)
    def hold(i, j):
        plane = w1.planes[j]
        into, source = (self_full[i], self_out[i]) if i < 3 else (cross_full[i - 3], cross_out[i - 3])
        return pltpu.make_async_copy(source.at[plane], into.at[plane], held.at[i, j])

    for j in range(3):
        w1.finish(j)
        for i in range(3):
            hold(i, j).start()
    rows_one.finish()
    w2.start()

    def keep(i, h=None):
        if h is None:
            return pltpu.make_async_copy(kept[i], outs[i], done.at[i, 0])
        return pltpu.make_async_copy(kept[i].at[h], outs[i].at[h], done.at[i, h])

    for i in range(2):
        keep(i).start()
    for j in range(3):
        for i in range(3):
            hold(i, j).wait()

    def body(k, carry):
        h = links.owner(lax.rem(k + 3, shards))
        nk = nall_ref[...].reshape(seqs * full, -1)
        q_ref[h] = padded(nt(n_ref[...], self_full[0][h, 0]).astype(BF16), pw)
        k_ref[h] = padded(nt(nk, self_full[1][h, 0]).astype(BF16), pw)
        v_ref[h] = padded(nt(nk, self_full[1][h, 1]).astype(BF16), pw)
        for s in range(seqs):
            c, lse_ref[h, s] = head_context(
                q_ref[h, s * block : (s + 1) * block, :],
                k_ref[h, s * full : (s + 1) * full, :],
                v_ref[h, s * full : (s + 1) * full, :],
                bias_ref[pl.ds(h * group, group)].reshape(group * block, full).astype(F32),
                key < len_ref[s],
                lanes,
            )
            c_ref[h, s * block : (s + 1) * block, :] = c
        for i in range(2, 7):
            keep(i, h).start()

        @pl.when(k == 0)
        def _():
            w2.arrive(0)
            w2.arrive(1)
            rows_memory.start()

        @pl.when(k == 1)
        def _():
            w2.arrive(2)

        return carry

    lax.fori_loop(0, shards, body, 0)
    joined = jnp.concatenate([c_ref[h][:, :win] for h in range(shards)], axis=1)
    out_weight = self_full[2][...].reshape(shards * win, -1)
    y = x_ref[...].astype(F32) + nn(joined, out_weight)
    y_ref[...] = y
    n2_ref[...] = (y * rms(y) * row(cross_gain_ref)).astype(BF16)
    for j in range(3):
        w2.share(j)
    rows_memory.forward()
    for j in range(3):
        w2.finish(j)
        for i in range(3, 6):
            hold(i, j).start()
    for j in range(3):
        for i in range(3, 6):
            hold(i, j).wait()

    def ask(h, carry):
        q2_ref[h] = padded(nt(n2_ref[...], cross_full[0][h, 0]).astype(BF16), pw)
        return carry

    lax.fori_loop(0, shards, ask, 0)

    def bring(plane, j):
        rows = pl.ds(pl.multiple_of(plane * block, block), block)
        return pltpu.make_async_copy(
            memory_out.at[:, rows, :], mem_ref.at[:, rows, :], local.at[j]
        )

    for j, (plane, slot) in enumerate(((me, None), (links.far, 1), (links.pair, 0), (links.cross, 2))):
        if slot is not None:
            if slot != 1:
                rows_memory.take(slot)
            bring(plane, j).start()
            bring(plane, j).wait()
        first = pl.multiple_of(plane * block, block)
        m = mem_ref[:, pl.ds(first, block), :].reshape(rows, -1)

        def answer(h, carry, first=first, m=m):
            for into, which in ((k2_ref, 0), (v2_ref, 1)):
                value = padded(nt(m, cross_full[1][h, which]).astype(BF16), pw)
                for s in range(seqs):
                    into[h, pl.ds(s * full + first, block), :] = value[s * block : (s + 1) * block]
            return carry

        lax.fori_loop(0, shards, answer, 0)

    def cross_body(h, carry):
        for s in range(seqs):
            c, lse2_ref[h, s] = head_context(
                q2_ref[h, s * block : (s + 1) * block, :],
                k2_ref[h, s * full : (s + 1) * full, :],
                v2_ref[h, s * full : (s + 1) * full, :],
                None,
                key < enc_ref[s],
                lanes,
            )
            c2_ref[h, s * block : (s + 1) * block, :] = c
        for i in range(7, 12):
            keep(i, h).start()
        return carry

    lax.fori_loop(0, shards, cross_body, 0)
    joined = jnp.concatenate([c2_ref[h][:, :win] for h in range(shards)], axis=1)
    out_weight = cross_full[2][...].reshape(shards * win, -1)
    y2 = y_ref[...] + nn(joined, out_weight)
    y2_ref[...] = y2
    n3_ref[...] = (y2 * rms(y2) * row(feed_gain_ref)).astype(BF16)
    w1.drain()
    w2.drain()
    rows_one.drain()
    rows_memory.drain()
    for copy in heard:
        copy.wait_send()
    for copy in put:
        copy.wait()
    for i in range(2):
        keep(i).wait()
    for h in range(shards):
        for i in range(2, 12):
            keep(i, h).wait()


def front(lens, encs, x, gains, table, memory, weights, shards, group, size):
    rows, width = x.shape
    seqs = lens.shape[0]
    block = rows // seqs
    full, keys = block * shards, rows * shards
    win = group * size
    pw = -(-win // 128) * 128
    fulls = [((shards, *w.shape), BF16) for w in weights]
    kept = [((seqs, full, width), BF16), ((shards * group, block, full), BF16)]
    kept += [((shards, n, pw), BF16) for n in (rows, keys, keys, rows)]
    kept.append(((shards, seqs, block, 128), F32))
    kept += kept[2:]
    dma = pltpu.SemaphoreType.DMA
    anywhere = pl.BlockSpec(memory_space=pl.ANY)
    return pl.pallas_call(
        functools.partial(front_kernel, group, size),
        out_shape=[
            sds((rows, width), BF16),
            sds((rows, width), F32),
            sds((rows, width), BF16),
            sds((rows, width), F32),
            sds((rows, width), BF16),
            sds((seqs, full, width), BF16),
        ]
        + [sds(*a) for a in fulls + kept],
        in_specs=[smem()] * 2 + [vmem()] * 5 + [anywhere] * 7,
        out_specs=[vmem()] * 5 + [anywhere] * 19,
        scratch_shapes=[pltpu.VMEM(*a) for a in kept + fulls]
        + [
            pltpu.VMEM((shards, 8, 128), BF16),
            pltpu.VMEM((block, full + block), F32),
            pltpu.VMEM((8, 2 * block), F32),
            pltpu.VMEM((seqs, full, width), BF16),
            dma((3,)),
            dma((3,)),
            dma((seqs, 3)),
            dma((seqs, 3)),
            dma((seqs, 3)),
            dma((seqs, 3)),
            dma((7,)),
            dma((6 + seqs,)),
            dma((6, 3)),
            dma((len(kept), shards)),
        ]
        + Weights.scratch(3)
        + Weights.scratch(3),
        compiler_params=pltpu.CompilerParams(
            collective_id=0, has_side_effects=True, vmem_limit_bytes=VMEM_LIMIT
        ),
        name="front",
    )(lens, encs, x, *gains, table, memory, *weights)


class Rows:
    @staticmethod
    def scratch(rows, width):
        dma = pltpu.SemaphoreType.DMA
        return [
            pltpu.VMEM((4, rows, width), BF16),
            pltpu.VMEM((3, rows, width), BF16),
            dma((3,)),
            dma((3,)),
        ]

    count = 4

    def __init__(self, links, refs):
        self.links = links
        self.buf, self.rx, self.ss, self.rs = refs

    def copy(self, slot):
        links = self.links
        block = (links.cross, links.far, links.pair)[slot]
        device = (links.to_cross, links.to_far, links.to_pair)[slot]
        return remote(
            self.buf.at[block], self.rx.at[slot], self.ss.at[slot], self.rs.at[slot], device
        )

    def start(self):
        for slot in range(3):
            self.copy(slot).start()

    def finish(self):
        for slot in range(3):
            self.copy(slot).wait_recv()
        return sum(self.rx[slot].astype(F32) for slot in range(3))

    def drain(self):
        for slot in range(3):
            self.copy(slot).wait_send()


def head_grads(qw, kw, vw, dcw, lse_tile, bias, keep, lanes):
    block, group = qw.shape[0], len(lanes)
    qcat, dcat = stack_heads(qw, lanes), stack_heads(dcw, lanes)
    sc = nt(qcat, kw)
    if bias is not None:
        sc = sc + bias
    sc = jnp.where(keep, sc, NEG)
    lse = jnp.concatenate([lse_tile[:, a : a + 1] for a in range(group)], axis=0)
    p = jnp.exp(sc - lse)
    dp = nt(dcat, vw)
    ds = (p * (dp - jnp.sum(p * dp, axis=-1, keepdims=True))).astype(BF16)
    dq = join_heads(nn(ds, kw), lanes, block).astype(BF16)
    dk = tn(ds, qcat).astype(BF16)
    dv = tn(p.astype(BF16), dcat).astype(BF16)
    return ds, dq, dk, dv


def diagonal_line(near, far_sum):
    block, width = near.shape
    half = block // 2
    while half >= 8:
        near = near[:half] + pltpu.roll(near[half:], width - half, 1)
        half //= 2
    row8 = lax.broadcasted_iota(jnp.int32, (8, width), 0)
    for bit in (4, 2, 1):
        near = jnp.where((row8 & bit) != 0, pltpu.roll(near, width - bit, 1), near)
    line = jnp.sum(near, axis=0, keepdims=True)
    lane = lax.broadcasted_iota(jnp.int32, (1, width), 1)
    return line + jnp.where(lane == width - 1, far_sum, 0.0)


def linked_kernel(biased, group, size, order, *refs):
    len_ref, dy_ref, gain_ref, given_ref, *refs = refs
    held_count = 11 if biased else 10
    held, refs = refs[:held_count], refs[held_count:]
    if biased:
        feed_ref, x_ref, rows_ref, gain2_ref, gain3_ref, *refs = refs
        grad_ref, mem_ref, feed_out, given_out, own_out, small_out, *refs = refs
    else:
        y_ref, dprev_ref, gg_ref, w_ref, later_ref, mem_ref, given_out, *refs = refs
    buffers, held_sem, refs = refs[:held_count], refs[held_count], refs[held_count + 1 :]
    nq_ref, nk_ref, c_ref, wo_ref, q_ref, k_ref, v_ref, lse_ref, wq_ref, wkv_ref = buffers[:10]
    bias_ref = buffers[-1]
    dq_ref, dkv_ref, acck_ref, accq_ref, nqt_ref, nkt_ref, dat_ref, wtmp_ref, *refs = refs
    links = Links()
    sums = Sums(links, refs[: Sums.count])
    refs = refs[Sums.count :]
    if biased:
        feed_sums = Sums(links, refs[: Sums.count])
        refs = refs[Sums.count :]
    exchanges = []
    for _ in range(3 if biased else 1):
        exchanges.append(Rows(links, refs[: Rows.count]))
        refs = refs[Rows.count :]
    if biased:
        ds_ref, ext_ref, diag_ref, sr, ms, mr = refs
    else:
        (w_sem,) = refs
    shards, rows, pw = q_ref.shape
    seqs = len_ref.shape[0]
    block = rows // seqs
    full = k_ref.shape[1] // seqs
    win = group * size
    lanes = lane_groups(pw, group, size)
    key = lax.broadcasted_iota(jnp.int32, (1, full), 1)
    me = links.me
    start = pl.multiple_of(me * block, block)
    def fetch(j, h=None):
        if h is None:
            return pltpu.make_async_copy(held[j], buffers[j], held_sem.at[j, 0])
        part = pl.ds(h * group, group) if j == 10 else h
        return pltpu.make_async_copy(held[j].at[part], buffers[j].at[part], held_sem.at[j, h])

    links.greet()
    if biased:
        exchanges[0].buf[...] = rows_ref[...]
        exchanges[0].start()
    for place in range(AHEAD):
        sums.load(given_ref, place)
    fetch(3).start()
    for k in range(shards):
        for j in range(4, held_count):
            fetch(j, links.owner(k)).start()
    for j in range(3):
        fetch(j).start()

    def stage(name, place):
        if name == "load":
            if not biased:
                sums.load(given_ref, place)
                return

            @pl.when(place < 4)
            def _():
                sums.load(given_ref, place)

            @pl.when(place >= 4)
            def _():
                feed_sums.load(feed_ref, place - 4, 2 * feed_sums.cols)

            return
        if not biased:
            run = getattr(sums, name)
            run(place, given_ref) if name == "core" else run(place)
            return

        @pl.when(place < 4)
        def _():
            sums.core(place, given_ref) if name == "core" else getattr(sums, name)(place)

        @pl.when((place >= 4) & (place < 8))
        def _():
            c = place - 4
            if name == "core":
                feed_sums.core(c, feed_ref, 2 * feed_sums.cols)
            else:
                getattr(feed_sums, name)(c)

        @pl.when(place >= 8)
        def _():
            getattr(sums, name)(place - 4)

    places = 12 if biased else sums.chunks
    late = (("load", -AHEAD), ("core", 0), ("first", 1), ("second", 3))

    def tick(t):
        for name, behind in late:
            place = t - behind

            @pl.when((place >= 0) & (place < (8 if name == "load" else places)))
            def _(name=name, place=place):
                stage(name, place)

    da = dy_ref[...].astype(BF16)
    if biased:
        ext_ref[:, :block] = jnp.zeros((block, block), F32)
        far = lax.broadcasted_iota(jnp.int32, ext_ref.shape, 1) < start
    fetch(3).wait()

    for s in range(seqs):
        mine = slice(s * block, (s + 1) * block)
        theirs = slice(s * full, (s + 1) * full)
        if s == seqs - 1:
            for j in (0, 2) if biased else range(3):
                fetch(j).wait()
            put_rows(nqt_ref, nq_ref[...].T, order)
            put_rows(nkt_ref, nk_ref[...].T, order)
            put_rows(dat_ref, da.T, order)

        def body(k, carry):
            h = links.owner(k)
            if s == 0:
                for j in range(4, held_count):
                    fetch(j, h).wait()
            wo_h = wo_ref[pl.ds(pl.multiple_of(h * win, size), win), :]
            dcw = padded(nt(da[mine], wo_h).astype(BF16), pw)
            bias = None
            if biased:
                bias = bias_ref[pl.ds(h * group, group)].reshape(group * block, full).astype(F32)
            ds, dq, dk, dv = head_grads(
                q_ref[h, mine, :],
                k_ref[h, theirs, :],
                v_ref[h, theirs, :],
                dcw,
                lse_ref[h, s],
                bias,
                key < len_ref[s],
                lanes,
            )
            dkv = jnp.concatenate([dk[:, :win], dv[:, :win]], axis=1)
            dkv_ref[h, theirs, :] = dkv
            dq_ref[h, mine, :] = dq
            kv_term = nn(dkv[:, :win], wkv_ref[h, 0]) + nn(dkv[:, win:], wkv_ref[h, 1])
            q_term = nn(dq[:, :win], wq_ref[h])

            @pl.when(k == 0)
            def _():
                acck_ref[...] = kv_term
                accq_ref[mine, :] = q_term

            @pl.when(k != 0)
            def _():
                acck_ref[...] += kv_term
                accq_ref[mine, :] += q_term

            if biased and s < seqs - 1:
                ds_ref[h] = ds if s == 0 else ds_ref[h] + ds
            if biased and s == seqs - 1:
                whole = ds_ref[h].astype(F32) + ds.astype(F32)
                for a in range(group):
                    ext_ref[:, block:] = whole[a * block : (a + 1) * block, :]
                    far_sum = jnp.sum(jnp.where(far, ext_ref[...], 0.0))
                    near = ext_ref[:, pl.ds(start, 2 * block)]
                    diag_ref[pl.ds(h * group + a, 1), :] = diagonal_line(near, far_sum)
            if s == seqs - 1:
                dkv = dkv_ref[h]

                def weight_rows(side):
                    rows = pl.ds(pl.multiple_of(side * 4 * w_rows, 4 * w_rows), 4 * w_rows)
                    return jnp.concatenate(
                        [
                            nn(nkt_ref[rows, :], dkv).astype(BF16),
                            nn(nqt_ref[rows, :], dq_ref[h][:, :win]).astype(BF16),
                            nn(dat_ref[rows, :], c_ref[h][:, :win]).astype(BF16),
                        ],
                        axis=1,
                    ).reshape(2, 2, w_rows, 4 * win)

                if biased:
                    wtmp_ref[k] = weight_rows(1 - links.core)
                    sums.over_core(4 + k, wtmp_ref.at[k]).start()
                    sums.own[4 + k] = weight_rows(links.core)
                else:
                    for side in range(2):
                        wtmp_ref[h, side] = weight_rows(side)
                    pltpu.make_async_copy(wtmp_ref.at[h], w_ref.at[h], w_sem.at[h]).start()
            tick(4 * s + k)
            return carry

        w_rows = nqt_ref.shape[0] // 8
        lax.fori_loop(0, shards, body, 0)
        if biased:
            acck_ref[pl.ds(start, block), :] += accq_ref[mine, :]
            total = acck_ref[...]
            if s == 0:
                fetch(1).wait()
            part = jnp.sum(total * nk_ref[theirs, :].astype(F32), axis=0, keepdims=True)
            gain1 = part if s == 0 else gain1 + part
            mover = exchanges[1 + s]
            mover.buf[...] = total.astype(BF16).reshape(shards, block, -1)
            mover.start()
            grad_ref[mine, :] = acck_ref[pl.ds(start, block), :]
        elif s == 0:
            exchanges[0].buf[...] = acck_ref[...].astype(BF16).reshape(shards, block, -1)
            exchanges[0].start()
            mem_ref[...] = acck_ref[pl.ds(start, block), :]
        else:
            later_ref[...] = acck_ref[...].astype(BF16).reshape(shards, block, -1)

    steps = range(4 * seqs, places + late[-1][1])
    if not biased:
        dy, gg = norm_grads(y_ref[...], row(gain_ref), accq_ref[...])
        dprev_ref[...] = dy_ref[...] + dy
        gg_ref[...] = gg
        for t in steps:
            tick(t)
        mem_ref[...] += exchanges[0].finish()
        for item in range(2):
            given_out[item] = sums.finish(item)
        for h in range(shards):
            pltpu.make_async_copy(wtmp_ref.at[h], w_ref.at[h], w_sem.at[h]).wait()
    else:
        gain1 = gain1 / row(gain_ref)
        width = gain1.shape[1]
        diag_ref[shards * group :, :] = jnp.zeros_like(diag_ref[shards * group :, :])
        sr[0, : diag_ref.shape[0], :] = diag_ref[...]
        sr[0, diag_ref.shape[0] :, :] = jnp.zeros_like(sr[0, diag_ref.shape[0] :, :])
        for i, line in enumerate((gain1, gain2_ref[...], gain3_ref[...])):
            for j in range(width // (2 * block)):
                at = diag_ref.shape[0] + i * width // (2 * block) + j
                sr[0, at : at + 1, :] = line[:, j * 2 * block : (j + 1) * 2 * block]
        plane = 2 + 2 * links.y + links.x
        hops = [(1, 0, links.over_core)]
        hops += [(plane, plane, to) for to in (links.over_x, links.over_y, links.over_plane)]
        hops += [(6 + me, 6 + me, to) for to in (links.to_pair, links.to_far, links.to_cross)]

        def hop(i):
            into, source, to = hops[i]
            return remote(sr.at[source], sr.at[into], ms.at[i], mr.at[i], to)

        hop(0).start()
        for i, t in enumerate(steps):
            tick(t)
            if i == 1:
                hop(0).wait_recv()
                sr[plane] = sr[0] + sr[1]
                for j in (1, 2, 3):
                    hop(j).start()
            if i == 3:
                for j in (1, 2, 3):
                    hop(j).wait_recv()
                sr[6 + me] = (sr[2] + sr[3]) + (sr[4] + sr[5])
                for j in (4, 5, 6):
                    hop(j).start()
        for j in (4, 5, 6):
            hop(j).wait_recv()
        small_out[...] = (sr[6] + sr[7]) + (sr[8] + sr[9])
        mem_ref[...] = exchanges[0].buf[me].astype(F32) + exchanges[0].finish()
        feed_out[...] = feed_sums.finish(0)
        given_out[...] = sums.finish(0)
        for s in range(seqs):
            mine = slice(s * block, (s + 1) * block)
            dn = grad_ref[mine, :] + exchanges[1 + s].finish()
            dx, _ = norm_grads(x_ref[mine, :].astype(F32), row(gain_ref), dn)
            grad_ref[mine, :] = dy_ref[mine, :] + dx
        own_out[...] = sums.finish(1)
        for i in range(len(hops)):
            hop(i).wait_send()
    for mover in exchanges:
        mover.drain()
    sums.drain()
    if biased:
        feed_sums.drain()


def linked_backward(lens, nq, nk, saved, wq, wkv, wo, dy, gain, given, extras, biased, group, size, order):
    q, k, v, c, lse = saved
    rows, width = nq.shape
    shards, keys, pw = k.shape
    seqs = lens.shape[0]
    block, full, win = rows // seqs, keys // seqs, group * size
    cols = 4 * win
    share = width // 8
    split = lambda w: w.reshape(shards, 2, 2, 2, share, -1)
    held = [nq, nk, c, wo, q, k, v, lse, wq, wkv]
    if biased:
        held.append(extras[1])
        extras = [split(extras[0]), *extras[2:]]
    args = [lens, dy, gain, split(given), *held, *extras]
    part = split(extras[0] if biased else given).shape[-1] // 3
    if biased:
        lines = -(-3 * width // (2 * block) // 8) * 8
        diag_rows = -(-shards * group // 8) * 8
        out_shape = [
            sds((rows, width), F32),
            sds((block, width), F32),
            sds((share, part), F32),
            sds((share, cols), F32),
            sds((share, cols), F32),
            sds((diag_rows + lines, 2 * block), F32),
        ]
    else:
        out_shape = [
            sds((rows, width), F32),
            sds((1, width), F32),
            sds((shards, 2, 2, 2, share, cols), BF16),
            sds((shards, block, width), BF16),
            sds((block, width), F32),
            sds((2, share, part), F32),
        ]
    scratch = [pltpu.VMEM(a.shape, a.dtype) for a in held]
    scratch += [
        pltpu.SemaphoreType.DMA((len(held), shards)),
        pltpu.VMEM((shards, rows, pw), BF16),
        pltpu.VMEM((shards, keys, 2 * win), BF16),
        pltpu.VMEM((full, width), F32),
        pltpu.VMEM((rows, width), F32),
        pltpu.VMEM((width, rows), BF16),
        pltpu.VMEM((width, keys), BF16),
        pltpu.VMEM((width, rows), BF16),
    ]
    scratch.append(pltpu.VMEM((shards, *(() if biased else (2,)), 2, 2, share, cols), BF16))
    scratch += Sums.scratch(8, share, cols if biased else part)
    if biased:
        scratch += Sums.scratch(4, share, part)
    for _ in range(3 if biased else 1):
        scratch += Rows.scratch(block, width)
    if biased:
        dma = pltpu.SemaphoreType.DMA
        scratch += [
            pltpu.VMEM((shards, group * block, full), BF16),
            pltpu.VMEM((block, full + block), F32),
            pltpu.VMEM((diag_rows, 2 * block), F32),
            pltpu.VMEM((10, diag_rows + lines, 2 * block), F32),
            dma((7,)),
            dma((7,)),
        ]
    else:
        scratch.append(pltpu.SemaphoreType.DMA((shards,)))
    anywhere = pl.BlockSpec(memory_space=pl.ANY)
    in_specs = [smem(), vmem(), vmem(), anywhere] + [anywhere] * len(held)
    in_specs += [anywhere if biased else vmem()] + [vmem()] * (len(extras) - 1)
    out_specs = [vmem()] * len(out_shape)
    if not biased:
        out_specs[2] = anywhere
    return pl.pallas_call(
        functools.partial(linked_kernel, biased, group, size, order),
        out_shape=out_shape,
        in_specs=in_specs,
        out_specs=out_specs,
        scratch_shapes=scratch,
        compiler_params=pltpu.CompilerParams(
            collective_id=2 if biased else 1, has_side_effects=True, vmem_limit_bytes=VMEM_LIMIT
        ),
        name="self_backward" if biased else "cross_backward",
    )(*args)


def arrange_kernel(
    shards, group, win, me_ref, grad_ref, first_ref, last_ref, gates_ref, hid_ref, cross_ref,
    self_ref, small_ref, grad_out, mem_out, gates_out, hid_out, table_out, *refs,
):
    gain_outs, weight_outs = refs[:3], refs[3:]
    grad_out[...] = grad_ref[...].reshape(grad_out.shape)
    mem_out[0] = first_ref[...]
    mem_out[1] = last_ref[...]
    gates_out[...] = gates_ref[...]
    hid_out[...] = hid_ref[...]
    for i, w_ref in enumerate((self_ref, cross_ref)):
        q_out, kv_out, o_out = weight_outs[3 * i : 3 * i + 3]
        w = w_ref[...]
        kv_out[0] = w[:, :win]
        kv_out[1] = w[:, win : 2 * win]
        q_out[...] = w[:, 2 * win : 3 * win]
        o_out[...] = w[:, 3 * win :].T
    head_rows = -(-shards * group // 8) * 8
    span = small_ref.shape[1]
    heads = lax.broadcasted_iota(jnp.int32, (8, head_rows), 0) + me_ref[0] * group
    pick = (heads == lax.broadcasted_iota(jnp.int32, (8, head_rows), 1)).astype(F32)
    mine = jnp.dot(pick, small_ref[:head_rows, :], precision=highest)
    onehot = bucket_rows(span // 2, NB).astype(F32)
    sums = lax.dot_general(mine, onehot, (((1,), (1,)), ((), ())), precision=highest)
    table_out[...] = sums[:group, :]
    for i, gain_out in enumerate(gain_outs):
        lines = [
            small_ref[head_rows + i * gain_out.shape[0] // span + j, :]
            for j in range(gain_out.shape[0] // span)
        ]
        gain_out[...] = jnp.concatenate(lines)


def arranged(
    me, result, grad, first, last, gates, hid, cross_w, self_w, small, shards, group, win
):
    rows, width = grad.shape
    block = first.shape[0]
    share, part = hid.shape
    weights = [sds((share, win), F32), sds((2, share, win), F32), sds((win, share), F32)]
    grad, mem, gates, hid, table, gain1, gain2, gain3, *weights = pl.pallas_call(
        functools.partial(arrange_kernel, shards, group, win),
        out_shape=[
            sds((rows // block, block, width), F32),
            sds((rows // block, block, width), F32),
            sds(gates.shape, F32),
            sds((share, part), F32),
            sds((group, NB), F32),
            sds((width,), F32),
            sds((width,), F32),
            sds((width,), F32),
            *weights,
            *weights,
        ],
        in_specs=[smem()] + [vmem()] * 8,
        out_specs=[vmem()] * 14,
        compiler_params=params(),
        name="arrange",
    )(me, grad, first, last, gates, hid, cross_w, self_w, small)
    result = result.reshape(grad.shape)
    return (
        result, grad, mem, gain1, *weights[:3], table.T, gain2, *weights[3:], gain3, gates, hid.T
    )


def per_device(
    layer_input,
    memory,
    dec_lengths,
    enc_lengths,
    self_gain,
    self_query,
    self_key_value,
    self_out,
    rel_bias,
    cross_gain,
    cross_query,
    cross_key_value,
    cross_out,
    feed_gain,
    feed_in,
    feed_out,
    out_cotangent,
):
    shards = lax.axis_size("head")
    me = lax.axis_index("head").astype(jnp.int32).reshape(1)
    batch_count = lax.axis_size("batch")
    seqs, block, width = layer_input.shape
    group = rel_bias.shape[1]
    size = self_query.shape[1] // group
    win = group * size
    full = block * shards
    enc_full = memory.shape[1] * shards
    rows = seqs * block
    part = feed_in.shape[2] // shards
    sg = self_gain.astype(F32).reshape(1, width)

    x = layer_input.reshape(rows, width)
    x32 = x.astype(F32)
    tight = batch_count == 8 and shards == 4 and seqs == 2
    order = tuple((i % 2) * 4 + i // 2 for i in range(8)) if tight else (0,)
    table = rel_bias.T
    flip = lambda w: jnp.swapaxes(w, -1, -2)
    weights = [flip(self_query)[None], flip(self_key_value), self_out[None]]
    weights += [flip(cross_query)[None], flip(cross_key_value), cross_out[None]]
    onehot = near_onehot(block)
    if tight:
        n1, y1, n2, y2, n3, memory_all, wq1, wkv1, wo1, wq2, wkv2, wo2, n1_all, bias, *saved = front(
            dec_lengths, enc_lengths, x, (self_gain, cross_gain, feed_gain), table, memory, weights,
            shards, group, size,
        )
        saved1, saved2 = saved[:5], saved[5:]
        n1_all = n1_all.reshape(seqs * full, width)
    else:
        n1 = (x32 * rms(x32) * sg).astype(BF16)
        n1_all = lax.all_gather(n1.reshape(seqs, block, width), "head", axis=1, tiled=True)
        n1_all = n1_all.reshape(seqs * full, width)
        wq1, wkv1, wo1, wq2, wkv2, wo2 = [lax.all_gather(w, "head", axis=0) for w in weights]
        table = jnp.pad(table, ((0, 8 - group), (0, 128 - NB)))
        tables = lax.all_gather(table, "head", axis=0)
        bias = bias_tiles(me, tables, group, block, full)
        memory_all = lax.all_gather(memory, "head", axis=1, tiled=True)
    memory_all = memory_all.reshape(seqs * enc_full, width)
    wq1, wq2 = wq1[:, 0], wq2[:, 0]
    wo1, wo2 = wo1.reshape(width, width), wo2.reshape(width, width)
    if not tight:
        *saved1, y1, n2 = attend_forward(
            dec_lengths, n1, n1_all, x, wq1, wkv1, wo1, cross_gain, bias, group, size
        )
        *saved2, y2, n3 = attend_forward(
            enc_lengths, n2, memory_all, y1, wq2, wkv2, wo2, feed_gain, None, group, size
        )
    result, dy2, gain3, feed_w = feed(
        y2, n3, out_cotangent.reshape(rows, width), feed_in, feed_out, feed_gain, shards, order
    )
    gain_rows = width // (2 * block)
    if tight:
        dy1, gain2, cross_w, memory_later, memory_first, feed_in_grad = linked_backward(
            enc_lengths, n2, memory_all, saved2, wq2, wkv2, wo2, dy2, cross_gain, feed_w, [y1],
            False, group, size, order,
        )
        input_grad, memory_last, feed_out_grad, cross_w, self_w, small = linked_backward(
            dec_lengths, n1, n1_all, saved1, wq1, wkv1, wo1, dy1, self_gain, cross_w,
            [feed_w, bias, x, memory_later, gain2, gain3], True, group, size, order,
        )
        return arranged(
            me, result, input_grad, memory_first, memory_last, feed_in_grad, feed_out_grad,
            cross_w, self_w, small, shards, group, win,
        )
    else:
        memory_part, gain2, cross_w, dy1 = attend_backward(
            enc_lengths, me, n2, memory_all, saved2, wq2, wkv2, wo2, dy2, cross_gain, y1,
            False, group, size, order,
        )
        input_part, gain1, self_w, diag = attend_backward(
            dec_lengths, me, n1, n1_all, saved1, wq1, wkv1, wo1, dy1, self_gain, bias,
            True, group, size, order,
        )
        memory_grad = lax.psum_scatter(
            memory_part.reshape(seqs, enc_full, width), "head", scatter_dimension=1, tiled=True
        ).astype(F32)
        dn1 = lax.psum_scatter(
            input_part.reshape(seqs, full, width), "head", scatter_dimension=1, tiled=True
        ).astype(F32)
        feed_w, cross_w, self_w = (
            lax.psum_scatter(
                w.reshape(shards * width, w.shape[2]).astype(F32),
                ("head", "batch"),
                scatter_dimension=0,
                tiled=True,
            )
            for w in (feed_w, cross_w, self_w)
        )
        lines = jnp.concatenate([gain1, gain2, gain3], axis=0).reshape(-1, 2 * block)
        diag, lines = lax.psum((diag, lines), ("batch", "head"))
        dx, _ = norm_grads(x32, sg, dn1.reshape(rows, width))
        input_grad = dy1 + dx
        feed_in_grad = jnp.stack([feed_w[:, :part], feed_w[:, part : 2 * part]])
        feed_out_grad = feed_w[:, 2 * part :]
    gains = lines[: 3 * gain_rows].reshape(3, width)
    diag = lax.dynamic_slice_in_dim(diag, me[0] * group, group, 0)
    table_grad = jnp.einsum("tb,ht->bh", onehot, diag, precision=highest)

    def split(w):
        kv = jnp.stack([w[:, :win], w[:, win : 2 * win]])
        return w[:, 2 * win : 3 * win], kv, w[:, 3 * win :].T

    self_q, self_kv, self_o = split(self_w)
    cross_q, cross_kv, cross_o = split(cross_w)
    return (
        result.reshape(seqs, block, width),
        input_grad.reshape(seqs, block, width),
        memory_grad,
        gains[0],
        self_q,
        self_kv,
        self_o,
        table_grad,
        gains[1],
        cross_q,
        cross_kv,
        cross_o,
        gains[2],
        feed_in_grad,
        feed_out_grad.T,
    )


def solution(mesh):
    return jax.shard_map(
        per_device,
        mesh=mesh,
        in_specs=(
            P("batch", "head", None),
            P("batch", "head", None),
            P("batch"),
            P("batch"),
            P(),
            P(None, "head"),
            P(None, None, "head"),
            P("head", None),
            P(None, "head"),
            P(),
            P(None, "head"),
            P(None, None, "head"),
            P("head", None),
            P(),
            P(),
            P(),
            P("batch", "head", None),
        ),
        out_specs=(
            P("batch", "head", None),
            P("batch", "head", None),
            P("batch", "head", None),
            P(),
            P("batch", "head"),
            P(None, "batch", "head"),
            P("head", "batch"),
            P(None, "head"),
            P(),
            P("batch", "head"),
            P(None, "batch", "head"),
            P("head", "batch"),
            P(),
            P(None, "batch", "head"),
            P("head", "batch"),
        ),
        check_vma=False,
    )
```

```python
import functools
import math

import jax
import jax.numpy as jnp
from jax import lax
from jax.experimental import pallas as pl
from jax.experimental.pallas import tpu as pltpu
from jax.sharding import PartitionSpec as P

NB = 32
MAX_DIST = 128
NEG = -1e30
VMEM_LIMIT = 60 * 1024 * 1024
F32 = jnp.float32
BF16 = jnp.bfloat16

highest = lax.Precision.HIGHEST


def bucket_edges(num_buckets, max_distance):
    exact_part = num_buckets // 2
    edge_list = []
    for target in range(1, num_buckets - exact_part):
        distance = exact_part
        while (
            math.floor(
                math.log(distance / exact_part)
                / math.log(max_distance / exact_part)
                * (num_buckets - exact_part)
            )
            < target
        ):
            distance += 1
        edge_list.append(distance)
    return edge_list


def bucket_of(distance, num_buckets, max_distance):
    exact_part = num_buckets // 2
    counted = jnp.zeros(distance.shape, jnp.int32)
    for edge_value in bucket_edges(num_buckets, max_distance):
        counted = counted + (distance >= edge_value).astype(jnp.int32)
    return jnp.where(distance < exact_part, distance, exact_part + counted).astype(jnp.int32)


def near_onehot(block):
    distance = block - jnp.arange(2 * block)
    distance = jnp.where(distance < 0, 2 * MAX_DIST, distance)
    return (
        bucket_of(distance, NB, MAX_DIST)[:, None] == jnp.arange(NB)[None, :]
    ).astype(F32)


def nn(a, b):
    return lax.dot_general(a, b, (((1,), (0,)), ((), ())), preferred_element_type=F32)


def nt(a, b):
    return lax.dot_general(a, b, (((1,), (1,)), ((), ())), preferred_element_type=F32)


def tn(a, b):
    return lax.dot_general(a, b, (((0,), (0,)), ((), ())), preferred_element_type=F32)


def rms(v):
    mean = jnp.mean(v * v, axis=-1, keepdims=True) + 1e-06
    r = lax.rsqrt(mean)
    return r * (1.5 - 0.5 * mean * r * r)


def norm_grads(y, gain, e):
    r = rms(y)
    xhat = y * r
    eg = e * gain
    dy = r * (eg - xhat * jnp.mean(eg * xhat, axis=-1, keepdims=True))
    return dy, jnp.sum(e * xhat, axis=0, keepdims=True)


def row(ref):
    return ref[...].astype(F32).reshape(1, -1)


def padded(v, width):
    extra = width - v.shape[1]
    if extra == 0:
        return v
    return jnp.concatenate([v, jnp.zeros((v.shape[0], extra), v.dtype)], axis=1)


def put_rows(ref, value, order):
    step = value.shape[0] // len(order)
    for source, slot in enumerate(order):
        ref[slot * step : (slot + 1) * step, :] = value[source * step : (source + 1) * step, :]


def vmem():
    return pl.BlockSpec(memory_space=pltpu.VMEM)


def smem():
    return pl.BlockSpec(memory_space=pltpu.SMEM)


def params():
    return pltpu.CompilerParams(vmem_limit_bytes=VMEM_LIMIT)


def sds(shape, dtype):
    return jax.ShapeDtypeStruct(shape, dtype)


def bucket_rows(block, count):
    distance = block - lax.broadcasted_iota(jnp.int32, (1, 2 * block), 1)
    distance = jnp.where(distance < 0, 2 * MAX_DIST, distance)
    bucket = bucket_of(distance, NB, MAX_DIST)
    return bucket == lax.broadcasted_iota(jnp.int32, (count, 2 * block), 0)


def build_bias(me, table_ref, b_ref, ext_ref, line_ref):
    heads, block, full = b_ref.shape
    shards = table_ref.shape[0]
    group = heads // shards
    start = pl.multiple_of(me * block, block)
    width = 2 * block
    row_i = lax.broadcasted_iota(jnp.int32, (block, width), 0)
    col_i = lax.broadcasted_iota(jnp.int32, (block, width), 1)
    masked = (col_i - row_i) > block
    far = lax.broadcasted_iota(jnp.int32, ext_ref.shape, 1) < start
    onehot = bucket_rows(block, table_ref.shape[2]).astype(BF16)

    def body(h, carry):
        line_ref[...] = nn(table_ref[h], onehot)
        for a in range(group):
            row = line_ref[a : a + 1, :]
            tile = pltpu.roll(
                jnp.broadcast_to(row, (block, width)), 0, 1, stride=1, stride_axis=0
            )
            ext_ref[...] = jnp.where(far, row[:, width - 1 : width], NEG)
            ext_ref[:, pl.ds(start, width)] = jnp.where(masked, NEG, tile)
            b_ref[h * group + a] = ext_ref[:, block:].astype(BF16)
        return carry

    lax.fori_loop(0, shards, body, 0)


def bias_kernel(me_ref, *refs):
    build_bias(me_ref[0], *refs)


def bias_tiles(me, tables, group, block, full):
    shards, lanes = tables.shape[:2]
    return pl.pallas_call(
        bias_kernel,
        out_shape=sds((shards * group, block, full), BF16),
        in_specs=[smem(), vmem()],
        out_specs=vmem(),
        scratch_shapes=[
            pltpu.VMEM((block, full + block), F32),
            pltpu.VMEM((lanes, 2 * block), F32),
        ],
        compiler_params=params(),
        name="bias_tiles",
    )(me, tables)


def lane_groups(width, group, size):
    lane = lax.broadcasted_iota(jnp.int32, (1, width), 1)
    return [(lane // size) == a for a in range(group)]


def stack_heads(win, lanes):
    return jnp.concatenate([jnp.where(m, win, jnp.zeros_like(win)) for m in lanes], axis=0)


def join_heads(tall, lanes, rows):
    total = jnp.where(lanes[0], tall[:rows], 0.0)
    for a in range(1, len(lanes)):
        total = total + jnp.where(lanes[a], tall[a * rows : (a + 1) * rows], 0.0)
    return total


def head_context(qw, kw, vw, bias, keep, lanes):
    block, group = qw.shape[0], len(lanes)
    sc = nt(stack_heads(qw, lanes), kw)
    if bias is not None:
        sc = sc + bias
    sc = jnp.where(keep, sc, NEG)
    top = jnp.max(sc, axis=-1, keepdims=True)
    e = jnp.exp(sc - top)
    total = jnp.sum(e, axis=-1, keepdims=True)
    p = (e * (1.0 / total)).astype(BF16)
    c = join_heads(nn(p, vw), lanes, block).astype(BF16)
    lse = top + jnp.log(total)
    lane = lax.broadcasted_iota(jnp.int32, (block, 128), 1)
    tile = jnp.zeros((block, 128), F32)
    for a in range(group):
        tile = jnp.where(lane == a, lse[a * block : (a + 1) * block], tile)
    return c, tile


def forward_kernel(
    biased, group, size, len_ref, nq_ref, nk_ref, res_ref, wq_ref, wkv_ref, wo_ref, gain_ref, *rest
):
    if biased:
        b_ref, *rest = rest
    q_ref, k_ref, v_ref, c_ref, lse_ref, y_ref, n_ref = rest
    shards, rows, pw = q_ref.shape
    seqs = len_ref.shape[0]
    block = rows // seqs
    full = k_ref.shape[1] // seqs
    win = group * size
    lanes = lane_groups(pw, group, size)
    key = lax.broadcasted_iota(jnp.int32, (1, full), 1)

    def body(h, carry):
        q_ref[h] = padded(nt(nq_ref[...], wq_ref[h]).astype(BF16), pw)
        k_ref[h] = padded(nt(nk_ref[...], wkv_ref[h, 0]).astype(BF16), pw)
        v_ref[h] = padded(nt(nk_ref[...], wkv_ref[h, 1]).astype(BF16), pw)
        for s in range(seqs):
            bias = None
            if biased:
                bias = b_ref[pl.ds(h * group, group)].reshape(group * block, full).astype(F32)
            c, lse_ref[h, s] = head_context(
                q_ref[h, s * block : (s + 1) * block, :],
                k_ref[h, s * full : (s + 1) * full, :],
                v_ref[h, s * full : (s + 1) * full, :],
                bias,
                key < len_ref[s],
                lanes,
            )
            c_ref[h, s * block : (s + 1) * block, :] = c
        return carry

    lax.fori_loop(0, shards, body, 0)
    joined = jnp.concatenate([c_ref[h][:, :win] for h in range(shards)], axis=1)
    y = res_ref[...].astype(F32) + nn(joined, wo_ref[...])
    y_ref[...] = y
    n_ref[...] = (y * rms(y) * row(gain_ref)).astype(BF16)


def attend_forward(lens, nq, nk, res, wq, wkv, wo, gain, bias, group, size):
    rows, width = nq.shape
    shards = wq.shape[0]
    pw = -(-group * size // 128) * 128
    seqs = lens.shape[0]
    args = [lens, nq, nk, res, wq, wkv, wo, gain] + ([bias] if bias is not None else [])
    keys = nk.shape[0]
    flops = 2 * (rows + 2 * keys + rows) * width * width + 4 * rows * keys * width
    return pl.pallas_call(
        functools.partial(forward_kernel, bias is not None, group, size),
        out_shape=[
            sds((shards, rows, pw), BF16),
            sds((shards, keys, pw), BF16),
            sds((shards, keys, pw), BF16),
            sds((shards, rows, pw), BF16),
            sds((shards, seqs, rows // seqs, 128), F32),
            sds((rows, width), F32),
            sds((rows, width), BF16),
        ],
        in_specs=[smem()] + [vmem()] * (len(args) - 1),
        out_specs=[vmem()] * 7,
        compiler_params=params(),
        cost_estimate=pl.CostEstimate(
            flops=flops, bytes_accessed=16 << 20, transcendentals=rows * keys * 6
        ),
        name="attend_forward",
    )(*args)


def backward_kernel(
    biased,
    group,
    size,
    order,
    len_ref,
    me_ref,
    nq_ref,
    nk_ref,
    q_ref,
    k_ref,
    v_ref,
    c_ref,
    lse_ref,
    wq_ref,
    wkv_ref,
    wo_ref,
    dy_ref,
    gain_ref,
    *rest,
):
    if biased:
        b_ref, part_ref, gg_ref, w_ref, diag_ref, dc_ref, dq_ref, dkv_ref, acc_ref, nqt_ref, nkt_ref, dat_ref, sum_ref, ext_ref = rest
    else:
        y_ref, part_ref, gg_ref, w_ref, dprev_ref, dc_ref, dq_ref, dkv_ref, acc_ref, nqt_ref, nkt_ref, dat_ref = rest
    shards, rows, pw = q_ref.shape
    seqs = len_ref.shape[0]
    block = rows // seqs
    full = k_ref.shape[1] // seqs
    win = group * size
    lanes = lane_groups(pw, group, size)
    key = lax.broadcasted_iota(jnp.int32, (1, full), 1)
    me = me_ref[0]

    da = dy_ref[...].astype(BF16)
    put_rows(nqt_ref, nq_ref[...].T, order)
    put_rows(nkt_ref, nk_ref[...].T, order)
    put_rows(dat_ref, da.T, order)
    if biased:
        ext_ref[:, :block] = jnp.zeros((block, block), F32)
        start = pl.multiple_of(me * block, block)
        far = lax.broadcasted_iota(jnp.int32, ext_ref.shape, 1) < start
        row8 = lax.broadcasted_iota(jnp.int32, (8, 2 * block), 0)
        lane_near = lax.broadcasted_iota(jnp.int32, (1, 2 * block), 1)

    def body(h, carry):
        wo_h = wo_ref[pl.ds(pl.multiple_of(h * win, size), win), :]
        dc_ref[...] = padded(nt(da, wo_h).astype(BF16), pw)
        for s in range(seqs):
            kw = k_ref[h, s * full : (s + 1) * full, :]
            vw = v_ref[h, s * full : (s + 1) * full, :]
            qcat = stack_heads(q_ref[h, s * block : (s + 1) * block, :], lanes)
            dcat = stack_heads(dc_ref[s * block : (s + 1) * block, :], lanes)
            sc = nt(qcat, kw)
            if biased:
                sc = sc + b_ref[pl.ds(h * group, group)].reshape(group * block, full).astype(F32)
            sc = jnp.where(key < len_ref[s], sc, NEG)
            lse_tile = lse_ref[h, s]
            lse = jnp.concatenate([lse_tile[:, a : a + 1] for a in range(group)], axis=0)
            p = jnp.exp(sc - lse)
            dp = nt(dcat, vw)
            ds = p * (dp - jnp.sum(p * dp, axis=-1, keepdims=True))
            ds = ds.astype(BF16)
            pb = p.astype(BF16)
            if biased:
                if s == 0:
                    sum_ref[...] = ds.astype(F32)
                else:
                    sum_ref[...] += ds.astype(F32)
            dq = join_heads(nn(ds, kw), lanes, block)
            dq_ref[s * block : (s + 1) * block, :] = dq.astype(BF16)
            dk = tn(ds, qcat).astype(BF16)
            dv = tn(pb, dcat).astype(BF16)
            dkv_ref[s * full : (s + 1) * full, :] = jnp.concatenate(
                [dk[:, :win], dv[:, :win]], axis=1
            )
        if biased:
            for a in range(group):
                ext_ref[:, block:] = sum_ref[a * block : (a + 1) * block, :]
                far_sum = jnp.sum(jnp.where(far, ext_ref[...], 0.0))
                fold = ext_ref[:, pl.ds(start, 2 * block)]
                half = block // 2
                while half >= 8:
                    fold = fold[:half] + pltpu.roll(fold[half:], 2 * block - half, 1)
                    half //= 2
                for bit in (4, 2, 1):
                    fold = jnp.where(
                        (row8 & bit) != 0, pltpu.roll(fold, 2 * block - bit, 1), fold
                    )
                line = jnp.sum(fold, axis=0, keepdims=True)
                line = line + jnp.where(lane_near == 2 * block - 1, far_sum, 0.0)
                diag_ref[pl.ds(h * group + a, 1), :] = line
        dkv = dkv_ref[...]
        dq_h = dq_ref[...][:, :win]
        kv_term = nn(dkv[:, :win], wkv_ref[h, 0]) + nn(dkv[:, win:], wkv_ref[h, 1])
        q_term = nn(dq_h, wq_ref[h])
        w_ref[h] = jnp.concatenate(
            [
                nn(nkt_ref[...], dkv).astype(BF16),
                nn(nqt_ref[...], dq_h).astype(BF16),
                nn(dat_ref[...], c_ref[h][:, :win]).astype(BF16),
            ],
            axis=1,
        )

        @pl.when(h == 0)
        def _():
            acc_ref[: seqs * full, :] = kv_term
            acc_ref[seqs * full :, :] = q_term

        @pl.when(h != 0)
        def _():
            acc_ref[: seqs * full, :] += kv_term
            acc_ref[seqs * full :, :] += q_term

        return carry

    lax.fori_loop(0, shards, body, 0)
    if biased:
        for s in range(seqs):
            own = pl.ds(pl.multiple_of(s * full + me * block, block), block)
            acc_ref[own, :] += acc_ref[seqs * full + s * block : seqs * full + (s + 1) * block, :]
        total = acc_ref[: seqs * full, :]
        part_ref[...] = total.astype(BF16)
        gg_ref[...] = (
            jnp.sum(total * nk_ref[...].astype(F32), axis=0, keepdims=True) / row(gain_ref)
        )
    else:
        part_ref[...] = acc_ref[: seqs * full, :].astype(BF16)
        dy, gg = norm_grads(y_ref[...], row(gain_ref), acc_ref[seqs * full :, :])
        dprev_ref[...] = dy_ref[...] + dy
        gg_ref[...] = gg


def attend_backward(
    lens, me, nq, nk, saved, wq, wkv, wo, dy, gain, extra, biased, group, size, order
):
    q, k, v, c, lse = saved
    rows, width = nq.shape
    shards, keys, pw = k.shape
    block = rows // lens.shape[0]
    full = keys // lens.shape[0]
    win = group * size
    args = [lens, me, nq, nk, q, k, v, c, lse, wq, wkv, wo, dy, gain, extra]
    out_shape = [
        sds((keys, width), BF16),
        sds((1, width), F32),
        sds((shards, width, 4 * win), BF16),
        sds((shards * group, 2 * block), F32) if biased else sds((rows, width), F32),
    ]
    scratch = [
        pltpu.VMEM((rows, pw), BF16),
        pltpu.VMEM((rows, pw), BF16),
        pltpu.VMEM((keys, 2 * win), BF16),
        pltpu.VMEM((keys + rows, width), F32),
        pltpu.VMEM((width, rows), BF16),
        pltpu.VMEM((width, keys), BF16),
        pltpu.VMEM((width, rows), BF16),
    ]
    if biased:
        scratch += [
            pltpu.VMEM((group * block, full), F32),
            pltpu.VMEM((block, full + block), F32),
        ]
    flops = 4 * (rows + 2 * keys + rows) * width * width + 10 * rows * full * width
    return pl.pallas_call(
        functools.partial(backward_kernel, biased, group, size, order),
        out_shape=out_shape,
        in_specs=[smem(), smem()] + [vmem()] * (len(args) - 2),
        out_specs=[vmem()] * 4,
        scratch_shapes=scratch,
        compiler_params=params(),
        cost_estimate=pl.CostEstimate(
            flops=flops, bytes_accessed=24 << 20, transcendentals=rows * full * 12
        ),
        name="attend_backward",
    )(*args)


def feed_tile(n, cot, w_gate, w_up, w_out):
    g = nn(n, w_gate)
    u = nn(n, w_up)
    dh = nt(cot, w_out)
    scale = math.sqrt(2.0 / math.pi)
    square = g * g
    t = jnp.tanh(scale * (g + 0.044715 * square * g))
    half = 0.5 * (1.0 + t)
    gelu = g * half
    hid = (gelu * u).astype(BF16)
    slope = half + 0.5 * g * (1.0 - t * t) * (scale * (1.0 + 3 * 0.044715 * square))
    return hid, (dh * u * slope).astype(BF16), (dh * gelu).astype(BF16)


def feed_kernel(
    order, y_ref, n_ref, cot_ref, win_ref, wout_ref, gain_ref, out_ref, dy_ref, gg_ref, w_ref,
    acc_ref, dn_ref, nt_ref, ct_ref,
):
    step = pl.program_id(0)
    part = wout_ref.shape[0]

    @pl.when(step == 0)
    def _():
        put_rows(nt_ref, n_ref[...].T, order)
        put_rows(ct_ref, cot_ref[...].T, order)
        acc_ref[...] = y_ref[...]
        dn_ref[...] = jnp.zeros_like(dn_ref)

    hid, dg, du = feed_tile(n_ref[...], cot_ref[...], win_ref[0], win_ref[1], wout_ref[...])
    acc_ref[...] += nn(hid, wout_ref[...])
    dn_ref[...] += nt(dg, win_ref[0]) + nt(du, win_ref[1])
    w_ref[0, :, :part] = nn(nt_ref[...], dg).astype(BF16)
    w_ref[0, :, part : 2 * part] = nn(nt_ref[...], du).astype(BF16)
    w_ref[0, :, 2 * part :] = nn(ct_ref[...], hid).astype(BF16)

    @pl.when(step == pl.num_programs(0) - 1)
    def _():
        out_ref[...] = acc_ref[...].astype(BF16)
        dy, gg = norm_grads(y_ref[...], row(gain_ref), dn_ref[...])
        dy_ref[...] = cot_ref[...].astype(F32) + dy
        gg_ref[...] = gg


def feed(y, n, cot, w_in, w_out, gain, shards, order):
    rows, width = y.shape
    hidden = w_out.shape[0]
    part = hidden // shards
    fixed = lambda shape: pl.BlockSpec(shape, lambda j: (0,) * len(shape))
    return pl.pallas_call(
        functools.partial(feed_kernel, order),
        grid=(shards,),
        out_shape=[
            sds((rows, width), BF16),
            sds((rows, width), F32),
            sds((1, width), F32),
            sds((shards, width, 3 * part), BF16),
        ],
        in_specs=[
            fixed((rows, width)),
            fixed((rows, width)),
            fixed((rows, width)),
            pl.BlockSpec((2, width, part), lambda j: (0, 0, j)),
            pl.BlockSpec((part, width), lambda j: (j, 0)),
            fixed((width,)),
        ],
        out_specs=[
            fixed((rows, width)),
            fixed((rows, width)),
            fixed((1, width)),
            pl.BlockSpec((1, width, 3 * part), lambda j: (j, 0, 0)),
        ],
        scratch_shapes=[
            pltpu.VMEM((rows, width), F32),
            pltpu.VMEM((rows, width), F32),
            pltpu.VMEM((width, rows), BF16),
            pltpu.VMEM((width, rows), BF16),
        ],
        compiler_params=params(),
        cost_estimate=pl.CostEstimate(
            flops=18 * rows * width * hidden, bytes_accessed=24 << 20, transcendentals=rows * hidden
        ),
        name="feed",
    )(y, n, cot, w_in, w_out, gain)


MESH = pl.DeviceIdType.MESH


def place():
    b = lax.axis_index("batch")
    me = lax.axis_index("head")
    core = lax.rem(b, 2)
    x = lax.rem(lax.div(b, 2), 2)
    y = lax.div(b, 4)
    return b, me, core, x, y


def greet(devices):
    barrier = pltpu.get_barrier_semaphore()
    for device in devices:
        pl.semaphore_signal(barrier, inc=1, device_id=device, device_id_type=MESH)
    pl.semaphore_wait(barrier, len(devices))


def remote(src, dst, send, recv, device):
    return pltpu.make_async_remote_copy(
        src_ref=src,
        dst_ref=dst,
        send_sem=send,
        recv_sem=recv,
        device_id=device,
        device_id_type=MESH,
    )


def flipped(bit, by):
    return bit + by - 2 * bit * by


AHEAD = 2


class Links:
    def __init__(self):
        b, me, core, x, y = place()
        self.me, self.core, self.x, self.y = me, core, x, y
        self.high, self.low = lax.div(me, 2), lax.rem(me, 2)
        self.pair, self.far, self.cross = self.owner(1), self.owner(2), self.owner(0)
        self.over_core = (b + 1 - 2 * core, me)
        self.over_x = (b + 2 - 4 * x, me)
        self.over_y = (b + 4 - 8 * y, me)
        self.over_plane = (b + 2 - 4 * x + 4 - 8 * y, me)
        self.to_pair, self.to_far, self.to_cross = (b, self.pair), (b, self.far), (b, self.cross)

    def owner(self, k):
        by_low, by_high = 1 - k // 2, 1 - k % 2
        return 2 * flipped(self.high, by_high) + flipped(self.low, by_low)

    def greet(self):
        greet(
            [self.over_core, self.over_x, self.over_y, self.over_plane]
            + [self.to_pair, self.to_far, self.to_cross]
        )


class Sums:
    @staticmethod
    def scratch(chunks, rows, cols):
        items, half = chunks // 4, cols // 2
        dma = pltpu.SemaphoreType.DMA
        return [
            pltpu.VMEM((chunks, 2, 2, rows, cols), BF16),
            pltpu.VMEM((chunks, 2, 2, rows, cols), BF16),
            pltpu.VMEM((chunks, 2, rows, half), BF16),
            pltpu.VMEM((chunks, 2, rows, half), BF16),
            pltpu.VMEM((chunks, rows, half), BF16),
            pltpu.VMEM((chunks, rows, half), BF16),
            pltpu.VMEM((chunks, rows, cols), BF16),
            pltpu.VMEM((items, 3, rows, cols), BF16),
            dma((chunks,)),
            dma((chunks,)),
            dma((chunks,)),
            dma((chunks, 2)),
            dma((chunks, 2)),
            dma((chunks, 2)),
            dma((chunks, 2)),
            dma((items, 3)),
            dma((items, 3)),
        ]

    count = 17

    def __init__(self, links, refs):
        (self.own, self.rc, self.r1a, self.r1b, self.r2a, self.r2b, self.tot, self.rz) = refs[:8]
        (self.ls, self.cs, self.cr, self.s1, self.q1, self.s2, self.q2, self.zs, self.zr) = refs[8:]
        self.links = links
        self.chunks, self.cols = self.own.shape[0], self.own.shape[-1]
        self.half = self.cols // 2

    def piece(self, w_ref, c, side, left):
        start = pl.multiple_of((c // 4) * self.cols + left, 128)
        return w_ref.at[self.links.owner(c % 4), side, :, :, :, pl.ds(start, self.cols)]

    def local(self, w_ref, c, left):
        return pltpu.make_async_copy(
            self.piece(w_ref, c, self.links.core, left), self.own.at[c], self.ls.at[c]
        )

    def over_core(self, c, source):
        return remote(
            source, self.rc.at[c], self.cs.at[c], self.cr.at[c], self.links.over_core
        )

    def load(self, w_ref, c, left=0):
        self.local(w_ref, c, left).start()
        self.over_core(c, self.piece(w_ref, c, 1 - self.links.core, left)).start()

    def firsts(self, c):
        links, half = self.links, self.half
        return (
            remote(
                self.own.at[c, :, 1 - links.x, :, pl.ds(0, half)],
                self.r1a.at[c],
                self.s1.at[c, 0],
                self.q1.at[c, 0],
                links.over_x,
            ),
            remote(
                self.own.at[c, 1 - links.y, :, :, pl.ds(half, half)],
                self.r1b.at[c],
                self.s1.at[c, 1],
                self.q1.at[c, 1],
                links.over_y,
            ),
        )

    def seconds(self, c):
        links = self.links
        return (
            remote(
                self.r1a.at[c, 1 - links.y],
                self.r2a.at[c],
                self.s2.at[c, 0],
                self.q2.at[c, 0],
                links.over_y,
            ),
            remote(
                self.r1b.at[c, 1 - links.x],
                self.r2b.at[c],
                self.s2.at[c, 1],
                self.q2.at[c, 1],
                links.over_x,
            ),
        )

    def along(self, item, slot, c):
        device = self.links.to_far if slot == 2 else self.links.to_pair
        return remote(
            self.tot.at[c],
            self.rz.at[item, slot],
            self.zs.at[item, slot],
            self.zr.at[item, slot],
            device,
        )

    def core(self, c, w_ref=None, left=0):
        if w_ref is not None:
            self.local(w_ref, c, left).wait()
        self.over_core(c, self.rc.at[c]).wait_recv()
        x, y, half = 1 - self.links.x, 1 - self.links.y, self.half
        self.own[c, :, x, :, :half] = self.own[c, :, x, :, :half] + self.rc[c, :, x, :, :half]
        self.own[c, y, :, :, half:] = self.own[c, y, :, :, half:] + self.rc[c, y, :, :, half:]
        for copy in self.firsts(c):
            copy.start()

    def left(self, c, y):
        x, half = self.links.x, self.half
        total = self.own[c, y, x, :, :half].astype(F32) + self.rc[c, y, x, :, :half].astype(F32)
        return total + self.r1a[c, y].astype(F32)

    def right(self, c, x):
        y, half = self.links.y, self.half
        total = self.own[c, y, x, :, half:].astype(F32) + self.rc[c, y, x, :, half:].astype(F32)
        return total + self.r1b[c, x].astype(F32)

    def first(self, c):
        for copy in self.firsts(c):
            copy.wait_recv()
        x, y = 1 - self.links.x, 1 - self.links.y
        self.r1a[c, y] = self.left(c, y).astype(BF16)
        self.r1b[c, x] = self.right(c, x).astype(BF16)
        for copy in self.seconds(c):
            copy.start()

    def whole(self, c):
        left = self.left(c, self.links.y) + self.r2a[c].astype(F32)
        right = self.right(c, self.links.x) + self.r2b[c].astype(F32)
        return jnp.concatenate([left, right], axis=1)

    def second(self, c):
        for copy in self.seconds(c):
            copy.wait_recv()
        item, k = c // 4, c % 4
        for slot in range(2):

            @pl.when(k == slot)
            def _(slot=slot):
                self.tot[c] = self.whole(c).astype(BF16)
                self.along(item, slot, c).start()

    def third(self, c):
        item, k = c // 4, c % 4

        @pl.when(k == 2)
        def _():
            self.along(item, 0, c).wait_recv()
            self.tot[c] = (self.whole(c) + self.rz[item, 0].astype(F32)).astype(BF16)
            self.along(item, 2, c).start()

    def finish(self, item):
        c = 4 * item
        for slot in (1, 2):
            self.along(item, slot, c).wait_recv()
        return self.whole(c + 3) + self.rz[item, 1].astype(F32) + self.rz[item, 2].astype(F32)

    def drain(self):
        def body(c, carry):
            self.over_core(c, self.rc.at[c]).wait_send()
            for copy in self.firsts(c) + self.seconds(c):
                copy.wait_send()
            return carry

        lax.fori_loop(0, self.chunks, body, 0)
        for item in range(self.chunks // 4):
            for slot in range(3):
                self.along(item, slot, 4 * item).wait_send()


class Weights:
    @staticmethod
    def scratch(n):
        dma = pltpu.SemaphoreType.DMA
        return [dma((n, 3)), dma((n, 3)), dma((n, 3, 3)), dma((n, 3, 3)), dma((n, 3)), dma((n, 3))]

    def __init__(self, links, shards, fulls, sems):
        self.links, self.shards, self.fulls = links, shards, fulls
        self.zs, self.zr, self.ps, self.pr, self.cs, self.cr = sems
        self.n = len(shards)
        self.planes = (links.pair, links.far, links.cross)
        self.slot = links.core * 4 + links.y * 2 + links.x

    def window(self, ref, first, count):
        step = ref.shape[-2] // 8
        return ref.at[:, pl.ds(pl.multiple_of(first * step, step), count * step), :]

    def along(self, i, slot):
        links = self.links
        source = self.planes[1] if slot == 2 else links.me
        into = self.window(self.fulls[i].at[source], self.slot, 1)
        mine = into if slot == 2 else self.window(self.shards[i], self.slot, 1)
        device = links.to_far if slot == 1 else links.to_pair
        return remote(mine, into, self.zs.at[i, slot], self.zr.at[i, slot], device)

    def across(self, i, j, d):
        links = self.links
        piece = self.window(self.fulls[i].at[self.planes[j]], self.slot, 1)
        device = (links.over_x, links.over_y, links.over_plane)[d]
        return remote(piece, piece, self.ps.at[i, j, d], self.pr.at[i, j, d], device)

    def core(self, i, j):
        half = self.window(self.fulls[i].at[self.planes[j]], self.links.core * 4, 4)
        return remote(half, half, self.cs.at[i, j], self.cr.at[i, j], self.links.over_core)

    def start(self):
        for i in range(self.n):
            for slot in (0, 1):
                self.along(i, slot).start()

    def arrive(self, j):
        for i in range(self.n):
            self.along(i, j).wait_recv()
            if j == 1:
                self.along(i, 2).start()
            for d in range(3):
                self.across(i, j, d).start()

    def share(self, j):
        for i in range(self.n):
            for d in range(3):
                self.across(i, j, d).wait_recv()
            self.core(i, j).start()

    def finish(self, j):
        for i in range(self.n):
            self.core(i, j).wait_recv()

    def drain(self):
        for i in range(self.n):
            for j in range(3):
                self.along(i, j).wait_send()
                self.core(i, j).wait_send()
                for d in range(3):
                    self.across(i, j, d).wait_send()


class Gathered:
    def __init__(self, links, source, into, sems):
        self.links, self.source, self.into = links, source, into
        self.ss, self.rs = sems
        self.seqs, self.block = into.shape[0], into.shape[1] // 4

    def window(self, s, plane):
        rows = pl.ds(pl.multiple_of(plane * self.block, self.block), self.block)
        return self.into.at[s, rows, :]

    def copy(self, s, slot):
        links = self.links
        into = self.window(s, links.far if slot == 2 else links.me)
        mine = into if slot == 2 else self.source(s)
        device = links.to_far if slot == 1 else links.to_pair
        return remote(mine, into, self.ss.at[s, slot], self.rs.at[s, slot], device)

    def start(self):
        for s in range(self.seqs):
            for slot in (1, 0):
                self.copy(s, slot).start()

    def forward(self):
        for s in range(self.seqs):
            self.copy(s, 1).wait_recv()
            self.copy(s, 2).start()

    def take(self, slot):
        for s in range(self.seqs):
            self.copy(s, slot).wait_recv()

    def finish(self):
        for slot in (0, 2):
            self.take(slot)

    def drain(self):
        for s in range(self.seqs):
            for slot in range(3):
                self.copy(s, slot).wait_send()


def front_kernel(group, size, *refs):
    len_ref, enc_ref, x_ref, self_gain_ref, cross_gain_ref, feed_gain_ref, table_ref, *refs = refs
    memory_ref, own_weights, refs = refs[0], refs[1:7], refs[7:]
    n_ref, y_ref, n2_ref, y2_ref, n3_ref, memory_out, *refs = refs
    self_out, cross_out, refs = refs[:3], refs[3:6], refs[6:]
    outs, kept, refs = refs[:12], refs[12:24], refs[24:]
    nall_ref, bias_ref, q_ref, k_ref, v_ref, c_ref, lse_ref = kept[:7]
    q2_ref, k2_ref, v2_ref, c2_ref, lse2_ref = kept[7:]
    self_full, cross_full, refs = refs[:3], refs[3:6], refs[6:]
    tables_ref, ext_ref, line_ref, mem_ref, *refs = refs
    (table_s, table_r, rows_s, rows_r, memory_s, memory_r, local, placed, held, done, *refs) = refs
    links = Links()
    me = links.me
    w1 = Weights(links, own_weights[:3], self_out, refs[:6])
    w2 = Weights(links, own_weights[3:], cross_out, refs[6:])
    shards, rows, pw = q_ref.shape
    seqs = len_ref.shape[0]
    block = rows // seqs
    full = block * shards
    win = group * size
    lanes = lane_groups(pw, group, size)
    key = lax.broadcasted_iota(jnp.int32, (1, full), 1)
    start = pl.multiple_of(me * block, block)
    rows_one = Gathered(
        links, lambda s: nall_ref.at[s, pl.ds(start, block), :], nall_ref, (rows_s, rows_r)
    )
    rows_memory = Gathered(
        links, lambda s: mem_ref.at[s, pl.ds(start, block), :], memory_out, (memory_s, memory_r)
    )

    line_ref[...] = jnp.zeros_like(line_ref)
    line_ref[:group, :NB] = table_ref[...].astype(F32)
    tables_ref[me] = line_ref[:, : tables_ref.shape[2]].astype(BF16)
    links.greet()
    w1.start()
    heard = [
        remote(tables_ref.at[me], tables_ref.at[me], table_s.at[i], table_r.at[i], to)
        for i, to in enumerate((links.to_pair, links.to_far, links.to_cross))
    ]
    for copy in heard:
        copy.start()
    taken = [
        pltpu.make_async_copy(own_weights[i], self_full[i].at[me], local.at[i]) for i in range(3)
    ]
    taken += [
        pltpu.make_async_copy(own_weights[3 + i], cross_full[i].at[me], local.at[3 + i])
        for i in range(3)
    ]
    taken.append(
        pltpu.make_async_copy(memory_ref, mem_ref.at[:, pl.ds(start, block), :], local.at[6])
    )
    for copy in taken:
        copy.start()
    x = x_ref[...].astype(F32)
    n_ref[...] = (x * rms(x) * row(self_gain_ref)).astype(BF16)
    for s in range(seqs):
        nall_ref[s, pl.ds(start, block), :] = n_ref[s * block : (s + 1) * block, :]
    w1.arrive(0)
    w1.arrive(1)
    rows_one.start()
    w1.arrive(2)
    for copy in heard:
        copy.wait_recv()
    build_bias(me, tables_ref, bias_ref, ext_ref, line_ref)
    for copy in taken:
        copy.wait()
    put = [
        pltpu.make_async_copy(cross_full[i].at[me], cross_out[i].at[me], placed.at[i])
        for i in range(3)
    ]
    put += [
        pltpu.make_async_copy(self_full[i].at[me], self_out[i].at[me], placed.at[3 + i])
        for i in range(3)
    ]
    put += [
        pltpu.make_async_copy(
            rows_memory.source(s), rows_memory.window(s, me), placed.at[6 + s]
        )
        for s in range(seqs)
    ]
    for copy in put:
        copy.start()
    rows_one.forward()
    for j in range(3):
        w1.share(j)
    def hold(i, j):
        plane = w1.planes[j]
        into, source = (self_full[i], self_out[i]) if i < 3 else (cross_full[i - 3], cross_out[i - 3])
        return pltpu.make_async_copy(source.at[plane], into.at[plane], held.at[i, j])

    for j in range(3):
        w1.finish(j)
        for i in range(3):
            hold(i, j).start()
    rows_one.finish()
    w2.start()

    def keep(i, h=None):
        if h is None:
            return pltpu.make_async_copy(kept[i], outs[i], done.at[i, 0])
        return pltpu.make_async_copy(kept[i].at[h], outs[i].at[h], done.at[i, h])

    for i in range(2):
        keep(i).start()
    for j in range(3):
        for i in range(3):
            hold(i, j).wait()

    def body(k, carry):
        h = links.owner(lax.rem(k + 3, shards))
        nk = nall_ref[...].reshape(seqs * full, -1)
        q_ref[h] = padded(nt(n_ref[...], self_full[0][h, 0]).astype(BF16), pw)
        k_ref[h] = padded(nt(nk, self_full[1][h, 0]).astype(BF16), pw)
        v_ref[h] = padded(nt(nk, self_full[1][h, 1]).astype(BF16), pw)
        for s in range(seqs):
            c, lse_ref[h, s] = head_context(
                q_ref[h, s * block : (s + 1) * block, :],
                k_ref[h, s * full : (s + 1) * full, :],
                v_ref[h, s * full : (s + 1) * full, :],
                bias_ref[pl.ds(h * group, group)].reshape(group * block, full).astype(F32),
                key < len_ref[s],
                lanes,
            )
            c_ref[h, s * block : (s + 1) * block, :] = c
        for i in range(2, 7):
            keep(i, h).start()

        @pl.when(k == 0)
        def _():
            w2.arrive(0)
            w2.arrive(1)
            rows_memory.start()

        @pl.when(k == 1)
        def _():
            w2.arrive(2)

        return carry

    lax.fori_loop(0, shards, body, 0)
    joined = jnp.concatenate([c_ref[h][:, :win] for h in range(shards)], axis=1)
    out_weight = self_full[2][...].reshape(shards * win, -1)
    y = x_ref[...].astype(F32) + nn(joined, out_weight)
    y_ref[...] = y
    n2_ref[...] = (y * rms(y) * row(cross_gain_ref)).astype(BF16)
    for j in range(3):
        w2.share(j)
    rows_memory.forward()
    for j in range(3):
        w2.finish(j)
        for i in range(3, 6):
            hold(i, j).start()
    for j in range(3):
        for i in range(3, 6):
            hold(i, j).wait()

    def ask(h, carry):
        q2_ref[h] = padded(nt(n2_ref[...], cross_full[0][h, 0]).astype(BF16), pw)
        return carry

    lax.fori_loop(0, shards, ask, 0)

    def bring(plane, j):
        rows = pl.ds(pl.multiple_of(plane * block, block), block)
        return pltpu.make_async_copy(
            memory_out.at[:, rows, :], mem_ref.at[:, rows, :], local.at[j]
        )

    for j, (plane, slot) in enumerate(((me, None), (links.far, 1), (links.pair, 0), (links.cross, 2))):
        if slot is not None:
            if slot != 1:
                rows_memory.take(slot)
            bring(plane, j).start()
            bring(plane, j).wait()
        first = pl.multiple_of(plane * block, block)
        m = mem_ref[:, pl.ds(first, block), :].reshape(rows, -1)

        def answer(h, carry, first=first, m=m):
            for into, which in ((k2_ref, 0), (v2_ref, 1)):
                value = padded(nt(m, cross_full[1][h, which]).astype(BF16), pw)
                for s in range(seqs):
                    into[h, pl.ds(s * full + first, block), :] = value[s * block : (s + 1) * block]
            return carry

        lax.fori_loop(0, shards, answer, 0)

    def cross_body(h, carry):
        for s in range(seqs):
            c, lse2_ref[h, s] = head_context(
                q2_ref[h, s * block : (s + 1) * block, :],
                k2_ref[h, s * full : (s + 1) * full, :],
                v2_ref[h, s * full : (s + 1) * full, :],
                None,
                key < enc_ref[s],
                lanes,
            )
            c2_ref[h, s * block : (s + 1) * block, :] = c
        for i in range(7, 12):
            keep(i, h).start()
        return carry

    lax.fori_loop(0, shards, cross_body, 0)
    joined = jnp.concatenate([c2_ref[h][:, :win] for h in range(shards)], axis=1)
    out_weight = cross_full[2][...].reshape(shards * win, -1)
    y2 = y_ref[...] + nn(joined, out_weight)
    y2_ref[...] = y2
    n3_ref[...] = (y2 * rms(y2) * row(feed_gain_ref)).astype(BF16)
    w1.drain()
    w2.drain()
    rows_one.drain()
    rows_memory.drain()
    for copy in heard:
        copy.wait_send()
    for copy in put:
        copy.wait()
    for i in range(2):
        keep(i).wait()
    for h in range(shards):
        for i in range(2, 12):
            keep(i, h).wait()


def front(lens, encs, x, gains, table, memory, weights, shards, group, size):
    rows, width = x.shape
    seqs = lens.shape[0]
    block = rows // seqs
    full, keys = block * shards, rows * shards
    win = group * size
    pw = -(-win // 128) * 128
    fulls = [((shards, *w.shape), BF16) for w in weights]
    kept = [((seqs, full, width), BF16), ((shards * group, block, full), BF16)]
    kept += [((shards, n, pw), BF16) for n in (rows, keys, keys, rows)]
    kept.append(((shards, seqs, block, 128), F32))
    kept += kept[2:]
    dma = pltpu.SemaphoreType.DMA
    anywhere = pl.BlockSpec(memory_space=pl.ANY)
    return pl.pallas_call(
        functools.partial(front_kernel, group, size),
        out_shape=[
            sds((rows, width), BF16),
            sds((rows, width), F32),
            sds((rows, width), BF16),
            sds((rows, width), F32),
            sds((rows, width), BF16),
            sds((seqs, full, width), BF16),
        ]
        + [sds(*a) for a in fulls + kept],
        in_specs=[smem()] * 2 + [vmem()] * 5 + [anywhere] * 7,
        out_specs=[vmem()] * 5 + [anywhere] * 19,
        scratch_shapes=[pltpu.VMEM(*a) for a in kept + fulls]
        + [
            pltpu.VMEM((shards, 8, 128), BF16),
            pltpu.VMEM((block, full + block), F32),
            pltpu.VMEM((8, 2 * block), F32),
            pltpu.VMEM((seqs, full, width), BF16),
            dma((3,)),
            dma((3,)),
            dma((seqs, 3)),
            dma((seqs, 3)),
            dma((seqs, 3)),
            dma((seqs, 3)),
            dma((7,)),
            dma((6 + seqs,)),
            dma((6, 3)),
            dma((len(kept), shards)),
        ]
        + Weights.scratch(3)
        + Weights.scratch(3),
        compiler_params=pltpu.CompilerParams(
            collective_id=0, has_side_effects=True, vmem_limit_bytes=VMEM_LIMIT
        ),
        name="front",
    )(lens, encs, x, *gains, table, memory, *weights)


class Rows:
    @staticmethod
    def scratch(rows, width):
        dma = pltpu.SemaphoreType.DMA
        return [
            pltpu.VMEM((4, rows, width), BF16),
            pltpu.VMEM((3, rows, width), BF16),
            dma((3,)),
            dma((3,)),
        ]

    count = 4

    def __init__(self, links, refs):
        self.links = links
        self.buf, self.rx, self.ss, self.rs = refs

    def copy(self, slot):
        links = self.links
        block = (links.cross, links.far, links.pair)[slot]
        device = (links.to_cross, links.to_far, links.to_pair)[slot]
        return remote(
            self.buf.at[block], self.rx.at[slot], self.ss.at[slot], self.rs.at[slot], device
        )

    def start(self):
        for slot in range(3):
            self.copy(slot).start()

    def finish(self):
        for slot in range(3):
            self.copy(slot).wait_recv()
        return sum(self.rx[slot].astype(F32) for slot in range(3))

    def drain(self):
        for slot in range(3):
            self.copy(slot).wait_send()


def head_grads(qw, kw, vw, dcw, lse_tile, bias, keep, lanes):
    block, group = qw.shape[0], len(lanes)
    qcat, dcat = stack_heads(qw, lanes), stack_heads(dcw, lanes)
    sc = nt(qcat, kw)
    if bias is not None:
        sc = sc + bias
    sc = jnp.where(keep, sc, NEG)
    lse = jnp.concatenate([lse_tile[:, a : a + 1] for a in range(group)], axis=0)
    p = jnp.exp(sc - lse)
    dp = nt(dcat, vw)
    ds = (p * (dp - jnp.sum(p * dp, axis=-1, keepdims=True))).astype(BF16)
    dq = join_heads(nn(ds, kw), lanes, block).astype(BF16)
    dk = tn(ds, qcat).astype(BF16)
    dv = tn(p.astype(BF16), dcat).astype(BF16)
    return ds, dq, dk, dv


def diagonal_line(near, far_sum):
    block, width = near.shape
    half = block // 2
    while half >= 8:
        near = near[:half] + pltpu.roll(near[half:], width - half, 1)
        half //= 2
    row8 = lax.broadcasted_iota(jnp.int32, (8, width), 0)
    for bit in (4, 2, 1):
        near = jnp.where((row8 & bit) != 0, pltpu.roll(near, width - bit, 1), near)
    line = jnp.sum(near, axis=0, keepdims=True)
    lane = lax.broadcasted_iota(jnp.int32, (1, width), 1)
    return line + jnp.where(lane == width - 1, far_sum, 0.0)


def linked_kernel(biased, group, size, order, *refs):
    len_ref, dy_ref, gain_ref, given_ref, *refs = refs
    held_count = 11 if biased else 10
    held, refs = refs[:held_count], refs[held_count:]
    if biased:
        feed_ref, x_ref, rows_ref, gain2_ref, gain3_ref, *refs = refs
        grad_ref, mem_ref, feed_out, given_out, own_out, small_out, *refs = refs
    else:
        feed_out_ref, y_ref, y2_ref, n3_ref, feed_gain_ref, *refs = refs
        dprev_ref, gg_ref, w_ref, later_ref, mem_ref, given_out, *refs = refs
        result_ref, gg3_ref, hid_out, *refs = refs
    buffers, held_sem, refs = refs[:held_count], refs[held_count], refs[held_count + 1 :]
    nq_ref, nk_ref, c_ref, wo_ref, q_ref, k_ref, v_ref, lse_ref, wq_ref, wkv_ref = buffers[:10]
    bias_ref = buffers[-1]
    dq_ref, dkv_ref, acck_ref, accq_ref, nqt_ref, nkt_ref, dat_ref, wtmp_ref, *refs = refs
    links = Links()
    sums = Sums(links, refs[: Sums.count])
    refs = refs[Sums.count :]
    if biased:
        feed_sums = Sums(links, refs[: Sums.count])
        refs = refs[Sums.count :]
    exchanges = []
    for _ in range(3 if biased else 1):
        exchanges.append(Rows(links, refs[: Rows.count]))
        refs = refs[Rows.count :]
    if biased:
        ds_ref, ext_ref, diag_ref, sr, ms, mr = refs
    else:
        cot_ref, feed_in_ref = dy_ref, given_ref
        w_sem, dy_ref, dn_ref, n3t_ref, ct_ref, wff_ref, hid_ref, win_ref, wout_ref, *refs = refs
        f_sem, hid_sem = refs
    shards, rows, pw = q_ref.shape
    seqs = len_ref.shape[0]
    block = rows // seqs
    full = k_ref.shape[1] // seqs
    win = group * size
    lanes = lane_groups(pw, group, size)
    key = lax.broadcasted_iota(jnp.int32, (1, full), 1)
    me = links.me
    start = pl.multiple_of(me * block, block)
    def fetch(j, h=None):
        if h is None:
            return pltpu.make_async_copy(held[j], buffers[j], held_sem.at[j, 0])
        part = pl.ds(h * group, group) if j == 10 else h
        return pltpu.make_async_copy(held[j].at[part], buffers[j].at[part], held_sem.at[j, h])

    links.greet()
    if biased:
        exchanges[0].buf[...] = rows_ref[...]
        exchanges[0].start()
        for place in range(AHEAD):
            sums.load(given_ref, place)
    else:
        part = wout_ref.shape[1]

        def feed_weights(k):
            columns = pl.ds(pl.multiple_of(links.owner(k) * part, part), part)
            slot = k % 2
            return (
                pltpu.make_async_copy(
                    feed_in_ref.at[:, :, columns], win_ref.at[slot], f_sem.at[slot, 0]
                ),
                pltpu.make_async_copy(
                    feed_out_ref.at[columns, :], wout_ref.at[slot], f_sem.at[slot, 1]
                ),
            )

        def hid_copy(k):
            return pltpu.make_async_copy(
                hid_ref.at[k % 2], hid_out.at[links.owner(k)], hid_sem.at[k]
            )

        for copy in feed_weights(0):
            copy.start()
    fetch(3).start()
    for k in range(shards):
        for j in range(4, held_count):
            fetch(j, links.owner(k)).start()
    for j in range(3):
        fetch(j).start()

    def stage(name, place):
        if name == "load":

            @pl.when(place < 4)
            def _():
                sums.load(given_ref, place)

            @pl.when(place >= 4)
            def _():
                feed_sums.load(feed_ref, place - 4)

            return
        if not biased:
            getattr(sums, name)(4 * (place % 2) + place // 2)
            return

        @pl.when(place < 4)
        def _():
            sums.core(place, given_ref) if name == "core" else getattr(sums, name)(place)

        @pl.when((place >= 4) & (place < 8))
        def _():
            c = place - 4
            if name == "core":
                feed_sums.core(c, feed_ref)
            else:
                getattr(feed_sums, name)(c)

        @pl.when(place >= 8)
        def _():
            getattr(sums, name)(place - 4)

    places = 12 if biased else sums.chunks
    late = (("core", 1), ("first", 3), ("second", 5), ("third", 7))
    if biased:
        late = (("load", -AHEAD), *late)

    def tick(t):
        for name, behind in late:
            place = t - behind

            @pl.when((place >= 0) & (place < (8 if name == "load" else places)))
            def _(name=name, place=place):
                stage(name, place)

    if not biased:
        share = nqt_ref.shape[0] // 8
        put_rows(n3t_ref, n3_ref[...].T, order)
        put_rows(ct_ref, cot_ref[...].T, order)
        dprev_ref[...] = y2_ref[...]
        dn_ref[...] = jnp.zeros_like(dn_ref)

        def feed_body(k, carry):
            @pl.when(k + 1 < shards)
            def _():
                for copy in feed_weights(k + 1):
                    copy.start()

            for copy in feed_weights(k):
                copy.wait()
            slot = k % 2
            w_gate, w_up, w_out = win_ref[slot, 0], win_ref[slot, 1], wout_ref[slot]
            hid, dg, du = feed_tile(n3_ref[...], cot_ref[...], w_gate, w_up, w_out)
            for item, right in enumerate((dg, du)):

                def rows_of(side, right=right):
                    rows = pl.ds(pl.multiple_of(side * 4 * share, 4 * share), 4 * share)
                    return nn(n3t_ref[rows, :], right).astype(BF16).reshape(2, 2, share, part)

                c = 4 * item + k
                wff_ref[c] = rows_of(1 - links.core)
                sums.over_core(c, wff_ref.at[c]).start()
                sums.own[c] = rows_of(links.core)

            @pl.when(k >= 2)
            def _():
                hid_copy(k - 2).wait()

            hid_ref[slot] = nn(ct_ref[...], hid).astype(BF16).reshape(2, 2, 2, share, part)
            hid_copy(k).start()
            dprev_ref[...] += nn(hid, w_out)
            dn_ref[...] += nt(dg, w_gate) + nt(du, w_up)
            tick(k)
            return carry

        lax.fori_loop(0, shards, feed_body, 0)
        result_ref[...] = dprev_ref[...].astype(BF16)
        dy, gg3_ref[...] = norm_grads(y2_ref[...], row(feed_gain_ref), dn_ref[...])
        dy_ref[...] = cot_ref[...].astype(F32) + dy

    da = dy_ref[...].astype(BF16)
    if biased:
        ext_ref[:, :block] = jnp.zeros((block, block), F32)
        far = lax.broadcasted_iota(jnp.int32, ext_ref.shape, 1) < start
    fetch(3).wait()
    first_tick = 0 if biased else shards

    for s in range(seqs):
        mine = slice(s * block, (s + 1) * block)
        theirs = slice(s * full, (s + 1) * full)
        if s == seqs - 1:
            for j in (0, 2) if biased else range(3):
                fetch(j).wait()
            put_rows(nqt_ref, nq_ref[...].T, order)
            put_rows(nkt_ref, nk_ref[...].T, order)
            put_rows(dat_ref, da.T, order)

        def body(k, carry):
            h = links.owner(k)
            if s == 0:
                for j in range(4, held_count):
                    fetch(j, h).wait()
            wo_h = wo_ref[pl.ds(pl.multiple_of(h * win, size), win), :]
            dcw = padded(nt(da[mine], wo_h).astype(BF16), pw)
            bias = None
            if biased:
                bias = bias_ref[pl.ds(h * group, group)].reshape(group * block, full).astype(F32)
            ds, dq, dk, dv = head_grads(
                q_ref[h, mine, :],
                k_ref[h, theirs, :],
                v_ref[h, theirs, :],
                dcw,
                lse_ref[h, s],
                bias,
                key < len_ref[s],
                lanes,
            )
            dkv = jnp.concatenate([dk[:, :win], dv[:, :win]], axis=1)
            dkv_ref[h, theirs, :] = dkv
            dq_ref[h, mine, :] = dq
            kv_term = nn(dkv[:, :win], wkv_ref[h, 0]) + nn(dkv[:, win:], wkv_ref[h, 1])
            q_term = nn(dq[:, :win], wq_ref[h])

            @pl.when(k == 0)
            def _():
                acck_ref[...] = kv_term
                accq_ref[mine, :] = q_term

            @pl.when(k != 0)
            def _():
                acck_ref[...] += kv_term
                accq_ref[mine, :] += q_term

            if biased and s < seqs - 1:
                ds_ref[h] = ds if s == 0 else ds_ref[h] + ds
            if biased and s == seqs - 1:
                whole = ds_ref[h].astype(F32) + ds.astype(F32)
                for a in range(group):
                    ext_ref[:, block:] = whole[a * block : (a + 1) * block, :]
                    far_sum = jnp.sum(jnp.where(far, ext_ref[...], 0.0))
                    near = ext_ref[:, pl.ds(start, 2 * block)]
                    diag_ref[pl.ds(h * group + a, 1), :] = diagonal_line(near, far_sum)
            if s == seqs - 1:
                dkv = dkv_ref[h]

                def weight_rows(side):
                    rows = pl.ds(pl.multiple_of(side * 4 * w_rows, 4 * w_rows), 4 * w_rows)
                    return jnp.concatenate(
                        [
                            nn(nkt_ref[rows, :], dkv).astype(BF16),
                            nn(nqt_ref[rows, :], dq_ref[h][:, :win]).astype(BF16),
                            nn(dat_ref[rows, :], c_ref[h][:, :win]).astype(BF16),
                        ],
                        axis=1,
                    ).reshape(2, 2, w_rows, 4 * win)

                if biased:
                    wtmp_ref[k] = weight_rows(1 - links.core)
                    sums.over_core(4 + k, wtmp_ref.at[k]).start()
                    sums.own[4 + k] = weight_rows(links.core)
                else:
                    for side in range(2):
                        wtmp_ref[h, side] = weight_rows(side)
                    pltpu.make_async_copy(wtmp_ref.at[h], w_ref.at[h], w_sem.at[h]).start()
            tick(first_tick + 4 * s + k)
            return carry

        w_rows = nqt_ref.shape[0] // 8
        lax.fori_loop(0, shards, body, 0)
        if biased:
            acck_ref[pl.ds(start, block), :] += accq_ref[mine, :]
            total = acck_ref[...]
            if s == 0:
                fetch(1).wait()
            part = jnp.sum(total * nk_ref[theirs, :].astype(F32), axis=0, keepdims=True)
            gain1 = part if s == 0 else gain1 + part
            mover = exchanges[1 + s]
            mover.buf[...] = total.astype(BF16).reshape(shards, block, -1)
            mover.start()
            grad_ref[mine, :] = acck_ref[pl.ds(start, block), :]
        elif s == 0:
            exchanges[0].buf[...] = acck_ref[...].astype(BF16).reshape(shards, block, -1)
            exchanges[0].start()
            mem_ref[...] = acck_ref[pl.ds(start, block), :]
        else:
            later_ref[...] = acck_ref[...].astype(BF16).reshape(shards, block, -1)

    steps = range(first_tick + 4 * seqs, places + late[-1][1])
    if not biased:
        dy, gg = norm_grads(y_ref[...], row(gain_ref), accq_ref[...])
        dprev_ref[...] = dy_ref[...] + dy
        gg_ref[...] = gg
        for t in steps:
            tick(t)
        mem_ref[...] += exchanges[0].finish()
        for item in range(2):
            given_out[item] = sums.finish(item)
        for h in range(shards):
            pltpu.make_async_copy(wtmp_ref.at[h], w_ref.at[h], w_sem.at[h]).wait()
        for k in range(2, shards):
            hid_copy(k).wait()
    else:
        gain1 = gain1 / row(gain_ref)
        width = gain1.shape[1]
        diag_ref[shards * group :, :] = jnp.zeros_like(diag_ref[shards * group :, :])
        sr[0, : diag_ref.shape[0], :] = diag_ref[...]
        sr[0, diag_ref.shape[0] :, :] = jnp.zeros_like(sr[0, diag_ref.shape[0] :, :])
        for i, line in enumerate((gain1, gain2_ref[...], gain3_ref[...])):
            for j in range(width // (2 * block)):
                at = diag_ref.shape[0] + i * width // (2 * block) + j
                sr[0, at : at + 1, :] = line[:, j * 2 * block : (j + 1) * 2 * block]
        plane = 2 + 2 * links.y + links.x
        hops = [(1, 0, links.over_core)]
        hops += [(plane, plane, to) for to in (links.over_x, links.over_y, links.over_plane)]
        hops += [(6 + me, 6 + me, to) for to in (links.to_pair, links.to_far, links.to_cross)]

        def hop(i):
            into, source, to = hops[i]
            return remote(sr.at[source], sr.at[into], ms.at[i], mr.at[i], to)

        hop(0).start()
        for i, t in enumerate(steps):
            tick(t)
            if i == 1:
                hop(0).wait_recv()
                sr[plane] = sr[0] + sr[1]
                for j in (1, 2, 3):
                    hop(j).start()
            if i == 3:
                for j in (1, 2, 3):
                    hop(j).wait_recv()
                sr[6 + me] = (sr[2] + sr[3]) + (sr[4] + sr[5])
                for j in (4, 5, 6):
                    hop(j).start()
        for j in (4, 5, 6):
            hop(j).wait_recv()
        small_out[...] = (sr[6] + sr[7]) + (sr[8] + sr[9])
        mem_ref[...] = exchanges[0].buf[me].astype(F32) + exchanges[0].finish()
        feed_out[...] = feed_sums.finish(0)
        given_out[...] = sums.finish(0)
        for s in range(seqs):
            mine = slice(s * block, (s + 1) * block)
            dn = grad_ref[mine, :] + exchanges[1 + s].finish()
            dx, _ = norm_grads(x_ref[mine, :].astype(F32), row(gain_ref), dn)
            grad_ref[mine, :] = dy_ref[mine, :] + dx
        own_out[...] = sums.finish(1)
        for i in range(len(hops)):
            hop(i).wait_send()
    for mover in exchanges:
        mover.drain()
    sums.drain()
    if biased:
        feed_sums.drain()


def linked_backward(lens, nq, nk, saved, wq, wkv, wo, dy, gain, given, extras, biased, group, size, order):
    q, k, v, c, lse = saved
    rows, width = nq.shape
    shards, keys, pw = k.shape
    seqs = lens.shape[0]
    block, full, win = rows // seqs, keys // seqs, group * size
    cols = 4 * win
    share = width // 8
    held = [nq, nk, c, wo, q, k, v, lse, wq, wkv]
    if biased:
        held.append(extras[1])
        extras = [extras[0], *extras[2:]]
        part = extras[0].shape[-1]
    else:
        part = given.shape[2] // shards
    args = [lens, dy, gain, given, *held, *extras]
    if biased:
        lines = -(-3 * width // (2 * block) // 8) * 8
        diag_rows = -(-shards * group // 8) * 8
        out_shape = [
            sds((rows, width), F32),
            sds((block, width), F32),
            sds((share, part), F32),
            sds((share, cols), F32),
            sds((share, cols), F32),
            sds((diag_rows + lines, 2 * block), F32),
        ]
    else:
        out_shape = [
            sds((rows, width), F32),
            sds((1, width), F32),
            sds((shards, 2, 2, 2, share, cols), BF16),
            sds((shards, block, width), BF16),
            sds((block, width), F32),
            sds((2, share, part), F32),
            sds((rows, width), BF16),
            sds((1, width), F32),
            sds((shards, 2, 2, 2, share, part), BF16),
        ]
    scratch = [pltpu.VMEM(a.shape, a.dtype) for a in held]
    scratch += [
        pltpu.SemaphoreType.DMA((len(held), shards)),
        pltpu.VMEM((shards, rows, pw), BF16),
        pltpu.VMEM((shards, keys, 2 * win), BF16),
        pltpu.VMEM((full, width), F32),
        pltpu.VMEM((rows, width), F32),
        pltpu.VMEM((width, rows), BF16),
        pltpu.VMEM((width, keys), BF16),
        pltpu.VMEM((width, rows), BF16),
    ]
    scratch.append(pltpu.VMEM((shards, *(() if biased else (2,)), 2, 2, share, cols), BF16))
    scratch += Sums.scratch(8, share, cols if biased else part)
    if biased:
        scratch += Sums.scratch(4, share, part)
    for _ in range(3 if biased else 1):
        scratch += Rows.scratch(block, width)
    dma = pltpu.SemaphoreType.DMA
    if biased:
        scratch += [
            pltpu.VMEM((shards, group * block, full), BF16),
            pltpu.VMEM((block, full + block), F32),
            pltpu.VMEM((diag_rows, 2 * block), F32),
            pltpu.VMEM((10, diag_rows + lines, 2 * block), F32),
            dma((7,)),
            dma((7,)),
        ]
    else:
        scratch += [
            dma((shards,)),
            pltpu.VMEM((rows, width), F32),
            pltpu.VMEM((rows, width), F32),
            pltpu.VMEM((width, rows), BF16),
            pltpu.VMEM((width, rows), BF16),
            pltpu.VMEM((8, 2, 2, share, part), BF16),
            pltpu.VMEM((2, 2, 2, 2, share, part), BF16),
            pltpu.VMEM((2, 2, width, part), BF16),
            pltpu.VMEM((2, part, width), BF16),
            dma((2, 2)),
            dma((shards,)),
        ]
    anywhere = pl.BlockSpec(memory_space=pl.ANY)
    in_specs = [smem(), vmem(), vmem(), anywhere] + [anywhere] * len(held)
    in_specs += [anywhere] + [vmem()] * (len(extras) - 1)
    out_specs = [vmem()] * len(out_shape)
    if not biased:
        out_specs[2] = out_specs[-1] = anywhere
    return pl.pallas_call(
        functools.partial(linked_kernel, biased, group, size, order),
        out_shape=out_shape,
        in_specs=in_specs,
        out_specs=out_specs,
        scratch_shapes=scratch,
        compiler_params=pltpu.CompilerParams(
            collective_id=2 if biased else 1, has_side_effects=True, vmem_limit_bytes=VMEM_LIMIT
        ),
        name="self_backward" if biased else "cross_backward",
    )(*args)


def arrange_kernel(
    shards, group, win, me_ref, grad_ref, first_ref, last_ref, gates_ref, hid_ref, cross_ref,
    self_ref, small_ref, grad_out, mem_out, gates_out, hid_out, table_out, *refs,
):
    gain_outs, weight_outs = refs[:3], refs[3:]
    grad_out[...] = grad_ref[...].reshape(grad_out.shape)
    mem_out[0] = first_ref[...]
    mem_out[1] = last_ref[...]
    gates_out[...] = gates_ref[...]
    hid_out[...] = hid_ref[...]
    for i, w_ref in enumerate((self_ref, cross_ref)):
        q_out, kv_out, o_out = weight_outs[3 * i : 3 * i + 3]
        w = w_ref[...]
        kv_out[0] = w[:, :win]
        kv_out[1] = w[:, win : 2 * win]
        q_out[...] = w[:, 2 * win : 3 * win]
        o_out[...] = w[:, 3 * win :].T
    head_rows = -(-shards * group // 8) * 8
    span = small_ref.shape[1]
    heads = lax.broadcasted_iota(jnp.int32, (8, head_rows), 0) + me_ref[0] * group
    pick = (heads == lax.broadcasted_iota(jnp.int32, (8, head_rows), 1)).astype(F32)
    mine = jnp.dot(pick, small_ref[:head_rows, :], precision=highest)
    onehot = bucket_rows(span // 2, NB).astype(F32)
    sums = lax.dot_general(mine, onehot, (((1,), (1,)), ((), ())), precision=highest)
    table_out[...] = sums[:group, :]
    for i, gain_out in enumerate(gain_outs):
        lines = [
            small_ref[head_rows + i * gain_out.shape[0] // span + j, :]
            for j in range(gain_out.shape[0] // span)
        ]
        gain_out[...] = jnp.concatenate(lines)


def arranged(
    me, result, grad, first, last, gates, hid, cross_w, self_w, small, shards, group, win
):
    rows, width = grad.shape
    block = first.shape[0]
    share, part = hid.shape
    weights = [sds((share, win), F32), sds((2, share, win), F32), sds((win, share), F32)]
    grad, mem, gates, hid, table, gain1, gain2, gain3, *weights = pl.pallas_call(
        functools.partial(arrange_kernel, shards, group, win),
        out_shape=[
            sds((rows // block, block, width), F32),
            sds((rows // block, block, width), F32),
            sds(gates.shape, F32),
            sds((share, part), F32),
            sds((group, NB), F32),
            sds((width,), F32),
            sds((width,), F32),
            sds((width,), F32),
            *weights,
            *weights,
        ],
        in_specs=[smem()] + [vmem()] * 8,
        out_specs=[vmem()] * 14,
        compiler_params=params(),
        name="arrange",
    )(me, grad, first, last, gates, hid, cross_w, self_w, small)
    result = result.reshape(grad.shape)
    return (
        result, grad, mem, gain1, *weights[:3], table.T, gain2, *weights[3:], gain3, gates, hid.T
    )


def per_device(
    layer_input,
    memory,
    dec_lengths,
    enc_lengths,
    self_gain,
    self_query,
    self_key_value,
    self_out,
    rel_bias,
    cross_gain,
    cross_query,
    cross_key_value,
    cross_out,
    feed_gain,
    feed_in,
    feed_out,
    out_cotangent,
):
    shards = lax.axis_size("head")
    me = lax.axis_index("head").astype(jnp.int32).reshape(1)
    batch_count = lax.axis_size("batch")
    seqs, block, width = layer_input.shape
    group = rel_bias.shape[1]
    size = self_query.shape[1] // group
    win = group * size
    full = block * shards
    enc_full = memory.shape[1] * shards
    rows = seqs * block
    part = feed_in.shape[2] // shards
    sg = self_gain.astype(F32).reshape(1, width)

    x = layer_input.reshape(rows, width)
    x32 = x.astype(F32)
    tight = batch_count == 8 and shards == 4 and seqs == 2
    order = tuple((i % 2) * 4 + i // 2 for i in range(8)) if tight else (0,)
    table = rel_bias.T
    flip = lambda w: jnp.swapaxes(w, -1, -2)
    weights = [flip(self_query)[None], flip(self_key_value), self_out[None]]
    weights += [flip(cross_query)[None], flip(cross_key_value), cross_out[None]]
    onehot = near_onehot(block)
    if tight:
        n1, y1, n2, y2, n3, memory_all, wq1, wkv1, wo1, wq2, wkv2, wo2, n1_all, bias, *saved = front(
            dec_lengths, enc_lengths, x, (self_gain, cross_gain, feed_gain), table, memory, weights,
            shards, group, size,
        )
        saved1, saved2 = saved[:5], saved[5:]
        n1_all = n1_all.reshape(seqs * full, width)
    else:
        n1 = (x32 * rms(x32) * sg).astype(BF16)
        n1_all = lax.all_gather(n1.reshape(seqs, block, width), "head", axis=1, tiled=True)
        n1_all = n1_all.reshape(seqs * full, width)
        wq1, wkv1, wo1, wq2, wkv2, wo2 = [lax.all_gather(w, "head", axis=0) for w in weights]
        table = jnp.pad(table, ((0, 8 - group), (0, 128 - NB)))
        tables = lax.all_gather(table, "head", axis=0)
        bias = bias_tiles(me, tables, group, block, full)
        memory_all = lax.all_gather(memory, "head", axis=1, tiled=True)
    memory_all = memory_all.reshape(seqs * enc_full, width)
    wq1, wq2 = wq1[:, 0], wq2[:, 0]
    wo1, wo2 = wo1.reshape(width, width), wo2.reshape(width, width)
    if not tight:
        *saved1, y1, n2 = attend_forward(
            dec_lengths, n1, n1_all, x, wq1, wkv1, wo1, cross_gain, bias, group, size
        )
        *saved2, y2, n3 = attend_forward(
            enc_lengths, n2, memory_all, y1, wq2, wkv2, wo2, feed_gain, None, group, size
        )
    gain_rows = width // (2 * block)
    cot = out_cotangent.reshape(rows, width)
    if tight:
        (
            dy1, gain2, cross_w, memory_later, memory_first, feed_in_grad, result, gain3, hid_w,
        ) = linked_backward(
            enc_lengths, n2, memory_all, saved2, wq2, wkv2, wo2, cot, cross_gain, feed_in,
            [feed_out, y1, y2, n3, feed_gain], False, group, size, order,
        )
        input_grad, memory_last, feed_out_grad, cross_w, self_w, small = linked_backward(
            dec_lengths, n1, n1_all, saved1, wq1, wkv1, wo1, dy1, self_gain, cross_w,
            [hid_w, bias, x, memory_later, gain2, gain3], True, group, size, order,
        )
        return arranged(
            me, result, input_grad, memory_first, memory_last, feed_in_grad, feed_out_grad,
            cross_w, self_w, small, shards, group, win,
        )
    else:
        result, dy2, gain3, feed_w = feed(
            y2, n3, cot, feed_in, feed_out, feed_gain, shards, order
        )
        memory_part, gain2, cross_w, dy1 = attend_backward(
            enc_lengths, me, n2, memory_all, saved2, wq2, wkv2, wo2, dy2, cross_gain, y1,
            False, group, size, order,
        )
        input_part, gain1, self_w, diag = attend_backward(
            dec_lengths, me, n1, n1_all, saved1, wq1, wkv1, wo1, dy1, self_gain, bias,
            True, group, size, order,
        )
        memory_grad = lax.psum_scatter(
            memory_part.reshape(seqs, enc_full, width), "head", scatter_dimension=1, tiled=True
        ).astype(F32)
        dn1 = lax.psum_scatter(
            input_part.reshape(seqs, full, width), "head", scatter_dimension=1, tiled=True
        ).astype(F32)
        feed_w, cross_w, self_w = (
            lax.psum_scatter(
                w.reshape(shards * width, w.shape[2]).astype(F32),
                ("head", "batch"),
                scatter_dimension=0,
                tiled=True,
            )
            for w in (feed_w, cross_w, self_w)
        )
        lines = jnp.concatenate([gain1, gain2, gain3], axis=0).reshape(-1, 2 * block)
        diag, lines = lax.psum((diag, lines), ("batch", "head"))
        dx, _ = norm_grads(x32, sg, dn1.reshape(rows, width))
        input_grad = dy1 + dx
        feed_in_grad = jnp.stack([feed_w[:, :part], feed_w[:, part : 2 * part]])
        feed_out_grad = feed_w[:, 2 * part :]
    gains = lines[: 3 * gain_rows].reshape(3, width)
    diag = lax.dynamic_slice_in_dim(diag, me[0] * group, group, 0)
    table_grad = jnp.einsum("tb,ht->bh", onehot, diag, precision=highest)

    def split(w):
        kv = jnp.stack([w[:, :win], w[:, win : 2 * win]])
        return w[:, 2 * win : 3 * win], kv, w[:, 3 * win :].T

    self_q, self_kv, self_o = split(self_w)
    cross_q, cross_kv, cross_o = split(cross_w)
    return (
        result.reshape(seqs, block, width),
        input_grad.reshape(seqs, block, width),
        memory_grad,
        gains[0],
        self_q,
        self_kv,
        self_o,
        table_grad,
        gains[1],
        cross_q,
        cross_kv,
        cross_o,
        gains[2],
        feed_in_grad,
        feed_out_grad.T,
    )


def solution(mesh):
    return jax.shard_map(
        per_device,
        mesh=mesh,
        in_specs=(
            P("batch", "head", None),
            P("batch", "head", None),
            P("batch"),
            P("batch"),
            P(),
            P(None, "head"),
            P(None, None, "head"),
            P("head", None),
            P(None, "head"),
            P(),
            P(None, "head"),
            P(None, None, "head"),
            P("head", None),
            P(),
            P(),
            P(),
            P("batch", "head", None),
        ),
        out_specs=(
            P("batch", "head", None),
            P("batch", "head", None),
            P("batch", "head", None),
            P(),
            P("batch", "head"),
            P(None, "batch", "head"),
            P("head", "batch"),
            P(None, "head"),
            P(),
            P("batch", "head"),
            P(None, "batch", "head"),
            P("head", "batch"),
            P(),
            P(None, "batch", "head"),
            P("head", "batch"),
        ),
        check_vma=False,
    )
```

```python
import functools
import math

import jax
import jax.numpy as jnp
from jax import lax
from jax.experimental import pallas as pl
from jax.experimental.pallas import tpu as pltpu
from jax.sharding import PartitionSpec as P

NB = 32
MAX_DIST = 128
NEG = -1e30
VMEM_LIMIT = 60 * 1024 * 1024
F32 = jnp.float32
BF16 = jnp.bfloat16

highest = lax.Precision.HIGHEST


def bucket_edges(num_buckets, max_distance):
    exact_part = num_buckets // 2
    edge_list = []
    for target in range(1, num_buckets - exact_part):
        distance = exact_part
        while (
            math.floor(
                math.log(distance / exact_part)
                / math.log(max_distance / exact_part)
                * (num_buckets - exact_part)
            )
            < target
        ):
            distance += 1
        edge_list.append(distance)
    return edge_list


def bucket_of(distance, num_buckets, max_distance):
    exact_part = num_buckets // 2
    counted = jnp.zeros(distance.shape, jnp.int32)
    for edge_value in bucket_edges(num_buckets, max_distance):
        counted = counted + (distance >= edge_value).astype(jnp.int32)
    return jnp.where(distance < exact_part, distance, exact_part + counted).astype(jnp.int32)


def near_onehot(block):
    distance = block - jnp.arange(2 * block)
    distance = jnp.where(distance < 0, 2 * MAX_DIST, distance)
    return (
        bucket_of(distance, NB, MAX_DIST)[:, None] == jnp.arange(NB)[None, :]
    ).astype(F32)


def nn(a, b):
    return lax.dot_general(a, b, (((1,), (0,)), ((), ())), preferred_element_type=F32)


def nt(a, b):
    return lax.dot_general(a, b, (((1,), (1,)), ((), ())), preferred_element_type=F32)


def tn(a, b):
    return lax.dot_general(a, b, (((0,), (0,)), ((), ())), preferred_element_type=F32)


def rms(v):
    mean = jnp.mean(v * v, axis=-1, keepdims=True) + 1e-06
    r = lax.rsqrt(mean)
    return r * (1.5 - 0.5 * mean * r * r)


def norm_grads(y, gain, e):
    r = rms(y)
    xhat = y * r
    eg = e * gain
    dy = r * (eg - xhat * jnp.mean(eg * xhat, axis=-1, keepdims=True))
    return dy, jnp.sum(e * xhat, axis=0, keepdims=True)


def row(ref):
    return ref[...].astype(F32).reshape(1, -1)


def padded(v, width):
    extra = width - v.shape[1]
    if extra == 0:
        return v
    return jnp.concatenate([v, jnp.zeros((v.shape[0], extra), v.dtype)], axis=1)


def put_rows(ref, value, order):
    step = value.shape[0] // len(order)
    for source, slot in enumerate(order):
        ref[slot * step : (slot + 1) * step, :] = value[source * step : (source + 1) * step, :]


def vmem():
    return pl.BlockSpec(memory_space=pltpu.VMEM)


def smem():
    return pl.BlockSpec(memory_space=pltpu.SMEM)


def params():
    return pltpu.CompilerParams(vmem_limit_bytes=VMEM_LIMIT)


def sds(shape, dtype):
    return jax.ShapeDtypeStruct(shape, dtype)


def bucket_rows(block, count):
    distance = block - lax.broadcasted_iota(jnp.int32, (1, 2 * block), 1)
    distance = jnp.where(distance < 0, 2 * MAX_DIST, distance)
    bucket = bucket_of(distance, NB, MAX_DIST)
    return bucket == lax.broadcasted_iota(jnp.int32, (count, 2 * block), 0)


def build_bias(me, table_ref, b_ref, ext_ref, line_ref):
    heads, block, full = b_ref.shape
    shards = table_ref.shape[0]
    group = heads // shards
    start = pl.multiple_of(me * block, block)
    width = 2 * block
    row_i = lax.broadcasted_iota(jnp.int32, (block, width), 0)
    col_i = lax.broadcasted_iota(jnp.int32, (block, width), 1)
    masked = (col_i - row_i) > block
    far = lax.broadcasted_iota(jnp.int32, ext_ref.shape, 1) < start
    onehot = bucket_rows(block, table_ref.shape[2]).astype(BF16)

    def body(h, carry):
        line_ref[...] = nn(table_ref[h], onehot)
        for a in range(group):
            row = line_ref[a : a + 1, :]
            tile = pltpu.roll(
                jnp.broadcast_to(row, (block, width)), 0, 1, stride=1, stride_axis=0
            )
            ext_ref[...] = jnp.where(far, row[:, width - 1 : width], NEG)
            ext_ref[:, pl.ds(start, width)] = jnp.where(masked, NEG, tile)
            b_ref[h * group + a] = ext_ref[:, block:].astype(BF16)
        return carry

    lax.fori_loop(0, shards, body, 0)


def bias_kernel(me_ref, *refs):
    build_bias(me_ref[0], *refs)


def bias_tiles(me, tables, group, block, full):
    shards, lanes = tables.shape[:2]
    return pl.pallas_call(
        bias_kernel,
        out_shape=sds((shards * group, block, full), BF16),
        in_specs=[smem(), vmem()],
        out_specs=vmem(),
        scratch_shapes=[
            pltpu.VMEM((block, full + block), F32),
            pltpu.VMEM((lanes, 2 * block), F32),
        ],
        compiler_params=params(),
        name="bias_tiles",
    )(me, tables)


def lane_groups(width, group, size):
    lane = lax.broadcasted_iota(jnp.int32, (1, width), 1)
    return [(lane // size) == a for a in range(group)]


def stack_heads(win, lanes):
    return jnp.concatenate([jnp.where(m, win, jnp.zeros_like(win)) for m in lanes], axis=0)


def join_heads(tall, lanes, rows):
    total = jnp.where(lanes[0], tall[:rows], 0.0)
    for a in range(1, len(lanes)):
        total = total + jnp.where(lanes[a], tall[a * rows : (a + 1) * rows], 0.0)
    return total


def head_context(qw, kw, vw, bias, keep, lanes):
    block, group = qw.shape[0], len(lanes)
    sc = nt(stack_heads(qw, lanes), kw)
    if bias is not None:
        sc = sc + bias
    sc = jnp.where(keep, sc, NEG)
    top = jnp.max(sc, axis=-1, keepdims=True)
    e = jnp.exp(sc - top)
    total = jnp.sum(e, axis=-1, keepdims=True)
    p = (e * (1.0 / total)).astype(BF16)
    c = join_heads(nn(p, vw), lanes, block).astype(BF16)
    lse = top + jnp.log(total)
    lane = lax.broadcasted_iota(jnp.int32, (block, 128), 1)
    tile = jnp.zeros((block, 128), F32)
    for a in range(group):
        tile = jnp.where(lane == a, lse[a * block : (a + 1) * block], tile)
    return c, tile


def forward_kernel(
    biased, group, size, len_ref, nq_ref, nk_ref, res_ref, wq_ref, wkv_ref, wo_ref, gain_ref, *rest
):
    if biased:
        b_ref, *rest = rest
    q_ref, k_ref, v_ref, c_ref, lse_ref, y_ref, n_ref = rest
    shards, rows, pw = q_ref.shape
    seqs = len_ref.shape[0]
    block = rows // seqs
    full = k_ref.shape[1] // seqs
    win = group * size
    lanes = lane_groups(pw, group, size)
    key = lax.broadcasted_iota(jnp.int32, (1, full), 1)

    def body(h, carry):
        q_ref[h] = padded(nt(nq_ref[...], wq_ref[h]).astype(BF16), pw)
        k_ref[h] = padded(nt(nk_ref[...], wkv_ref[h, 0]).astype(BF16), pw)
        v_ref[h] = padded(nt(nk_ref[...], wkv_ref[h, 1]).astype(BF16), pw)
        for s in range(seqs):
            bias = None
            if biased:
                bias = b_ref[pl.ds(h * group, group)].reshape(group * block, full).astype(F32)
            c, lse_ref[h, s] = head_context(
                q_ref[h, s * block : (s + 1) * block, :],
                k_ref[h, s * full : (s + 1) * full, :],
                v_ref[h, s * full : (s + 1) * full, :],
                bias,
                key < len_ref[s],
                lanes,
            )
            c_ref[h, s * block : (s + 1) * block, :] = c
        return carry

    lax.fori_loop(0, shards, body, 0)
    joined = jnp.concatenate([c_ref[h][:, :win] for h in range(shards)], axis=1)
    y = res_ref[...].astype(F32) + nn(joined, wo_ref[...])
    y_ref[...] = y
    n_ref[...] = (y * rms(y) * row(gain_ref)).astype(BF16)


def attend_forward(lens, nq, nk, res, wq, wkv, wo, gain, bias, group, size):
    rows, width = nq.shape
    shards = wq.shape[0]
    pw = -(-group * size // 128) * 128
    seqs = lens.shape[0]
    args = [lens, nq, nk, res, wq, wkv, wo, gain] + ([bias] if bias is not None else [])
    keys = nk.shape[0]
    flops = 2 * (rows + 2 * keys + rows) * width * width + 4 * rows * keys * width
    return pl.pallas_call(
        functools.partial(forward_kernel, bias is not None, group, size),
        out_shape=[
            sds((shards, rows, pw), BF16),
            sds((shards, keys, pw), BF16),
            sds((shards, keys, pw), BF16),
            sds((shards, rows, pw), BF16),
            sds((shards, seqs, rows // seqs, 128), F32),
            sds((rows, width), F32),
            sds((rows, width), BF16),
        ],
        in_specs=[smem()] + [vmem()] * (len(args) - 1),
        out_specs=[vmem()] * 7,
        compiler_params=params(),
        cost_estimate=pl.CostEstimate(
            flops=flops, bytes_accessed=16 << 20, transcendentals=rows * keys * 6
        ),
        name="attend_forward",
    )(*args)


def backward_kernel(
    biased,
    group,
    size,
    order,
    len_ref,
    me_ref,
    nq_ref,
    nk_ref,
    q_ref,
    k_ref,
    v_ref,
    c_ref,
    lse_ref,
    wq_ref,
    wkv_ref,
    wo_ref,
    dy_ref,
    gain_ref,
    *rest,
):
    if biased:
        b_ref, part_ref, gg_ref, w_ref, diag_ref, dc_ref, dq_ref, dkv_ref, acc_ref, nqt_ref, nkt_ref, dat_ref, sum_ref, ext_ref = rest
    else:
        y_ref, part_ref, gg_ref, w_ref, dprev_ref, dc_ref, dq_ref, dkv_ref, acc_ref, nqt_ref, nkt_ref, dat_ref = rest
    shards, rows, pw = q_ref.shape
    seqs = len_ref.shape[0]
    block = rows // seqs
    full = k_ref.shape[1] // seqs
    win = group * size
    lanes = lane_groups(pw, group, size)
    key = lax.broadcasted_iota(jnp.int32, (1, full), 1)
    me = me_ref[0]

    da = dy_ref[...].astype(BF16)
    put_rows(nqt_ref, nq_ref[...].T, order)
    put_rows(nkt_ref, nk_ref[...].T, order)
    put_rows(dat_ref, da.T, order)
    if biased:
        ext_ref[:, :block] = jnp.zeros((block, block), F32)
        start = pl.multiple_of(me * block, block)
        far = lax.broadcasted_iota(jnp.int32, ext_ref.shape, 1) < start
        row8 = lax.broadcasted_iota(jnp.int32, (8, 2 * block), 0)
        lane_near = lax.broadcasted_iota(jnp.int32, (1, 2 * block), 1)

    def body(h, carry):
        wo_h = wo_ref[pl.ds(pl.multiple_of(h * win, size), win), :]
        dc_ref[...] = padded(nt(da, wo_h).astype(BF16), pw)
        for s in range(seqs):
            kw = k_ref[h, s * full : (s + 1) * full, :]
            vw = v_ref[h, s * full : (s + 1) * full, :]
            qcat = stack_heads(q_ref[h, s * block : (s + 1) * block, :], lanes)
            dcat = stack_heads(dc_ref[s * block : (s + 1) * block, :], lanes)
            sc = nt(qcat, kw)
            if biased:
                sc = sc + b_ref[pl.ds(h * group, group)].reshape(group * block, full).astype(F32)
            sc = jnp.where(key < len_ref[s], sc, NEG)
            lse_tile = lse_ref[h, s]
            lse = jnp.concatenate([lse_tile[:, a : a + 1] for a in range(group)], axis=0)
            p = jnp.exp(sc - lse)
            dp = nt(dcat, vw)
            ds = p * (dp - jnp.sum(p * dp, axis=-1, keepdims=True))
            ds = ds.astype(BF16)
            pb = p.astype(BF16)
            if biased:
                if s == 0:
                    sum_ref[...] = ds.astype(F32)
                else:
                    sum_ref[...] += ds.astype(F32)
            dq = join_heads(nn(ds, kw), lanes, block)
            dq_ref[s * block : (s + 1) * block, :] = dq.astype(BF16)
            dk = tn(ds, qcat).astype(BF16)
            dv = tn(pb, dcat).astype(BF16)
            dkv_ref[s * full : (s + 1) * full, :] = jnp.concatenate(
                [dk[:, :win], dv[:, :win]], axis=1
            )
        if biased:
            for a in range(group):
                ext_ref[:, block:] = sum_ref[a * block : (a + 1) * block, :]
                far_sum = jnp.sum(jnp.where(far, ext_ref[...], 0.0))
                fold = ext_ref[:, pl.ds(start, 2 * block)]
                half = block // 2
                while half >= 8:
                    fold = fold[:half] + pltpu.roll(fold[half:], 2 * block - half, 1)
                    half //= 2
                for bit in (4, 2, 1):
                    fold = jnp.where(
                        (row8 & bit) != 0, pltpu.roll(fold, 2 * block - bit, 1), fold
                    )
                line = jnp.sum(fold, axis=0, keepdims=True)
                line = line + jnp.where(lane_near == 2 * block - 1, far_sum, 0.0)
                diag_ref[pl.ds(h * group + a, 1), :] = line
        dkv = dkv_ref[...]
        dq_h = dq_ref[...][:, :win]
        kv_term = nn(dkv[:, :win], wkv_ref[h, 0]) + nn(dkv[:, win:], wkv_ref[h, 1])
        q_term = nn(dq_h, wq_ref[h])
        w_ref[h] = jnp.concatenate(
            [
                nn(nkt_ref[...], dkv).astype(BF16),
                nn(nqt_ref[...], dq_h).astype(BF16),
                nn(dat_ref[...], c_ref[h][:, :win]).astype(BF16),
            ],
            axis=1,
        )

        @pl.when(h == 0)
        def _():
            acc_ref[: seqs * full, :] = kv_term
            acc_ref[seqs * full :, :] = q_term

        @pl.when(h != 0)
        def _():
            acc_ref[: seqs * full, :] += kv_term
            acc_ref[seqs * full :, :] += q_term

        return carry

    lax.fori_loop(0, shards, body, 0)
    if biased:
        for s in range(seqs):
            own = pl.ds(pl.multiple_of(s * full + me * block, block), block)
            acc_ref[own, :] += acc_ref[seqs * full + s * block : seqs * full + (s + 1) * block, :]
        total = acc_ref[: seqs * full, :]
        part_ref[...] = total.astype(BF16)
        gg_ref[...] = (
            jnp.sum(total * nk_ref[...].astype(F32), axis=0, keepdims=True) / row(gain_ref)
        )
    else:
        part_ref[...] = acc_ref[: seqs * full, :].astype(BF16)
        dy, gg = norm_grads(y_ref[...], row(gain_ref), acc_ref[seqs * full :, :])
        dprev_ref[...] = dy_ref[...] + dy
        gg_ref[...] = gg


def attend_backward(
    lens, me, nq, nk, saved, wq, wkv, wo, dy, gain, extra, biased, group, size, order
):
    q, k, v, c, lse = saved
    rows, width = nq.shape
    shards, keys, pw = k.shape
    block = rows // lens.shape[0]
    full = keys // lens.shape[0]
    win = group * size
    args = [lens, me, nq, nk, q, k, v, c, lse, wq, wkv, wo, dy, gain, extra]
    out_shape = [
        sds((keys, width), BF16),
        sds((1, width), F32),
        sds((shards, width, 4 * win), BF16),
        sds((shards * group, 2 * block), F32) if biased else sds((rows, width), F32),
    ]
    scratch = [
        pltpu.VMEM((rows, pw), BF16),
        pltpu.VMEM((rows, pw), BF16),
        pltpu.VMEM((keys, 2 * win), BF16),
        pltpu.VMEM((keys + rows, width), F32),
        pltpu.VMEM((width, rows), BF16),
        pltpu.VMEM((width, keys), BF16),
        pltpu.VMEM((width, rows), BF16),
    ]
    if biased:
        scratch += [
            pltpu.VMEM((group * block, full), F32),
            pltpu.VMEM((block, full + block), F32),
        ]
    flops = 4 * (rows + 2 * keys + rows) * width * width + 10 * rows * full * width
    return pl.pallas_call(
        functools.partial(backward_kernel, biased, group, size, order),
        out_shape=out_shape,
        in_specs=[smem(), smem()] + [vmem()] * (len(args) - 2),
        out_specs=[vmem()] * 4,
        scratch_shapes=scratch,
        compiler_params=params(),
        cost_estimate=pl.CostEstimate(
            flops=flops, bytes_accessed=24 << 20, transcendentals=rows * full * 12
        ),
        name="attend_backward",
    )(*args)


def feed_tile(n, cot, w_gate, w_up, w_out):
    g = nn(n, w_gate)
    u = nn(n, w_up)
    dh = nt(cot, w_out)
    scale = math.sqrt(2.0 / math.pi)
    square = g * g
    t = jnp.tanh(scale * (g + 0.044715 * square * g))
    half = 0.5 * (1.0 + t)
    gelu = g * half
    hid = (gelu * u).astype(BF16)
    slope = half + 0.5 * g * (1.0 - t * t) * (scale * (1.0 + 3 * 0.044715 * square))
    return hid, (dh * u * slope).astype(BF16), (dh * gelu).astype(BF16)


def feed_kernel(
    order, y_ref, n_ref, cot_ref, win_ref, wout_ref, gain_ref, out_ref, dy_ref, gg_ref, w_ref,
    acc_ref, dn_ref, nt_ref, ct_ref,
):
    step = pl.program_id(0)
    part = wout_ref.shape[0]

    @pl.when(step == 0)
    def _():
        put_rows(nt_ref, n_ref[...].T, order)
        put_rows(ct_ref, cot_ref[...].T, order)
        acc_ref[...] = y_ref[...]
        dn_ref[...] = jnp.zeros_like(dn_ref)

    hid, dg, du = feed_tile(n_ref[...], cot_ref[...], win_ref[0], win_ref[1], wout_ref[...])
    acc_ref[...] += nn(hid, wout_ref[...])
    dn_ref[...] += nt(dg, win_ref[0]) + nt(du, win_ref[1])
    w_ref[0, :, :part] = nn(nt_ref[...], dg).astype(BF16)
    w_ref[0, :, part : 2 * part] = nn(nt_ref[...], du).astype(BF16)
    w_ref[0, :, 2 * part :] = nn(ct_ref[...], hid).astype(BF16)

    @pl.when(step == pl.num_programs(0) - 1)
    def _():
        out_ref[...] = acc_ref[...].astype(BF16)
        dy, gg = norm_grads(y_ref[...], row(gain_ref), dn_ref[...])
        dy_ref[...] = cot_ref[...].astype(F32) + dy
        gg_ref[...] = gg


def feed(y, n, cot, w_in, w_out, gain, shards, order):
    rows, width = y.shape
    hidden = w_out.shape[0]
    part = hidden // shards
    fixed = lambda shape: pl.BlockSpec(shape, lambda j: (0,) * len(shape))
    return pl.pallas_call(
        functools.partial(feed_kernel, order),
        grid=(shards,),
        out_shape=[
            sds((rows, width), BF16),
            sds((rows, width), F32),
            sds((1, width), F32),
            sds((shards, width, 3 * part), BF16),
        ],
        in_specs=[
            fixed((rows, width)),
            fixed((rows, width)),
            fixed((rows, width)),
            pl.BlockSpec((2, width, part), lambda j: (0, 0, j)),
            pl.BlockSpec((part, width), lambda j: (j, 0)),
            fixed((width,)),
        ],
        out_specs=[
            fixed((rows, width)),
            fixed((rows, width)),
            fixed((1, width)),
            pl.BlockSpec((1, width, 3 * part), lambda j: (j, 0, 0)),
        ],
        scratch_shapes=[
            pltpu.VMEM((rows, width), F32),
            pltpu.VMEM((rows, width), F32),
            pltpu.VMEM((width, rows), BF16),
            pltpu.VMEM((width, rows), BF16),
        ],
        compiler_params=params(),
        cost_estimate=pl.CostEstimate(
            flops=18 * rows * width * hidden, bytes_accessed=24 << 20, transcendentals=rows * hidden
        ),
        name="feed",
    )(y, n, cot, w_in, w_out, gain)


MESH = pl.DeviceIdType.MESH


def place():
    b = lax.axis_index("batch")
    me = lax.axis_index("head")
    core = lax.rem(b, 2)
    x = lax.rem(lax.div(b, 2), 2)
    y = lax.div(b, 4)
    return b, me, core, x, y


def greet(devices):
    barrier = pltpu.get_barrier_semaphore()
    for device in devices:
        pl.semaphore_signal(barrier, inc=1, device_id=device, device_id_type=MESH)
    pl.semaphore_wait(barrier, len(devices))


def remote(src, dst, send, recv, device):
    return pltpu.make_async_remote_copy(
        src_ref=src,
        dst_ref=dst,
        send_sem=send,
        recv_sem=recv,
        device_id=device,
        device_id_type=MESH,
    )


def flipped(bit, by):
    return bit + by - 2 * bit * by


AHEAD = 2


class Links:
    def __init__(self):
        b, me, core, x, y = place()
        self.me, self.core, self.x, self.y = me, core, x, y
        self.high, self.low = lax.div(me, 2), lax.rem(me, 2)
        self.pair, self.far, self.cross = self.owner(1), self.owner(2), self.owner(0)
        self.over_core = (b + 1 - 2 * core, me)
        self.over_x = (b + 2 - 4 * x, me)
        self.over_y = (b + 4 - 8 * y, me)
        self.over_plane = (b + 2 - 4 * x + 4 - 8 * y, me)
        self.to_pair, self.to_far, self.to_cross = (b, self.pair), (b, self.far), (b, self.cross)

    def owner(self, k):
        by_low, by_high = 1 - k // 2, 1 - k % 2
        return 2 * flipped(self.high, by_high) + flipped(self.low, by_low)

    def greet(self):
        greet(
            [self.over_core, self.over_x, self.over_y, self.over_plane]
            + [self.to_pair, self.to_far, self.to_cross]
        )


class Sums:
    @staticmethod
    def scratch(chunks, rows, cols):
        items, half = chunks // 4, cols // 2
        dma = pltpu.SemaphoreType.DMA
        return [
            pltpu.VMEM((chunks, 2, 2, rows, cols), BF16),
            pltpu.VMEM((chunks, 2, 2, rows, cols), BF16),
            pltpu.VMEM((chunks, 2, rows, half), BF16),
            pltpu.VMEM((chunks, 2, rows, half), BF16),
            pltpu.VMEM((chunks, rows, half), BF16),
            pltpu.VMEM((chunks, rows, half), BF16),
            pltpu.VMEM((chunks, rows, cols), BF16),
            pltpu.VMEM((items, 3, rows, cols), BF16),
            dma((chunks,)),
            dma((chunks,)),
            dma((chunks,)),
            dma((chunks, 2)),
            dma((chunks, 2)),
            dma((chunks, 2)),
            dma((chunks, 2)),
            dma((items, 3)),
            dma((items, 3)),
        ]

    count = 17

    def __init__(self, links, refs):
        (self.own, self.rc, self.r1a, self.r1b, self.r2a, self.r2b, self.tot, self.rz) = refs[:8]
        (self.ls, self.cs, self.cr, self.s1, self.q1, self.s2, self.q2, self.zs, self.zr) = refs[8:]
        self.links = links
        self.chunks, self.cols = self.own.shape[0], self.own.shape[-1]
        self.half = self.cols // 2

    def piece(self, w_ref, c, side, left):
        start = pl.multiple_of((c // 4) * self.cols + left, 128)
        return w_ref.at[self.links.owner(c % 4), side, :, :, :, pl.ds(start, self.cols)]

    def local(self, w_ref, c, left):
        return pltpu.make_async_copy(
            self.piece(w_ref, c, self.links.core, left), self.own.at[c], self.ls.at[c]
        )

    def over_core(self, c, source):
        return remote(
            source, self.rc.at[c], self.cs.at[c], self.cr.at[c], self.links.over_core
        )

    def load(self, w_ref, c, left=0):
        self.local(w_ref, c, left).start()
        self.over_core(c, self.piece(w_ref, c, 1 - self.links.core, left)).start()

    def firsts(self, c):
        links, half = self.links, self.half
        return (
            remote(
                self.own.at[c, :, 1 - links.x, :, pl.ds(0, half)],
                self.r1a.at[c],
                self.s1.at[c, 0],
                self.q1.at[c, 0],
                links.over_x,
            ),
            remote(
                self.own.at[c, 1 - links.y, :, :, pl.ds(half, half)],
                self.r1b.at[c],
                self.s1.at[c, 1],
                self.q1.at[c, 1],
                links.over_y,
            ),
        )

    def seconds(self, c):
        links = self.links
        return (
            remote(
                self.r1a.at[c, 1 - links.y],
                self.r2a.at[c],
                self.s2.at[c, 0],
                self.q2.at[c, 0],
                links.over_y,
            ),
            remote(
                self.r1b.at[c, 1 - links.x],
                self.r2b.at[c],
                self.s2.at[c, 1],
                self.q2.at[c, 1],
                links.over_x,
            ),
        )

    def along(self, item, slot, c):
        device = self.links.to_far if slot == 2 else self.links.to_pair
        return remote(
            self.tot.at[c],
            self.rz.at[item, slot],
            self.zs.at[item, slot],
            self.zr.at[item, slot],
            device,
        )

    def core(self, c, w_ref=None, left=0):
        if w_ref is not None:
            self.local(w_ref, c, left).wait()
        self.over_core(c, self.rc.at[c]).wait_recv()
        x, y, half = 1 - self.links.x, 1 - self.links.y, self.half
        self.own[c, :, x, :, :half] = self.own[c, :, x, :, :half] + self.rc[c, :, x, :, :half]
        self.own[c, y, :, :, half:] = self.own[c, y, :, :, half:] + self.rc[c, y, :, :, half:]
        for copy in self.firsts(c):
            copy.start()

    def left(self, c, y):
        x, half = self.links.x, self.half
        total = self.own[c, y, x, :, :half].astype(F32) + self.rc[c, y, x, :, :half].astype(F32)
        return total + self.r1a[c, y].astype(F32)

    def right(self, c, x):
        y, half = self.links.y, self.half
        total = self.own[c, y, x, :, half:].astype(F32) + self.rc[c, y, x, :, half:].astype(F32)
        return total + self.r1b[c, x].astype(F32)

    def first(self, c):
        for copy in self.firsts(c):
            copy.wait_recv()
        x, y = 1 - self.links.x, 1 - self.links.y
        self.r1a[c, y] = self.left(c, y).astype(BF16)
        self.r1b[c, x] = self.right(c, x).astype(BF16)
        for copy in self.seconds(c):
            copy.start()

    def whole(self, c):
        left = self.left(c, self.links.y) + self.r2a[c].astype(F32)
        right = self.right(c, self.links.x) + self.r2b[c].astype(F32)
        return jnp.concatenate([left, right], axis=1)

    def second(self, c):
        for copy in self.seconds(c):
            copy.wait_recv()
        item, k = c // 4, c % 4
        for slot in range(2):

            @pl.when(k == slot)
            def _(slot=slot):
                self.tot[c] = self.whole(c).astype(BF16)
                self.along(item, slot, c).start()

    def third(self, c):
        item, k = c // 4, c % 4

        @pl.when(k == 2)
        def _():
            self.along(item, 0, c).wait_recv()
            self.tot[c] = (self.whole(c) + self.rz[item, 0].astype(F32)).astype(BF16)
            self.along(item, 2, c).start()

    def finish(self, item):
        c = 4 * item
        for slot in (1, 2):
            self.along(item, slot, c).wait_recv()
        return self.whole(c + 3) + self.rz[item, 1].astype(F32) + self.rz[item, 2].astype(F32)

    def drain(self):
        def body(c, carry):
            self.over_core(c, self.rc.at[c]).wait_send()
            for copy in self.firsts(c) + self.seconds(c):
                copy.wait_send()
            return carry

        lax.fori_loop(0, self.chunks, body, 0)
        for item in range(self.chunks // 4):
            for slot in range(3):
                self.along(item, slot, 4 * item).wait_send()


class Weights:
    @staticmethod
    def scratch(n):
        dma = pltpu.SemaphoreType.DMA
        return [dma((n, 3)), dma((n, 3)), dma((n, 3, 3)), dma((n, 3, 3)), dma((n, 3)), dma((n, 3))]

    def __init__(self, links, shards, fulls, sems):
        self.links, self.shards, self.fulls = links, shards, fulls
        self.zs, self.zr, self.ps, self.pr, self.cs, self.cr = sems
        self.n = len(shards)
        self.planes = (links.pair, links.far, links.cross)
        self.slot = links.core * 4 + links.y * 2 + links.x

    def window(self, ref, first, count):
        step = ref.shape[-2] // 8
        return ref.at[:, pl.ds(pl.multiple_of(first * step, step), count * step), :]

    def along(self, i, slot):
        links = self.links
        source = self.planes[1] if slot == 2 else links.me
        into = self.window(self.fulls[i].at[source], self.slot, 1)
        mine = into if slot == 2 else self.window(self.shards[i], self.slot, 1)
        device = links.to_far if slot == 1 else links.to_pair
        return remote(mine, into, self.zs.at[i, slot], self.zr.at[i, slot], device)

    def across(self, i, j, d):
        links = self.links
        piece = self.window(self.fulls[i].at[self.planes[j]], self.slot, 1)
        device = (links.over_x, links.over_y, links.over_plane)[d]
        return remote(piece, piece, self.ps.at[i, j, d], self.pr.at[i, j, d], device)

    def core(self, i, j):
        half = self.window(self.fulls[i].at[self.planes[j]], self.links.core * 4, 4)
        return remote(half, half, self.cs.at[i, j], self.cr.at[i, j], self.links.over_core)

    def start(self):
        for i in range(self.n):
            for slot in (0, 1):
                self.along(i, slot).start()

    def arrive(self, j):
        for i in range(self.n):
            self.along(i, j).wait_recv()
            if j == 1:
                self.along(i, 2).start()
            for d in range(3):
                self.across(i, j, d).start()

    def share(self, j):
        for i in range(self.n):
            for d in range(3):
                self.across(i, j, d).wait_recv()
            self.core(i, j).start()

    def finish(self, j):
        for i in range(self.n):
            self.core(i, j).wait_recv()

    def drain(self):
        for i in range(self.n):
            for j in range(3):
                self.along(i, j).wait_send()
                self.core(i, j).wait_send()
                for d in range(3):
                    self.across(i, j, d).wait_send()


class Gathered:
    def __init__(self, links, source, into, sems):
        self.links, self.source, self.into = links, source, into
        self.ss, self.rs = sems
        self.seqs, self.block = into.shape[0], into.shape[1] // 4

    def window(self, s, plane):
        rows = pl.ds(pl.multiple_of(plane * self.block, self.block), self.block)
        return self.into.at[s, rows, :]

    def copy(self, s, slot):
        links = self.links
        into = self.window(s, links.far if slot == 2 else links.me)
        mine = into if slot == 2 else self.source(s)
        device = links.to_far if slot == 1 else links.to_pair
        return remote(mine, into, self.ss.at[s, slot], self.rs.at[s, slot], device)

    def start(self, those=(0, 1)):
        for s in those:
            for slot in (1, 0):
                self.copy(s, slot).start()

    def forward(self):
        for s in range(self.seqs):
            self.copy(s, 1).wait_recv()
            self.copy(s, 2).start()

    def take(self, slot):
        for s in range(self.seqs):
            self.copy(s, slot).wait_recv()

    def finish(self):
        for slot in (0, 2):
            self.take(slot)

    def drain(self):
        for s in range(self.seqs):
            for slot in range(3):
                self.copy(s, slot).wait_send()


def front_kernel(group, size, *refs):
    len_ref, enc_ref, x_ref, self_gain_ref, cross_gain_ref, feed_gain_ref, table_ref, *refs = refs
    memory_ref, own_weights, refs = refs[0], refs[1:7], refs[7:]
    n_ref, y_ref, n2_ref, y2_ref, n3_ref, memory_out, *refs = refs
    self_out, cross_out, refs = refs[:3], refs[3:6], refs[6:]
    outs, kept, refs = refs[:12], refs[12:24], refs[24:]
    nall_ref, bias_ref, q_ref, k_ref, v_ref, c_ref, lse_ref = kept[:7]
    q2_ref, k2_ref, v2_ref, c2_ref, lse2_ref = kept[7:]
    self_full, cross_full, refs = refs[:3], refs[3:6], refs[6:]
    tables_ref, ext_ref, line_ref, mem_ref, *refs = refs
    (table_s, table_r, rows_s, rows_r, memory_s, memory_r, local, placed, held, done, *refs) = refs
    links = Links()
    me = links.me
    w1 = Weights(links, own_weights[:3], self_out, refs[:6])
    w2 = Weights(links, own_weights[3:], cross_out, refs[6:])
    shards, rows, pw = q_ref.shape
    seqs = len_ref.shape[0]
    block = rows // seqs
    full = block * shards
    win = group * size
    lanes = lane_groups(pw, group, size)
    key = lax.broadcasted_iota(jnp.int32, (1, full), 1)
    start = pl.multiple_of(me * block, block)
    rows_one = Gathered(
        links, lambda s: nall_ref.at[s, pl.ds(start, block), :], nall_ref, (rows_s, rows_r)
    )
    rows_memory = Gathered(
        links, lambda s: mem_ref.at[s, pl.ds(start, block), :], memory_out, (memory_s, memory_r)
    )

    line_ref[...] = jnp.zeros_like(line_ref)
    line_ref[:group, :NB] = table_ref[...].astype(F32)
    tables_ref[me] = line_ref[:, : tables_ref.shape[2]].astype(BF16)
    links.greet()
    w1.start()
    heard = [
        remote(tables_ref.at[me], tables_ref.at[me], table_s.at[i], table_r.at[i], to)
        for i, to in enumerate((links.to_pair, links.to_far, links.to_cross))
    ]
    for copy in heard:
        copy.start()
    taken = [
        pltpu.make_async_copy(own_weights[i], self_full[i].at[me], local.at[i]) for i in range(3)
    ]
    taken += [
        pltpu.make_async_copy(own_weights[3 + i], cross_full[i].at[me], local.at[3 + i])
        for i in range(3)
    ]
    taken.append(
        pltpu.make_async_copy(memory_ref, mem_ref.at[:, pl.ds(start, block), :], local.at[6])
    )
    for copy in taken:
        copy.start()
    x = x_ref[...].astype(F32)
    n_ref[...] = (x * rms(x) * row(self_gain_ref)).astype(BF16)
    for s in range(seqs):
        nall_ref[s, pl.ds(start, block), :] = n_ref[s * block : (s + 1) * block, :]
    rows_one.start((0,))
    w1.arrive(0)
    w1.arrive(1)
    rows_one.start((1,))
    w1.arrive(2)
    for copy in heard:
        copy.wait_recv()
    build_bias(me, tables_ref, bias_ref, ext_ref, line_ref)
    for copy in taken:
        copy.wait()
    put = [
        pltpu.make_async_copy(cross_full[i].at[me], cross_out[i].at[me], placed.at[i])
        for i in range(3)
    ]
    put += [
        pltpu.make_async_copy(self_full[i].at[me], self_out[i].at[me], placed.at[3 + i])
        for i in range(3)
    ]
    put += [
        pltpu.make_async_copy(
            rows_memory.source(s), rows_memory.window(s, me), placed.at[6 + s]
        )
        for s in range(seqs)
    ]
    for copy in put:
        copy.start()
    rows_one.forward()
    for j in range(3):
        w1.share(j)
    def hold(i, j):
        plane = w1.planes[j]
        into, source = (self_full[i], self_out[i]) if i < 3 else (cross_full[i - 3], cross_out[i - 3])
        return pltpu.make_async_copy(source.at[plane], into.at[plane], held.at[i, j])

    for j in range(3):
        w1.finish(j)
        for i in range(3):
            hold(i, j).start()
    rows_one.finish()
    w2.start()

    def keep(i, h=None):
        if h is None:
            return pltpu.make_async_copy(kept[i], outs[i], done.at[i, 0])
        return pltpu.make_async_copy(kept[i].at[h], outs[i].at[h], done.at[i, h])

    for i in range(2):
        keep(i).start()
    for j in range(3):
        for i in range(3):
            hold(i, j).wait()

    def body(k, carry):
        h = links.owner(lax.rem(k + 3, shards))
        nk = nall_ref[...].reshape(seqs * full, -1)
        q_ref[h] = padded(nt(n_ref[...], self_full[0][h, 0]).astype(BF16), pw)
        k_ref[h] = padded(nt(nk, self_full[1][h, 0]).astype(BF16), pw)
        v_ref[h] = padded(nt(nk, self_full[1][h, 1]).astype(BF16), pw)
        for s in range(seqs):
            c, lse_ref[h, s] = head_context(
                q_ref[h, s * block : (s + 1) * block, :],
                k_ref[h, s * full : (s + 1) * full, :],
                v_ref[h, s * full : (s + 1) * full, :],
                bias_ref[pl.ds(h * group, group)].reshape(group * block, full).astype(F32),
                key < len_ref[s],
                lanes,
            )
            c_ref[h, s * block : (s + 1) * block, :] = c
        for i in range(2, 7):
            keep(i, h).start()

        @pl.when(k == 0)
        def _():
            w2.arrive(0)
            w2.arrive(1)
            rows_memory.start()

        @pl.when(k == 1)
        def _():
            w2.arrive(2)

        return carry

    lax.fori_loop(0, shards, body, 0)
    joined = jnp.concatenate([c_ref[h][:, :win] for h in range(shards)], axis=1)
    out_weight = self_full[2][...].reshape(shards * win, -1)
    y = x_ref[...].astype(F32) + nn(joined, out_weight)
    y_ref[...] = y
    n2_ref[...] = (y * rms(y) * row(cross_gain_ref)).astype(BF16)
    for j in range(3):
        w2.share(j)
    rows_memory.forward()
    for j in range(3):
        w2.finish(j)
        for i in range(3, 6):
            hold(i, j).start()
    for j in range(3):
        for i in range(3, 6):
            hold(i, j).wait()

    def ask(h, carry):
        q2_ref[h] = padded(nt(n2_ref[...], cross_full[0][h, 0]).astype(BF16), pw)
        return carry

    lax.fori_loop(0, shards, ask, 0)

    def bring(plane, j):
        rows = pl.ds(pl.multiple_of(plane * block, block), block)
        return pltpu.make_async_copy(
            memory_out.at[:, rows, :], mem_ref.at[:, rows, :], local.at[j]
        )

    for j, (plane, slot) in enumerate(((me, None), (links.far, 1), (links.pair, 0), (links.cross, 2))):
        if slot is not None:
            if slot != 1:
                rows_memory.take(slot)
            bring(plane, j).start()
            bring(plane, j).wait()
        first = pl.multiple_of(plane * block, block)
        m = mem_ref[:, pl.ds(first, block), :].reshape(rows, -1)

        def answer(h, carry, first=first, m=m):
            for into, which in ((k2_ref, 0), (v2_ref, 1)):
                value = padded(nt(m, cross_full[1][h, which]).astype(BF16), pw)
                for s in range(seqs):
                    into[h, pl.ds(s * full + first, block), :] = value[s * block : (s + 1) * block]
            return carry

        lax.fori_loop(0, shards, answer, 0)

    def cross_body(h, carry):
        for s in range(seqs):
            c, lse2_ref[h, s] = head_context(
                q2_ref[h, s * block : (s + 1) * block, :],
                k2_ref[h, s * full : (s + 1) * full, :],
                v2_ref[h, s * full : (s + 1) * full, :],
                None,
                key < enc_ref[s],
                lanes,
            )
            c2_ref[h, s * block : (s + 1) * block, :] = c
        for i in range(7, 12):
            keep(i, h).start()
        return carry

    lax.fori_loop(0, shards, cross_body, 0)
    joined = jnp.concatenate([c2_ref[h][:, :win] for h in range(shards)], axis=1)
    out_weight = cross_full[2][...].reshape(shards * win, -1)
    y2 = y_ref[...] + nn(joined, out_weight)
    y2_ref[...] = y2
    n3_ref[...] = (y2 * rms(y2) * row(feed_gain_ref)).astype(BF16)
    w1.drain()
    w2.drain()
    rows_one.drain()
    rows_memory.drain()
    for copy in heard:
        copy.wait_send()
    for copy in put:
        copy.wait()
    for i in range(2):
        keep(i).wait()
    for h in range(shards):
        for i in range(2, 12):
            keep(i, h).wait()


def front(lens, encs, x, gains, table, memory, weights, shards, group, size):
    rows, width = x.shape
    seqs = lens.shape[0]
    block = rows // seqs
    full, keys = block * shards, rows * shards
    win = group * size
    pw = -(-win // 128) * 128
    fulls = [((shards, *w.shape), BF16) for w in weights]
    kept = [((seqs, full, width), BF16), ((shards * group, block, full), BF16)]
    kept += [((shards, n, pw), BF16) for n in (rows, keys, keys, rows)]
    kept.append(((shards, seqs, block, 128), F32))
    kept += kept[2:]
    dma = pltpu.SemaphoreType.DMA
    anywhere = pl.BlockSpec(memory_space=pl.ANY)
    return pl.pallas_call(
        functools.partial(front_kernel, group, size),
        out_shape=[
            sds((rows, width), BF16),
            sds((rows, width), F32),
            sds((rows, width), BF16),
            sds((rows, width), F32),
            sds((rows, width), BF16),
            sds((seqs, full, width), BF16),
        ]
        + [sds(*a) for a in fulls + kept],
        in_specs=[smem()] * 2 + [vmem()] * 5 + [anywhere] * 7,
        out_specs=[vmem()] * 5 + [anywhere] * 19,
        scratch_shapes=[pltpu.VMEM(*a) for a in kept + fulls]
        + [
            pltpu.VMEM((shards, 8, 128), BF16),
            pltpu.VMEM((block, full + block), F32),
            pltpu.VMEM((8, 2 * block), F32),
            pltpu.VMEM((seqs, full, width), BF16),
            dma((3,)),
            dma((3,)),
            dma((seqs, 3)),
            dma((seqs, 3)),
            dma((seqs, 3)),
            dma((seqs, 3)),
            dma((7,)),
            dma((6 + seqs,)),
            dma((6, 3)),
            dma((len(kept), shards)),
        ]
        + Weights.scratch(3)
        + Weights.scratch(3),
        compiler_params=pltpu.CompilerParams(
            collective_id=0, has_side_effects=True, vmem_limit_bytes=VMEM_LIMIT
        ),
        name="front",
    )(lens, encs, x, *gains, table, memory, *weights)


class Rows:
    @staticmethod
    def scratch(rows, width):
        dma = pltpu.SemaphoreType.DMA
        return [
            pltpu.VMEM((4, rows, width), BF16),
            pltpu.VMEM((3, rows, width), BF16),
            dma((3,)),
            dma((3,)),
        ]

    count = 4

    def __init__(self, links, refs):
        self.links = links
        self.buf, self.rx, self.ss, self.rs = refs

    def copy(self, slot):
        links = self.links
        block = (links.cross, links.far, links.pair)[slot]
        device = (links.to_cross, links.to_far, links.to_pair)[slot]
        return remote(
            self.buf.at[block], self.rx.at[slot], self.ss.at[slot], self.rs.at[slot], device
        )

    def start(self):
        for slot in range(3):
            self.copy(slot).start()

    def finish(self):
        for slot in range(3):
            self.copy(slot).wait_recv()
        return sum(self.rx[slot].astype(F32) for slot in range(3))

    def drain(self):
        for slot in range(3):
            self.copy(slot).wait_send()


def head_grads(qw, kw, vw, dcw, lse_tile, bias, keep, lanes):
    block, group = qw.shape[0], len(lanes)
    qcat, dcat = stack_heads(qw, lanes), stack_heads(dcw, lanes)
    sc = nt(qcat, kw)
    if bias is not None:
        sc = sc + bias
    sc = jnp.where(keep, sc, NEG)
    lse = jnp.concatenate([lse_tile[:, a : a + 1] for a in range(group)], axis=0)
    p = jnp.exp(sc - lse)
    dp = nt(dcat, vw)
    ds = (p * (dp - jnp.sum(p * dp, axis=-1, keepdims=True))).astype(BF16)
    dq = join_heads(nn(ds, kw), lanes, block).astype(BF16)
    dk = tn(ds, qcat).astype(BF16)
    dv = tn(p.astype(BF16), dcat).astype(BF16)
    return ds, dq, dk, dv


def diagonal_line(near, far_sum):
    block, width = near.shape
    half = block // 2
    while half >= 8:
        near = near[:half] + pltpu.roll(near[half:], width - half, 1)
        half //= 2
    row8 = lax.broadcasted_iota(jnp.int32, (8, width), 0)
    for bit in (4, 2, 1):
        near = jnp.where((row8 & bit) != 0, pltpu.roll(near, width - bit, 1), near)
    line = jnp.sum(near, axis=0, keepdims=True)
    lane = lax.broadcasted_iota(jnp.int32, (1, width), 1)
    return line + jnp.where(lane == width - 1, far_sum, 0.0)


def linked_kernel(biased, group, size, order, *refs):
    len_ref, dy_ref, gain_ref, given_ref, *refs = refs
    held_count = 11 if biased else 10
    held, refs = refs[:held_count], refs[held_count:]
    if biased:
        feed_ref, x_ref, rows_ref, gain2_ref, gain3_ref, *refs = refs
        grad_ref, mem_ref, feed_out, given_out, own_out, small_out, *refs = refs
    else:
        feed_out_ref, y_ref, y2_ref, n3_ref, feed_gain_ref, *refs = refs
        dprev_ref, gg_ref, w_ref, later_ref, mem_ref, given_out, *refs = refs
        result_ref, gg3_ref, hid_out, *refs = refs
    buffers, held_sem, refs = refs[:held_count], refs[held_count], refs[held_count + 1 :]
    nq_ref, nk_ref, c_ref, wo_ref, q_ref, k_ref, v_ref, lse_ref, wq_ref, wkv_ref = buffers[:10]
    bias_ref = buffers[-1]
    dq_ref, dkv_ref, acck_ref, accq_ref, nqt_ref, nkt_ref, dat_ref, wtmp_ref, *refs = refs
    links = Links()
    sums = Sums(links, refs[: Sums.count])
    refs = refs[Sums.count :]
    if biased:
        feed_sums = Sums(links, refs[: Sums.count])
        refs = refs[Sums.count :]
    exchanges = []
    for _ in range(3 if biased else 1):
        exchanges.append(Rows(links, refs[: Rows.count]))
        refs = refs[Rows.count :]
    if biased:
        ds_ref, ext_ref, diag_ref, sr, ms, mr = refs
    else:
        cot_ref, feed_in_ref = dy_ref, given_ref
        w_sem, dy_ref, dn_ref, n3t_ref, ct_ref, wff_ref, hid_ref, win_ref, wout_ref, *refs = refs
        f_sem, hid_sem = refs
    shards, rows, pw = q_ref.shape
    seqs = len_ref.shape[0]
    block = rows // seqs
    full = k_ref.shape[1] // seqs
    win = group * size
    lanes = lane_groups(pw, group, size)
    key = lax.broadcasted_iota(jnp.int32, (1, full), 1)
    me = links.me
    start = pl.multiple_of(me * block, block)
    def fetch(j, h=None):
        if h is None:
            return pltpu.make_async_copy(held[j], buffers[j], held_sem.at[j, 0])
        part = pl.ds(h * group, group) if j == 10 else h
        return pltpu.make_async_copy(held[j].at[part], buffers[j].at[part], held_sem.at[j, h])

    links.greet()
    if biased:
        exchanges[0].buf[...] = rows_ref[...]
        exchanges[0].start()
        for place in range(AHEAD):
            sums.load(given_ref, place)
    else:
        part = wout_ref.shape[1]

        def feed_weights(k):
            columns = pl.ds(pl.multiple_of(links.owner(k) * part, part), part)
            slot = k % 2
            return (
                pltpu.make_async_copy(
                    feed_in_ref.at[:, :, columns], win_ref.at[slot], f_sem.at[slot, 0]
                ),
                pltpu.make_async_copy(
                    feed_out_ref.at[columns, :], wout_ref.at[slot], f_sem.at[slot, 1]
                ),
            )

        def hid_copy(k):
            return pltpu.make_async_copy(
                hid_ref.at[k % 2], hid_out.at[links.owner(k)], hid_sem.at[k]
            )

        for copy in feed_weights(0):
            copy.start()
    fetch(3).start()
    for k in range(shards):
        for j in range(4, held_count):
            fetch(j, links.owner(k)).start()
    for j in range(3):
        fetch(j).start()

    def stage(name, place):
        if name == "load":

            @pl.when(place < 4)
            def _():
                sums.load(given_ref, place)

            @pl.when(place >= 4)
            def _():
                feed_sums.load(feed_ref, place - 4)

            return
        if not biased:
            getattr(sums, name)(4 * (place % 2) + place // 2)
            return

        @pl.when(place < 4)
        def _():
            sums.core(place, given_ref) if name == "core" else getattr(sums, name)(place)

        @pl.when((place >= 4) & (place < 8))
        def _():
            c = place - 4
            if name == "core":
                feed_sums.core(c, feed_ref)
            else:
                getattr(feed_sums, name)(c)

        @pl.when(place >= 8)
        def _():
            getattr(sums, name)(place - 4)

    places = 12 if biased else sums.chunks
    late = (("core", 1), ("first", 3), ("second", 5), ("third", 7))
    if biased:
        late = (("load", -AHEAD), *late)

    def tick(t):
        for name, behind in late:
            place = t - behind

            @pl.when((place >= 0) & (place < (8 if name == "load" else places)))
            def _(name=name, place=place):
                stage(name, place)

    if not biased:
        share = nqt_ref.shape[0] // 8
        put_rows(n3t_ref, n3_ref[...].T, order)
        put_rows(ct_ref, cot_ref[...].T, order)
        dprev_ref[...] = y2_ref[...]
        dn_ref[...] = jnp.zeros_like(dn_ref)

        def feed_body(k, carry):
            @pl.when(k + 1 < shards)
            def _():
                for copy in feed_weights(k + 1):
                    copy.start()

            for copy in feed_weights(k):
                copy.wait()
            slot = k % 2
            w_gate, w_up, w_out = win_ref[slot, 0], win_ref[slot, 1], wout_ref[slot]
            hid, dg, du = feed_tile(n3_ref[...], cot_ref[...], w_gate, w_up, w_out)
            for item, right in enumerate((dg, du)):

                def rows_of(side, right=right):
                    rows = pl.ds(pl.multiple_of(side * 4 * share, 4 * share), 4 * share)
                    return nn(n3t_ref[rows, :], right).astype(BF16).reshape(2, 2, share, part)

                c = 4 * item + k
                wff_ref[c] = rows_of(1 - links.core)
                sums.over_core(c, wff_ref.at[c]).start()
                sums.own[c] = rows_of(links.core)

            @pl.when(k >= 2)
            def _():
                hid_copy(k - 2).wait()

            hid_ref[slot] = nn(ct_ref[...], hid).astype(BF16).reshape(2, 2, 2, share, part)
            hid_copy(k).start()
            dprev_ref[...] += nn(hid, w_out)
            dn_ref[...] += nt(dg, w_gate) + nt(du, w_up)
            tick(k)
            return carry

        lax.fori_loop(0, shards, feed_body, 0)
        result_ref[...] = dprev_ref[...].astype(BF16)
        dy, gg3_ref[...] = norm_grads(y2_ref[...], row(feed_gain_ref), dn_ref[...])
        dy_ref[...] = cot_ref[...].astype(F32) + dy

    da = dy_ref[...].astype(BF16)
    if biased:
        ext_ref[:, :block] = jnp.zeros((block, block), F32)
        far = lax.broadcasted_iota(jnp.int32, ext_ref.shape, 1) < start
    fetch(3).wait()
    first_tick = 0 if biased else shards

    for s in range(seqs):
        mine = slice(s * block, (s + 1) * block)
        theirs = slice(s * full, (s + 1) * full)
        if s == seqs - 1:
            for j in (0, 2) if biased else range(3):
                fetch(j).wait()
            put_rows(nqt_ref, nq_ref[...].T, order)
            put_rows(nkt_ref, nk_ref[...].T, order)
            put_rows(dat_ref, da.T, order)

        def body(k, carry):
            h = links.owner(k)
            if s == 0:
                for j in range(4, held_count):
                    fetch(j, h).wait()
            wo_h = wo_ref[pl.ds(pl.multiple_of(h * win, size), win), :]
            dcw = padded(nt(da[mine], wo_h).astype(BF16), pw)
            bias = None
            if biased:
                bias = bias_ref[pl.ds(h * group, group)].reshape(group * block, full).astype(F32)
            ds, dq, dk, dv = head_grads(
                q_ref[h, mine, :],
                k_ref[h, theirs, :],
                v_ref[h, theirs, :],
                dcw,
                lse_ref[h, s],
                bias,
                key < len_ref[s],
                lanes,
            )
            dkv = jnp.concatenate([dk[:, :win], dv[:, :win]], axis=1)
            dkv_ref[h, theirs, :] = dkv
            dq_ref[h, mine, :] = dq
            kv_term = nn(dkv[:, :win], wkv_ref[h, 0]) + nn(dkv[:, win:], wkv_ref[h, 1])
            q_term = nn(dq[:, :win], wq_ref[h])

            @pl.when(k == 0)
            def _():
                acck_ref[...] = kv_term
                accq_ref[mine, :] = q_term

            @pl.when(k != 0)
            def _():
                acck_ref[...] += kv_term
                accq_ref[mine, :] += q_term

            if biased and s < seqs - 1:
                ds_ref[h] = ds if s == 0 else ds_ref[h] + ds
            if biased and s == seqs - 1:
                whole = ds_ref[h].astype(F32) + ds.astype(F32)
                for a in range(group):
                    ext_ref[:, block:] = whole[a * block : (a + 1) * block, :]
                    far_sum = jnp.sum(jnp.where(far, ext_ref[...], 0.0))
                    near = ext_ref[:, pl.ds(start, 2 * block)]
                    diag_ref[pl.ds(h * group + a, 1), :] = diagonal_line(near, far_sum)
            if s == seqs - 1:
                dkv = dkv_ref[h]

                def weight_rows(side):
                    rows = pl.ds(pl.multiple_of(side * 4 * w_rows, 4 * w_rows), 4 * w_rows)
                    return jnp.concatenate(
                        [
                            nn(nkt_ref[rows, :], dkv).astype(BF16),
                            nn(nqt_ref[rows, :], dq_ref[h][:, :win]).astype(BF16),
                            nn(dat_ref[rows, :], c_ref[h][:, :win]).astype(BF16),
                        ],
                        axis=1,
                    ).reshape(2, 2, w_rows, 4 * win)

                if biased:
                    wtmp_ref[k] = weight_rows(1 - links.core)
                    sums.over_core(4 + k, wtmp_ref.at[k]).start()
                    sums.own[4 + k] = weight_rows(links.core)
                else:
                    for side in range(2):
                        wtmp_ref[h, side] = weight_rows(side)
                    pltpu.make_async_copy(wtmp_ref.at[h], w_ref.at[h], w_sem.at[h]).start()
            tick(first_tick + 4 * s + k)
            return carry

        w_rows = nqt_ref.shape[0] // 8
        lax.fori_loop(0, shards, body, 0)
        if biased:
            acck_ref[pl.ds(start, block), :] += accq_ref[mine, :]
            total = acck_ref[...]
            if s == 0:
                fetch(1).wait()
            part = jnp.sum(total * nk_ref[theirs, :].astype(F32), axis=0, keepdims=True)
            gain1 = part if s == 0 else gain1 + part
            mover = exchanges[1 + s]
            mover.buf[...] = total.astype(BF16).reshape(shards, block, -1)
            mover.start()
            grad_ref[mine, :] = acck_ref[pl.ds(start, block), :]
        elif s == 0:
            exchanges[0].buf[...] = acck_ref[...].astype(BF16).reshape(shards, block, -1)
            exchanges[0].start()
            mem_ref[...] = acck_ref[pl.ds(start, block), :]
        else:
            later_ref[...] = acck_ref[...].astype(BF16).reshape(shards, block, -1)

    steps = range(first_tick + 4 * seqs, places + late[-1][1])
    if not biased:
        dy, gg = norm_grads(y_ref[...], row(gain_ref), accq_ref[...])
        dprev_ref[...] = dy_ref[...] + dy
        gg_ref[...] = gg
        for t in steps:
            tick(t)
        mem_ref[...] += exchanges[0].finish()
        for item in range(2):
            given_out[item] = sums.finish(item)
        for h in range(shards):
            pltpu.make_async_copy(wtmp_ref.at[h], w_ref.at[h], w_sem.at[h]).wait()
        for k in range(2, shards):
            hid_copy(k).wait()
    else:
        gain1 = gain1 / row(gain_ref)
        width = gain1.shape[1]
        diag_ref[shards * group :, :] = jnp.zeros_like(diag_ref[shards * group :, :])
        sr[0, : diag_ref.shape[0], :] = diag_ref[...]
        sr[0, diag_ref.shape[0] :, :] = jnp.zeros_like(sr[0, diag_ref.shape[0] :, :])
        for i, line in enumerate((gain1, gain2_ref[...], gain3_ref[...])):
            for j in range(width // (2 * block)):
                at = diag_ref.shape[0] + i * width // (2 * block) + j
                sr[0, at : at + 1, :] = line[:, j * 2 * block : (j + 1) * 2 * block]
        plane = 2 + 2 * links.y + links.x
        hops = [(1, 0, links.over_core)]
        hops += [(plane, plane, to) for to in (links.over_x, links.over_y, links.over_plane)]
        hops += [(6 + me, 6 + me, to) for to in (links.to_pair, links.to_far, links.to_cross)]

        def hop(i):
            into, source, to = hops[i]
            return remote(sr.at[source], sr.at[into], ms.at[i], mr.at[i], to)

        hop(0).start()
        for i, t in enumerate(steps):
            tick(t)
            if i == 1:
                hop(0).wait_recv()
                sr[plane] = sr[0] + sr[1]
                for j in (1, 2, 3):
                    hop(j).start()
            if i == 3:
                for j in (1, 2, 3):
                    hop(j).wait_recv()
                sr[6 + me] = (sr[2] + sr[3]) + (sr[4] + sr[5])
                for j in (4, 5, 6):
                    hop(j).start()
        for j in (4, 5, 6):
            hop(j).wait_recv()
        small_out[...] = (sr[6] + sr[7]) + (sr[8] + sr[9])
        mem_ref[...] = exchanges[0].buf[me].astype(F32) + exchanges[0].finish()
        feed_out[...] = feed_sums.finish(0)
        given_out[...] = sums.finish(0)
        for s in range(seqs):
            mine = slice(s * block, (s + 1) * block)
            dn = grad_ref[mine, :] + exchanges[1 + s].finish()
            dx, _ = norm_grads(x_ref[mine, :].astype(F32), row(gain_ref), dn)
            grad_ref[mine, :] = dy_ref[mine, :] + dx
        own_out[...] = sums.finish(1)
        for i in range(len(hops)):
            hop(i).wait_send()
    for mover in exchanges:
        mover.drain()
    sums.drain()
    if biased:
        feed_sums.drain()


def linked_backward(lens, nq, nk, saved, wq, wkv, wo, dy, gain, given, extras, biased, group, size, order):
    q, k, v, c, lse = saved
    rows, width = nq.shape
    shards, keys, pw = k.shape
    seqs = lens.shape[0]
    block, full, win = rows // seqs, keys // seqs, group * size
    cols = 4 * win
    share = width // 8
    held = [nq, nk, c, wo, q, k, v, lse, wq, wkv]
    if biased:
        held.append(extras[1])
        extras = [extras[0], *extras[2:]]
        part = extras[0].shape[-1]
    else:
        part = given.shape[2] // shards
    args = [lens, dy, gain, given, *held, *extras]
    if biased:
        lines = -(-3 * width // (2 * block) // 8) * 8
        diag_rows = -(-shards * group // 8) * 8
        out_shape = [
            sds((rows, width), F32),
            sds((block, width), F32),
            sds((share, part), F32),
            sds((share, cols), F32),
            sds((share, cols), F32),
            sds((diag_rows + lines, 2 * block), F32),
        ]
    else:
        out_shape = [
            sds((rows, width), F32),
            sds((1, width), F32),
            sds((shards, 2, 2, 2, share, cols), BF16),
            sds((shards, block, width), BF16),
            sds((block, width), F32),
            sds((2, share, part), F32),
            sds((rows, width), BF16),
            sds((1, width), F32),
            sds((shards, 2, 2, 2, share, part), BF16),
        ]
    scratch = [pltpu.VMEM(a.shape, a.dtype) for a in held]
    scratch += [
        pltpu.SemaphoreType.DMA((len(held), shards)),
        pltpu.VMEM((shards, rows, pw), BF16),
        pltpu.VMEM((shards, keys, 2 * win), BF16),
        pltpu.VMEM((full, width), F32),
        pltpu.VMEM((rows, width), F32),
        pltpu.VMEM((width, rows), BF16),
        pltpu.VMEM((width, keys), BF16),
        pltpu.VMEM((width, rows), BF16),
    ]
    scratch.append(pltpu.VMEM((shards, *(() if biased else (2,)), 2, 2, share, cols), BF16))
    scratch += Sums.scratch(8, share, cols if biased else part)
    if biased:
        scratch += Sums.scratch(4, share, part)
    for _ in range(3 if biased else 1):
        scratch += Rows.scratch(block, width)
    dma = pltpu.SemaphoreType.DMA
    if biased:
        scratch += [
            pltpu.VMEM((shards, group * block, full), BF16),
            pltpu.VMEM((block, full + block), F32),
            pltpu.VMEM((diag_rows, 2 * block), F32),
            pltpu.VMEM((10, diag_rows + lines, 2 * block), F32),
            dma((7,)),
            dma((7,)),
        ]
    else:
        scratch += [
            dma((shards,)),
            pltpu.VMEM((rows, width), F32),
            pltpu.VMEM((rows, width), F32),
            pltpu.VMEM((width, rows), BF16),
            pltpu.VMEM((width, rows), BF16),
            pltpu.VMEM((8, 2, 2, share, part), BF16),
            pltpu.VMEM((2, 2, 2, 2, share, part), BF16),
            pltpu.VMEM((2, 2, width, part), BF16),
            pltpu.VMEM((2, part, width), BF16),
            dma((2, 2)),
            dma((shards,)),
        ]
    anywhere = pl.BlockSpec(memory_space=pl.ANY)
    in_specs = [smem(), vmem(), vmem(), anywhere] + [anywhere] * len(held)
    in_specs += [anywhere] + [vmem()] * (len(extras) - 1)
    out_specs = [vmem()] * len(out_shape)
    if not biased:
        out_specs[2] = out_specs[-1] = anywhere
    return pl.pallas_call(
        functools.partial(linked_kernel, biased, group, size, order),
        out_shape=out_shape,
        in_specs=in_specs,
        out_specs=out_specs,
        scratch_shapes=scratch,
        compiler_params=pltpu.CompilerParams(
            collective_id=2 if biased else 1, has_side_effects=True, vmem_limit_bytes=VMEM_LIMIT
        ),
        name="self_backward" if biased else "cross_backward",
    )(*args)


def arrange_kernel(
    shards, group, win, me_ref, grad_ref, first_ref, last_ref, gates_ref, hid_ref, cross_ref,
    self_ref, small_ref, grad_out, mem_out, gates_out, hid_out, table_out, *refs,
):
    gain_outs, weight_outs = refs[:3], refs[3:]
    grad_out[...] = grad_ref[...].reshape(grad_out.shape)
    mem_out[0] = first_ref[...]
    mem_out[1] = last_ref[...]
    gates_out[...] = gates_ref[...]
    hid_out[...] = hid_ref[...]
    for i, w_ref in enumerate((self_ref, cross_ref)):
        q_out, kv_out, o_out = weight_outs[3 * i : 3 * i + 3]
        w = w_ref[...]
        kv_out[0] = w[:, :win]
        kv_out[1] = w[:, win : 2 * win]
        q_out[...] = w[:, 2 * win : 3 * win]
        o_out[...] = w[:, 3 * win :].T
    head_rows = -(-shards * group // 8) * 8
    span = small_ref.shape[1]
    heads = lax.broadcasted_iota(jnp.int32, (8, head_rows), 0) + me_ref[0] * group
    pick = (heads == lax.broadcasted_iota(jnp.int32, (8, head_rows), 1)).astype(F32)
    mine = jnp.dot(pick, small_ref[:head_rows, :], precision=highest)
    onehot = bucket_rows(span // 2, NB).astype(F32)
    sums = lax.dot_general(mine, onehot, (((1,), (1,)), ((), ())), precision=highest)
    table_out[...] = sums[:group, :]
    for i, gain_out in enumerate(gain_outs):
        lines = [
            small_ref[head_rows + i * gain_out.shape[0] // span + j, :]
            for j in range(gain_out.shape[0] // span)
        ]
        gain_out[...] = jnp.concatenate(lines)


def arranged(
    me, result, grad, first, last, gates, hid, cross_w, self_w, small, shards, group, win
):
    rows, width = grad.shape
    block = first.shape[0]
    share, part = hid.shape
    weights = [sds((share, win), F32), sds((2, share, win), F32), sds((win, share), F32)]
    grad, mem, gates, hid, table, gain1, gain2, gain3, *weights = pl.pallas_call(
        functools.partial(arrange_kernel, shards, group, win),
        out_shape=[
            sds((rows // block, block, width), F32),
            sds((rows // block, block, width), F32),
            sds(gates.shape, F32),
            sds((share, part), F32),
            sds((group, NB), F32),
            sds((width,), F32),
            sds((width,), F32),
            sds((width,), F32),
            *weights,
            *weights,
        ],
        in_specs=[smem()] + [vmem()] * 8,
        out_specs=[vmem()] * 14,
        compiler_params=params(),
        name="arrange",
    )(me, grad, first, last, gates, hid, cross_w, self_w, small)
    result = result.reshape(grad.shape)
    return (
        result, grad, mem, gain1, *weights[:3], table.T, gain2, *weights[3:], gain3, gates, hid.T
    )


def per_device(
    layer_input,
    memory,
    dec_lengths,
    enc_lengths,
    self_gain,
    self_query,
    self_key_value,
    self_out,
    rel_bias,
    cross_gain,
    cross_query,
    cross_key_value,
    cross_out,
    feed_gain,
    feed_in,
    feed_out,
    out_cotangent,
):
    shards = lax.axis_size("head")
    me = lax.axis_index("head").astype(jnp.int32).reshape(1)
    batch_count = lax.axis_size("batch")
    seqs, block, width = layer_input.shape
    group = rel_bias.shape[1]
    size = self_query.shape[1] // group
    win = group * size
    full = block * shards
    enc_full = memory.shape[1] * shards
    rows = seqs * block
    part = feed_in.shape[2] // shards
    sg = self_gain.astype(F32).reshape(1, width)

    x = layer_input.reshape(rows, width)
    x32 = x.astype(F32)
    tight = batch_count == 8 and shards == 4 and seqs == 2
    order = tuple((i % 2) * 4 + i // 2 for i in range(8)) if tight else (0,)
    table = rel_bias.T
    flip = lambda w: jnp.swapaxes(w, -1, -2)
    weights = [flip(self_query)[None], flip(self_key_value), self_out[None]]
    weights += [flip(cross_query)[None], flip(cross_key_value), cross_out[None]]
    onehot = near_onehot(block)
    if tight:
        n1, y1, n2, y2, n3, memory_all, wq1, wkv1, wo1, wq2, wkv2, wo2, n1_all, bias, *saved = front(
            dec_lengths, enc_lengths, x, (self_gain, cross_gain, feed_gain), table, memory, weights,
            shards, group, size,
        )
        saved1, saved2 = saved[:5], saved[5:]
        n1_all = n1_all.reshape(seqs * full, width)
    else:
        n1 = (x32 * rms(x32) * sg).astype(BF16)
        n1_all = lax.all_gather(n1.reshape(seqs, block, width), "head", axis=1, tiled=True)
        n1_all = n1_all.reshape(seqs * full, width)
        wq1, wkv1, wo1, wq2, wkv2, wo2 = [lax.all_gather(w, "head", axis=0) for w in weights]
        table = jnp.pad(table, ((0, 8 - group), (0, 128 - NB)))
        tables = lax.all_gather(table, "head", axis=0)
        bias = bias_tiles(me, tables, group, block, full)
        memory_all = lax.all_gather(memory, "head", axis=1, tiled=True)
    memory_all = memory_all.reshape(seqs * enc_full, width)
    wq1, wq2 = wq1[:, 0], wq2[:, 0]
    wo1, wo2 = wo1.reshape(width, width), wo2.reshape(width, width)
    if not tight:
        *saved1, y1, n2 = attend_forward(
            dec_lengths, n1, n1_all, x, wq1, wkv1, wo1, cross_gain, bias, group, size
        )
        *saved2, y2, n3 = attend_forward(
            enc_lengths, n2, memory_all, y1, wq2, wkv2, wo2, feed_gain, None, group, size
        )
    gain_rows = width // (2 * block)
    cot = out_cotangent.reshape(rows, width)
    if tight:
        (
            dy1, gain2, cross_w, memory_later, memory_first, feed_in_grad, result, gain3, hid_w,
        ) = linked_backward(
            enc_lengths, n2, memory_all, saved2, wq2, wkv2, wo2, cot, cross_gain, feed_in,
            [feed_out, y1, y2, n3, feed_gain], False, group, size, order,
        )
        input_grad, memory_last, feed_out_grad, cross_w, self_w, small = linked_backward(
            dec_lengths, n1, n1_all, saved1, wq1, wkv1, wo1, dy1, self_gain, cross_w,
            [hid_w, bias, x, memory_later, gain2, gain3], True, group, size, order,
        )
        return arranged(
            me, result, input_grad, memory_first, memory_last, feed_in_grad, feed_out_grad,
            cross_w, self_w, small, shards, group, win,
        )
    else:
        result, dy2, gain3, feed_w = feed(
            y2, n3, cot, feed_in, feed_out, feed_gain, shards, order
        )
        memory_part, gain2, cross_w, dy1 = attend_backward(
            enc_lengths, me, n2, memory_all, saved2, wq2, wkv2, wo2, dy2, cross_gain, y1,
            False, group, size, order,
        )
        input_part, gain1, self_w, diag = attend_backward(
            dec_lengths, me, n1, n1_all, saved1, wq1, wkv1, wo1, dy1, self_gain, bias,
            True, group, size, order,
        )
        memory_grad = lax.psum_scatter(
            memory_part.reshape(seqs, enc_full, width), "head", scatter_dimension=1, tiled=True
        ).astype(F32)
        dn1 = lax.psum_scatter(
            input_part.reshape(seqs, full, width), "head", scatter_dimension=1, tiled=True
        ).astype(F32)
        feed_w, cross_w, self_w = (
            lax.psum_scatter(
                w.reshape(shards * width, w.shape[2]).astype(F32),
                ("head", "batch"),
                scatter_dimension=0,
                tiled=True,
            )
            for w in (feed_w, cross_w, self_w)
        )
        lines = jnp.concatenate([gain1, gain2, gain3], axis=0).reshape(-1, 2 * block)
        diag, lines = lax.psum((diag, lines), ("batch", "head"))
        dx, _ = norm_grads(x32, sg, dn1.reshape(rows, width))
        input_grad = dy1 + dx
        feed_in_grad = jnp.stack([feed_w[:, :part], feed_w[:, part : 2 * part]])
        feed_out_grad = feed_w[:, 2 * part :]
    gains = lines[: 3 * gain_rows].reshape(3, width)
    diag = lax.dynamic_slice_in_dim(diag, me[0] * group, group, 0)
    table_grad = jnp.einsum("tb,ht->bh", onehot, diag, precision=highest)

    def split(w):
        kv = jnp.stack([w[:, :win], w[:, win : 2 * win]])
        return w[:, 2 * win : 3 * win], kv, w[:, 3 * win :].T

    self_q, self_kv, self_o = split(self_w)
    cross_q, cross_kv, cross_o = split(cross_w)
    return (
        result.reshape(seqs, block, width),
        input_grad.reshape(seqs, block, width),
        memory_grad,
        gains[0],
        self_q,
        self_kv,
        self_o,
        table_grad,
        gains[1],
        cross_q,
        cross_kv,
        cross_o,
        gains[2],
        feed_in_grad,
        feed_out_grad.T,
    )


def solution(mesh):
    return jax.shard_map(
        per_device,
        mesh=mesh,
        in_specs=(
            P("batch", "head", None),
            P("batch", "head", None),
            P("batch"),
            P("batch"),
            P(),
            P(None, "head"),
            P(None, None, "head"),
            P("head", None),
            P(None, "head"),
            P(),
            P(None, "head"),
            P(None, None, "head"),
            P("head", None),
            P(),
            P(),
            P(),
            P("batch", "head", None),
        ),
        out_specs=(
            P("batch", "head", None),
            P("batch", "head", None),
            P("batch", "head", None),
            P(),
            P("batch", "head"),
            P(None, "batch", "head"),
            P("head", "batch"),
            P(None, "head"),
            P(),
            P("batch", "head"),
            P(None, "batch", "head"),
            P("head", "batch"),
            P(),
            P(None, "batch", "head"),
            P("head", "batch"),
        ),
        check_vma=False,
    )
```
